32 devices in a mesh: dp: 8 (over y, x, core), seq: 4 (over z).
Axes of the slice: x: 2, y: 2, z: 4, core: 2. Of those that a mesh axis runs over, the one named last changes fastest.
Arguments:
- x_in: bfloat16 [8, 1024, 1024], P('dp', 'seq'), may hold values from -6 to 6
- w_qkv: bfloat16 [1024, 3072], P(('dp', 'seq')), may hold values from -0.25 to 0.25
- q_bias: bfloat16 [1024], P(('dp', 'seq')), may hold values from -3 to 3
- v_bias: bfloat16 [1024], P(('dp', 'seq')), may hold values from -3 to 3
- w_out: bfloat16 [1024, 1024], P(('dp', 'seq')), may hold values from -0.75 to 0.75
- out_bias: bfloat16 [1024], P(('dp', 'seq')), may hold values from -3 to 3
- ln1_gain: bfloat16 [1024], P(('dp', 'seq')), may hold values from 0.5 to 1.5
- ln1_shift: bfloat16 [1024], P(('dp', 'seq')), may hold values from -3 to 3
- w_up: bfloat16 [1024, 4096], P(('dp', 'seq')), may hold values from -0.1875 to 0.1875
- up_bias: bfloat16 [4096], P(('dp', 'seq')), may hold values from -3 to 3
- w_down: bfloat16 [4096, 1024], P(('dp', 'seq')), may hold values from -0.125 to 0.125
- down_bias: bfloat16 [1024], P(('dp', 'seq')), may hold values from -3 to 3
- ln2_gain: bfloat16 [1024], P(('dp', 'seq')), may hold values from 0.5 to 1.5
- ln2_shift: bfloat16 [1024], P(('dp', 'seq')), may hold values from -3 to 3
- valid: int32 [8], P('dp'), may hold values from 513 to 1024, as said below
- cotangent: bfloat16 [8, 1024, 1024], P('dp', 'seq'), may hold values from -6 to 6
Outputs:
- output: bfloat16 [8, 1024, 1024], P('dp', 'seq')
- grad_in: bfloat16 [8, 1024, 1024], P('dp', 'seq')
- grad_w_qkv: float32 [1024, 3072], P(('dp', 'seq'))
- grad_q_bias: float32 [1024], P(('dp', 'seq'))
- grad_v_bias: float32 [1024], P(('dp', 'seq'))
- grad_w_out: float32 [1024, 1024], P(('dp', 'seq'))
- grad_out_bias: float32 [1024], P(('dp', 'seq'))
- grad_ln1_gain: float32 [1024], P(('dp', 'seq'))
- grad_ln1_shift: float32 [1024], P(('dp', 'seq'))
- grad_w_up: float32 [1024, 4096], P(('dp', 'seq'))
- grad_up_bias: float32 [4096], P(('dp', 'seq'))
- grad_w_down: float32 [4096, 1024], P(('dp', 'seq'))
- grad_down_bias: float32 [1024], P(('dp', 'seq'))
- grad_ln2_gain: float32 [1024], P(('dp', 'seq'))
- grad_ln2_shift: float32 [1024], P(('dp', 'seq'))
The draws below stay inside these ranges and needn't reach their ends.
Inputs may be any that keep to these rules, and one draw needn't show every extreme that they name: `valid`: at least half of each page's tokens are unpadded; some page has no padding.
All inputs are finite; a program needn't handle non-finite values.
Results may differ from the reference program's by a relative error of at most 0.022.
Values may be sent and summed in bfloat16 or wider, within the bound.
A program may use at most 192 MiB of HBM per device.

```python
import math
import jax
import jax.numpy as jnp
from jax import lax

D = 1024
HEADS = 16
FF = 4096
PAGES = 8
STREAM = 1024
QROWS = 512


def draw_valid(key, part):
    padding = jax.random.randint(jax.random.fold_in(key, 21), (PAGES,), 0, STREAM // 2, dtype=jnp.int32)
    full_page = jax.random.randint(jax.random.fold_in(key, 22), (), 0, PAGES, dtype=jnp.int32)
    counts = STREAM - padding
    return jnp.where(jnp.arange(PAGES, dtype=jnp.int32) == full_page, STREAM, counts).astype(jnp.int32)


def shard_levels(rng, dims, pieces, least, high):
    factor_of = 1.0
    for position, blocks in pieces:
        heights = jax.random.uniform(jax.random.fold_in(jax.random.fold_in(rng, 6), position), (blocks,), jnp.float32, least / len(pieces), high / len(pieces))
        factor_of = factor_of * jnp.repeat(jnp.exp(heights), dims[position] // blocks).reshape((-1,) + (1,) * (len(dims) - 1 - position))
    return factor_of


def bell_draw(own_key, shape, scale, most, pieces=(), kind=jnp.bfloat16):
    values = jax.random.normal(own_key, shape, jnp.float32) * scale
    if len(pieces) > 0:
        values = shard_levels(own_key, shape, pieces, -0.22, 0.18) * values
    return jnp.clip(values, min=-most, max=most).astype(kind)


def setup_inputs(seed: int = 0) -> dict:
    keys = jax.random.split(jax.random.key(seed), 17)
    return {
        "x_in": bell_draw(keys[0], (PAGES, STREAM, D), 1.0, 6.0, ((0, 8), (1, 4))),
        "w_qkv": bell_draw(keys[1], (D, 3 * D), (D // 2) ** -0.5, 0.25, ((0, 32),)),
        "q_bias": bell_draw(keys[2], (D,), 0.5, 3.0, ((0, 32),)),
        "v_bias": bell_draw(keys[3], (D,), 0.5, 3.0, ((0, 32),)),
        "w_out": bell_draw(keys[4], (D, D), (D // 16) ** -0.5, 0.75, ((0, 32),)),
        "out_bias": bell_draw(keys[5], (D,), 0.5, 3.0, ((0, 32),)),
        "ln1_gain": jnp.clip(1.0 + 0.1 * jax.random.normal(keys[6], (D,), jnp.float32), 0.5, 1.5).astype(jnp.bfloat16),
        "ln1_shift": bell_draw(keys[7], (D,), 0.5, 3.0, ((0, 32),)),
        "w_up": bell_draw(keys[8], (D, FF), D ** -0.5, 0.1875, ((0, 32),)),
        "up_bias": bell_draw(keys[9], (FF,), 0.5, 3.0, ((0, 32),)),
        "w_down": bell_draw(keys[10], (FF, D), (FF // 2) ** -0.5, 0.125, ((0, 32),)),
        "down_bias": bell_draw(keys[11], (D,), 0.5, 3.0, ((0, 32),)),
        "ln2_gain": jnp.clip(1.0 + 0.1 * jax.random.normal(keys[12], (D,), jnp.float32), 0.5, 1.5).astype(jnp.bfloat16),
        "ln2_shift": bell_draw(keys[13], (D,), 0.5, 3.0, ((0, 32),)),
        "valid": draw_valid(jax.random.fold_in(keys[16], 71), 0),
        "cotangent": bell_draw(keys[15], (PAGES, STREAM, D), 1.0, 6.0, ((0, 8), (1, 4))),
    }


eps_norm = 1e-05

@jax.custom_vjp
def low(v):
    return lax.optimization_barrier(v.astype(jnp.bfloat16)).astype(jnp.float32)

@jax.custom_vjp
def low_back(v):
    return v

def low_keep(v):
    return (low(v), None)

def low_pass(kept, grad):
    return (grad,)

def back_keep(v):
    return (v, None)

def back_low(kept, grad):
    return (low(grad),)
low.defvjp(low_keep, low_pass)
low_back.defvjp(back_keep, back_low)

def dense(left, right):
    return jnp.dot(left, right, precision=lax.Precision.HIGHEST, preferred_element_type=jnp.float32)

def layer_norm(rows, gain, shift):
    center = rows - lax.optimization_barrier(jnp.mean(rows, axis=-1, keepdims=True))
    spread = lax.optimization_barrier(jnp.mean(center * center, axis=-1, keepdims=True))
    return center * lax.rsqrt(spread + eps_norm) * gain + shift

def forward(rows, weights, limit):
    w_qkv, q_bias, v_bias, w_out, out_bias, ln1_gain, ln1_shift, w_up, up_bias, w_down, down_bias, ln2_gain, ln2_shift = weights
    width = rows.shape[1]
    head_dim = width // HEADS
    scale = 1.0 / math.sqrt(head_dim)
    bias_row = jnp.concatenate([q_bias, jnp.zeros_like(q_bias), v_bias])
    project = low(low_back(dense(rows, w_qkv) + bias_row))
    shaped = project.reshape(STREAM, 3, HEADS, head_dim)
    queries = shaped[:, 0].reshape(STREAM // QROWS, QROWS, HEADS, head_dim)
    key_rows = shaped[:, 1]
    value_rows = shaped[:, 2]
    keep = jnp.arange(STREAM, dtype=jnp.int32) < limit

    def attend(query):
        scores = jnp.einsum('qhd,khd->hqk', query, key_rows, precision=lax.Precision.HIGHEST) * scale
        scores = low_back(scores)
        scores = jnp.where(keep[None, None, :], scores, -1e+30)
        peak = lax.optimization_barrier(jnp.max(scores, axis=-1, keepdims=True))
        raised = jnp.exp(scores - peak)
        probs = low(raised / lax.optimization_barrier(jnp.sum(raised, axis=-1, keepdims=True)))
        return jnp.einsum('hqk,khd->qhd', probs, value_rows, precision=lax.Precision.HIGHEST)
    context = lax.map(jax.checkpoint(attend), queries)
    context = low(low_back(context.reshape(rows.shape[0], width)))
    attn_out = low_back(dense(context, w_out) + out_bias)
    hidden = layer_norm(rows + attn_out, ln1_gain, ln1_shift)
    up_act = low_back(dense(low(hidden), w_up) + up_bias)
    gelu_low = low(jax.nn.gelu(up_act, approximate=False))
    branch = low_back(dense(gelu_low, w_down) + down_bias)
    return layer_norm(hidden + branch, ln2_gain, ln2_shift)

def reference(x_in, w_qkv, q_bias, v_bias, w_out, out_bias, ln1_gain, ln1_shift, w_up, up_bias, w_down, down_bias, ln2_gain, ln2_shift, valid, cotangent):
    weights = tuple((item.astype(jnp.float32) for item in (w_qkv, q_bias, v_bias, w_out, out_bias, ln1_gain, ln1_shift, w_up, up_bias, w_down, down_bias, ln2_gain, ln2_shift)))

    def one_page(total, inputs):
        rows_in, cot_rows, limit = inputs

        def run(rows_now, weights_now):
            return forward(rows_now, weights_now, limit)
        result, pull = jax.vjp(run, rows_in.astype(jnp.float32), weights)
        grad_rows, grad_weights = pull(cot_rows.astype(jnp.float32))
        total = jax.tree.map(lambda a, b: a + b, total, grad_weights)
        return (total, (result.astype(jnp.bfloat16), grad_rows.astype(jnp.bfloat16)))
    zeros = jax.tree.map(jnp.zeros_like, weights)
    total, (output, grad_in) = lax.scan(one_page, zeros, (x_in, cotangent, valid))
    return (output, grad_in, total[0], total[1], total[2], total[3], total[4], total[5], total[6], total[7], total[8], total[9], total[10], total[11], total[12])
```

```python
import math

import jax
import jax.numpy as jnp
from jax import lax
from jax.experimental import pallas as pl
from jax.experimental.pallas import tpu as pltpu
from jax.sharding import PartitionSpec as P

HEADS = 16


eps_norm = 1e-05


def outer_sum(left, right):
    return lax.dot_general(
        left, right, (((0,), (0,)), ((), ())), preferred_element_type=jnp.float32
    )


def times_back(rows, matrix):
    return lax.dot_general(
        rows, matrix, (((1,), (1,)), ((), ())), preferred_element_type=jnp.float32
    )


def gelu_exact(values):
    return jax.nn.gelu(values, approximate=False)


def norm_forward(rows, gain, shift):
    center = rows - jnp.mean(rows, axis=-1, keepdims=True)
    inv_std = lax.rsqrt(jnp.mean(center * center, axis=-1, keepdims=True) + eps_norm)
    normed = center * inv_std
    return (normed * gain + shift, normed, inv_std)


def norm_backward(grad_out, normed, inv_std, gain):
    scaled = grad_out * gain
    grad_rows = inv_std * (
        scaled
        - jnp.mean(scaled, axis=-1, keepdims=True)
        - normed * jnp.mean(scaled * normed, axis=-1, keepdims=True)
    )
    return (grad_rows, jnp.sum(grad_out * normed, axis=0), jnp.sum(grad_out, axis=0))


def to_heads(rows, groups):
    count, width = rows.shape
    return rows.reshape(count, groups, width // groups).transpose(1, 0, 2).reshape(groups, -1)


def from_heads(pieces, part_width):
    groups = pieces.shape[0]
    return (
        pieces.reshape(groups, -1, part_width).transpose(1, 0, 2).reshape(-1, groups * part_width)
    )


def general_plan(
    x_in,
    w_qkv,
    q_bias,
    v_bias,
    w_out,
    out_bias,
    ln1_gain,
    ln1_shift,
    w_up,
    up_bias,
    w_down,
    down_bias,
    ln2_gain,
    ln2_shift,
    valid,
    cotangent,
):
    shards = (
        w_qkv,
        q_bias,
        v_bias,
        w_out,
        out_bias,
        ln1_gain,
        ln1_shift,
        w_up,
        up_bias,
        w_down,
        down_bias,
        ln2_gain,
        ln2_shift,
    )
    weights = (
        lax.all_gather(shards[0], ("dp", "seq"), axis=0, tiled=True),
        lax.all_gather(shards[1], ("dp", "seq"), axis=0, tiled=True),
        lax.all_gather(shards[2], ("dp", "seq"), axis=0, tiled=True),
        lax.all_gather(shards[3], ("dp", "seq"), axis=0, tiled=True),
        lax.all_gather(shards[4], ("dp", "seq"), axis=0, tiled=True),
        lax.all_gather(shards[5], ("dp", "seq"), axis=0, tiled=True),
        lax.all_gather(shards[6], ("dp", "seq"), axis=0, tiled=True),
        lax.all_gather(shards[7], ("dp", "seq"), axis=0, tiled=True),
        lax.all_gather(shards[8], ("dp", "seq"), axis=0, tiled=True),
        lax.all_gather(shards[9], ("dp", "seq"), axis=0, tiled=True),
        lax.all_gather(shards[10], ("dp", "seq"), axis=0, tiled=True),
        lax.all_gather(shards[11], ("dp", "seq"), axis=0, tiled=True),
        lax.all_gather(shards[12], ("dp", "seq"), axis=0, tiled=True),
    )
    (
        full_qkv,
        full_qbias,
        full_vbias,
        full_out,
        full_obias,
        full_gain1,
        full_shift1,
        full_up,
        full_ubias,
        full_down,
        full_dbias,
        full_gain2,
        full_shift2,
    ) = weights
    groups = lax.axis_size("seq")
    rows = x_in[0]
    count, width = rows.shape
    head_dim = width // HEADS
    part_width = width // groups
    local_heads = HEADS // groups
    stream = count * groups
    qrows = min(512, stream)
    nblocks = stream // qrows
    scale = 1.0 / math.sqrt(head_dim)
    keep = jnp.arange(stream, dtype=jnp.int32) < valid[0]
    bias_row = jnp.concatenate([full_qbias, jnp.zeros_like(full_qbias), full_vbias]).astype(
        jnp.float32
    )
    project = (jnp.dot(rows, full_qkv, preferred_element_type=jnp.float32) + bias_row).astype(
        jnp.bfloat16
    )
    sent = (
        to_heads(project[:, :width], groups),
        to_heads(project[:, width : 2 * width], groups),
        to_heads(project[:, 2 * width :], groups),
    )
    arrived = (
        lax.all_to_all(sent[0], "seq", split_axis=0, concat_axis=0, tiled=True),
        lax.all_to_all(sent[1], "seq", split_axis=0, concat_axis=0, tiled=True),
        lax.all_to_all(sent[2], "seq", split_axis=0, concat_axis=0, tiled=True),
    )
    query_blocks = arrived[0].reshape(nblocks, qrows, local_heads, head_dim)
    key_heads = arrived[1].reshape(stream, local_heads, head_dim)
    value_heads = arrived[2].reshape(stream, local_heads, head_dim)

    def masked_scores(query):
        scores = (
            jnp.einsum("qhd,khd->hqk", query, key_heads, preferred_element_type=jnp.float32) * scale
        )
        return jnp.where(keep[None, None, :], scores, -1e30)

    def attend_forward(query):
        scores = masked_scores(query)
        peak = jnp.max(scores, axis=-1, keepdims=True)
        raised = jnp.exp(scores - peak)
        total = jnp.sum(raised, axis=-1, keepdims=True)
        probs = (raised / total).astype(jnp.bfloat16)
        context = jnp.einsum("hqk,khd->qhd", probs, value_heads, preferred_element_type=jnp.float32)
        return (context.astype(jnp.bfloat16), (peak + jnp.log(total))[..., 0])

    context, log_sums = lax.map(attend_forward, query_blocks)
    returned_ctx = lax.all_to_all(
        context.reshape(groups, -1), "seq", split_axis=0, concat_axis=0, tiled=True
    )
    context_rows = from_heads(returned_ctx, part_width)
    attn_out = jnp.dot(
        context_rows, full_out, preferred_element_type=jnp.float32
    ) + full_obias.astype(jnp.float32)
    first_rows = rows.astype(jnp.float32) + attn_out
    hidden, normed_one, inv_one = norm_forward(
        first_rows, full_gain1.astype(jnp.float32), full_shift1.astype(jnp.float32)
    )
    hidden_low = hidden.astype(jnp.bfloat16)
    up_act = jnp.dot(hidden_low, full_up, preferred_element_type=jnp.float32) + full_ubias.astype(
        jnp.float32
    )
    gelu_low = gelu_exact(up_act).astype(jnp.bfloat16)
    branch = jnp.dot(gelu_low, full_down, preferred_element_type=jnp.float32) + full_dbias.astype(
        jnp.float32
    )
    output, normed_two, inv_two = norm_forward(
        hidden + branch, full_gain2.astype(jnp.float32), full_shift2.astype(jnp.float32)
    )
    again = (
        lax.all_gather(shards[0], ("dp", "seq"), axis=0, tiled=True),
        lax.all_gather(shards[1], ("dp", "seq"), axis=0, tiled=True),
        lax.all_gather(shards[2], ("dp", "seq"), axis=0, tiled=True),
        lax.all_gather(shards[3], ("dp", "seq"), axis=0, tiled=True),
        lax.all_gather(shards[4], ("dp", "seq"), axis=0, tiled=True),
        lax.all_gather(shards[5], ("dp", "seq"), axis=0, tiled=True),
        lax.all_gather(shards[6], ("dp", "seq"), axis=0, tiled=True),
        lax.all_gather(shards[7], ("dp", "seq"), axis=0, tiled=True),
        lax.all_gather(shards[8], ("dp", "seq"), axis=0, tiled=True),
        lax.all_gather(shards[9], ("dp", "seq"), axis=0, tiled=True),
        lax.all_gather(shards[10], ("dp", "seq"), axis=0, tiled=True),
        lax.all_gather(shards[11], ("dp", "seq"), axis=0, tiled=True),
        lax.all_gather(shards[12], ("dp", "seq"), axis=0, tiled=True),
    )
    back_qkv, back_out, back_gain1, back_up, back_down, back_gain2 = (
        again[0],
        again[3],
        again[5],
        again[7],
        again[9],
        again[11],
    )
    grad_out = cotangent[0].astype(jnp.float32)
    grad_mid, grad_ln2_gain, grad_ln2_shift = norm_backward(
        grad_out, normed_two, inv_two, back_gain2.astype(jnp.float32)
    )
    grad_branch = grad_mid.astype(jnp.bfloat16)
    grad_w_down = outer_sum(gelu_low, grad_branch)
    grad_down_bias = jnp.sum(grad_branch.astype(jnp.float32), axis=0)
    grad_gelu = times_back(grad_branch, back_down)
    grad_up = jax.vjp(gelu_exact, up_act)[1](grad_gelu)[0].astype(jnp.bfloat16)
    grad_w_up = outer_sum(hidden_low, grad_up)
    grad_up_bias = jnp.sum(grad_up.astype(jnp.float32), axis=0)
    grad_hidden = times_back(grad_up, back_up) + grad_mid
    grad_first, grad_ln1_gain, grad_ln1_shift = norm_backward(
        grad_hidden, normed_one, inv_one, back_gain1.astype(jnp.float32)
    )
    grad_attn = grad_first.astype(jnp.bfloat16)
    grad_w_out = outer_sum(context_rows, grad_attn)
    grad_out_bias = jnp.sum(grad_attn.astype(jnp.float32), axis=0)
    grad_context = times_back(grad_attn, back_out).astype(jnp.bfloat16)
    grad_ctx_heads = lax.all_to_all(
        to_heads(grad_context, groups), "seq", split_axis=0, concat_axis=0, tiled=True
    )
    grad_ctx_blocks = grad_ctx_heads.reshape(nblocks, qrows, local_heads, head_dim)

    def attend_backward(carry, inputs):
        key_total, value_total = carry
        query, grad_ctx, log_rows = inputs
        scores = masked_scores(query)
        probs = jnp.exp(scores - log_rows[..., None])
        probs_low = probs.astype(jnp.bfloat16)
        d_probs = jnp.einsum(
            "qhd,khd->hqk", grad_ctx, value_heads, preferred_element_type=jnp.float32
        )
        centre = jnp.sum(probs * d_probs, axis=-1, keepdims=True)
        grad_scores = (probs * (d_probs - centre)).astype(jnp.bfloat16)
        grad_query = (
            jnp.einsum("hqk,khd->qhd", grad_scores, key_heads, preferred_element_type=jnp.float32)
            * scale
        )
        key_total = (
            key_total
            + jnp.einsum("hqk,qhd->khd", grad_scores, query, preferred_element_type=jnp.float32)
            * scale
        )
        value_total = value_total + jnp.einsum(
            "hqk,qhd->khd", probs_low, grad_ctx, preferred_element_type=jnp.float32
        )
        return ((key_total, value_total), grad_query.astype(jnp.bfloat16))

    empty = jnp.zeros((stream, local_heads, head_dim), jnp.float32)
    (key_total, value_total), grad_query = lax.scan(
        attend_backward, (empty, empty), (query_blocks, grad_ctx_blocks, log_sums)
    )
    grad_key = key_total.astype(jnp.bfloat16)
    grad_value = value_total.astype(jnp.bfloat16)
    grad_pieces = (
        lax.all_to_all(
            grad_query.reshape(groups, -1), "seq", split_axis=0, concat_axis=0, tiled=True
        ),
        lax.all_to_all(
            grad_key.reshape(groups, -1), "seq", split_axis=0, concat_axis=0, tiled=True
        ),
        lax.all_to_all(
            grad_value.reshape(groups, -1), "seq", split_axis=0, concat_axis=0, tiled=True
        ),
    )
    grad_project = jnp.concatenate(
        [
            from_heads(grad_pieces[0], part_width),
            from_heads(grad_pieces[1], part_width),
            from_heads(grad_pieces[2], part_width),
        ],
        axis=1,
    )
    grad_w_qkv = outer_sum(rows, grad_project)
    bias_sums = jnp.sum(grad_project.astype(jnp.float32), axis=0)
    grad_q_bias = bias_sums[:width]
    grad_v_bias = bias_sums[2 * width :]
    grad_rows = times_back(grad_project, back_qkv) + grad_first
    terms = (
        grad_w_qkv,
        grad_q_bias,
        grad_v_bias,
        grad_w_out,
        grad_out_bias,
        grad_ln1_gain,
        grad_ln1_shift,
        grad_w_up,
        grad_up_bias,
        grad_w_down,
        grad_down_bias,
        grad_ln2_gain,
        grad_ln2_shift,
    )
    page_sums = (
        lax.psum_scatter(
            terms[0].astype(jnp.bfloat16), "dp", scatter_dimension=0, tiled=True
        ).astype(jnp.float32),
        lax.psum_scatter(
            terms[1].astype(jnp.bfloat16), "dp", scatter_dimension=0, tiled=True
        ).astype(jnp.float32),
        lax.psum_scatter(
            terms[2].astype(jnp.bfloat16), "dp", scatter_dimension=0, tiled=True
        ).astype(jnp.float32),
        lax.psum_scatter(
            terms[3].astype(jnp.bfloat16), "dp", scatter_dimension=0, tiled=True
        ).astype(jnp.float32),
        lax.psum_scatter(
            terms[4].astype(jnp.bfloat16), "dp", scatter_dimension=0, tiled=True
        ).astype(jnp.float32),
        lax.psum_scatter(
            terms[5].astype(jnp.bfloat16), "dp", scatter_dimension=0, tiled=True
        ).astype(jnp.float32),
        lax.psum_scatter(
            terms[6].astype(jnp.bfloat16), "dp", scatter_dimension=0, tiled=True
        ).astype(jnp.float32),
        lax.psum_scatter(
            terms[7].astype(jnp.bfloat16), "dp", scatter_dimension=0, tiled=True
        ).astype(jnp.float32),
        lax.psum_scatter(
            terms[8].astype(jnp.bfloat16), "dp", scatter_dimension=0, tiled=True
        ).astype(jnp.float32),
        lax.psum_scatter(
            terms[9].astype(jnp.bfloat16), "dp", scatter_dimension=0, tiled=True
        ).astype(jnp.float32),
        lax.psum_scatter(
            terms[10].astype(jnp.bfloat16), "dp", scatter_dimension=0, tiled=True
        ).astype(jnp.float32),
        lax.psum_scatter(
            terms[11].astype(jnp.bfloat16), "dp", scatter_dimension=0, tiled=True
        ).astype(jnp.float32),
        lax.psum_scatter(
            terms[12].astype(jnp.bfloat16), "dp", scatter_dimension=0, tiled=True
        ).astype(jnp.float32),
    )
    sums = (
        lax.psum_scatter(
            page_sums[0].astype(jnp.bfloat16), "seq", scatter_dimension=0, tiled=True
        ).astype(jnp.float32),
        lax.psum_scatter(
            page_sums[1].astype(jnp.bfloat16), "seq", scatter_dimension=0, tiled=True
        ).astype(jnp.float32),
        lax.psum_scatter(
            page_sums[2].astype(jnp.bfloat16), "seq", scatter_dimension=0, tiled=True
        ).astype(jnp.float32),
        lax.psum_scatter(
            page_sums[3].astype(jnp.bfloat16), "seq", scatter_dimension=0, tiled=True
        ).astype(jnp.float32),
        lax.psum_scatter(
            page_sums[4].astype(jnp.bfloat16), "seq", scatter_dimension=0, tiled=True
        ).astype(jnp.float32),
        lax.psum_scatter(
            page_sums[5].astype(jnp.bfloat16), "seq", scatter_dimension=0, tiled=True
        ).astype(jnp.float32),
        lax.psum_scatter(
            page_sums[6].astype(jnp.bfloat16), "seq", scatter_dimension=0, tiled=True
        ).astype(jnp.float32),
        lax.psum_scatter(
            page_sums[7].astype(jnp.bfloat16), "seq", scatter_dimension=0, tiled=True
        ).astype(jnp.float32),
        lax.psum_scatter(
            page_sums[8].astype(jnp.bfloat16), "seq", scatter_dimension=0, tiled=True
        ).astype(jnp.float32),
        lax.psum_scatter(
            page_sums[9].astype(jnp.bfloat16), "seq", scatter_dimension=0, tiled=True
        ).astype(jnp.float32),
        lax.psum_scatter(
            page_sums[10].astype(jnp.bfloat16), "seq", scatter_dimension=0, tiled=True
        ).astype(jnp.float32),
        lax.psum_scatter(
            page_sums[11].astype(jnp.bfloat16), "seq", scatter_dimension=0, tiled=True
        ).astype(jnp.float32),
        lax.psum_scatter(
            page_sums[12].astype(jnp.bfloat16), "seq", scatter_dimension=0, tiled=True
        ).astype(jnp.float32),
    )
    return (
        output.astype(jnp.bfloat16)[None],
        grad_rows.astype(jnp.bfloat16)[None],
        sums[0],
        sums[1],
        sums[2],
        sums[3],
        sums[4],
        sums[5],
        sums[6],
        sums[7],
        sums[8],
        sums[9],
        sums[10],
        sums[11],
        sums[12],
    )


MESH = pl.DeviceIdType.MESH
CHUNK = 256
MASKED = -1e30


def flip(index, mask):
    for b in range(mask.bit_length()):
        if mask >> b & 1:
            bit = 1 << b
            index = index + bit - 2 * bit * (index // bit % 2)
    return index


class Wires:
    def __init__(self, sems, sizes):
        self.sems, self.sizes = sems, sizes
        self.dp, self.z = lax.axis_index("dp"), lax.axis_index("seq")
        self.dps = [flip(self.dp, m) for m in range(sizes[0])]
        self.zs = [flip(self.z, m) for m in range(sizes[1])]
        self.started = []

    def peer(self, offset, step):
        return (self.dps[offset], self.zs[step])

    def send(self, src, dst, recv_sem, device):
        copy = pltpu.make_async_remote_copy(
            src_ref=src,
            dst_ref=dst,
            send_sem=self.sems.at[len(self.started)],
            recv_sem=recv_sem,
            device_id=device,
            device_id_type=MESH,
        )
        copy.start()
        self.started.append(copy)

    def arrived(self, dst, recv_sem):
        pltpu.make_async_remote_copy(
            src_ref=dst,
            dst_ref=dst,
            send_sem=self.sems.at[0],
            recv_sem=recv_sem,
            device_id=self.peer(1, 0),
            device_id_type=MESH,
        ).wait_recv()

    def drain(self):
        for copy in self.started:
            copy.wait_send()

    def greet(self):
        n_dp, n_seq = self.sizes
        barrier = pltpu.get_barrier_semaphore()
        masks = [1 << b for b in range(n_dp.bit_length() - 1)]
        partners = [self.peer(m, 0) for m in masks] + [self.peer(0, i) for i in range(1, n_seq)]
        for device in partners:
            pl.semaphore_signal(barrier, inc=1, device_id=device, device_id_type=MESH)
        pl.semaphore_wait(barrier, len(partners))


class Gather:
    def __init__(self, wires, src, full, recv, local):
        self.w, self.src, self.full, self.recv, self.local = wires, src, full, recv, local
        n_dp, self.n_seq = wires.sizes
        self.chips = [1 << b for b in range(1, n_dp.bit_length() - 1)]

    def at(self, offset, step):
        return self.full.at[self.w.dps[offset] * self.n_seq + self.w.zs[step]]

    def order(self, step):
        return self.chips if step % 2 == 0 else self.chips[::-1]

    def forward(self, src, offset, step, masks):
        for m in masks:
            self.w.send(src, self.at(offset, step), self.recv.at[offset ^ m, step], self.w.peer(m, 0))

    def wait(self, offset, step):
        self.w.arrived(self.at(offset, step), self.recv.at[offset, step])

    def own(self):
        self.kept = pltpu.make_async_copy(self.src, self.at(0, 0), self.local)
        self.kept.start()
        for i in range(1, self.n_seq):
            self.w.send(self.src, self.at(0, 0), self.recv.at[0, i], self.w.peer(0, i))
        self.forward(self.src, 0, 0, self.order(0) + [1])

    def along_seq(self, i):
        self.wait(0, i)
        self.forward(self.at(0, i), 0, i, self.order(i) + [1])

    def stages(self, step):
        have, out = [0], []
        masks = self.order(step)
        for t, m in enumerate(masks):
            out.append([(o ^ m, masks[t + 1 :] + [1]) for o in have])
            have = have + [o ^ m for o in have]
        return out

    def over_chips(self, t, step):
        for offset, masks in self.stages(step)[t]:
            self.wait(offset, step)
            self.forward(self.at(offset, step), offset, step, masks)

    def over_cores(self):
        n_dp = self.w.sizes[0]
        for offset in range(1, n_dp, 2):
            for i in range(self.n_seq):
                self.wait(offset, i)
        self.kept.wait()

    def steps(self):
        yield self.own
        for i in range(1, self.n_seq):
            yield lambda i=i: self.along_seq(i)
        for t in range(len(self.chips)):
            for i in range(self.n_seq):
                yield lambda t=t, i=i: self.over_chips(t, i)
        yield self.over_cores


def sends_of_gather(n_dp, n_seq):
    return n_seq - 1 + n_seq * (n_dp - 1)


def lanes_of(packed, row, n_dp, n_seq):
    pieces = []
    for d in range(n_dp):
        total = packed[d * n_seq, row : row + 1, :]
        for s in range(1, n_seq):
            total = total + packed[d * n_seq + s, row : row + 1, :]
        pieces.append(total)
    return jnp.concatenate(pieces, axis=1)


def front_kernel(
    sizes,
    heads,
    valid_ref,
    x_ref,
    vec_ref,
    qkv_ref,
    out_ref,
    up_ref,
    down_ref,
    full_vec,
    full_qkv,
    full_out,
    full_up,
    full_down,
    query_out,
    key_out,
    value_out,
    context_out,
    logs_out,
    packed,
    weight,
    sent,
    held,
    context_sent,
    context_held,
    context_turned,
    value_turned,
    logs,
    send_sems,
    gather_sems,
    heads_sems,
    context_sems,
    local_sems,
):
    n_dp, n_seq = sizes
    w = Wires(send_sems, sizes)
    rows, width = x_ref.shape
    part = width // n_seq
    head_dim = width // heads
    local_heads = heads // n_seq
    stream = rows * n_seq
    w.greet()
    sources = ((vec_ref, packed), (qkv_ref, full_qkv), (out_ref, full_out), (up_ref, full_up), (down_ref, full_down))
    gathers = [
        Gather(w, src, dst, gather_sems.at[k], local_sems.at[k]) for k, (src, dst) in enumerate(sources)
    ]
    vec, qkv, out, up, down = [list(g.steps()) for g in gathers]
    queue = []

    def pump(count):
        for _ in range(min(count, len(queue))):
            queue.pop(0)()

    vec[0]()
    qkv[0]()
    for step in vec[1:n_seq]:
        step()
    for step in qkv[1:n_seq]:
        step()
    out[0]()
    for step in vec[n_seq:-1]:
        step()
    for step in qkv[n_seq : 2 * n_seq]:
        step()
    for step in out[1:n_seq]:
        step()
    up[0]()
    for step in qkv[2 * n_seq :]:
        step()
    vec[-1]()
    loads = []
    for t in range(3):
        loads.append(
            pltpu.make_async_copy(
                full_qkv.at[:, :, pl.ds(t * width, width)], weight.at[t], local_sems.at[5 + t]
            )
        )
        loads[-1].start()
    store_vec = pltpu.make_async_copy(packed, full_vec, local_sems.at[8])
    store_vec.start()
    queue.extend(out[n_seq:] + up[1:])
    x = x_ref[...]
    for t in range(3):
        loads[t].wait()
        for j in range(n_seq):
            columns = slice(j * part, (j + 1) * part)
            block = weight[t, :, :, columns].reshape(width, part)
            piece = jnp.dot(x, block, preferred_element_type=jnp.float32)
            if t != 1:
                piece = piece + lanes_of(packed, t // 2, n_dp, n_seq)[:, columns]
            sent[t, j] = piece.astype(jnp.bfloat16)
        for i in range(1, n_seq):
            w.send(sent.at[t, w.zs[i]], held.at[t, w.z], heads_sems.at[t, i], w.peer(0, i))
        held[t, w.z] = sent[t, w.z]
    pump(2 * n_seq)
    queue.append(down[0])
    queue.extend(down[1:])
    pump(n_seq)
    for t in range(3):
        for i in range(1, n_seq):
            w.arrived(held.at[t, w.zs[i]], heads_sems.at[t, i])
    keeps = []
    for t, ref in enumerate((query_out, key_out, value_out)):
        keeps.append(pltpu.make_async_copy(held.at[t], ref, local_sems.at[9 + t]))
        keeps[-1].start()
    position = lax.broadcasted_iota(jnp.int32, (stream, 128), 0)
    lane = lax.broadcasted_iota(jnp.int32, (stream, 128), 1)
    guard = jnp.where((position >= valid_ref[0]) & (lane == 0), MASKED, 0.0).astype(jnp.bfloat16)
    value_turned[...] = held[2].reshape(stream, part).T
    one_lane = lax.broadcasted_iota(jnp.int32, (CHUNK, 128), 1)
    ones = jnp.where(one_lane == 0, 1.0, 0.0).astype(jnp.bfloat16)
    per_block = 128 // head_dim
    scale = 1.0 / math.sqrt(head_dim)
    pumps = -(-len(queue) // local_heads)
    for h in range(local_heads):
        pair = slice(h // per_block * 128, h // per_block * 128 + 128)
        low = h % per_block * head_dim
        keys = jnp.concatenate([held[1, :, :, pair].reshape(stream, 128), guard], axis=1)

        def attend(c, _, keys=keys, pair=pair, low=low, h=h):
            query = held[0, c, :, pair]
            mine = (one_lane >= low) & (one_lane < low + head_dim)
            query = jnp.where(mine, query.astype(jnp.float32) * scale, 0.0).astype(jnp.bfloat16)
            query = jnp.concatenate([query, ones], axis=1)
            scores = lax.dot_general(
                keys, query, (((1,), (1,)), ((), ())), preferred_element_type=jnp.float32
            )
            peak = jnp.max(scores, axis=0, keepdims=True)
            raised = jnp.exp(scores - peak)
            total = jnp.sum(raised, axis=0, keepdims=True)
            mixed = jnp.dot(
                value_turned[h * head_dim : (h + 1) * head_dim, :],
                raised.astype(jnp.bfloat16),
                preferred_element_type=jnp.float32,
            )
            context_turned[c, h * head_dim : (h + 1) * head_dim, :] = mixed / total
            logs[c, h : h + 1, :] = peak + jnp.log(total)
            return 0

        lax.fori_loop(0, n_seq, attend, 0)
        pump(pumps)
    for j in range(n_seq):
        context_sent[j] = context_turned[j].T.astype(jnp.bfloat16)
    for i in range(1, n_seq):
        w.send(context_sent.at[w.zs[i]], context_held.at[w.z], context_sems.at[i], w.peer(0, i))
    context_held[w.z] = context_sent[w.z]
    store_logs = pltpu.make_async_copy(logs, logs_out, local_sems.at[12])
    store_logs.start()
    pump(len(queue))
    for i in range(1, n_seq):
        w.arrived(context_held.at[w.zs[i]], context_sems.at[i])
    for j in range(n_seq):
        keeps.append(
            pltpu.make_async_copy(
                context_held.at[j], context_out.at[:, pl.ds(j * part, part)], local_sems.at[13 + j]
            )
        )
        keeps[-1].start()
    for copy in keeps:
        copy.wait()
    store_logs.wait()
    store_vec.wait()
    w.drain()


def front(sizes, heads, valid, rows, vec, w_qkv, w_out, w_up, w_down):
    n_dp, n_seq = sizes
    devices = n_dp * n_seq
    count, width = rows.shape
    part = width // n_seq
    stream = count * n_seq
    low = jnp.bfloat16
    pieces = jax.ShapeDtypeStruct((n_seq, count, part), low)

    def full(shard):
        return jax.ShapeDtypeStruct((devices,) + shard.shape, shard.dtype)

    anywhere = pl.BlockSpec(memory_space=pl.ANY)
    sends = 5 * sends_of_gather(n_dp, n_seq) + 4 * (n_seq - 1)
    return pl.pallas_call(
        lambda *refs: front_kernel(sizes, heads, *refs),
        out_shape=(
            full(vec),
            full(w_qkv),
            full(w_out),
            full(w_up),
            full(w_down),
            pieces,
            pieces,
            pieces,
            jax.ShapeDtypeStruct((count, width), low),
            jax.ShapeDtypeStruct((n_seq, 8, count), jnp.float32),
        ),
        in_specs=[
            pl.BlockSpec(memory_space=pltpu.SMEM),
            pl.BlockSpec(memory_space=pltpu.VMEM),
        ]
        + [anywhere] * 5,
        out_specs=[anywhere] * 10,
        scratch_shapes=[
            pltpu.VMEM((devices,) + vec.shape, jnp.float32),
            pltpu.VMEM((3, devices, w_qkv.shape[0], width), low),
            pltpu.VMEM((3, n_seq, count, part), low),
            pltpu.VMEM((3, n_seq, count, part), low),
            pltpu.VMEM((n_seq, count, part), low),
            pltpu.VMEM((n_seq, count, part), low),
            pltpu.VMEM((n_seq, part, count), jnp.float32),
            pltpu.VMEM((part, stream), low),
            pltpu.VMEM((n_seq, 8, count), jnp.float32),
            pltpu.SemaphoreType.DMA((sends,)),
            pltpu.SemaphoreType.DMA((5, n_dp, n_seq)),
            pltpu.SemaphoreType.DMA((3, n_seq)),
            pltpu.SemaphoreType.DMA((n_seq,)),
            pltpu.SemaphoreType.DMA((13 + n_seq,)),
        ],
        compiler_params=pltpu.CompilerParams(
            collective_id=0, has_side_effects=True, vmem_limit_bytes=56 * 2**20
        ),
        name="front",
    )(valid, rows, vec, w_qkv, w_out, w_up, w_down)


def spread_lanes(vectors, n_seq):
    stacked = jnp.stack(vectors).astype(jnp.float32)
    tiled = jnp.tile(stacked, (1, n_seq))
    owner = jnp.arange(tiled.shape[1], dtype=jnp.int32) // stacked.shape[1]
    return jnp.where(owner[None, :] == lax.axis_index("seq"), tiled, 0.0)


def kernel_plan(
    x_in,
    w_qkv,
    q_bias,
    v_bias,
    w_out,
    out_bias,
    ln1_gain,
    ln1_shift,
    w_up,
    up_bias,
    w_down,
    down_bias,
    ln2_gain,
    ln2_shift,
    valid,
    cotangent,
):
    sizes = (lax.axis_size("dp"), lax.axis_size("seq"))
    n_dp, groups = sizes
    rows = x_in[0]
    count, width = rows.shape
    head_dim = width // HEADS
    part_width = width // groups
    local_heads = HEADS // groups
    stream = count * groups
    qrows = min(512, stream)
    nblocks = stream // qrows
    scale = 1.0 / math.sqrt(head_dim)
    keep = jnp.arange(stream, dtype=jnp.int32) < valid[0]
    vectors = (q_bias, v_bias, out_bias, ln1_gain, ln1_shift, down_bias, ln2_gain, ln2_shift)
    spread = spread_lanes(vectors, groups)
    vec = jnp.concatenate(
        [spread, up_bias.astype(jnp.float32)[None], jnp.zeros((7, spread.shape[1]), jnp.float32)]
    )
    (
        full_vec,
        full_qkv,
        full_out,
        full_up,
        full_down,
        query_heads,
        key_heads,
        value_heads,
        context_rows,
        logs,
    ) = front(sizes, HEADS, valid, rows, vec, w_qkv, w_out, w_up, w_down)
    full_qkv = full_qkv.reshape(width, -1)
    full_out = full_out.reshape(width, -1)
    full_up = full_up.reshape(width, -1)
    full_down = full_down.reshape(-1, width)
    by_page = full_vec.reshape(n_dp, groups, 16, -1)
    lined = by_page[:, :, :8].sum(axis=1).transpose(1, 0, 2).reshape(8, width)
    full_obias, full_gain1, full_shift1, full_dbias, full_gain2, full_shift2 = (
        lined[2],
        lined[3],
        lined[4],
        lined[5],
        lined[6],
        lined[7],
    )
    full_ubias = by_page[:, :, 8].reshape(-1)
    query_blocks = query_heads.reshape(nblocks, qrows, local_heads, head_dim)
    key_heads = key_heads.reshape(stream, local_heads, head_dim)
    value_heads = value_heads.reshape(stream, local_heads, head_dim)
    log_sums = (
        logs[:, :local_heads]
        .transpose(1, 0, 2)
        .reshape(local_heads, nblocks, qrows)
        .transpose(1, 0, 2)
    )

    def masked_scores(query):
        scores = (
            jnp.einsum("qhd,khd->hqk", query, key_heads, preferred_element_type=jnp.float32) * scale
        )
        return jnp.where(keep[None, None, :], scores, -1e30)

    attn_out = jnp.dot(
        context_rows, full_out, preferred_element_type=jnp.float32
    ) + full_obias.astype(jnp.float32)
    first_rows = rows.astype(jnp.float32) + attn_out
    hidden, normed_one, inv_one = norm_forward(
        first_rows, full_gain1.astype(jnp.float32), full_shift1.astype(jnp.float32)
    )
    hidden_low = hidden.astype(jnp.bfloat16)
    up_act = jnp.dot(hidden_low, full_up, preferred_element_type=jnp.float32) + full_ubias.astype(
        jnp.float32
    )
    gelu_low = gelu_exact(up_act).astype(jnp.bfloat16)
    branch = jnp.dot(gelu_low, full_down, preferred_element_type=jnp.float32) + full_dbias.astype(
        jnp.float32
    )
    output, normed_two, inv_two = norm_forward(
        hidden + branch, full_gain2.astype(jnp.float32), full_shift2.astype(jnp.float32)
    )
    back_qkv, back_out, back_gain1, back_up, back_down, back_gain2 = (
        full_qkv,
        full_out,
        full_gain1,
        full_up,
        full_down,
        full_gain2,
    )
    grad_out = cotangent[0].astype(jnp.float32)
    grad_mid, grad_ln2_gain, grad_ln2_shift = norm_backward(
        grad_out, normed_two, inv_two, back_gain2.astype(jnp.float32)
    )
    grad_branch = grad_mid.astype(jnp.bfloat16)
    grad_w_down = outer_sum(gelu_low, grad_branch)
    grad_down_bias = jnp.sum(grad_branch.astype(jnp.float32), axis=0)
    grad_gelu = times_back(grad_branch, back_down)
    grad_up = jax.vjp(gelu_exact, up_act)[1](grad_gelu)[0].astype(jnp.bfloat16)
    grad_w_up = outer_sum(hidden_low, grad_up)
    grad_up_bias = jnp.sum(grad_up.astype(jnp.float32), axis=0)
    grad_hidden = times_back(grad_up, back_up) + grad_mid
    grad_first, grad_ln1_gain, grad_ln1_shift = norm_backward(
        grad_hidden, normed_one, inv_one, back_gain1.astype(jnp.float32)
    )
    grad_attn = grad_first.astype(jnp.bfloat16)
    grad_w_out = outer_sum(context_rows, grad_attn)
    grad_out_bias = jnp.sum(grad_attn.astype(jnp.float32), axis=0)
    grad_context = times_back(grad_attn, back_out).astype(jnp.bfloat16)
    grad_ctx_heads = lax.all_to_all(
        to_heads(grad_context, groups), "seq", split_axis=0, concat_axis=0, tiled=True
    )
    grad_ctx_blocks = grad_ctx_heads.reshape(nblocks, qrows, local_heads, head_dim)

    def attend_backward(carry, inputs):
        key_total, value_total = carry
        query, grad_ctx, log_rows = inputs
        scores = masked_scores(query)
        probs = jnp.exp(scores - log_rows[..., None])
        probs_low = probs.astype(jnp.bfloat16)
        d_probs = jnp.einsum(
            "qhd,khd->hqk", grad_ctx, value_heads, preferred_element_type=jnp.float32
        )
        centre = jnp.sum(probs * d_probs, axis=-1, keepdims=True)
        grad_scores = (probs * (d_probs - centre)).astype(jnp.bfloat16)
        grad_query = (
            jnp.einsum("hqk,khd->qhd", grad_scores, key_heads, preferred_element_type=jnp.float32)
            * scale
        )
        key_total = (
            key_total
            + jnp.einsum("hqk,qhd->khd", grad_scores, query, preferred_element_type=jnp.float32)
            * scale
        )
        value_total = value_total + jnp.einsum(
            "hqk,qhd->khd", probs_low, grad_ctx, preferred_element_type=jnp.float32
        )
        return ((key_total, value_total), grad_query.astype(jnp.bfloat16))

    empty = jnp.zeros((stream, local_heads, head_dim), jnp.float32)
    (key_total, value_total), grad_query = lax.scan(
        attend_backward, (empty, empty), (query_blocks, grad_ctx_blocks, log_sums)
    )
    grad_key = key_total.astype(jnp.bfloat16)
    grad_value = value_total.astype(jnp.bfloat16)
    grad_pieces = (
        lax.all_to_all(
            grad_query.reshape(groups, -1), "seq", split_axis=0, concat_axis=0, tiled=True
        ),
        lax.all_to_all(
            grad_key.reshape(groups, -1), "seq", split_axis=0, concat_axis=0, tiled=True
        ),
        lax.all_to_all(
            grad_value.reshape(groups, -1), "seq", split_axis=0, concat_axis=0, tiled=True
        ),
    )
    grad_project = jnp.concatenate(
        [
            from_heads(grad_pieces[0], part_width),
            from_heads(grad_pieces[1], part_width),
            from_heads(grad_pieces[2], part_width),
        ],
        axis=1,
    )
    grad_w_qkv = outer_sum(rows, grad_project)
    bias_sums = jnp.sum(grad_project.astype(jnp.float32), axis=0)
    grad_q_bias = bias_sums[:width]
    grad_v_bias = bias_sums[2 * width :]
    grad_rows = times_back(grad_project, back_qkv) + grad_first
    terms = (
        grad_w_qkv,
        grad_q_bias,
        grad_v_bias,
        grad_w_out,
        grad_out_bias,
        grad_ln1_gain,
        grad_ln1_shift,
        grad_w_up,
        grad_up_bias,
        grad_w_down,
        grad_down_bias,
        grad_ln2_gain,
        grad_ln2_shift,
    )
    page_sums = (
        lax.psum_scatter(
            terms[0].astype(jnp.bfloat16), "dp", scatter_dimension=0, tiled=True
        ).astype(jnp.float32),
        lax.psum_scatter(
            terms[1].astype(jnp.bfloat16), "dp", scatter_dimension=0, tiled=True
        ).astype(jnp.float32),
        lax.psum_scatter(
            terms[2].astype(jnp.bfloat16), "dp", scatter_dimension=0, tiled=True
        ).astype(jnp.float32),
        lax.psum_scatter(
            terms[3].astype(jnp.bfloat16), "dp", scatter_dimension=0, tiled=True
        ).astype(jnp.float32),
        lax.psum_scatter(
            terms[4].astype(jnp.bfloat16), "dp", scatter_dimension=0, tiled=True
        ).astype(jnp.float32),
        lax.psum_scatter(
            terms[5].astype(jnp.bfloat16), "dp", scatter_dimension=0, tiled=True
        ).astype(jnp.float32),
        lax.psum_scatter(
            terms[6].astype(jnp.bfloat16), "dp", scatter_dimension=0, tiled=True
        ).astype(jnp.float32),
        lax.psum_scatter(
            terms[7].astype(jnp.bfloat16), "dp", scatter_dimension=0, tiled=True
        ).astype(jnp.float32),
        lax.psum_scatter(
            terms[8].astype(jnp.bfloat16), "dp", scatter_dimension=0, tiled=True
        ).astype(jnp.float32),
        lax.psum_scatter(
            terms[9].astype(jnp.bfloat16), "dp", scatter_dimension=0, tiled=True
        ).astype(jnp.float32),
        lax.psum_scatter(
            terms[10].astype(jnp.bfloat16), "dp", scatter_dimension=0, tiled=True
        ).astype(jnp.float32),
        lax.psum_scatter(
            terms[11].astype(jnp.bfloat16), "dp", scatter_dimension=0, tiled=True
        ).astype(jnp.float32),
        lax.psum_scatter(
            terms[12].astype(jnp.bfloat16), "dp", scatter_dimension=0, tiled=True
        ).astype(jnp.float32),
    )
    sums = (
        lax.psum_scatter(
            page_sums[0].astype(jnp.bfloat16), "seq", scatter_dimension=0, tiled=True
        ).astype(jnp.float32),
        lax.psum_scatter(
            page_sums[1].astype(jnp.bfloat16), "seq", scatter_dimension=0, tiled=True
        ).astype(jnp.float32),
        lax.psum_scatter(
            page_sums[2].astype(jnp.bfloat16), "seq", scatter_dimension=0, tiled=True
        ).astype(jnp.float32),
        lax.psum_scatter(
            page_sums[3].astype(jnp.bfloat16), "seq", scatter_dimension=0, tiled=True
        ).astype(jnp.float32),
        lax.psum_scatter(
            page_sums[4].astype(jnp.bfloat16), "seq", scatter_dimension=0, tiled=True
        ).astype(jnp.float32),
        lax.psum_scatter(
            page_sums[5].astype(jnp.bfloat16), "seq", scatter_dimension=0, tiled=True
        ).astype(jnp.float32),
        lax.psum_scatter(
            page_sums[6].astype(jnp.bfloat16), "seq", scatter_dimension=0, tiled=True
        ).astype(jnp.float32),
        lax.psum_scatter(
            page_sums[7].astype(jnp.bfloat16), "seq", scatter_dimension=0, tiled=True
        ).astype(jnp.float32),
        lax.psum_scatter(
            page_sums[8].astype(jnp.bfloat16), "seq", scatter_dimension=0, tiled=True
        ).astype(jnp.float32),
        lax.psum_scatter(
            page_sums[9].astype(jnp.bfloat16), "seq", scatter_dimension=0, tiled=True
        ).astype(jnp.float32),
        lax.psum_scatter(
            page_sums[10].astype(jnp.bfloat16), "seq", scatter_dimension=0, tiled=True
        ).astype(jnp.float32),
        lax.psum_scatter(
            page_sums[11].astype(jnp.bfloat16), "seq", scatter_dimension=0, tiled=True
        ).astype(jnp.float32),
        lax.psum_scatter(
            page_sums[12].astype(jnp.bfloat16), "seq", scatter_dimension=0, tiled=True
        ).astype(jnp.float32),
    )
    return (
        output.astype(jnp.bfloat16)[None],
        grad_rows.astype(jnp.bfloat16)[None],
        sums[0],
        sums[1],
        sums[2],
        sums[3],
        sums[4],
        sums[5],
        sums[6],
        sums[7],
        sums[8],
        sums[9],
        sums[10],
        sums[11],
        sums[12],
    )


def solution(mesh):
    n_dp, n_seq = mesh.shape["dp"], mesh.shape["seq"]

    def per_device(x_in, w_qkv, *rest):
        part, width = w_qkv.shape[0], x_in.shape[2]
        fits = part % 32 == 0 and part * n_seq == 128 and width // n_seq % 128 == 0 and x_in.shape[0] == 1
        plan = kernel_plan if fits else general_plan
        return plan(x_in, w_qkv, *rest)

    return jax.shard_map(
        per_device,
        mesh=mesh,
        in_specs=(
            P("dp", "seq", None),
            P(("dp", "seq"), None),
            P(("dp", "seq")),
            P(("dp", "seq")),
            P(("dp", "seq"), None),
            P(("dp", "seq")),
            P(("dp", "seq")),
            P(("dp", "seq")),
            P(("dp", "seq"), None),
            P(("dp", "seq")),
            P(("dp", "seq"), None),
            P(("dp", "seq")),
            P(("dp", "seq")),
            P(("dp", "seq")),
            P("dp"),
            P("dp", "seq", None),
        ),
        out_specs=(
            P("dp", "seq", None),
            P("dp", "seq", None),
            P(("dp", "seq"), None),
            P(("dp", "seq")),
            P(("dp", "seq")),
            P(("dp", "seq"), None),
            P(("dp", "seq")),
            P(("dp", "seq")),
            P(("dp", "seq")),
            P(("dp", "seq"), None),
            P(("dp", "seq")),
            P(("dp", "seq"), None),
            P(("dp", "seq")),
            P(("dp", "seq")),
            P(("dp", "seq")),
        ),
        check_vma=False,
    )
```

```python
import math

import jax
import jax.numpy as jnp
from jax import lax
from jax.experimental import pallas as pl
from jax.experimental.pallas import tpu as pltpu
from jax.sharding import PartitionSpec as P

HEADS = 16


eps_norm = 1e-05


def outer_sum(left, right):
    return lax.dot_general(
        left, right, (((0,), (0,)), ((), ())), preferred_element_type=jnp.float32
    )


def times_back(rows, matrix):
    return lax.dot_general(
        rows, matrix, (((1,), (1,)), ((), ())), preferred_element_type=jnp.float32
    )


def gelu_exact(values):
    return jax.nn.gelu(values, approximate=False)


def norm_forward(rows, gain, shift):
    center = rows - jnp.mean(rows, axis=-1, keepdims=True)
    inv_std = lax.rsqrt(jnp.mean(center * center, axis=-1, keepdims=True) + eps_norm)
    normed = center * inv_std
    return (normed * gain + shift, normed, inv_std)


def norm_backward(grad_out, normed, inv_std, gain):
    scaled = grad_out * gain
    grad_rows = inv_std * (
        scaled
        - jnp.mean(scaled, axis=-1, keepdims=True)
        - normed * jnp.mean(scaled * normed, axis=-1, keepdims=True)
    )
    return (grad_rows, jnp.sum(grad_out * normed, axis=0), jnp.sum(grad_out, axis=0))


def to_heads(rows, groups):
    count, width = rows.shape
    return rows.reshape(count, groups, width // groups).transpose(1, 0, 2).reshape(groups, -1)


def from_heads(pieces, part_width):
    groups = pieces.shape[0]
    return (
        pieces.reshape(groups, -1, part_width).transpose(1, 0, 2).reshape(-1, groups * part_width)
    )


def general_plan(
    x_in,
    w_qkv,
    q_bias,
    v_bias,
    w_out,
    out_bias,
    ln1_gain,
    ln1_shift,
    w_up,
    up_bias,
    w_down,
    down_bias,
    ln2_gain,
    ln2_shift,
    valid,
    cotangent,
):
    shards = (
        w_qkv,
        q_bias,
        v_bias,
        w_out,
        out_bias,
        ln1_gain,
        ln1_shift,
        w_up,
        up_bias,
        w_down,
        down_bias,
        ln2_gain,
        ln2_shift,
    )
    weights = (
        lax.all_gather(shards[0], ("dp", "seq"), axis=0, tiled=True),
        lax.all_gather(shards[1], ("dp", "seq"), axis=0, tiled=True),
        lax.all_gather(shards[2], ("dp", "seq"), axis=0, tiled=True),
        lax.all_gather(shards[3], ("dp", "seq"), axis=0, tiled=True),
        lax.all_gather(shards[4], ("dp", "seq"), axis=0, tiled=True),
        lax.all_gather(shards[5], ("dp", "seq"), axis=0, tiled=True),
        lax.all_gather(shards[6], ("dp", "seq"), axis=0, tiled=True),
        lax.all_gather(shards[7], ("dp", "seq"), axis=0, tiled=True),
        lax.all_gather(shards[8], ("dp", "seq"), axis=0, tiled=True),
        lax.all_gather(shards[9], ("dp", "seq"), axis=0, tiled=True),
        lax.all_gather(shards[10], ("dp", "seq"), axis=0, tiled=True),
        lax.all_gather(shards[11], ("dp", "seq"), axis=0, tiled=True),
        lax.all_gather(shards[12], ("dp", "seq"), axis=0, tiled=True),
    )
    (
        full_qkv,
        full_qbias,
        full_vbias,
        full_out,
        full_obias,
        full_gain1,
        full_shift1,
        full_up,
        full_ubias,
        full_down,
        full_dbias,
        full_gain2,
        full_shift2,
    ) = weights
    groups = lax.axis_size("seq")
    rows = x_in[0]
    count, width = rows.shape
    head_dim = width // HEADS
    part_width = width // groups
    local_heads = HEADS // groups
    stream = count * groups
    qrows = min(512, stream)
    nblocks = stream // qrows
    scale = 1.0 / math.sqrt(head_dim)
    keep = jnp.arange(stream, dtype=jnp.int32) < valid[0]
    bias_row = jnp.concatenate([full_qbias, jnp.zeros_like(full_qbias), full_vbias]).astype(
        jnp.float32
    )
    project = (jnp.dot(rows, full_qkv, preferred_element_type=jnp.float32) + bias_row).astype(
        jnp.bfloat16
    )
    sent = (
        to_heads(project[:, :width], groups),
        to_heads(project[:, width : 2 * width], groups),
        to_heads(project[:, 2 * width :], groups),
    )
    arrived = (
        lax.all_to_all(sent[0], "seq", split_axis=0, concat_axis=0, tiled=True),
        lax.all_to_all(sent[1], "seq", split_axis=0, concat_axis=0, tiled=True),
        lax.all_to_all(sent[2], "seq", split_axis=0, concat_axis=0, tiled=True),
    )
    query_blocks = arrived[0].reshape(nblocks, qrows, local_heads, head_dim)
    key_heads = arrived[1].reshape(stream, local_heads, head_dim)
    value_heads = arrived[2].reshape(stream, local_heads, head_dim)

    def masked_scores(query):
        scores = (
            jnp.einsum("qhd,khd->hqk", query, key_heads, preferred_element_type=jnp.float32) * scale
        )
        return jnp.where(keep[None, None, :], scores, -1e30)

    def attend_forward(query):
        scores = masked_scores(query)
        peak = jnp.max(scores, axis=-1, keepdims=True)
        raised = jnp.exp(scores - peak)
        total = jnp.sum(raised, axis=-1, keepdims=True)
        probs = (raised / total).astype(jnp.bfloat16)
        context = jnp.einsum("hqk,khd->qhd", probs, value_heads, preferred_element_type=jnp.float32)
        return (context.astype(jnp.bfloat16), (peak + jnp.log(total))[..., 0])

    context, log_sums = lax.map(attend_forward, query_blocks)
    returned_ctx = lax.all_to_all(
        context.reshape(groups, -1), "seq", split_axis=0, concat_axis=0, tiled=True
    )
    context_rows = from_heads(returned_ctx, part_width)
    attn_out = jnp.dot(
        context_rows, full_out, preferred_element_type=jnp.float32
    ) + full_obias.astype(jnp.float32)
    first_rows = rows.astype(jnp.float32) + attn_out
    hidden, normed_one, inv_one = norm_forward(
        first_rows, full_gain1.astype(jnp.float32), full_shift1.astype(jnp.float32)
    )
    hidden_low = hidden.astype(jnp.bfloat16)
    up_act = jnp.dot(hidden_low, full_up, preferred_element_type=jnp.float32) + full_ubias.astype(
        jnp.float32
    )
    gelu_low = gelu_exact(up_act).astype(jnp.bfloat16)
    branch = jnp.dot(gelu_low, full_down, preferred_element_type=jnp.float32) + full_dbias.astype(
        jnp.float32
    )
    output, normed_two, inv_two = norm_forward(
        hidden + branch, full_gain2.astype(jnp.float32), full_shift2.astype(jnp.float32)
    )
    again = (
        lax.all_gather(shards[0], ("dp", "seq"), axis=0, tiled=True),
        lax.all_gather(shards[1], ("dp", "seq"), axis=0, tiled=True),
        lax.all_gather(shards[2], ("dp", "seq"), axis=0, tiled=True),
        lax.all_gather(shards[3], ("dp", "seq"), axis=0, tiled=True),
        lax.all_gather(shards[4], ("dp", "seq"), axis=0, tiled=True),
        lax.all_gather(shards[5], ("dp", "seq"), axis=0, tiled=True),
        lax.all_gather(shards[6], ("dp", "seq"), axis=0, tiled=True),
        lax.all_gather(shards[7], ("dp", "seq"), axis=0, tiled=True),
        lax.all_gather(shards[8], ("dp", "seq"), axis=0, tiled=True),
        lax.all_gather(shards[9], ("dp", "seq"), axis=0, tiled=True),
        lax.all_gather(shards[10], ("dp", "seq"), axis=0, tiled=True),
        lax.all_gather(shards[11], ("dp", "seq"), axis=0, tiled=True),
        lax.all_gather(shards[12], ("dp", "seq"), axis=0, tiled=True),
    )
    back_qkv, back_out, back_gain1, back_up, back_down, back_gain2 = (
        again[0],
        again[3],
        again[5],
        again[7],
        again[9],
        again[11],
    )
    grad_out = cotangent[0].astype(jnp.float32)
    grad_mid, grad_ln2_gain, grad_ln2_shift = norm_backward(
        grad_out, normed_two, inv_two, back_gain2.astype(jnp.float32)
    )
    grad_branch = grad_mid.astype(jnp.bfloat16)
    grad_w_down = outer_sum(gelu_low, grad_branch)
    grad_down_bias = jnp.sum(grad_branch.astype(jnp.float32), axis=0)
    grad_gelu = times_back(grad_branch, back_down)
    grad_up = jax.vjp(gelu_exact, up_act)[1](grad_gelu)[0].astype(jnp.bfloat16)
    grad_w_up = outer_sum(hidden_low, grad_up)
    grad_up_bias = jnp.sum(grad_up.astype(jnp.float32), axis=0)
    grad_hidden = times_back(grad_up, back_up) + grad_mid
    grad_first, grad_ln1_gain, grad_ln1_shift = norm_backward(
        grad_hidden, normed_one, inv_one, back_gain1.astype(jnp.float32)
    )
    grad_attn = grad_first.astype(jnp.bfloat16)
    grad_w_out = outer_sum(context_rows, grad_attn)
    grad_out_bias = jnp.sum(grad_attn.astype(jnp.float32), axis=0)
    grad_context = times_back(grad_attn, back_out).astype(jnp.bfloat16)
    grad_ctx_heads = lax.all_to_all(
        to_heads(grad_context, groups), "seq", split_axis=0, concat_axis=0, tiled=True
    )
    grad_ctx_blocks = grad_ctx_heads.reshape(nblocks, qrows, local_heads, head_dim)

    def attend_backward(carry, inputs):
        key_total, value_total = carry
        query, grad_ctx, log_rows = inputs
        scores = masked_scores(query)
        probs = jnp.exp(scores - log_rows[..., None])
        probs_low = probs.astype(jnp.bfloat16)
        d_probs = jnp.einsum(
            "qhd,khd->hqk", grad_ctx, value_heads, preferred_element_type=jnp.float32
        )
        centre = jnp.sum(probs * d_probs, axis=-1, keepdims=True)
        grad_scores = (probs * (d_probs - centre)).astype(jnp.bfloat16)
        grad_query = (
            jnp.einsum("hqk,khd->qhd", grad_scores, key_heads, preferred_element_type=jnp.float32)
            * scale
        )
        key_total = (
            key_total
            + jnp.einsum("hqk,qhd->khd", grad_scores, query, preferred_element_type=jnp.float32)
            * scale
        )
        value_total = value_total + jnp.einsum(
            "hqk,qhd->khd", probs_low, grad_ctx, preferred_element_type=jnp.float32
        )
        return ((key_total, value_total), grad_query.astype(jnp.bfloat16))

    empty = jnp.zeros((stream, local_heads, head_dim), jnp.float32)
    (key_total, value_total), grad_query = lax.scan(
        attend_backward, (empty, empty), (query_blocks, grad_ctx_blocks, log_sums)
    )
    grad_key = key_total.astype(jnp.bfloat16)
    grad_value = value_total.astype(jnp.bfloat16)
    grad_pieces = (
        lax.all_to_all(
            grad_query.reshape(groups, -1), "seq", split_axis=0, concat_axis=0, tiled=True
        ),
        lax.all_to_all(
            grad_key.reshape(groups, -1), "seq", split_axis=0, concat_axis=0, tiled=True
        ),
        lax.all_to_all(
            grad_value.reshape(groups, -1), "seq", split_axis=0, concat_axis=0, tiled=True
        ),
    )
    grad_project = jnp.concatenate(
        [
            from_heads(grad_pieces[0], part_width),
            from_heads(grad_pieces[1], part_width),
            from_heads(grad_pieces[2], part_width),
        ],
        axis=1,
    )
    grad_w_qkv = outer_sum(rows, grad_project)
    bias_sums = jnp.sum(grad_project.astype(jnp.float32), axis=0)
    grad_q_bias = bias_sums[:width]
    grad_v_bias = bias_sums[2 * width :]
    grad_rows = times_back(grad_project, back_qkv) + grad_first
    terms = (
        grad_w_qkv,
        grad_q_bias,
        grad_v_bias,
        grad_w_out,
        grad_out_bias,
        grad_ln1_gain,
        grad_ln1_shift,
        grad_w_up,
        grad_up_bias,
        grad_w_down,
        grad_down_bias,
        grad_ln2_gain,
        grad_ln2_shift,
    )
    page_sums = (
        lax.psum_scatter(
            terms[0].astype(jnp.bfloat16), "dp", scatter_dimension=0, tiled=True
        ).astype(jnp.float32),
        lax.psum_scatter(
            terms[1].astype(jnp.bfloat16), "dp", scatter_dimension=0, tiled=True
        ).astype(jnp.float32),
        lax.psum_scatter(
            terms[2].astype(jnp.bfloat16), "dp", scatter_dimension=0, tiled=True
        ).astype(jnp.float32),
        lax.psum_scatter(
            terms[3].astype(jnp.bfloat16), "dp", scatter_dimension=0, tiled=True
        ).astype(jnp.float32),
        lax.psum_scatter(
            terms[4].astype(jnp.bfloat16), "dp", scatter_dimension=0, tiled=True
        ).astype(jnp.float32),
        lax.psum_scatter(
            terms[5].astype(jnp.bfloat16), "dp", scatter_dimension=0, tiled=True
        ).astype(jnp.float32),
        lax.psum_scatter(
            terms[6].astype(jnp.bfloat16), "dp", scatter_dimension=0, tiled=True
        ).astype(jnp.float32),
        lax.psum_scatter(
            terms[7].astype(jnp.bfloat16), "dp", scatter_dimension=0, tiled=True
        ).astype(jnp.float32),
        lax.psum_scatter(
            terms[8].astype(jnp.bfloat16), "dp", scatter_dimension=0, tiled=True
        ).astype(jnp.float32),
        lax.psum_scatter(
            terms[9].astype(jnp.bfloat16), "dp", scatter_dimension=0, tiled=True
        ).astype(jnp.float32),
        lax.psum_scatter(
            terms[10].astype(jnp.bfloat16), "dp", scatter_dimension=0, tiled=True
        ).astype(jnp.float32),
        lax.psum_scatter(
            terms[11].astype(jnp.bfloat16), "dp", scatter_dimension=0, tiled=True
        ).astype(jnp.float32),
        lax.psum_scatter(
            terms[12].astype(jnp.bfloat16), "dp", scatter_dimension=0, tiled=True
        ).astype(jnp.float32),
    )
    sums = (
        lax.psum_scatter(
            page_sums[0].astype(jnp.bfloat16), "seq", scatter_dimension=0, tiled=True
        ).astype(jnp.float32),
        lax.psum_scatter(
            page_sums[1].astype(jnp.bfloat16), "seq", scatter_dimension=0, tiled=True
        ).astype(jnp.float32),
        lax.psum_scatter(
            page_sums[2].astype(jnp.bfloat16), "seq", scatter_dimension=0, tiled=True
        ).astype(jnp.float32),
        lax.psum_scatter(
            page_sums[3].astype(jnp.bfloat16), "seq", scatter_dimension=0, tiled=True
        ).astype(jnp.float32),
        lax.psum_scatter(
            page_sums[4].astype(jnp.bfloat16), "seq", scatter_dimension=0, tiled=True
        ).astype(jnp.float32),
        lax.psum_scatter(
            page_sums[5].astype(jnp.bfloat16), "seq", scatter_dimension=0, tiled=True
        ).astype(jnp.float32),
        lax.psum_scatter(
            page_sums[6].astype(jnp.bfloat16), "seq", scatter_dimension=0, tiled=True
        ).astype(jnp.float32),
        lax.psum_scatter(
            page_sums[7].astype(jnp.bfloat16), "seq", scatter_dimension=0, tiled=True
        ).astype(jnp.float32),
        lax.psum_scatter(
            page_sums[8].astype(jnp.bfloat16), "seq", scatter_dimension=0, tiled=True
        ).astype(jnp.float32),
        lax.psum_scatter(
            page_sums[9].astype(jnp.bfloat16), "seq", scatter_dimension=0, tiled=True
        ).astype(jnp.float32),
        lax.psum_scatter(
            page_sums[10].astype(jnp.bfloat16), "seq", scatter_dimension=0, tiled=True
        ).astype(jnp.float32),
        lax.psum_scatter(
            page_sums[11].astype(jnp.bfloat16), "seq", scatter_dimension=0, tiled=True
        ).astype(jnp.float32),
        lax.psum_scatter(
            page_sums[12].astype(jnp.bfloat16), "seq", scatter_dimension=0, tiled=True
        ).astype(jnp.float32),
    )
    return (
        output.astype(jnp.bfloat16)[None],
        grad_rows.astype(jnp.bfloat16)[None],
        sums[0],
        sums[1],
        sums[2],
        sums[3],
        sums[4],
        sums[5],
        sums[6],
        sums[7],
        sums[8],
        sums[9],
        sums[10],
        sums[11],
        sums[12],
    )


MESH = pl.DeviceIdType.MESH
CHUNK = 256
MASKED = -1e30


def flip(index, mask):
    for b in range(mask.bit_length()):
        if mask >> b & 1:
            bit = 1 << b
            index = index + bit - 2 * bit * (index // bit % 2)
    return index


class Wires:
    def __init__(self, sems, sizes):
        self.sems, self.sizes = sems, sizes
        self.dp, self.z = lax.axis_index("dp"), lax.axis_index("seq")
        self.dps = [flip(self.dp, m) for m in range(sizes[0])]
        self.zs = [flip(self.z, m) for m in range(sizes[1])]
        self.started = []

    def peer(self, offset, step):
        return (self.dps[offset], self.zs[step])

    def send(self, src, dst, recv_sem, device):
        copy = pltpu.make_async_remote_copy(
            src_ref=src,
            dst_ref=dst,
            send_sem=self.sems.at[len(self.started)],
            recv_sem=recv_sem,
            device_id=device,
            device_id_type=MESH,
        )
        copy.start()
        self.started.append(copy)

    def arrived(self, dst, recv_sem):
        pltpu.make_async_remote_copy(
            src_ref=dst,
            dst_ref=dst,
            send_sem=self.sems.at[0],
            recv_sem=recv_sem,
            device_id=self.peer(1, 0),
            device_id_type=MESH,
        ).wait_recv()

    def drain(self):
        for copy in self.started:
            copy.wait_send()

    def greet(self):
        n_dp, n_seq = self.sizes
        barrier = pltpu.get_barrier_semaphore()
        masks = [1 << b for b in range(n_dp.bit_length() - 1)]
        partners = [self.peer(m, 0) for m in masks] + [self.peer(0, i) for i in range(1, n_seq)]
        for device in partners:
            pl.semaphore_signal(barrier, inc=1, device_id=device, device_id_type=MESH)
        pl.semaphore_wait(barrier, len(partners))


class Gather:
    def __init__(self, wires, src, full, recv, local):
        self.w, self.src, self.full, self.recv, self.local = wires, src, full, recv, local
        n_dp, self.n_seq = wires.sizes
        self.chips = [1 << b for b in range(1, n_dp.bit_length() - 1)]

    def at(self, offset, step):
        return self.full.at[self.w.dps[offset] * self.n_seq + self.w.zs[step]]

    def order(self, step):
        return self.chips if step % 2 == 0 else self.chips[::-1]

    def forward(self, src, offset, step, masks):
        for m in masks:
            self.w.send(src, self.at(offset, step), self.recv.at[offset ^ m, step], self.w.peer(m, 0))

    def wait(self, offset, step):
        self.w.arrived(self.at(offset, step), self.recv.at[offset, step])

    def own(self):
        self.kept = pltpu.make_async_copy(self.src, self.at(0, 0), self.local)
        self.kept.start()
        for i in range(1, self.n_seq):
            self.w.send(self.src, self.at(0, 0), self.recv.at[0, i], self.w.peer(0, i))
        self.forward(self.src, 0, 0, self.order(0) + [1])

    def along_seq(self, i):
        self.wait(0, i)
        self.forward(self.at(0, i), 0, i, self.order(i) + [1])

    def stages(self, step):
        have, out = [0], []
        masks = self.order(step)
        for t, m in enumerate(masks):
            out.append([(o ^ m, masks[t + 1 :] + [1]) for o in have])
            have = have + [o ^ m for o in have]
        return out

    def over_chips(self, t, step):
        for offset, masks in self.stages(step)[t]:
            self.wait(offset, step)
            self.forward(self.at(offset, step), offset, step, masks)

    def over_cores(self):
        n_dp = self.w.sizes[0]
        for offset in range(1, n_dp, 2):
            for i in range(self.n_seq):
                self.wait(offset, i)
        self.kept.wait()

    def steps(self):
        yield self.own
        for i in range(1, self.n_seq):
            yield lambda i=i: self.along_seq(i)
        for t in range(len(self.chips)):
            for i in range(self.n_seq):
                yield lambda t=t, i=i: self.over_chips(t, i)
        yield self.over_cores


def sends_of_gather(n_dp, n_seq):
    return n_seq - 1 + n_seq * (n_dp - 1)


def lanes_of(packed, row, n_dp, n_seq):
    pieces = []
    for d in range(n_dp):
        total = packed[d * n_seq, row : row + 1, :]
        for s in range(1, n_seq):
            total = total + packed[d * n_seq + s, row : row + 1, :]
        pieces.append(total)
    return jnp.concatenate(pieces, axis=1)


def front_kernel(
    sizes,
    heads,
    valid_ref,
    x_ref,
    vec_ref,
    qkv_ref,
    out_ref,
    up_ref,
    down_ref,
    full_vec,
    full_qkv,
    full_out,
    full_up,
    full_down,
    query_out,
    key_out,
    value_out,
    context_out,
    logs_out,
    packed,
    weight,
    sent,
    held,
    context_sent,
    context_held,
    context_turned,
    value_turned,
    logs,
    send_sems,
    gather_sems,
    heads_sems,
    context_sems,
    local_sems,
):
    n_dp, n_seq = sizes
    w = Wires(send_sems, sizes)
    rows, width = x_ref.shape
    part = width // n_seq
    head_dim = width // heads
    local_heads = heads // n_seq
    stream = rows * n_seq
    w.greet()
    sources = ((vec_ref, packed), (qkv_ref, full_qkv), (out_ref, full_out), (up_ref, full_up), (down_ref, full_down))
    gathers = [
        Gather(w, src, dst, gather_sems.at[k], local_sems.at[k]) for k, (src, dst) in enumerate(sources)
    ]
    vec, qkv, out, up, down = [list(g.steps()) for g in gathers]
    queue = []

    def pump(count):
        for _ in range(min(count, len(queue))):
            queue.pop(0)()

    vec[0]()
    qkv[0]()
    for step in vec[1:n_seq]:
        step()
    for step in qkv[1:n_seq]:
        step()
    out[0]()
    for step in vec[n_seq:-1]:
        step()
    for step in qkv[n_seq : 2 * n_seq]:
        step()
    for step in out[1:n_seq]:
        step()
    up[0]()
    for step in qkv[2 * n_seq :]:
        step()
    vec[-1]()
    loads = []
    for t in range(3):
        loads.append(
            pltpu.make_async_copy(
                full_qkv.at[:, :, pl.ds(t * width, width)], weight.at[t], local_sems.at[5 + t]
            )
        )
        loads[-1].start()
    store_vec = pltpu.make_async_copy(packed, full_vec, local_sems.at[8])
    store_vec.start()
    queue.extend(out[n_seq:] + up[1:])
    x = x_ref[...]
    for t in range(3):
        loads[t].wait()
        for j in range(n_seq):
            columns = slice(j * part, (j + 1) * part)
            block = weight[t, :, :, columns].reshape(width, part)
            piece = jnp.dot(x, block, preferred_element_type=jnp.float32)
            if t != 1:
                piece = piece + lanes_of(packed, t // 2, n_dp, n_seq)[:, columns]
            sent[t, j] = piece.astype(jnp.bfloat16)
        for i in range(1, n_seq):
            w.send(sent.at[t, w.zs[i]], held.at[t, w.z], heads_sems.at[t, i], w.peer(0, i))
        held[t, w.z] = sent[t, w.z]
    pump(2 * n_seq)
    queue.append(down[0])
    queue.extend(down[1:])
    pump(n_seq)
    for t in range(3):
        for i in range(1, n_seq):
            w.arrived(held.at[t, w.zs[i]], heads_sems.at[t, i])
    keeps = []
    for t, ref in enumerate((query_out, key_out, value_out)):
        keeps.append(pltpu.make_async_copy(held.at[t], ref, local_sems.at[9 + t]))
        keeps[-1].start()
    position = lax.broadcasted_iota(jnp.int32, (stream, 128), 0)
    lane = lax.broadcasted_iota(jnp.int32, (stream, 128), 1)
    guard = jnp.where((position >= valid_ref[0]) & (lane == 0), MASKED, 0.0).astype(jnp.bfloat16)
    value_turned[...] = held[2].reshape(stream, part).T
    one_lane = lax.broadcasted_iota(jnp.int32, (CHUNK, 128), 1)
    ones = jnp.where(one_lane == 0, 1.0, 0.0).astype(jnp.bfloat16)
    per_block = 128 // head_dim
    scale = 1.0 / math.sqrt(head_dim)
    pumps = -(-len(queue) // local_heads)
    for h in range(local_heads):
        pair = slice(h // per_block * 128, h // per_block * 128 + 128)
        low = h % per_block * head_dim
        keys = jnp.concatenate([held[1, :, :, pair].reshape(stream, 128), guard], axis=1)

        def attend(c, _, keys=keys, pair=pair, low=low, h=h):
            query = held[0, c, :, pair]
            mine = (one_lane >= low) & (one_lane < low + head_dim)
            query = jnp.where(mine, query.astype(jnp.float32) * scale, 0.0).astype(jnp.bfloat16)
            query = jnp.concatenate([query, ones], axis=1)
            scores = lax.dot_general(
                keys, query, (((1,), (1,)), ((), ())), preferred_element_type=jnp.float32
            )
            peak = jnp.max(scores, axis=0, keepdims=True)
            raised = jnp.exp(scores - peak)
            total = jnp.sum(raised, axis=0, keepdims=True)
            mixed = jnp.dot(
                value_turned[h * head_dim : (h + 1) * head_dim, :],
                raised.astype(jnp.bfloat16),
                preferred_element_type=jnp.float32,
            )
            context_turned[c, h * head_dim : (h + 1) * head_dim, :] = mixed / total
            logs[c, h : h + 1, :] = peak + jnp.log(total)
            return 0

        lax.fori_loop(0, n_seq, attend, 0)
        pump(pumps)
    for j in range(n_seq):
        context_sent[j] = context_turned[j].T.astype(jnp.bfloat16)
    for i in range(1, n_seq):
        w.send(context_sent.at[w.zs[i]], context_held.at[w.z], context_sems.at[i], w.peer(0, i))
    context_held[w.z] = context_sent[w.z]
    store_logs = pltpu.make_async_copy(logs, logs_out, local_sems.at[12])
    store_logs.start()
    pump(len(queue))
    for i in range(1, n_seq):
        w.arrived(context_held.at[w.zs[i]], context_sems.at[i])
    for j in range(n_seq):
        keeps.append(
            pltpu.make_async_copy(
                context_held.at[j], context_out.at[:, pl.ds(j * part, part)], local_sems.at[13 + j]
            )
        )
        keeps[-1].start()
    for copy in keeps:
        copy.wait()
    store_logs.wait()
    store_vec.wait()
    w.drain()


def front(sizes, heads, valid, rows, vec, w_qkv, w_out, w_up, w_down):
    n_dp, n_seq = sizes
    devices = n_dp * n_seq
    count, width = rows.shape
    part = width // n_seq
    stream = count * n_seq
    low = jnp.bfloat16
    pieces = jax.ShapeDtypeStruct((n_seq, count, part), low)

    def full(shard):
        return jax.ShapeDtypeStruct((devices,) + shard.shape, shard.dtype)

    anywhere = pl.BlockSpec(memory_space=pl.ANY)
    sends = 5 * sends_of_gather(n_dp, n_seq) + 4 * (n_seq - 1)
    return pl.pallas_call(
        lambda *refs: front_kernel(sizes, heads, *refs),
        out_shape=(
            full(vec),
            full(w_qkv),
            full(w_out),
            full(w_up),
            full(w_down),
            pieces,
            pieces,
            pieces,
            jax.ShapeDtypeStruct((count, width), low),
            jax.ShapeDtypeStruct((n_seq, 8, count), jnp.float32),
        ),
        in_specs=[
            pl.BlockSpec(memory_space=pltpu.SMEM),
            pl.BlockSpec(memory_space=pltpu.VMEM),
        ]
        + [anywhere] * 5,
        out_specs=[anywhere] * 10,
        scratch_shapes=[
            pltpu.VMEM((devices,) + vec.shape, jnp.float32),
            pltpu.VMEM((3, devices, w_qkv.shape[0], width), low),
            pltpu.VMEM((3, n_seq, count, part), low),
            pltpu.VMEM((3, n_seq, count, part), low),
            pltpu.VMEM((n_seq, count, part), low),
            pltpu.VMEM((n_seq, count, part), low),
            pltpu.VMEM((n_seq, part, count), jnp.float32),
            pltpu.VMEM((part, stream), low),
            pltpu.VMEM((n_seq, 8, count), jnp.float32),
            pltpu.SemaphoreType.DMA((sends,)),
            pltpu.SemaphoreType.DMA((5, n_dp, n_seq)),
            pltpu.SemaphoreType.DMA((3, n_seq)),
            pltpu.SemaphoreType.DMA((n_seq,)),
            pltpu.SemaphoreType.DMA((13 + n_seq,)),
        ],
        compiler_params=pltpu.CompilerParams(
            collective_id=0, has_side_effects=True, vmem_limit_bytes=56 * 2**20
        ),
        name="front",
    )(valid, rows, vec, w_qkv, w_out, w_up, w_down)


class Scatter:
    def __init__(self, wires, source, resident, bufs, sems, local, out, out_sem):
        self.w, self.source, self.resident = wires, source, resident
        self.mine, self.total, self.first, self.second, self.last = bufs
        self.core_sems, self.first_sems, self.second_sems, self.last_sems = sems
        self.local, self.out, self.out_sem = local, out, out_sem
        self.n_seq = wires.sizes[1]
        self.offsets = [6, 2, 4, 0]
        self.loads = {}

    def order(self, step):
        return (2, 4) if step % 2 == 0 else (4, 2)

    def group(self, offset):
        return self.source.at[pl.ds(self.w.dps[offset] * self.n_seq, self.n_seq)]

    def load(self, k):
        if self.resident or k >= 4:
            return
        self.loads[k] = pltpu.make_async_copy(
            self.group(self.offsets[k]), self.mine.at[k % 2], self.local.at[k % 2]
        )
        self.loads[k].start()

    def start(self):
        for k, o in enumerate(self.offsets):
            self.w.send(self.group(o ^ 1), self.total.at[o // 2], self.core_sems.at[o // 2], self.w.peer(1, 0))
        self.load(0)
        self.load(1)

    def add(self, into, term):
        rows = into.shape[0]
        step = min(16, rows)

        def body(r, _):
            at = pl.ds(pl.multiple_of(r * step, step), step)
            total = into[at, :].astype(jnp.float32) + term[at, :].astype(jnp.float32)
            into[at, :] = total.astype(into.dtype)
            return 0

        lax.fori_loop(0, rows // step, body, 0)

    def over_cores(self, k):
        o = self.offsets[k]
        self.w.arrived(self.total.at[o // 2], self.core_sems.at[o // 2])
        if not self.resident:
            self.loads[k].wait()
        for i in range(self.n_seq):
            slot = self.w.zs[i]
            mask = self.order(i)[0]
            block = self.total.at[o // 2, slot]
            if self.resident:
                own = self.source.at[self.w.dps[o] * self.n_seq + slot]
            else:
                own = self.mine.at[k % 2, slot]
            self.add(block, own)
            if o & mask:
                keep = (o ^ mask) // mask_rest(mask)
                self.w.send(block, self.first.at[i, keep], self.first_sems.at[i, keep], self.w.peer(mask, 0))
        self.load(k + 2)

    def over_chips(self, i):
        mask = self.order(i)[1]
        for keep in (1, 0):
            o = mask * keep
            block = self.total.at[o // 2, self.w.zs[i]]
            self.w.arrived(self.first.at[i, keep], self.first_sems.at[i, keep])
            self.add(block, self.first.at[i, keep])
            if keep:
                self.w.send(block, self.second.at[i], self.second_sems.at[i], self.w.peer(mask, 0))

    def to_seq(self, i):
        block = self.total.at[0, self.w.zs[i]]
        self.w.arrived(self.second.at[i], self.second_sems.at[i])
        self.add(block, self.second.at[i])
        if i:
            self.w.send(block, self.last.at[i], self.last_sems.at[i], self.w.peer(0, i))

    def finish(self):
        for i in range(1, self.n_seq):
            self.w.arrived(self.last.at[i], self.last_sems.at[i])
        rows = self.out.shape[0]
        step = min(16, rows)
        block = self.total.at[0, self.w.z]

        def body(r, _):
            at = pl.ds(pl.multiple_of(r * step, step), step)
            total = block[at, :].astype(jnp.float32)
            for i in range(1, self.n_seq):
                total = total + self.last[i, at, :].astype(jnp.float32)
            self.out[at, :] = total
            return 0

        lax.fori_loop(0, rows // step, body, 0)

    def steps(self):
        for k in range(4):
            yield lambda k=k: self.over_cores(k)
        for i in range(self.n_seq):
            yield lambda i=i: self.over_chips(i)
        for i in range(self.n_seq):
            yield lambda i=i: self.to_seq(i)
        yield self.finish


def mask_rest(mask):
    return 6 ^ mask


def back_kernel(sizes, heads, *refs):
    n_dp, n_seq = sizes
    (
        valid_ref,
        x_ref,
        grad_context,
        grad_first,
        query_in,
        key_in,
        value_in,
        logs,
        full_qkv,
        down_in,
        up_in,
        out_in,
        vec_in,
        grad_rows,
        *outs,
    ) = refs[:21]
    scratch = list(refs[21:])

    def take(count):
        got = scratch[:count]
        del scratch[:count]
        return got

    send_sems, core_sems, first_sems, second_sems, last_sems, load_sems = take(6)
    head_sems, local_sems = take(2)
    held, masked_query, masked_grad, keys, values, key_turned = take(6)
    query_grad, key_grad, value_grad = take(3)
    sent, landed, x_turned, weight, vec = take(5)
    partials = take(3)
    units = []
    for k in range(7):
        units.append(take(5 if k < 3 else 4))
    w = Wires(send_sems, sizes)
    rows, width = x_ref.shape
    part = width // n_seq
    head_dim = width // heads
    local_heads = heads // n_seq
    stream = rows * n_seq
    per_block = 128 // head_dim
    scale = 1.0 / math.sqrt(head_dim)
    loads = []
    for t, ref in enumerate((query_in, key_in, value_in)):
        loads.append(pltpu.make_async_copy(ref, held.at[t], local_sems.at[t]))
        loads[-1].start()
    load_vec = pltpu.make_async_copy(vec_in, vec, local_sems.at[3])
    load_vec.start()
    w.greet()

    def columns(j):
        return pl.ds(pl.multiple_of(j * part, part), part)

    for i in range(1, n_seq):
        w.send(grad_context.at[:, columns(w.zs[i])], held.at[3, w.z], head_sems.at[3, i], w.peer(0, i))
    own_grad = pltpu.make_async_copy(grad_context.at[:, columns(w.z)], held.at[3, w.z], local_sems.at[4])
    own_grad.start()
    sources = (down_in, up_in, out_in, partials[0], partials[1], partials[2], vec)
    scatters = []
    for k in range(7):
        bufs = units[k] if k < 3 else [None] + units[k]
        scatters.append(
            Scatter(
                w,
                sources[k],
                k >= 3,
                bufs,
                (core_sems.at[k], first_sems.at[k], second_sems.at[k], last_sems.at[k]),
                load_sems.at[min(k, 2)],
                outs[k],
                None,
            )
        )
    down, up, out, dq, dk, dv, small = scatters
    for unit in (down, up, out):
        unit.start()
    queue = []

    def pump(count):
        for _ in range(min(count, len(queue))):
            queue.pop(0)()

    for copy in loads:
        copy.wait()
    lane = lax.broadcasted_iota(jnp.int32, (stream, 128), 1)
    position = lax.broadcasted_iota(jnp.int32, (stream, 128), 0)
    guard = jnp.where((position >= valid_ref[0]) & (lane == 0), MASKED, 0.0).astype(jnp.bfloat16)

    def spread(source, h, factor):
        block = h // per_block * 128
        low = h % per_block * head_dim
        rows_of = source[:, :, block : block + 128].reshape(stream, 128).astype(jnp.float32)
        mine = (lane >= low) & (lane < low + head_dim)
        return jnp.where(mine, rows_of * factor, 0.0).astype(jnp.bfloat16).reshape(n_seq, rows, 128)

    for h in range(local_heads):
        masked_query[h] = spread(held.at[0], h, scale)
    for b in range(local_heads // per_block):
        lanes = slice(b * 128, (b + 1) * 128)
        keys[b, :, :128] = held[1, :, :, lanes].reshape(stream, 128)
        keys[b, :, 128:] = guard
        values[b] = held[2, :, :, lanes].reshape(stream, 128)
    turned = held[1].reshape(stream, part).T
    for h in range(local_heads):
        key_turned[h] = turned[h * head_dim : (h + 1) * head_dim, :]
    key_grad[...] = jnp.zeros_like(key_grad)
    value_grad[...] = jnp.zeros_like(value_grad)
    x_turned[...] = x_ref[...].T
    queue.extend(list(down.steps())[:4])
    pump(4)
    own_grad.wait()
    for i in range(1, n_seq):
        w.arrived(held.at[3, w.zs[i]], head_sems.at[3, i])
    for h in range(local_heads):
        masked_grad[h] = spread(held.at[3], h, 1.0)
    queue.extend(list(up.steps())[:4])
    queue.extend(list(down.steps())[4:])
    queue.extend(list(out.steps())[:4])
    queue.extend(list(up.steps())[4:])
    queue.extend(list(out.steps())[4:])
    pump(4)
    ones = jnp.where(lax.broadcasted_iota(jnp.int32, (rows, 128), 1) == 0, 1.0, 0.0).astype(jnp.bfloat16)
    flat = (((1,), (1,)), ((), ()))
    for i in [1, 2, 3, 0] if n_seq == 4 else list(range(1, n_seq)) + [0]:
        c = w.zs[i]

        def head(h, _, c=c):
            block = h // per_block
            query, grad = masked_query[h, c], masked_grad[h, c]
            scores = lax.dot_general(
                keys[block], jnp.concatenate([query, ones], axis=1), flat, preferred_element_type=jnp.float32
            )
            probs = jnp.exp(scores - logs[c, pl.ds(h, 1), :])
            moved = lax.dot_general(values[block], grad, flat, preferred_element_type=jnp.float32)
            centre = jnp.sum(probs * moved, axis=0, keepdims=True)
            slope = (probs * (moved - centre)).astype(jnp.bfloat16)
            query_grad[h] = jnp.dot(key_turned[h], slope, preferred_element_type=jnp.float32) * scale
            key_grad[block] += jnp.dot(slope, query, preferred_element_type=jnp.float32)
            value_grad[block] += jnp.dot(
                probs.astype(jnp.bfloat16), grad, preferred_element_type=jnp.float32
            )
            return 0

        lax.fori_loop(0, local_heads, head, 0)
        piece = query_grad[...].reshape(part, rows).T.astype(jnp.bfloat16)
        if i:
            sent[0, c] = piece
            w.send(sent.at[0, c], landed.at[0, w.z], head_sems.at[0, i], w.peer(0, i))
        else:
            landed[0, c] = piece
        pump(5)
    for t, total in ((1, key_grad), (2, value_grad)):
        for j in range(n_seq):
            for b in range(local_heads // per_block):
                sent[t, j, :, b * 128 : (b + 1) * 128] = total[b, j * rows : (j + 1) * rows, :].astype(
                    jnp.bfloat16
                )
        for i in range(1, n_seq):
            w.send(sent.at[t, w.zs[i]], landed.at[t, w.z], head_sems.at[t, i], w.peer(0, i))
        landed[t, w.z] = sent[t, w.z]
    weights = [
        pltpu.make_async_copy(full_qkv.at[:, :, pl.ds(t * width, width)], weight.at[t % 2], local_sems.at[5 + t])
        for t in range(3)
    ]
    weights[0].start()
    weights[1].start()
    load_vec.wait()
    turned_x = x_turned[...]
    total_rows = grad_first[...]
    for t, unit in ((0, dq), (1, dk), (2, dv)):
        for i in range(1, n_seq):
            w.arrived(landed.at[t, w.zs[i]], head_sems.at[t, i])
        for j in range(n_seq):
            block = jnp.dot(turned_x, landed[t, j], preferred_element_type=jnp.float32)
            unit.source[:, :, j * part : (j + 1) * part] = block.astype(jnp.bfloat16).reshape(
                n_dp * n_seq, -1, part
            )
        unit.start()
        if t != 1:
            for j in range(n_seq):
                sums = jnp.sum(landed[t, j].astype(jnp.float32), axis=0, keepdims=True)
                for p in range(part // 128):
                    for s in range(n_seq):
                        d = j * (part // 128) + p
                        vec[d * n_seq + s, t // 2 : t // 2 + 1, :] = sums[:, p * 128 : (p + 1) * 128]
        weights[t].wait()
        project = jnp.concatenate([landed[t, j] for j in range(n_seq)], axis=1)
        total_rows = total_rows + lax.dot_general(
            project, weight[t % 2].reshape(width, width), flat, preferred_element_type=jnp.float32
        )
        if t == 0:
            weights[2].start()
        pump(4)
        queue.extend(list(unit.steps())[:4])
        pump(4)
    grad_rows[...] = total_rows.astype(jnp.bfloat16)
    small.start()
    pump(len(queue))
    tails = [list(unit.steps())[4:] for unit in (dq, dk, dv)]
    smalls = list(small.steps())
    order = smalls[:4] + tails[0][:n_seq] + tails[1][:n_seq] + tails[2][:n_seq] + smalls[4 : 4 + n_seq]
    for unit in tails:
        order += unit[n_seq : 2 * n_seq]
    order += smalls[4 + n_seq : 4 + 2 * n_seq] + [unit[-1] for unit in tails] + smalls[-1:]
    for step in order:
        step()
    w.drain()


def back(sizes, heads, valid, rows, grad_context, grad_first, heads_in, logs, full_qkv, partial_sums):
    n_dp, n_seq = sizes
    devices = n_dp * n_seq
    count, width = rows.shape
    part = width // n_seq
    stream = count * n_seq
    head_dim = width // heads
    local_heads = heads // n_seq
    blocks = local_heads * head_dim // 128
    low = jnp.bfloat16
    shard = width // devices
    shapes = [p.shape[1:] for p in partial_sums[:3]] + [(shard, width)] * 3 + [partial_sums[3].shape[1:]]
    kinds = [low] * 6 + [jnp.float32]
    anywhere = pl.BlockSpec(memory_space=pl.ANY)
    local = pl.BlockSpec(memory_space=pltpu.VMEM)
    sends = 7 * (4 + 3 * n_seq + n_seq - 1) + 4 * (n_seq - 1)
    chips = n_dp // 2
    scratch = [
        pltpu.SemaphoreType.DMA((sends,)),
        pltpu.SemaphoreType.DMA((7, chips)),
        pltpu.SemaphoreType.DMA((7, n_seq, 2)),
        pltpu.SemaphoreType.DMA((7, n_seq)),
        pltpu.SemaphoreType.DMA((7, n_seq)),
        pltpu.SemaphoreType.DMA((3, 2)),
        pltpu.SemaphoreType.DMA((4, n_seq)),
        pltpu.SemaphoreType.DMA((8,)),
        pltpu.VMEM((4, n_seq, count, part), low),
        pltpu.VMEM((local_heads, n_seq, count, 128), low),
        pltpu.VMEM((local_heads, n_seq, count, 128), low),
        pltpu.VMEM((blocks, stream, 256), low),
        pltpu.VMEM((blocks, stream, 128), low),
        pltpu.VMEM((local_heads, head_dim, stream), low),
        pltpu.VMEM((local_heads, head_dim, count), jnp.float32),
        pltpu.VMEM((blocks, stream, 128), jnp.float32),
        pltpu.VMEM((blocks, stream, 128), jnp.float32),
        pltpu.VMEM((3, n_seq, count, part), low),
        pltpu.VMEM((3, n_seq, count, part), low),
        pltpu.VMEM((width, count), low),
        pltpu.VMEM((2, devices, shard, width), low),
        pltpu.VMEM(partial_sums[3].shape, jnp.float32),
    ]
    scratch += [pltpu.VMEM((devices, shard, width), low)] * 3
    for k, (shape, kind) in enumerate(zip(shapes, kinds)):
        if k < 3:
            scratch.append(pltpu.VMEM((2, n_seq) + shape, kind))
        scratch += [
            pltpu.VMEM((chips, n_seq) + shape, kind),
            pltpu.VMEM((n_seq, 2) + shape, kind),
            pltpu.VMEM((n_seq,) + shape, kind),
            pltpu.VMEM((n_seq,) + shape, kind),
        ]
    return pl.pallas_call(
        lambda *refs: back_kernel(sizes, heads, *refs),
        out_shape=[jax.ShapeDtypeStruct((count, width), low)]
        + [jax.ShapeDtypeStruct(shape, jnp.float32) for shape in shapes],
        in_specs=[pl.BlockSpec(memory_space=pltpu.SMEM), local, anywhere, local]
        + [anywhere] * 3
        + [local]
        + [anywhere] * 5,
        out_specs=[local] * 8,
        scratch_shapes=scratch,
        compiler_params=pltpu.CompilerParams(
            collective_id=1, has_side_effects=True, vmem_limit_bytes=62 * 2**20
        ),
        name="back",
    )(valid, rows, grad_context, grad_first, *heads_in, logs, full_qkv, *partial_sums)


def spread_lanes(vectors, n_seq):
    stacked = jnp.stack(vectors).astype(jnp.float32)
    tiled = jnp.tile(stacked, (1, n_seq))
    owner = jnp.arange(tiled.shape[1], dtype=jnp.int32) // stacked.shape[1]
    return jnp.where(owner[None, :] == lax.axis_index("seq"), tiled, 0.0)


def kernel_plan(
    x_in,
    w_qkv,
    q_bias,
    v_bias,
    w_out,
    out_bias,
    ln1_gain,
    ln1_shift,
    w_up,
    up_bias,
    w_down,
    down_bias,
    ln2_gain,
    ln2_shift,
    valid,
    cotangent,
):
    sizes = (lax.axis_size("dp"), lax.axis_size("seq"))
    n_dp, groups = sizes
    rows = x_in[0]
    count, width = rows.shape
    vectors = (q_bias, v_bias, out_bias, ln1_gain, ln1_shift, down_bias, ln2_gain, ln2_shift)
    spread = spread_lanes(vectors, groups)
    vec = jnp.concatenate(
        [spread, up_bias.astype(jnp.float32)[None], jnp.zeros((7, spread.shape[1]), jnp.float32)]
    )
    (
        full_vec,
        full_qkv,
        full_out,
        full_up,
        full_down,
        query_heads,
        key_heads,
        value_heads,
        context_rows,
        logs,
    ) = front(sizes, HEADS, valid, rows, vec, w_qkv, w_out, w_up, w_down)
    full_qkv_shards = full_qkv
    full_out = full_out.reshape(width, -1)
    full_up = full_up.reshape(width, -1)
    full_down = full_down.reshape(-1, width)
    by_page = full_vec.reshape(n_dp, groups, 16, -1)
    lined = by_page[:, :, :8].sum(axis=1).transpose(1, 0, 2).reshape(8, width)
    full_obias, full_gain1, full_shift1, full_dbias, full_gain2, full_shift2 = (
        lined[2],
        lined[3],
        lined[4],
        lined[5],
        lined[6],
        lined[7],
    )
    full_ubias = by_page[:, :, 8].reshape(-1)
    attn_out = jnp.dot(
        context_rows, full_out, preferred_element_type=jnp.float32
    ) + full_obias.astype(jnp.float32)
    first_rows = rows.astype(jnp.float32) + attn_out
    hidden, normed_one, inv_one = norm_forward(
        first_rows, full_gain1.astype(jnp.float32), full_shift1.astype(jnp.float32)
    )
    hidden_low = hidden.astype(jnp.bfloat16)
    up_act = jnp.dot(hidden_low, full_up, preferred_element_type=jnp.float32) + full_ubias.astype(
        jnp.float32
    )
    gelu_low = gelu_exact(up_act).astype(jnp.bfloat16)
    branch = jnp.dot(gelu_low, full_down, preferred_element_type=jnp.float32) + full_dbias.astype(
        jnp.float32
    )
    output, normed_two, inv_two = norm_forward(
        hidden + branch, full_gain2.astype(jnp.float32), full_shift2.astype(jnp.float32)
    )
    back_out, back_gain1, back_up, back_down, back_gain2 = (
        full_out,
        full_gain1,
        full_up,
        full_down,
        full_gain2,
    )
    grad_out = cotangent[0].astype(jnp.float32)
    grad_mid, grad_ln2_gain, grad_ln2_shift = norm_backward(
        grad_out, normed_two, inv_two, back_gain2.astype(jnp.float32)
    )
    grad_branch = grad_mid.astype(jnp.bfloat16)
    grad_w_down = outer_sum(gelu_low, grad_branch)
    grad_down_bias = jnp.sum(grad_branch.astype(jnp.float32), axis=0)
    grad_gelu = times_back(grad_branch, back_down)
    grad_up = jax.vjp(gelu_exact, up_act)[1](grad_gelu)[0].astype(jnp.bfloat16)
    grad_w_up = outer_sum(hidden_low, grad_up)
    grad_up_bias = jnp.sum(grad_up.astype(jnp.float32), axis=0)
    grad_hidden = times_back(grad_up, back_up) + grad_mid
    grad_first, grad_ln1_gain, grad_ln1_shift = norm_backward(
        grad_hidden, normed_one, inv_one, back_gain1.astype(jnp.float32)
    )
    grad_attn = grad_first.astype(jnp.bfloat16)
    grad_w_out = outer_sum(context_rows, grad_attn)
    grad_out_bias = jnp.sum(grad_attn.astype(jnp.float32), axis=0)
    grad_context = times_back(grad_attn, back_out).astype(jnp.bfloat16)
    def packed(vector):
        return vector.reshape(n_dp, 1, -1)

    zero = jnp.zeros((width,), jnp.float32)
    sums = (zero, zero, grad_out_bias, grad_ln1_gain, grad_ln1_shift)
    sums += (grad_down_bias, grad_ln2_gain, grad_ln2_shift)
    by_group = jnp.concatenate([packed(v) for v in sums], axis=1)
    by_group = jnp.broadcast_to(by_group[:, None], (n_dp, groups) + by_group.shape[1:])
    by_device = jnp.concatenate(
        [
            by_group.reshape(n_dp * groups, 8, -1),
            grad_up_bias.reshape(n_dp * groups, 1, -1),
            jnp.zeros((n_dp * groups, 7, by_group.shape[-1]), jnp.float32),
        ],
        axis=1,
    )
    devices = n_dp * groups

    def cut(grad):
        return grad.astype(jnp.bfloat16).reshape(devices, -1, grad.shape[1])

    grad_rows, *sums = back(
        sizes,
        HEADS,
        valid,
        rows,
        grad_context,
        grad_first,
        (query_heads, key_heads, value_heads),
        logs,
        full_qkv_shards,
        (cut(grad_w_down), cut(grad_w_up), cut(grad_w_out), by_device),
    )
    vec_sums = sums[6]
    mine = lax.dynamic_slice(
        vec_sums[:8], (0, lax.axis_index("seq") * (width // devices)), (8, width // devices)
    )
    return (
        output.astype(jnp.bfloat16)[None],
        grad_rows[None],
        jnp.concatenate(sums[3:6], axis=1),
        mine[0],
        mine[1],
        sums[2],
        mine[2],
        mine[3],
        mine[4],
        sums[1],
        vec_sums[8],
        sums[0],
        mine[5],
        mine[6],
        mine[7],
    )


def solution(mesh):
    n_dp, n_seq = mesh.shape["dp"], mesh.shape["seq"]

    def per_device(x_in, w_qkv, *rest):
        part, width = w_qkv.shape[0], x_in.shape[2]
        fits = part % 32 == 0 and part * n_seq == 128 and width // n_seq % 128 == 0 and x_in.shape[0] == 1
        plan = kernel_plan if fits else general_plan
        return plan(x_in, w_qkv, *rest)

    return jax.shard_map(
        per_device,
        mesh=mesh,
        in_specs=(
            P("dp", "seq", None),
            P(("dp", "seq"), None),
            P(("dp", "seq")),
            P(("dp", "seq")),
            P(("dp", "seq"), None),
            P(("dp", "seq")),
            P(("dp", "seq")),
            P(("dp", "seq")),
            P(("dp", "seq"), None),
            P(("dp", "seq")),
            P(("dp", "seq"), None),
            P(("dp", "seq")),
            P(("dp", "seq")),
            P(("dp", "seq")),
            P("dp"),
            P("dp", "seq", None),
        ),
        out_specs=(
            P("dp", "seq", None),
            P("dp", "seq", None),
            P(("dp", "seq"), None),
            P(("dp", "seq")),
            P(("dp", "seq")),
            P(("dp", "seq"), None),
            P(("dp", "seq")),
            P(("dp", "seq")),
            P(("dp", "seq")),
            P(("dp", "seq"), None),
            P(("dp", "seq")),
            P(("dp", "seq"), None),
            P(("dp", "seq")),
            P(("dp", "seq")),
            P(("dp", "seq")),
        ),
        check_vma=False,
    )
```

```python
import math

import jax
import jax.numpy as jnp
from jax import lax
from jax.experimental import pallas as pl
from jax.experimental.pallas import tpu as pltpu
from jax.sharding import PartitionSpec as P

HEADS = 16


eps_norm = 1e-05


def outer_sum(left, right):
    return lax.dot_general(
        left, right, (((0,), (0,)), ((), ())), preferred_element_type=jnp.float32
    )


def times_back(rows, matrix):
    return lax.dot_general(
        rows, matrix, (((1,), (1,)), ((), ())), preferred_element_type=jnp.float32
    )


def gelu_exact(values):
    return jax.nn.gelu(values, approximate=False)


def norm_forward(rows, gain, shift):
    center = rows - jnp.mean(rows, axis=-1, keepdims=True)
    inv_std = lax.rsqrt(jnp.mean(center * center, axis=-1, keepdims=True) + eps_norm)
    normed = center * inv_std
    return (normed * gain + shift, normed, inv_std)


def norm_backward(grad_out, normed, inv_std, gain):
    scaled = grad_out * gain
    grad_rows = inv_std * (
        scaled
        - jnp.mean(scaled, axis=-1, keepdims=True)
        - normed * jnp.mean(scaled * normed, axis=-1, keepdims=True)
    )
    return (grad_rows, jnp.sum(grad_out * normed, axis=0), jnp.sum(grad_out, axis=0))


def to_heads(rows, groups):
    count, width = rows.shape
    return rows.reshape(count, groups, width // groups).transpose(1, 0, 2).reshape(groups, -1)


def from_heads(pieces, part_width):
    groups = pieces.shape[0]
    return (
        pieces.reshape(groups, -1, part_width).transpose(1, 0, 2).reshape(-1, groups * part_width)
    )


def general_plan(
    x_in,
    w_qkv,
    q_bias,
    v_bias,
    w_out,
    out_bias,
    ln1_gain,
    ln1_shift,
    w_up,
    up_bias,
    w_down,
    down_bias,
    ln2_gain,
    ln2_shift,
    valid,
    cotangent,
):
    shards = (
        w_qkv,
        q_bias,
        v_bias,
        w_out,
        out_bias,
        ln1_gain,
        ln1_shift,
        w_up,
        up_bias,
        w_down,
        down_bias,
        ln2_gain,
        ln2_shift,
    )
    weights = (
        lax.all_gather(shards[0], ("dp", "seq"), axis=0, tiled=True),
        lax.all_gather(shards[1], ("dp", "seq"), axis=0, tiled=True),
        lax.all_gather(shards[2], ("dp", "seq"), axis=0, tiled=True),
        lax.all_gather(shards[3], ("dp", "seq"), axis=0, tiled=True),
        lax.all_gather(shards[4], ("dp", "seq"), axis=0, tiled=True),
        lax.all_gather(shards[5], ("dp", "seq"), axis=0, tiled=True),
        lax.all_gather(shards[6], ("dp", "seq"), axis=0, tiled=True),
        lax.all_gather(shards[7], ("dp", "seq"), axis=0, tiled=True),
        lax.all_gather(shards[8], ("dp", "seq"), axis=0, tiled=True),
        lax.all_gather(shards[9], ("dp", "seq"), axis=0, tiled=True),
        lax.all_gather(shards[10], ("dp", "seq"), axis=0, tiled=True),
        lax.all_gather(shards[11], ("dp", "seq"), axis=0, tiled=True),
        lax.all_gather(shards[12], ("dp", "seq"), axis=0, tiled=True),
    )
    (
        full_qkv,
        full_qbias,
        full_vbias,
        full_out,
        full_obias,
        full_gain1,
        full_shift1,
        full_up,
        full_ubias,
        full_down,
        full_dbias,
        full_gain2,
        full_shift2,
    ) = weights
    groups = lax.axis_size("seq")
    rows = x_in[0]
    count, width = rows.shape
    head_dim = width // HEADS
    part_width = width // groups
    local_heads = HEADS // groups
    stream = count * groups
    qrows = min(512, stream)
    nblocks = stream // qrows
    scale = 1.0 / math.sqrt(head_dim)
    keep = jnp.arange(stream, dtype=jnp.int32) < valid[0]
    bias_row = jnp.concatenate([full_qbias, jnp.zeros_like(full_qbias), full_vbias]).astype(
        jnp.float32
    )
    project = (jnp.dot(rows, full_qkv, preferred_element_type=jnp.float32) + bias_row).astype(
        jnp.bfloat16
    )
    sent = (
        to_heads(project[:, :width], groups),
        to_heads(project[:, width : 2 * width], groups),
        to_heads(project[:, 2 * width :], groups),
    )
    arrived = (
        lax.all_to_all(sent[0], "seq", split_axis=0, concat_axis=0, tiled=True),
        lax.all_to_all(sent[1], "seq", split_axis=0, concat_axis=0, tiled=True),
        lax.all_to_all(sent[2], "seq", split_axis=0, concat_axis=0, tiled=True),
    )
    query_blocks = arrived[0].reshape(nblocks, qrows, local_heads, head_dim)
    key_heads = arrived[1].reshape(stream, local_heads, head_dim)
    value_heads = arrived[2].reshape(stream, local_heads, head_dim)

    def masked_scores(query):
        scores = (
            jnp.einsum("qhd,khd->hqk", query, key_heads, preferred_element_type=jnp.float32) * scale
        )
        return jnp.where(keep[None, None, :], scores, -1e30)

    def attend_forward(query):
        scores = masked_scores(query)
        peak = jnp.max(scores, axis=-1, keepdims=True)
        raised = jnp.exp(scores - peak)
        total = jnp.sum(raised, axis=-1, keepdims=True)
        probs = (raised / total).astype(jnp.bfloat16)
        context = jnp.einsum("hqk,khd->qhd", probs, value_heads, preferred_element_type=jnp.float32)
        return (context.astype(jnp.bfloat16), (peak + jnp.log(total))[..., 0])

    context, log_sums = lax.map(attend_forward, query_blocks)
    returned_ctx = lax.all_to_all(
        context.reshape(groups, -1), "seq", split_axis=0, concat_axis=0, tiled=True
    )
    context_rows = from_heads(returned_ctx, part_width)
    attn_out = jnp.dot(
        context_rows, full_out, preferred_element_type=jnp.float32
    ) + full_obias.astype(jnp.float32)
    first_rows = rows.astype(jnp.float32) + attn_out
    hidden, normed_one, inv_one = norm_forward(
        first_rows, full_gain1.astype(jnp.float32), full_shift1.astype(jnp.float32)
    )
    hidden_low = hidden.astype(jnp.bfloat16)
    up_act = jnp.dot(hidden_low, full_up, preferred_element_type=jnp.float32) + full_ubias.astype(
        jnp.float32
    )
    gelu_low = gelu_exact(up_act).astype(jnp.bfloat16)
    branch = jnp.dot(gelu_low, full_down, preferred_element_type=jnp.float32) + full_dbias.astype(
        jnp.float32
    )
    output, normed_two, inv_two = norm_forward(
        hidden + branch, full_gain2.astype(jnp.float32), full_shift2.astype(jnp.float32)
    )
    again = (
        lax.all_gather(shards[0], ("dp", "seq"), axis=0, tiled=True),
        lax.all_gather(shards[1], ("dp", "seq"), axis=0, tiled=True),
        lax.all_gather(shards[2], ("dp", "seq"), axis=0, tiled=True),
        lax.all_gather(shards[3], ("dp", "seq"), axis=0, tiled=True),
        lax.all_gather(shards[4], ("dp", "seq"), axis=0, tiled=True),
        lax.all_gather(shards[5], ("dp", "seq"), axis=0, tiled=True),
        lax.all_gather(shards[6], ("dp", "seq"), axis=0, tiled=True),
        lax.all_gather(shards[7], ("dp", "seq"), axis=0, tiled=True),
        lax.all_gather(shards[8], ("dp", "seq"), axis=0, tiled=True),
        lax.all_gather(shards[9], ("dp", "seq"), axis=0, tiled=True),
        lax.all_gather(shards[10], ("dp", "seq"), axis=0, tiled=True),
        lax.all_gather(shards[11], ("dp", "seq"), axis=0, tiled=True),
        lax.all_gather(shards[12], ("dp", "seq"), axis=0, tiled=True),
    )
    back_qkv, back_out, back_gain1, back_up, back_down, back_gain2 = (
        again[0],
        again[3],
        again[5],
        again[7],
        again[9],
        again[11],
    )
    grad_out = cotangent[0].astype(jnp.float32)
    grad_mid, grad_ln2_gain, grad_ln2_shift = norm_backward(
        grad_out, normed_two, inv_two, back_gain2.astype(jnp.float32)
    )
    grad_branch = grad_mid.astype(jnp.bfloat16)
    grad_w_down = outer_sum(gelu_low, grad_branch)
    grad_down_bias = jnp.sum(grad_branch.astype(jnp.float32), axis=0)
    grad_gelu = times_back(grad_branch, back_down)
    grad_up = jax.vjp(gelu_exact, up_act)[1](grad_gelu)[0].astype(jnp.bfloat16)
    grad_w_up = outer_sum(hidden_low, grad_up)
    grad_up_bias = jnp.sum(grad_up.astype(jnp.float32), axis=0)
    grad_hidden = times_back(grad_up, back_up) + grad_mid
    grad_first, grad_ln1_gain, grad_ln1_shift = norm_backward(
        grad_hidden, normed_one, inv_one, back_gain1.astype(jnp.float32)
    )
    grad_attn = grad_first.astype(jnp.bfloat16)
    grad_w_out = outer_sum(context_rows, grad_attn)
    grad_out_bias = jnp.sum(grad_attn.astype(jnp.float32), axis=0)
    grad_context = times_back(grad_attn, back_out).astype(jnp.bfloat16)
    grad_ctx_heads = lax.all_to_all(
        to_heads(grad_context, groups), "seq", split_axis=0, concat_axis=0, tiled=True
    )
    grad_ctx_blocks = grad_ctx_heads.reshape(nblocks, qrows, local_heads, head_dim)

    def attend_backward(carry, inputs):
        key_total, value_total = carry
        query, grad_ctx, log_rows = inputs
        scores = masked_scores(query)
        probs = jnp.exp(scores - log_rows[..., None])
        probs_low = probs.astype(jnp.bfloat16)
        d_probs = jnp.einsum(
            "qhd,khd->hqk", grad_ctx, value_heads, preferred_element_type=jnp.float32
        )
        centre = jnp.sum(probs * d_probs, axis=-1, keepdims=True)
        grad_scores = (probs * (d_probs - centre)).astype(jnp.bfloat16)
        grad_query = (
            jnp.einsum("hqk,khd->qhd", grad_scores, key_heads, preferred_element_type=jnp.float32)
            * scale
        )
        key_total = (
            key_total
            + jnp.einsum("hqk,qhd->khd", grad_scores, query, preferred_element_type=jnp.float32)
            * scale
        )
        value_total = value_total + jnp.einsum(
            "hqk,qhd->khd", probs_low, grad_ctx, preferred_element_type=jnp.float32
        )
        return ((key_total, value_total), grad_query.astype(jnp.bfloat16))

    empty = jnp.zeros((stream, local_heads, head_dim), jnp.float32)
    (key_total, value_total), grad_query = lax.scan(
        attend_backward, (empty, empty), (query_blocks, grad_ctx_blocks, log_sums)
    )
    grad_key = key_total.astype(jnp.bfloat16)
    grad_value = value_total.astype(jnp.bfloat16)
    grad_pieces = (
        lax.all_to_all(
            grad_query.reshape(groups, -1), "seq", split_axis=0, concat_axis=0, tiled=True
        ),
        lax.all_to_all(
            grad_key.reshape(groups, -1), "seq", split_axis=0, concat_axis=0, tiled=True
        ),
        lax.all_to_all(
            grad_value.reshape(groups, -1), "seq", split_axis=0, concat_axis=0, tiled=True
        ),
    )
    grad_project = jnp.concatenate(
        [
            from_heads(grad_pieces[0], part_width),
            from_heads(grad_pieces[1], part_width),
            from_heads(grad_pieces[2], part_width),
        ],
        axis=1,
    )
    grad_w_qkv = outer_sum(rows, grad_project)
    bias_sums = jnp.sum(grad_project.astype(jnp.float32), axis=0)
    grad_q_bias = bias_sums[:width]
    grad_v_bias = bias_sums[2 * width :]
    grad_rows = times_back(grad_project, back_qkv) + grad_first
    terms = (
        grad_w_qkv,
        grad_q_bias,
        grad_v_bias,
        grad_w_out,
        grad_out_bias,
        grad_ln1_gain,
        grad_ln1_shift,
        grad_w_up,
        grad_up_bias,
        grad_w_down,
        grad_down_bias,
        grad_ln2_gain,
        grad_ln2_shift,
    )
    page_sums = (
        lax.psum_scatter(
            terms[0].astype(jnp.bfloat16), "dp", scatter_dimension=0, tiled=True
        ).astype(jnp.float32),
        lax.psum_scatter(
            terms[1].astype(jnp.bfloat16), "dp", scatter_dimension=0, tiled=True
        ).astype(jnp.float32),
        lax.psum_scatter(
            terms[2].astype(jnp.bfloat16), "dp", scatter_dimension=0, tiled=True
        ).astype(jnp.float32),
        lax.psum_scatter(
            terms[3].astype(jnp.bfloat16), "dp", scatter_dimension=0, tiled=True
        ).astype(jnp.float32),
        lax.psum_scatter(
            terms[4].astype(jnp.bfloat16), "dp", scatter_dimension=0, tiled=True
        ).astype(jnp.float32),
        lax.psum_scatter(
            terms[5].astype(jnp.bfloat16), "dp", scatter_dimension=0, tiled=True
        ).astype(jnp.float32),
        lax.psum_scatter(
            terms[6].astype(jnp.bfloat16), "dp", scatter_dimension=0, tiled=True
        ).astype(jnp.float32),
        lax.psum_scatter(
            terms[7].astype(jnp.bfloat16), "dp", scatter_dimension=0, tiled=True
        ).astype(jnp.float32),
        lax.psum_scatter(
            terms[8].astype(jnp.bfloat16), "dp", scatter_dimension=0, tiled=True
        ).astype(jnp.float32),
        lax.psum_scatter(
            terms[9].astype(jnp.bfloat16), "dp", scatter_dimension=0, tiled=True
        ).astype(jnp.float32),
        lax.psum_scatter(
            terms[10].astype(jnp.bfloat16), "dp", scatter_dimension=0, tiled=True
        ).astype(jnp.float32),
        lax.psum_scatter(
            terms[11].astype(jnp.bfloat16), "dp", scatter_dimension=0, tiled=True
        ).astype(jnp.float32),
        lax.psum_scatter(
            terms[12].astype(jnp.bfloat16), "dp", scatter_dimension=0, tiled=True
        ).astype(jnp.float32),
    )
    sums = (
        lax.psum_scatter(
            page_sums[0].astype(jnp.bfloat16), "seq", scatter_dimension=0, tiled=True
        ).astype(jnp.float32),
        lax.psum_scatter(
            page_sums[1].astype(jnp.bfloat16), "seq", scatter_dimension=0, tiled=True
        ).astype(jnp.float32),
        lax.psum_scatter(
            page_sums[2].astype(jnp.bfloat16), "seq", scatter_dimension=0, tiled=True
        ).astype(jnp.float32),
        lax.psum_scatter(
            page_sums[3].astype(jnp.bfloat16), "seq", scatter_dimension=0, tiled=True
        ).astype(jnp.float32),
        lax.psum_scatter(
            page_sums[4].astype(jnp.bfloat16), "seq", scatter_dimension=0, tiled=True
        ).astype(jnp.float32),
        lax.psum_scatter(
            page_sums[5].astype(jnp.bfloat16), "seq", scatter_dimension=0, tiled=True
        ).astype(jnp.float32),
        lax.psum_scatter(
            page_sums[6].astype(jnp.bfloat16), "seq", scatter_dimension=0, tiled=True
        ).astype(jnp.float32),
        lax.psum_scatter(
            page_sums[7].astype(jnp.bfloat16), "seq", scatter_dimension=0, tiled=True
        ).astype(jnp.float32),
        lax.psum_scatter(
            page_sums[8].astype(jnp.bfloat16), "seq", scatter_dimension=0, tiled=True
        ).astype(jnp.float32),
        lax.psum_scatter(
            page_sums[9].astype(jnp.bfloat16), "seq", scatter_dimension=0, tiled=True
        ).astype(jnp.float32),
        lax.psum_scatter(
            page_sums[10].astype(jnp.bfloat16), "seq", scatter_dimension=0, tiled=True
        ).astype(jnp.float32),
        lax.psum_scatter(
            page_sums[11].astype(jnp.bfloat16), "seq", scatter_dimension=0, tiled=True
        ).astype(jnp.float32),
        lax.psum_scatter(
            page_sums[12].astype(jnp.bfloat16), "seq", scatter_dimension=0, tiled=True
        ).astype(jnp.float32),
    )
    return (
        output.astype(jnp.bfloat16)[None],
        grad_rows.astype(jnp.bfloat16)[None],
        sums[0],
        sums[1],
        sums[2],
        sums[3],
        sums[4],
        sums[5],
        sums[6],
        sums[7],
        sums[8],
        sums[9],
        sums[10],
        sums[11],
        sums[12],
    )


MESH = pl.DeviceIdType.MESH
CHUNK = 256
MASKED = -1e30
FLAT = (((1,), (1,)), ((), ()))


def flip(index, mask):
    for b in range(mask.bit_length()):
        if mask >> b & 1:
            bit = 1 << b
            index = index + bit - 2 * bit * (index // bit % 2)
    return index


def guarded(when, action):
    if when is None:
        action()
    else:
        pl.when(when)(action)


class Wires:
    def __init__(self, sems, sizes):
        self.sems, self.sizes = sems, sizes
        self.dp, self.z = lax.axis_index("dp"), lax.axis_index("seq")
        self.dps = [flip(self.dp, m) for m in range(sizes[0])]
        self.zs = [flip(self.z, m) for m in range(sizes[1])]
        last = sizes[1] - 1
        half = self.z // 2
        step = 1 - 2 * half
        depth = self.z * step + last * half
        self.inner, self.outer = depth == 1, depth == 0
        self.right = self.z + step
        self.left = self.z - step * depth
        self.far = [self.z] + [t * step + last * half for t in (1 - depth, 2, 3)]
        self.started = []

    def peer(self, offset, step):
        return (self.dps[offset], self.zs[step])

    def send(self, src, dst, recv_sem, device, when=None):
        copy = pltpu.make_async_remote_copy(
            src_ref=src,
            dst_ref=dst,
            send_sem=self.sems.at[len(self.started)],
            recv_sem=recv_sem,
            device_id=device,
            device_id_type=MESH,
        )
        guarded(when, copy.start)
        self.started.append((copy, when))

    def arrived(self, dst, recv_sem, when=None):
        copy = pltpu.make_async_remote_copy(
            src_ref=dst,
            dst_ref=dst,
            send_sem=self.sems.at[0],
            recv_sem=recv_sem,
            device_id=self.peer(1, 0),
            device_id_type=MESH,
        )
        guarded(when, copy.wait_recv)

    def drain(self):
        for copy, when in self.started:
            guarded(when, copy.wait_send)

    def greet(self):
        n_dp, n_seq = self.sizes
        barrier = pltpu.get_barrier_semaphore()
        masks = [1 << b for b in range(n_dp.bit_length() - 1)]
        partners = [self.peer(m, 0) for m in masks] + [self.peer(0, i) for i in range(1, n_seq)]
        for device in partners:
            pl.semaphore_signal(barrier, inc=1, device_id=device, device_id_type=MESH)
        pl.semaphore_wait(barrier, len(partners))


class Line:
    def __init__(self, wires, slot, recv):
        self.w, self.slot, self.recv = wires, slot, recv

    def pass_on(self, k, src, to_left):
        w = self.w
        s = w.far[k]
        dst = self.slot(s)
        if to_left:
            w.send(src, dst, self.recv.at[s], (w.dp, w.left), w.inner)
        else:
            w.send(src, dst, self.recv.at[s], (w.dp, w.right), None if k == 0 else w.inner)

    def own(self, src):
        self.pass_on(0, src, False)
        self.pass_on(0, src, True)

    def take(self, k):
        s = self.w.far[k]
        self.w.arrived(self.slot(s), self.recv.at[s])
        self.pass_on(k, self.slot(s), k > 1)


class Gather:
    def __init__(self, wires, src, full, recv, local):
        self.w, self.src, self.full, self.recv, self.local = wires, src, full, recv, local
        n_dp, self.n_seq = wires.sizes
        self.chips = [1 << b for b in range(1, n_dp.bit_length() - 1)]
        self.slots = wires.far
        self.line = Line(wires, lambda s: full.at[wires.dp * self.n_seq + s], recv.at[0])

    def at(self, offset, step):
        return self.full.at[self.w.dps[offset] * self.n_seq + self.slots[step]]

    def order(self, step):
        return self.chips if step % 2 == 0 else self.chips[::-1]

    def forward(self, src, offset, step, masks):
        for m in masks:
            sem = self.recv.at[offset ^ m, self.slots[step]]
            self.w.send(src, self.at(offset, step), sem, self.w.peer(m, 0))

    def wait(self, offset, step):
        self.w.arrived(self.at(offset, step), self.recv.at[offset, self.slots[step]])

    def mine(self):
        return self.src

    def own_chips(self):
        self.kept = pltpu.make_async_copy(self.mine(), self.at(0, 0), self.local)
        self.kept.start()
        self.forward(self.mine(), 0, 0, self.order(0) + [1])

    def own_seq(self):
        self.line.own(self.src)

    def along_seq(self, i):
        self.line.take(i)
        self.forward(self.at(0, i), 0, i, self.order(i) + [1])

    def stages(self, step):
        have, out = [0], []
        masks = self.order(step)
        for t, m in enumerate(masks):
            out.append([(o ^ m, masks[t + 1 :] + [1]) for o in have])
            have = have + [o ^ m for o in have]
        return out

    def over_chips(self, t, step):
        for offset, masks in self.stages(step)[t]:
            self.wait(offset, step)
            self.forward(self.at(offset, step), offset, step, masks)

    def over_cores(self):
        n_dp = self.w.sizes[0]
        for offset in range(1, n_dp, 2):
            for i in range(self.n_seq):
                self.wait(offset, i)
        self.kept.wait()

    def seq_steps(self):
        return [lambda i=i: self.along_seq(i) for i in range(1, self.n_seq)]

    def chip_steps(self, t):
        return [lambda i=i: self.over_chips(t, i) for i in range(self.n_seq)]


class GatherColumns(Gather):
    def __init__(self, *args):
        super().__init__(*args)
        self.slots = self.w.zs

    def mine(self):
        return self.src.at[self.w.z]

    def own_seq(self):
        for i in range(1, self.n_seq):
            sem = self.recv.at[0, self.w.z]
            self.w.send(self.src.at[self.w.zs[i]], self.at(0, 0), sem, self.w.peer(0, i))

    def along_seq(self, i):
        self.wait(0, i)
        self.forward(self.at(0, i), 0, i, self.order(i) + [1])


def sends_of_gather(n_dp, n_seq):
    return 2 + n_seq - 1 + n_seq * (n_dp - 1)


def group_lanes(packed, row, group, n_seq):
    total = packed[group * n_seq, row : row + 1, :]
    for s in range(1, n_seq):
        total = total + packed[group * n_seq + s, row : row + 1, :]
    return total


def front_kernel(
    sizes,
    heads,
    valid_ref,
    x_ref,
    vec_ref,
    qkv_ref,
    out_ref,
    up_ref,
    down_ref,
    full_vec,
    columns_out,
    full_out,
    full_up,
    full_down,
    page_out,
    query_out,
    key_out,
    value_out,
    context_out,
    logs_out,
    packed,
    columns,
    page,
    held,
    context_sent,
    context_held,
    context_turned,
    value_turned,
    logs,
    send_sems,
    gather_sems,
    page_sems,
    context_sems,
    local_sems,
):
    n_dp, n_seq = sizes
    w = Wires(send_sems, sizes)
    rows, width = x_ref.shape
    part = width // n_seq
    head_dim = width // heads
    local_heads = heads // n_seq
    stream = rows * n_seq
    w.greet()
    line = Line(w, lambda s: page.at[s], page_sems)
    line.own(x_ref)
    sources = ((vec_ref, packed), (qkv_ref, columns), (out_ref, full_out), (up_ref, full_up), (down_ref, full_down))
    vec, qkv, out, up, down = [
        (GatherColumns if k == 1 else Gather)(w, src, dst, gather_sems.at[k], local_sems.at[k])
        for k, (src, dst) in enumerate(sources)
    ]
    queue = []

    def pump(count):
        for _ in range(min(count, len(queue))):
            queue.pop(0)()

    def run(steps):
        for step in steps:
            step()

    for unit in (qkv, vec):
        unit.own_seq()
        unit.own_chips()
    out.own_chips()
    up.own_chips()
    page[w.z] = x_ref[...]
    for unit in (qkv, vec):
        run(unit.seq_steps())
    line.take(1)
    out.own_seq()
    for unit in (qkv, vec):
        run(unit.chip_steps(0))
    for unit in (qkv, vec):
        run(unit.chip_steps(1))
    line.take(2)
    up.own_seq()
    qkv.over_cores()
    vec.over_cores()
    keeps = [
        pltpu.make_async_copy(packed, full_vec, local_sems.at[5]),
        pltpu.make_async_copy(columns, columns_out, local_sems.at[6]),
    ]
    for copy in keeps:
        copy.start()
    groups = part // 128
    biases = [
        jnp.concatenate([group_lanes(packed, b, w.z * groups + g, n_seq) for g in range(groups)], axis=1)
        for b in range(2)
    ]
    matrix = columns[...].reshape(width, 3 * part)

    def project(s):
        piece = jnp.dot(page[s], matrix, preferred_element_type=jnp.float32)
        for t in range(3):
            third = piece[:, t * part : (t + 1) * part]
            if t != 1:
                third = third + biases[t // 2]
            held[t, s] = third.astype(jnp.bfloat16)

    project(w.z)
    project(w.far[1])
    run(out.seq_steps())
    down.own_chips()
    project(w.far[2])
    line.take(3)
    project(w.far[3])
    keeps.append(pltpu.make_async_copy(page, page_out, local_sems.at[7]))
    keeps[-1].start()
    for t, ref in enumerate((query_out, key_out, value_out)):
        keeps.append(pltpu.make_async_copy(held.at[t], ref, local_sems.at[8 + t]))
        keeps[-1].start()
    position = lax.broadcasted_iota(jnp.int32, (stream, 128), 0)
    lane = lax.broadcasted_iota(jnp.int32, (stream, 128), 1)
    guard = jnp.where((position >= valid_ref[0]) & (lane == 0), MASKED, 0.0).astype(jnp.bfloat16)
    value_turned[...] = held[2].reshape(stream, part).T
    one_lane = lax.broadcasted_iota(jnp.int32, (rows, 128), 1)
    ones = jnp.where(one_lane == 0, 1.0, 0.0).astype(jnp.bfloat16)
    per_block = 128 // head_dim
    scale = 1.0 / math.sqrt(head_dim)
    queue += up.seq_steps()[:1] + out.chip_steps(0) + up.seq_steps()[1:] + [down.own_seq]
    queue += out.chip_steps(1) + up.chip_steps(0) + down.seq_steps()
    counts = (2, 4, 3, 5)
    for h in range(local_heads):
        pair = slice(h // per_block * 128, h // per_block * 128 + 128)
        low = h % per_block * head_dim
        keys = jnp.concatenate([held[1, :, :, pair].reshape(stream, 128), guard], axis=1)

        def attend(c, _, keys=keys, pair=pair, low=low, h=h):
            query = held[0, c, :, pair]
            mine = (one_lane >= low) & (one_lane < low + head_dim)
            query = jnp.where(mine, query.astype(jnp.float32) * scale, 0.0).astype(jnp.bfloat16)
            query = jnp.concatenate([query, ones], axis=1)
            scores = lax.dot_general(keys, query, FLAT, preferred_element_type=jnp.float32)
            peak = jnp.max(scores, axis=0, keepdims=True)
            raised = jnp.exp(scores - peak)
            total = jnp.sum(raised, axis=0, keepdims=True)
            mixed = jnp.dot(
                value_turned[h * head_dim : (h + 1) * head_dim, :],
                raised.astype(jnp.bfloat16),
                preferred_element_type=jnp.float32,
            )
            context_turned[c, h * head_dim : (h + 1) * head_dim, :] = mixed / total
            logs[c, h : h + 1, :] = peak + jnp.log(total)
            return 0

        lax.fori_loop(0, n_seq, attend, 0)
        pump(counts[h])
    for j in range(n_seq):
        context_sent[j] = context_turned[j].T.astype(jnp.bfloat16)
    for i in range(1, n_seq):
        w.send(context_sent.at[w.zs[i]], context_held.at[w.z], context_sems.at[i], w.peer(0, i))
    context_held[w.z] = context_sent[w.z]
    keeps.append(pltpu.make_async_copy(logs, logs_out, local_sems.at[11]))
    keeps[-1].start()
    pump(len(queue))
    run(up.chip_steps(1))
    run(down.chip_steps(0))
    run(down.chip_steps(1))
    for i in range(1, n_seq):
        w.arrived(context_held.at[w.zs[i]], context_sems.at[i])
    for j in range(n_seq):
        keeps.append(
            pltpu.make_async_copy(
                context_held.at[j], context_out.at[:, pl.ds(j * part, part)], local_sems.at[12 + j]
            )
        )
        keeps[-1].start()
    for unit in (out, up, down):
        unit.over_cores()
    for copy in keeps:
        copy.wait()
    w.drain()


def front(sizes, heads, valid, rows, vec, w_columns, w_out, w_up, w_down):
    n_dp, n_seq = sizes
    devices = n_dp * n_seq
    count, width = rows.shape
    part = width // n_seq
    stream = count * n_seq
    low = jnp.bfloat16
    pieces = jax.ShapeDtypeStruct((n_seq, count, part), low)

    def full(shard):
        return jax.ShapeDtypeStruct((devices,) + shard.shape, shard.dtype)

    anywhere = pl.BlockSpec(memory_space=pl.ANY)
    sends = 5 * sends_of_gather(n_dp, n_seq) + 5 + n_seq - 1
    return pl.pallas_call(
        lambda *refs: front_kernel(sizes, heads, *refs),
        out_shape=(
            full(vec),
            jax.ShapeDtypeStruct((devices,) + w_columns.shape[1:], low),
            full(w_out),
            full(w_up),
            full(w_down),
            jax.ShapeDtypeStruct((n_seq, count, width), low),
            pieces,
            pieces,
            pieces,
            jax.ShapeDtypeStruct((count, width), low),
            jax.ShapeDtypeStruct((n_seq, 8, count), jnp.float32),
        ),
        in_specs=[
            pl.BlockSpec(memory_space=pltpu.SMEM),
            pl.BlockSpec(memory_space=pltpu.VMEM),
        ]
        + [anywhere] * 5,
        out_specs=[anywhere] * 11,
        scratch_shapes=[
            pltpu.VMEM((devices,) + vec.shape, jnp.float32),
            pltpu.VMEM((devices,) + w_columns.shape[1:], low),
            pltpu.VMEM((n_seq, count, width), low),
            pltpu.VMEM((3, n_seq, count, part), low),
            pltpu.VMEM((n_seq, count, part), low),
            pltpu.VMEM((n_seq, count, part), low),
            pltpu.VMEM((n_seq, part, count), jnp.float32),
            pltpu.VMEM((part, stream), low),
            pltpu.VMEM((n_seq, 8, count), jnp.float32),
            pltpu.SemaphoreType.DMA((sends,)),
            pltpu.SemaphoreType.DMA((5, n_dp, n_seq)),
            pltpu.SemaphoreType.DMA((n_seq,)),
            pltpu.SemaphoreType.DMA((n_seq,)),
            pltpu.SemaphoreType.DMA((12 + n_seq,)),
        ],
        compiler_params=pltpu.CompilerParams(
            collective_id=0, has_side_effects=True, vmem_limit_bytes=56 * 2**20
        ),
        name="front",
    )(valid, rows, vec, w_columns, w_out, w_up, w_down)


def add_rows(into, term):
    rows = into.shape[0]
    step = min(16, rows)

    def body(r, _):
        at = pl.ds(pl.multiple_of(r * step, step), step)
        total = into[at, :].astype(jnp.float32) + term[at, :].astype(jnp.float32)
        into[at, :] = total.astype(into.dtype)
        return 0

    lax.fori_loop(0, rows // step, body, 0)


class LineSum:
    def __init__(self, wires, block, last, sems):
        self.w, self.block, self.last, self.sems = wires, block, last, sems

    def into(self, src, index, device, when):
        self.w.send(src, self.last.at[index], self.sems.at[index], device, when)

    def add(self, k, index):
        def action():
            self.w.arrived(self.last.at[index], self.sems.at[index])
            add_rows(self.block(k), self.last.at[index])

        pl.when(self.w.inner)(action)

    def offer(self, k):
        self.into(self.block(k), k - 1, (self.w.dp, self.w.right), self.w.outer)

    def relay(self, k):
        w, block = self.w, self.block(k)
        if k == 1:
            self.add(1, 4)
            self.into(block, 3, (w.dp, w.left), w.inner)
        else:
            self.add(k, k - 1)
            self.into(block, 3 if k == 2 else 4, (w.dp, w.right), w.inner)

    def finish(self, start, out):
        w = self.w
        w.arrived(self.last.at[3], self.sems.at[3])
        w.arrived(self.last.at[0], self.sems.at[0], w.inner)
        rows = out.shape[0]
        step = min(16, rows)

        def total_of(count):
            def body(r, _):
                at = pl.ds(pl.multiple_of(r * step, step), step)
                total = start(at) + self.last[3, at, :].astype(jnp.float32)
                if count == 2:
                    total = total + self.last[0, at, :].astype(jnp.float32)
                out[at, :] = total.astype(out.dtype)
                return 0

            lax.fori_loop(0, rows // step, body, 0)

        pl.when(w.inner)(lambda: total_of(2))
        pl.when(w.outer)(lambda: total_of(1))


class Scatter:
    def __init__(self, wires, kind, source, resident, bufs, sems, local, out):
        self.w, self.kind, self.source, self.resident = wires, kind, source, resident
        self.mine, self.total, self.first, self.second, self.last = bufs
        self.core_sems, self.first_sems, self.second_sems, self.last_sems = sems
        self.local, self.out = local, out
        self.n_seq = wires.sizes[1]
        self.offsets = [6, 2, 4, 0]
        self.loads = {}
        self.slots = wires.far if kind == "line" else wires.zs
        self.line = LineSum(wires, lambda k: self.total.at[0, self.slots[k]], self.last, self.last_sems)

    def order(self, step):
        return (2, 4) if step % 2 == 0 else (4, 2)

    def group(self, offset):
        return self.source.at[pl.ds(self.w.dps[offset] * self.n_seq, self.n_seq)]

    def load(self, k):
        if self.resident or k >= 4:
            return
        self.loads[k] = pltpu.make_async_copy(
            self.group(self.offsets[k]), self.mine.at[k % 2], self.local.at[k % 2]
        )
        self.loads[k].start()

    def start(self):
        for o in self.offsets:
            self.w.send(self.group(o ^ 1), self.total.at[o // 2], self.core_sems.at[o // 2], self.w.peer(1, 0))
        self.load(0)
        self.load(1)

    def over_cores(self, k):
        o = self.offsets[k]
        self.w.arrived(self.total.at[o // 2], self.core_sems.at[o // 2])
        if not self.resident:
            self.loads[k].wait()
        for i in range(self.n_seq):
            slot = self.slots[i]
            mask = self.order(i)[0]
            block = self.total.at[o // 2, slot]
            if self.resident:
                own = self.source.at[self.w.dps[o] * self.n_seq + slot]
            else:
                own = self.mine.at[k % 2, slot]
            add_rows(block, own)
            if o & mask:
                keep = (o ^ mask) // (6 ^ mask)
                self.w.send(block, self.first.at[i, keep], self.first_sems.at[i, keep], self.w.peer(mask, 0))
        self.load(k + 2)

    def over_chips(self, i):
        mask = self.order(i)[1]
        for keep in (1, 0):
            o = mask * keep
            block = self.total.at[o // 2, self.slots[i]]
            self.w.arrived(self.first.at[i, keep], self.first_sems.at[i, keep])
            add_rows(block, self.first.at[i, keep])
            if keep:
                self.w.send(block, self.second.at[i], self.second_sems.at[i], self.w.peer(mask, 0))

    def to_seq(self, i):
        block = self.total.at[0, self.slots[i]]
        self.w.arrived(self.second.at[i], self.second_sems.at[i])
        add_rows(block, self.second.at[i])
        if self.kind == "line":
            if i:
                self.line.offer(i)
                self.line.relay(i)
        elif i:
            self.w.send(block, self.last.at[i], self.last_sems.at[i], self.w.peer(0, i))

    def finish(self):
        block = self.total.at[0, self.w.z]
        if self.kind == "line":
            self.line.finish(lambda at: block[at, :].astype(jnp.float32), self.out)
            return
        self.out[self.w.z] = block[...].astype(jnp.float32)
        for i in range(1, self.n_seq):
            self.w.arrived(self.last.at[i], self.last_sems.at[i])
            self.out[self.w.zs[i]] = self.last[i].astype(jnp.float32)

    def core_steps(self):
        return [lambda k=k: self.over_cores(k) for k in range(4)]

    def chip_steps(self):
        return [lambda i=i: self.over_chips(i) for i in range(self.n_seq)]

    def seq_steps(self):
        return [lambda i=i: self.to_seq(i) for i in (3, 2, 1, 0)]


def back_kernel(sizes, heads, *refs):
    n_dp, n_seq = sizes
    (
        valid_ref,
        page_in,
        grad_context,
        grad_first,
        query_in,
        key_in,
        value_in,
        logs,
        columns_in,
        down_in,
        up_in,
        out_in,
        vec_in,
        grad_rows,
        *outs,
    ) = refs[:19]
    scratch = list(refs[19:])

    def take(count):
        got = scratch[:count]
        del scratch[:count]
        return got

    send_sems, core_sems, first_sems, second_sems, last_sems, load_sems = take(6)
    head_sems, local_sems, row_sems = take(3)
    held, masked_query, masked_grad, keys, values, key_turned = take(6)
    query_grad, key_grad, value_grad = take(3)
    project, page, page_turned, columns, vec = take(5)
    row_terms, row_last, own_rows, partial = take(4)
    units = [take(5 if k < 3 else 4) for k in range(5)]
    w = Wires(send_sems, sizes)
    rows, width = grad_first.shape
    part = width // n_seq
    head_dim = width // heads
    local_heads = heads // n_seq
    stream = rows * n_seq
    per_block = 128 // head_dim
    scale = 1.0 / math.sqrt(head_dim)
    loads = []
    for t, (ref, into) in enumerate(
        (
            (query_in, held.at[0]),
            (key_in, held.at[1]),
            (value_in, held.at[2]),
            (vec_in, vec),
            (page_in, page),
            (columns_in, columns),
        )
    ):
        loads.append(pltpu.make_async_copy(ref, into, local_sems.at[t]))
        loads[-1].start()
    w.greet()

    def lanes_of_part(j):
        return pl.ds(pl.multiple_of(j * part, part), part)

    for i in range(1, n_seq):
        w.send(grad_context.at[:, lanes_of_part(w.zs[i])], held.at[3, w.z], head_sems.at[i], w.peer(0, i))
    own_grad = pltpu.make_async_copy(grad_context.at[:, lanes_of_part(w.z)], held.at[3, w.z], local_sems.at[6])
    own_grad.start()
    sources = (down_in, up_in, out_in, partial, vec)
    scatters = []
    for k in range(5):
        bufs = units[k] if k < 3 else [None] + units[k]
        scatters.append(
            Scatter(
                w,
                "columns" if k == 3 else "line",
                sources[k],
                k >= 3,
                bufs,
                (core_sems.at[k], first_sems.at[k], second_sems.at[k], last_sems.at[k]),
                load_sems.at[min(k, 2)],
                outs[k],
            )
        )
    down, up, out, qkv, small = scatters
    for unit in (down, up, out):
        unit.start()
    queue = []

    def pump(count):
        for _ in range(min(count, len(queue))):
            queue.pop(0)()

    for copy in loads:
        copy.wait()
    lane = lax.broadcasted_iota(jnp.int32, (stream, 128), 1)
    position = lax.broadcasted_iota(jnp.int32, (stream, 128), 0)
    guard = jnp.where((position >= valid_ref[0]) & (lane == 0), MASKED, 0.0).astype(jnp.bfloat16)

    def spread(source, h, factor):
        block = h // per_block * 128
        low = h % per_block * head_dim
        rows_of = source[:, :, block : block + 128].reshape(stream, 128).astype(jnp.float32)
        mine = (lane >= low) & (lane < low + head_dim)
        return jnp.where(mine, rows_of * factor, 0.0).astype(jnp.bfloat16).reshape(n_seq, rows, 128)

    for h in range(local_heads):
        masked_query[h] = spread(held.at[0], h, scale)
    for b in range(local_heads // per_block):
        lanes = slice(b * 128, (b + 1) * 128)
        keys[b, :, :128] = held[1, :, :, lanes].reshape(stream, 128)
        keys[b, :, 128:] = guard
        values[b] = held[2, :, :, lanes].reshape(stream, 128)
    turned = held[1].reshape(stream, part).T
    for h in range(local_heads):
        key_turned[h] = turned[h * head_dim : (h + 1) * head_dim, :]
    key_grad[...] = jnp.zeros_like(key_grad)
    value_grad[...] = jnp.zeros_like(value_grad)
    queue += down.core_steps()
    pump(4)
    for s in range(n_seq):
        page_turned[:, s * rows : (s + 1) * rows] = page[s].T
    own_grad.wait()
    for i in range(1, n_seq):
        w.arrived(held.at[3, w.zs[i]], head_sems.at[i])
    for h in range(local_heads):
        masked_grad[h] = spread(held.at[3], h, 1.0)
    queue += up.core_steps() + down.chip_steps() + out.core_steps() + down.seq_steps()[:2] + up.chip_steps()
    queue += down.seq_steps()[2:] + out.chip_steps() + up.seq_steps() + out.seq_steps()
    pump(4)
    ones = jnp.where(lax.broadcasted_iota(jnp.int32, (rows, 128), 1) == 0, 1.0, 0.0).astype(jnp.bfloat16)
    for c in range(n_seq):

        def head(h, _, c=c):
            block = h // per_block
            query, grad = masked_query[h, c], masked_grad[h, c]
            scores = lax.dot_general(
                keys[block], jnp.concatenate([query, ones], axis=1), FLAT, preferred_element_type=jnp.float32
            )
            probs = jnp.exp(scores - logs[c, pl.ds(h, 1), :])
            moved = lax.dot_general(values[block], grad, FLAT, preferred_element_type=jnp.float32)
            centre = jnp.sum(probs * moved, axis=0, keepdims=True)
            slope = (probs * (moved - centre)).astype(jnp.bfloat16)
            query_grad[h] = jnp.dot(key_turned[h], slope, preferred_element_type=jnp.float32) * scale
            key_grad[block] += jnp.dot(slope, query, preferred_element_type=jnp.float32)
            value_grad[block] += jnp.dot(
                probs.astype(jnp.bfloat16), grad, preferred_element_type=jnp.float32
            )
            return 0

        lax.fori_loop(0, local_heads, head, 0)
        project[c * rows : (c + 1) * rows, :part] = (
            query_grad[...].reshape(part, rows).T.astype(jnp.bfloat16)
        )
        pump(5)
    for t, total in ((1, key_grad), (2, value_grad)):
        for b in range(local_heads // per_block):
            at = t * part + b * 128
            project[:, at : at + 128] = total[b].astype(jnp.bfloat16)
    matrix = columns[...].reshape(width, 3 * part)
    row_sum = LineSum(w, lambda k: row_terms.at[k], row_last, row_sems)

    def row_term(k):
        at = pl.ds(pl.multiple_of(w.far[k] * rows, rows), rows)
        return lax.dot_general(project[at, :], matrix, FLAT, preferred_element_type=jnp.float32)

    for k in (3, 2, 1):
        row_terms[k] = row_term(k).astype(jnp.bfloat16)
        row_sum.offer(k)
    for t in range(3):
        block = jnp.dot(
            page_turned[...], project[:, t * part : (t + 1) * part], preferred_element_type=jnp.float32
        )
        partial[:, :, t * part : (t + 1) * part] = block.astype(jnp.bfloat16).reshape(n_dp * n_seq, -1, part)
    qkv.start()
    groups = part // 128
    for b, t in ((0, 0), (1, 2)):
        sums = jnp.sum(project[:, t * part : (t + 1) * part].astype(jnp.float32), axis=0, keepdims=True)
        for g in range(groups):
            for s in range(n_seq):
                vec[(w.z * groups + g) * n_seq + s, b : b + 1, :] = sums[:, g * 128 : (g + 1) * 128]
    small.start()
    row_sum.relay(3)
    row_sum.relay(2)
    own_rows[...] = row_term(0) + grad_first[...]
    queue[:0] = qkv.core_steps() + small.core_steps()
    pump(8)
    row_sum.relay(1)
    queue += qkv.chip_steps() + small.chip_steps() + qkv.seq_steps() + small.seq_steps()
    pump(len(queue))
    for unit in scatters:
        unit.finish()
    row_sum.finish(lambda at: own_rows[at, :], grad_rows)
    w.drain()


def back(sizes, heads, valid, page, grad_context, grad_first, heads_in, logs, columns, partial_sums):
    n_dp, n_seq = sizes
    devices = n_dp * n_seq
    count, width = grad_first.shape
    part = width // n_seq
    stream = count * n_seq
    head_dim = width // heads
    local_heads = heads // n_seq
    blocks = local_heads * head_dim // 128
    low = jnp.bfloat16
    shapes = [p.shape[1:] for p in partial_sums[:3]] + [columns.shape[1:], partial_sums[3].shape[1:]]
    kinds = [low] * 4 + [jnp.float32]
    results = [jax.ShapeDtypeStruct(shape, jnp.float32) for shape in shapes]
    results[3] = jax.ShapeDtypeStruct((n_seq,) + shapes[3], jnp.float32)
    anywhere = pl.BlockSpec(memory_space=pl.ANY)
    local = pl.BlockSpec(memory_space=pltpu.VMEM)
    sends = 5 * (4 + 3 * n_seq + 6) + 6 + n_seq - 1
    chips = n_dp // 2
    scratch = [
        pltpu.SemaphoreType.DMA((sends,)),
        pltpu.SemaphoreType.DMA((5, chips)),
        pltpu.SemaphoreType.DMA((5, n_seq, 2)),
        pltpu.SemaphoreType.DMA((5, n_seq)),
        pltpu.SemaphoreType.DMA((5, 5)),
        pltpu.SemaphoreType.DMA((3, 2)),
        pltpu.SemaphoreType.DMA((n_seq,)),
        pltpu.SemaphoreType.DMA((7,)),
        pltpu.SemaphoreType.DMA((5,)),
        pltpu.VMEM((4, n_seq, count, part), low),
        pltpu.VMEM((local_heads, n_seq, count, 128), low),
        pltpu.VMEM((local_heads, n_seq, count, 128), low),
        pltpu.VMEM((blocks, stream, 256), low),
        pltpu.VMEM((blocks, stream, 128), low),
        pltpu.VMEM((local_heads, head_dim, stream), low),
        pltpu.VMEM((local_heads, head_dim, count), jnp.float32),
        pltpu.VMEM((blocks, stream, 128), jnp.float32),
        pltpu.VMEM((blocks, stream, 128), jnp.float32),
        pltpu.VMEM((stream, 3 * part), low),
        pltpu.VMEM((n_seq, count, width), low),
        pltpu.VMEM((width, stream), low),
        pltpu.VMEM(columns.shape, low),
        pltpu.VMEM(partial_sums[3].shape, jnp.float32),
        pltpu.VMEM((n_seq, count, width), low),
        pltpu.VMEM((5, count, width), low),
        pltpu.VMEM((count, width), jnp.float32),
        pltpu.VMEM(columns.shape, low),
    ]
    for k, (shape, kind) in enumerate(zip(shapes, kinds)):
        if k < 3:
            scratch.append(pltpu.VMEM((2, n_seq) + shape, kind))
        scratch += [
            pltpu.VMEM((chips, n_seq) + shape, kind),
            pltpu.VMEM((n_seq, 2) + shape, kind),
            pltpu.VMEM((n_seq,) + shape, kind),
            pltpu.VMEM((5,) + shape, kind),
        ]
    return pl.pallas_call(
        lambda *refs: back_kernel(sizes, heads, *refs),
        out_shape=[jax.ShapeDtypeStruct((count, width), low)] + results,
        in_specs=[pl.BlockSpec(memory_space=pltpu.SMEM), anywhere, anywhere, local]
        + [anywhere] * 3
        + [local]
        + [anywhere] * 5,
        out_specs=[local] * 6,
        scratch_shapes=scratch,
        compiler_params=pltpu.CompilerParams(
            collective_id=1, has_side_effects=True, vmem_limit_bytes=62 * 2**20
        ),
        name="back",
    )(valid, page, grad_context, grad_first, *heads_in, logs, columns, *partial_sums)


def spread_lanes(vectors, n_seq):
    stacked = jnp.stack(vectors).astype(jnp.float32)
    tiled = jnp.tile(stacked, (1, n_seq))
    owner = jnp.arange(tiled.shape[1], dtype=jnp.int32) // stacked.shape[1]
    return jnp.where(owner[None, :] == lax.axis_index("seq"), tiled, 0.0)


def kernel_plan(
    x_in,
    w_qkv,
    q_bias,
    v_bias,
    w_out,
    out_bias,
    ln1_gain,
    ln1_shift,
    w_up,
    up_bias,
    w_down,
    down_bias,
    ln2_gain,
    ln2_shift,
    valid,
    cotangent,
):
    sizes = (lax.axis_size("dp"), lax.axis_size("seq"))
    n_dp, groups = sizes
    rows = x_in[0]
    count, width = rows.shape
    vectors = (q_bias, v_bias, out_bias, ln1_gain, ln1_shift, down_bias, ln2_gain, ln2_shift)
    spread = spread_lanes(vectors, groups)
    vec = jnp.concatenate(
        [spread, up_bias.astype(jnp.float32)[None], jnp.zeros((7, spread.shape[1]), jnp.float32)]
    )
    third = width // groups
    w_columns = (
        w_qkv.reshape(-1, 3, groups, third).transpose(2, 0, 1, 3).reshape(groups, -1, 3 * third)
    )
    (
        full_vec,
        columns,
        full_out,
        full_up,
        full_down,
        page,
        query_heads,
        key_heads,
        value_heads,
        context_rows,
        logs,
    ) = front(sizes, HEADS, valid, rows, vec, w_columns, w_out, w_up, w_down)
    full_out = full_out.reshape(width, -1)
    full_up = full_up.reshape(width, -1)
    full_down = full_down.reshape(-1, width)
    by_page = full_vec.reshape(n_dp, groups, 16, -1)
    lined = by_page[:, :, :8].sum(axis=1).transpose(1, 0, 2).reshape(8, width)
    full_obias, full_gain1, full_shift1, full_dbias, full_gain2, full_shift2 = (
        lined[2],
        lined[3],
        lined[4],
        lined[5],
        lined[6],
        lined[7],
    )
    full_ubias = by_page[:, :, 8].reshape(-1)
    attn_out = jnp.dot(
        context_rows, full_out, preferred_element_type=jnp.float32
    ) + full_obias.astype(jnp.float32)
    first_rows = rows.astype(jnp.float32) + attn_out
    hidden, normed_one, inv_one = norm_forward(
        first_rows, full_gain1.astype(jnp.float32), full_shift1.astype(jnp.float32)
    )
    hidden_low = hidden.astype(jnp.bfloat16)
    up_act = jnp.dot(hidden_low, full_up, preferred_element_type=jnp.float32) + full_ubias.astype(
        jnp.float32
    )
    gelu_low = gelu_exact(up_act).astype(jnp.bfloat16)
    branch = jnp.dot(gelu_low, full_down, preferred_element_type=jnp.float32) + full_dbias.astype(
        jnp.float32
    )
    output, normed_two, inv_two = norm_forward(
        hidden + branch, full_gain2.astype(jnp.float32), full_shift2.astype(jnp.float32)
    )
    back_out, back_gain1, back_up, back_down, back_gain2 = (
        full_out,
        full_gain1,
        full_up,
        full_down,
        full_gain2,
    )
    grad_out = cotangent[0].astype(jnp.float32)
    grad_mid, grad_ln2_gain, grad_ln2_shift = norm_backward(
        grad_out, normed_two, inv_two, back_gain2.astype(jnp.float32)
    )
    grad_branch = grad_mid.astype(jnp.bfloat16)
    grad_w_down = outer_sum(gelu_low, grad_branch)
    grad_down_bias = jnp.sum(grad_branch.astype(jnp.float32), axis=0)
    grad_gelu = times_back(grad_branch, back_down)
    grad_up = jax.vjp(gelu_exact, up_act)[1](grad_gelu)[0].astype(jnp.bfloat16)
    grad_w_up = outer_sum(hidden_low, grad_up)
    grad_up_bias = jnp.sum(grad_up.astype(jnp.float32), axis=0)
    grad_hidden = times_back(grad_up, back_up) + grad_mid
    grad_first, grad_ln1_gain, grad_ln1_shift = norm_backward(
        grad_hidden, normed_one, inv_one, back_gain1.astype(jnp.float32)
    )
    grad_attn = grad_first.astype(jnp.bfloat16)
    grad_w_out = outer_sum(context_rows, grad_attn)
    grad_out_bias = jnp.sum(grad_attn.astype(jnp.float32), axis=0)
    grad_context = times_back(grad_attn, back_out).astype(jnp.bfloat16)
    def packed(vector):
        return vector.reshape(n_dp, 1, -1)

    zero = jnp.zeros((width,), jnp.float32)
    sums = (zero, zero, grad_out_bias, grad_ln1_gain, grad_ln1_shift)
    sums += (grad_down_bias, grad_ln2_gain, grad_ln2_shift)
    by_group = jnp.concatenate([packed(v) for v in sums], axis=1)
    by_group = jnp.broadcast_to(by_group[:, None], (n_dp, groups) + by_group.shape[1:])
    by_device = jnp.concatenate(
        [
            by_group.reshape(n_dp * groups, 8, -1),
            grad_up_bias.reshape(n_dp * groups, 1, -1),
            jnp.zeros((n_dp * groups, 7, by_group.shape[-1]), jnp.float32),
        ],
        axis=1,
    )
    devices = n_dp * groups

    def cut(grad):
        return grad.astype(jnp.bfloat16).reshape(devices, -1, grad.shape[1])

    grad_rows, *sums = back(
        sizes,
        HEADS,
        valid,
        page,
        grad_context,
        grad_first,
        (query_heads, key_heads, value_heads),
        logs,
        columns,
        (cut(grad_w_down), cut(grad_w_up), cut(grad_w_out), by_device),
    )
    vec_sums = sums[4]
    mine = lax.dynamic_slice(
        vec_sums[:8], (0, lax.axis_index("seq") * (width // devices)), (8, width // devices)
    )
    return (
        output.astype(jnp.bfloat16)[None],
        grad_rows[None],
        sums[3].reshape(groups, -1, 3, third).transpose(1, 2, 0, 3).reshape(-1, 3 * width),
        mine[0],
        mine[1],
        sums[2],
        mine[2],
        mine[3],
        mine[4],
        sums[1],
        vec_sums[8],
        sums[0],
        mine[5],
        mine[6],
        mine[7],
    )


def solution(mesh):
    n_dp, n_seq = mesh.shape["dp"], mesh.shape["seq"]

    def per_device(x_in, w_qkv, *rest):
        part, width = w_qkv.shape[0], x_in.shape[2]
        fits = (n_dp, n_seq) == (8, 4) and part % 32 == 0 and part * n_seq == 128 and width // n_seq % 128 == 0 and x_in.shape[0] == 1
        plan = kernel_plan if fits else general_plan
        return plan(x_in, w_qkv, *rest)

    return jax.shard_map(
        per_device,
        mesh=mesh,
        in_specs=(
            P("dp", "seq", None),
            P(("dp", "seq"), None),
            P(("dp", "seq")),
            P(("dp", "seq")),
            P(("dp", "seq"), None),
            P(("dp", "seq")),
            P(("dp", "seq")),
            P(("dp", "seq")),
            P(("dp", "seq"), None),
            P(("dp", "seq")),
            P(("dp", "seq"), None),
            P(("dp", "seq")),
            P(("dp", "seq")),
            P(("dp", "seq")),
            P("dp"),
            P("dp", "seq", None),
        ),
        out_specs=(
            P("dp", "seq", None),
            P("dp", "seq", None),
            P(("dp", "seq"), None),
            P(("dp", "seq")),
            P(("dp", "seq")),
            P(("dp", "seq"), None),
            P(("dp", "seq")),
            P(("dp", "seq")),
            P(("dp", "seq")),
            P(("dp", "seq"), None),
            P(("dp", "seq")),
            P(("dp", "seq"), None),
            P(("dp", "seq")),
            P(("dp", "seq")),
            P(("dp", "seq")),
        ),
        check_vma=False,
    )
```

```python
import math

import jax
import jax.numpy as jnp
from jax import lax
from jax.experimental import pallas as pl
from jax.experimental.pallas import tpu as pltpu
from jax.sharding import PartitionSpec as P

HEADS = 16


eps_norm = 1e-05


def outer_sum(left, right):
    return lax.dot_general(
        left, right, (((0,), (0,)), ((), ())), preferred_element_type=jnp.float32
    )


def times_back(rows, matrix):
    return lax.dot_general(
        rows, matrix, (((1,), (1,)), ((), ())), preferred_element_type=jnp.float32
    )


def gelu_exact(values):
    return jax.nn.gelu(values, approximate=False)


def norm_forward(rows, gain, shift):
    center = rows - jnp.mean(rows, axis=-1, keepdims=True)
    inv_std = lax.rsqrt(jnp.mean(center * center, axis=-1, keepdims=True) + eps_norm)
    normed = center * inv_std
    return (normed * gain + shift, normed, inv_std)


def norm_backward(grad_out, normed, inv_std, gain):
    scaled = grad_out * gain
    grad_rows = inv_std * (
        scaled
        - jnp.mean(scaled, axis=-1, keepdims=True)
        - normed * jnp.mean(scaled * normed, axis=-1, keepdims=True)
    )
    return (grad_rows, jnp.sum(grad_out * normed, axis=0), jnp.sum(grad_out, axis=0))


def to_heads(rows, groups):
    count, width = rows.shape
    return rows.reshape(count, groups, width // groups).transpose(1, 0, 2).reshape(groups, -1)


def from_heads(pieces, part_width):
    groups = pieces.shape[0]
    return (
        pieces.reshape(groups, -1, part_width).transpose(1, 0, 2).reshape(-1, groups * part_width)
    )


def general_plan(
    x_in,
    w_qkv,
    q_bias,
    v_bias,
    w_out,
    out_bias,
    ln1_gain,
    ln1_shift,
    w_up,
    up_bias,
    w_down,
    down_bias,
    ln2_gain,
    ln2_shift,
    valid,
    cotangent,
):
    shards = (
        w_qkv,
        q_bias,
        v_bias,
        w_out,
        out_bias,
        ln1_gain,
        ln1_shift,
        w_up,
        up_bias,
        w_down,
        down_bias,
        ln2_gain,
        ln2_shift,
    )
    weights = (
        lax.all_gather(shards[0], ("dp", "seq"), axis=0, tiled=True),
        lax.all_gather(shards[1], ("dp", "seq"), axis=0, tiled=True),
        lax.all_gather(shards[2], ("dp", "seq"), axis=0, tiled=True),
        lax.all_gather(shards[3], ("dp", "seq"), axis=0, tiled=True),
        lax.all_gather(shards[4], ("dp", "seq"), axis=0, tiled=True),
        lax.all_gather(shards[5], ("dp", "seq"), axis=0, tiled=True),
        lax.all_gather(shards[6], ("dp", "seq"), axis=0, tiled=True),
        lax.all_gather(shards[7], ("dp", "seq"), axis=0, tiled=True),
        lax.all_gather(shards[8], ("dp", "seq"), axis=0, tiled=True),
        lax.all_gather(shards[9], ("dp", "seq"), axis=0, tiled=True),
        lax.all_gather(shards[10], ("dp", "seq"), axis=0, tiled=True),
        lax.all_gather(shards[11], ("dp", "seq"), axis=0, tiled=True),
        lax.all_gather(shards[12], ("dp", "seq"), axis=0, tiled=True),
    )
    (
        full_qkv,
        full_qbias,
        full_vbias,
        full_out,
        full_obias,
        full_gain1,
        full_shift1,
        full_up,
        full_ubias,
        full_down,
        full_dbias,
        full_gain2,
        full_shift2,
    ) = weights
    groups = lax.axis_size("seq")
    rows = x_in[0]
    count, width = rows.shape
    head_dim = width // HEADS
    part_width = width // groups
    local_heads = HEADS // groups
    stream = count * groups
    qrows = min(512, stream)
    nblocks = stream // qrows
    scale = 1.0 / math.sqrt(head_dim)
    keep = jnp.arange(stream, dtype=jnp.int32) < valid[0]
    bias_row = jnp.concatenate([full_qbias, jnp.zeros_like(full_qbias), full_vbias]).astype(
        jnp.float32
    )
    project = (jnp.dot(rows, full_qkv, preferred_element_type=jnp.float32) + bias_row).astype(
        jnp.bfloat16
    )
    sent = (
        to_heads(project[:, :width], groups),
        to_heads(project[:, width : 2 * width], groups),
        to_heads(project[:, 2 * width :], groups),
    )
    arrived = (
        lax.all_to_all(sent[0], "seq", split_axis=0, concat_axis=0, tiled=True),
        lax.all_to_all(sent[1], "seq", split_axis=0, concat_axis=0, tiled=True),
        lax.all_to_all(sent[2], "seq", split_axis=0, concat_axis=0, tiled=True),
    )
    query_blocks = arrived[0].reshape(nblocks, qrows, local_heads, head_dim)
    key_heads = arrived[1].reshape(stream, local_heads, head_dim)
    value_heads = arrived[2].reshape(stream, local_heads, head_dim)

    def masked_scores(query):
        scores = (
            jnp.einsum("qhd,khd->hqk", query, key_heads, preferred_element_type=jnp.float32) * scale
        )
        return jnp.where(keep[None, None, :], scores, -1e30)

    def attend_forward(query):
        scores = masked_scores(query)
        peak = jnp.max(scores, axis=-1, keepdims=True)
        raised = jnp.exp(scores - peak)
        total = jnp.sum(raised, axis=-1, keepdims=True)
        probs = (raised / total).astype(jnp.bfloat16)
        context = jnp.einsum("hqk,khd->qhd", probs, value_heads, preferred_element_type=jnp.float32)
        return (context.astype(jnp.bfloat16), (peak + jnp.log(total))[..., 0])

    context, log_sums = lax.map(attend_forward, query_blocks)
    returned_ctx = lax.all_to_all(
        context.reshape(groups, -1), "seq", split_axis=0, concat_axis=0, tiled=True
    )
    context_rows = from_heads(returned_ctx, part_width)
    attn_out = jnp.dot(
        context_rows, full_out, preferred_element_type=jnp.float32
    ) + full_obias.astype(jnp.float32)
    first_rows = rows.astype(jnp.float32) + attn_out
    hidden, normed_one, inv_one = norm_forward(
        first_rows, full_gain1.astype(jnp.float32), full_shift1.astype(jnp.float32)
    )
    hidden_low = hidden.astype(jnp.bfloat16)
    up_act = jnp.dot(hidden_low, full_up, preferred_element_type=jnp.float32) + full_ubias.astype(
        jnp.float32
    )
    gelu_low = gelu_exact(up_act).astype(jnp.bfloat16)
    branch = jnp.dot(gelu_low, full_down, preferred_element_type=jnp.float32) + full_dbias.astype(
        jnp.float32
    )
    output, normed_two, inv_two = norm_forward(
        hidden + branch, full_gain2.astype(jnp.float32), full_shift2.astype(jnp.float32)
    )
    again = (
        lax.all_gather(shards[0], ("dp", "seq"), axis=0, tiled=True),
        lax.all_gather(shards[1], ("dp", "seq"), axis=0, tiled=True),
        lax.all_gather(shards[2], ("dp", "seq"), axis=0, tiled=True),
        lax.all_gather(shards[3], ("dp", "seq"), axis=0, tiled=True),
        lax.all_gather(shards[4], ("dp", "seq"), axis=0, tiled=True),
        lax.all_gather(shards[5], ("dp", "seq"), axis=0, tiled=True),
        lax.all_gather(shards[6], ("dp", "seq"), axis=0, tiled=True),
        lax.all_gather(shards[7], ("dp", "seq"), axis=0, tiled=True),
        lax.all_gather(shards[8], ("dp", "seq"), axis=0, tiled=True),
        lax.all_gather(shards[9], ("dp", "seq"), axis=0, tiled=True),
        lax.all_gather(shards[10], ("dp", "seq"), axis=0, tiled=True),
        lax.all_gather(shards[11], ("dp", "seq"), axis=0, tiled=True),
        lax.all_gather(shards[12], ("dp", "seq"), axis=0, tiled=True),
    )
    back_qkv, back_out, back_gain1, back_up, back_down, back_gain2 = (
        again[0],
        again[3],
        again[5],
        again[7],
        again[9],
        again[11],
    )
    grad_out = cotangent[0].astype(jnp.float32)
    grad_mid, grad_ln2_gain, grad_ln2_shift = norm_backward(
        grad_out, normed_two, inv_two, back_gain2.astype(jnp.float32)
    )
    grad_branch = grad_mid.astype(jnp.bfloat16)
    grad_w_down = outer_sum(gelu_low, grad_branch)
    grad_down_bias = jnp.sum(grad_branch.astype(jnp.float32), axis=0)
    grad_gelu = times_back(grad_branch, back_down)
    grad_up = jax.vjp(gelu_exact, up_act)[1](grad_gelu)[0].astype(jnp.bfloat16)
    grad_w_up = outer_sum(hidden_low, grad_up)
    grad_up_bias = jnp.sum(grad_up.astype(jnp.float32), axis=0)
    grad_hidden = times_back(grad_up, back_up) + grad_mid
    grad_first, grad_ln1_gain, grad_ln1_shift = norm_backward(
        grad_hidden, normed_one, inv_one, back_gain1.astype(jnp.float32)
    )
    grad_attn = grad_first.astype(jnp.bfloat16)
    grad_w_out = outer_sum(context_rows, grad_attn)
    grad_out_bias = jnp.sum(grad_attn.astype(jnp.float32), axis=0)
    grad_context = times_back(grad_attn, back_out).astype(jnp.bfloat16)
    grad_ctx_heads = lax.all_to_all(
        to_heads(grad_context, groups), "seq", split_axis=0, concat_axis=0, tiled=True
    )
    grad_ctx_blocks = grad_ctx_heads.reshape(nblocks, qrows, local_heads, head_dim)

    def attend_backward(carry, inputs):
        key_total, value_total = carry
        query, grad_ctx, log_rows = inputs
        scores = masked_scores(query)
        probs = jnp.exp(scores - log_rows[..., None])
        probs_low = probs.astype(jnp.bfloat16)
        d_probs = jnp.einsum(
            "qhd,khd->hqk", grad_ctx, value_heads, preferred_element_type=jnp.float32
        )
        centre = jnp.sum(probs * d_probs, axis=-1, keepdims=True)
        grad_scores = (probs * (d_probs - centre)).astype(jnp.bfloat16)
        grad_query = (
            jnp.einsum("hqk,khd->qhd", grad_scores, key_heads, preferred_element_type=jnp.float32)
            * scale
        )
        key_total = (
            key_total
            + jnp.einsum("hqk,qhd->khd", grad_scores, query, preferred_element_type=jnp.float32)
            * scale
        )
        value_total = value_total + jnp.einsum(
            "hqk,qhd->khd", probs_low, grad_ctx, preferred_element_type=jnp.float32
        )
        return ((key_total, value_total), grad_query.astype(jnp.bfloat16))

    empty = jnp.zeros((stream, local_heads, head_dim), jnp.float32)
    (key_total, value_total), grad_query = lax.scan(
        attend_backward, (empty, empty), (query_blocks, grad_ctx_blocks, log_sums)
    )
    grad_key = key_total.astype(jnp.bfloat16)
    grad_value = value_total.astype(jnp.bfloat16)
    grad_pieces = (
        lax.all_to_all(
            grad_query.reshape(groups, -1), "seq", split_axis=0, concat_axis=0, tiled=True
        ),
        lax.all_to_all(
            grad_key.reshape(groups, -1), "seq", split_axis=0, concat_axis=0, tiled=True
        ),
        lax.all_to_all(
            grad_value.reshape(groups, -1), "seq", split_axis=0, concat_axis=0, tiled=True
        ),
    )
    grad_project = jnp.concatenate(
        [
            from_heads(grad_pieces[0], part_width),
            from_heads(grad_pieces[1], part_width),
            from_heads(grad_pieces[2], part_width),
        ],
        axis=1,
    )
    grad_w_qkv = outer_sum(rows, grad_project)
    bias_sums = jnp.sum(grad_project.astype(jnp.float32), axis=0)
    grad_q_bias = bias_sums[:width]
    grad_v_bias = bias_sums[2 * width :]
    grad_rows = times_back(grad_project, back_qkv) + grad_first
    terms = (
        grad_w_qkv,
        grad_q_bias,
        grad_v_bias,
        grad_w_out,
        grad_out_bias,
        grad_ln1_gain,
        grad_ln1_shift,
        grad_w_up,
        grad_up_bias,
        grad_w_down,
        grad_down_bias,
        grad_ln2_gain,
        grad_ln2_shift,
    )
    page_sums = (
        lax.psum_scatter(
            terms[0].astype(jnp.bfloat16), "dp", scatter_dimension=0, tiled=True
        ).astype(jnp.float32),
        lax.psum_scatter(
            terms[1].astype(jnp.bfloat16), "dp", scatter_dimension=0, tiled=True
        ).astype(jnp.float32),
        lax.psum_scatter(
            terms[2].astype(jnp.bfloat16), "dp", scatter_dimension=0, tiled=True
        ).astype(jnp.float32),
        lax.psum_scatter(
            terms[3].astype(jnp.bfloat16), "dp", scatter_dimension=0, tiled=True
        ).astype(jnp.float32),
        lax.psum_scatter(
            terms[4].astype(jnp.bfloat16), "dp", scatter_dimension=0, tiled=True
        ).astype(jnp.float32),
        lax.psum_scatter(
            terms[5].astype(jnp.bfloat16), "dp", scatter_dimension=0, tiled=True
        ).astype(jnp.float32),
        lax.psum_scatter(
            terms[6].astype(jnp.bfloat16), "dp", scatter_dimension=0, tiled=True
        ).astype(jnp.float32),
        lax.psum_scatter(
            terms[7].astype(jnp.bfloat16), "dp", scatter_dimension=0, tiled=True
        ).astype(jnp.float32),
        lax.psum_scatter(
            terms[8].astype(jnp.bfloat16), "dp", scatter_dimension=0, tiled=True
        ).astype(jnp.float32),
        lax.psum_scatter(
            terms[9].astype(jnp.bfloat16), "dp", scatter_dimension=0, tiled=True
        ).astype(jnp.float32),
        lax.psum_scatter(
            terms[10].astype(jnp.bfloat16), "dp", scatter_dimension=0, tiled=True
        ).astype(jnp.float32),
        lax.psum_scatter(
            terms[11].astype(jnp.bfloat16), "dp", scatter_dimension=0, tiled=True
        ).astype(jnp.float32),
        lax.psum_scatter(
            terms[12].astype(jnp.bfloat16), "dp", scatter_dimension=0, tiled=True
        ).astype(jnp.float32),
    )
    sums = (
        lax.psum_scatter(
            page_sums[0].astype(jnp.bfloat16), "seq", scatter_dimension=0, tiled=True
        ).astype(jnp.float32),
        lax.psum_scatter(
            page_sums[1].astype(jnp.bfloat16), "seq", scatter_dimension=0, tiled=True
        ).astype(jnp.float32),
        lax.psum_scatter(
            page_sums[2].astype(jnp.bfloat16), "seq", scatter_dimension=0, tiled=True
        ).astype(jnp.float32),
        lax.psum_scatter(
            page_sums[3].astype(jnp.bfloat16), "seq", scatter_dimension=0, tiled=True
        ).astype(jnp.float32),
        lax.psum_scatter(
            page_sums[4].astype(jnp.bfloat16), "seq", scatter_dimension=0, tiled=True
        ).astype(jnp.float32),
        lax.psum_scatter(
            page_sums[5].astype(jnp.bfloat16), "seq", scatter_dimension=0, tiled=True
        ).astype(jnp.float32),
        lax.psum_scatter(
            page_sums[6].astype(jnp.bfloat16), "seq", scatter_dimension=0, tiled=True
        ).astype(jnp.float32),
        lax.psum_scatter(
            page_sums[7].astype(jnp.bfloat16), "seq", scatter_dimension=0, tiled=True
        ).astype(jnp.float32),
        lax.psum_scatter(
            page_sums[8].astype(jnp.bfloat16), "seq", scatter_dimension=0, tiled=True
        ).astype(jnp.float32),
        lax.psum_scatter(
            page_sums[9].astype(jnp.bfloat16), "seq", scatter_dimension=0, tiled=True
        ).astype(jnp.float32),
        lax.psum_scatter(
            page_sums[10].astype(jnp.bfloat16), "seq", scatter_dimension=0, tiled=True
        ).astype(jnp.float32),
        lax.psum_scatter(
            page_sums[11].astype(jnp.bfloat16), "seq", scatter_dimension=0, tiled=True
        ).astype(jnp.float32),
        lax.psum_scatter(
            page_sums[12].astype(jnp.bfloat16), "seq", scatter_dimension=0, tiled=True
        ).astype(jnp.float32),
    )
    return (
        output.astype(jnp.bfloat16)[None],
        grad_rows.astype(jnp.bfloat16)[None],
        sums[0],
        sums[1],
        sums[2],
        sums[3],
        sums[4],
        sums[5],
        sums[6],
        sums[7],
        sums[8],
        sums[9],
        sums[10],
        sums[11],
        sums[12],
    )


MESH = pl.DeviceIdType.MESH
CHUNK = 256
MASKED = -1e30
FLAT = (((1,), (1,)), ((), ()))


def flip(index, mask):
    for b in range(mask.bit_length()):
        if mask >> b & 1:
            bit = 1 << b
            index = index + bit - 2 * bit * (index // bit % 2)
    return index


def guarded(when, action):
    if when is None:
        action()
    else:
        pl.when(when)(action)


class Wires:
    def __init__(self, sems, sizes):
        self.sems, self.sizes = sems, sizes
        self.dp, self.z = lax.axis_index("dp"), lax.axis_index("seq")
        self.dps = [flip(self.dp, m) for m in range(sizes[0])]
        self.zs = [flip(self.z, m) for m in range(sizes[1])]
        last = sizes[1] - 1
        half = self.z // 2
        step = 1 - 2 * half
        depth = self.z * step + last * half
        self.inner, self.outer = depth == 1, depth == 0
        self.right = self.z + step
        self.left = self.z - step * depth
        self.far = [self.z] + [t * step + last * half for t in (1 - depth, 2, 3)]
        self.started = []

    def peer(self, offset, step):
        return (self.dps[offset], self.zs[step])

    def send(self, src, dst, recv_sem, device, when=None):
        copy = pltpu.make_async_remote_copy(
            src_ref=src,
            dst_ref=dst,
            send_sem=self.sems.at[len(self.started)],
            recv_sem=recv_sem,
            device_id=device,
            device_id_type=MESH,
        )
        guarded(when, copy.start)
        self.started.append((copy, when))

    def arrived(self, dst, recv_sem, when=None):
        copy = pltpu.make_async_remote_copy(
            src_ref=dst,
            dst_ref=dst,
            send_sem=self.sems.at[0],
            recv_sem=recv_sem,
            device_id=self.peer(1, 0),
            device_id_type=MESH,
        )
        guarded(when, copy.wait_recv)

    def drain(self):
        for copy, when in self.started:
            guarded(when, copy.wait_send)

    def greet(self):
        n_dp, n_seq = self.sizes
        barrier = pltpu.get_barrier_semaphore()
        masks = [1 << b for b in range(n_dp.bit_length() - 1)]
        partners = [self.peer(m, 0) for m in masks] + [self.peer(0, i) for i in range(1, n_seq)]
        for device in partners:
            pl.semaphore_signal(barrier, inc=1, device_id=device, device_id_type=MESH)
        pl.semaphore_wait(barrier, len(partners))


class Line:
    def __init__(self, wires, slot, recv):
        self.w, self.slot, self.recv = wires, slot, recv

    def pass_on(self, k, src, to_left):
        w = self.w
        s = w.far[k]
        dst = self.slot(s)
        if to_left:
            w.send(src, dst, self.recv.at[s], (w.dp, w.left), w.inner)
        else:
            w.send(src, dst, self.recv.at[s], (w.dp, w.right), None if k == 0 else w.inner)

    def own(self, src):
        self.pass_on(0, src, False)
        self.pass_on(0, src, True)

    def take(self, k):
        s = self.w.far[k]
        self.w.arrived(self.slot(s), self.recv.at[s])
        self.pass_on(k, self.slot(s), k > 1)


class Gather:
    def __init__(self, wires, src, full, recv, local):
        self.w, self.src, self.full, self.recv, self.local = wires, src, full, recv, local
        n_dp, self.n_seq = wires.sizes
        self.chips = [1 << b for b in range(1, n_dp.bit_length() - 1)]
        self.slots = wires.far
        self.line = Line(wires, lambda s: full.at[wires.dp * self.n_seq + s], recv.at[0])

    def at(self, offset, step):
        return self.full.at[self.w.dps[offset] * self.n_seq + self.slots[step]]

    def order(self, step):
        return self.chips if step % 2 == 0 else self.chips[::-1]

    def forward(self, src, offset, step, masks):
        for m in masks:
            sem = self.recv.at[offset ^ m, self.slots[step]]
            self.w.send(src, self.at(offset, step), sem, self.w.peer(m, 0))

    def wait(self, offset, step):
        self.w.arrived(self.at(offset, step), self.recv.at[offset, self.slots[step]])

    def mine(self):
        return self.src

    def own_chips(self):
        self.kept = pltpu.make_async_copy(self.mine(), self.at(0, 0), self.local)
        self.kept.start()
        self.forward(self.mine(), 0, 0, self.order(0) + [1])

    def own_seq(self):
        self.line.own(self.src)

    def along_seq(self, i):
        self.line.take(i)
        self.forward(self.at(0, i), 0, i, self.order(i) + [1])

    def stages(self, step):
        have, out = [0], []
        masks = self.order(step)
        for t, m in enumerate(masks):
            out.append([(o ^ m, masks[t + 1 :] + [1]) for o in have])
            have = have + [o ^ m for o in have]
        return out

    def over_chips(self, t, step):
        for offset, masks in self.stages(step)[t]:
            self.wait(offset, step)
            self.forward(self.at(offset, step), offset, step, masks)

    def over_cores(self):
        n_dp = self.w.sizes[0]
        for offset in range(1, n_dp, 2):
            for i in range(self.n_seq):
                self.wait(offset, i)
        self.kept.wait()

    def seq_steps(self):
        return [lambda i=i: self.along_seq(i) for i in range(1, self.n_seq)]

    def chip_steps(self, t):
        return [lambda i=i: self.over_chips(t, i) for i in range(self.n_seq)]


class GatherColumns(Gather):
    def __init__(self, *args):
        super().__init__(*args)
        self.slots = self.w.zs

    def mine(self):
        return self.src.at[self.w.z]

    def own_seq(self):
        for i in range(1, self.n_seq):
            sem = self.recv.at[0, self.w.z]
            self.w.send(self.src.at[self.w.zs[i]], self.at(0, 0), sem, self.w.peer(0, i))

    def along_seq(self, i):
        self.wait(0, i)
        self.forward(self.at(0, i), 0, i, self.order(i) + [1])


def sends_of_gather(n_dp, n_seq):
    return 2 + n_seq - 1 + n_seq * (n_dp - 1)


def group_lanes(packed, row, group, n_seq):
    total = packed[group * n_seq, row : row + 1, :]
    for s in range(1, n_seq):
        total = total + packed[group * n_seq + s, row : row + 1, :]
    return total


def front_kernel(
    sizes,
    heads,
    valid_ref,
    x_ref,
    cotangent,
    vec_ref,
    qkv_ref,
    out_ref,
    up_ref,
    down_ref,
    columns_out,
    full_out,
    full_up,
    full_down,
    page_out,
    query_out,
    key_out,
    value_out,
    context_out,
    logs_out,
    hidden_out,
    gelu_out,
    slope_out,
    output,
    normed_one,
    inv_one,
    grad_mid,
    sums_out,
    packed,
    columns,
    page,
    held,
    context_sent,
    context_held,
    context_turned,
    value_turned,
    logs,
    out_matrix,
    up_matrix,
    down_matrix,
    page_turned,
    context_rows_turned,
    hidden,
    hidden_low,
    hidden_turned,
    gelu_low,
    gelu_turned,
    slopes,
    branch,
    send_sems,
    gather_sems,
    page_sems,
    context_sems,
    local_sems,
):
    n_dp, n_seq = sizes
    w = Wires(send_sems, sizes)
    rows, width = x_ref.shape
    part = width // n_seq
    head_dim = width // heads
    local_heads = heads // n_seq
    stream = rows * n_seq
    w.greet()
    line = Line(w, lambda s: page.at[s], page_sems)
    line.own(x_ref)
    sources = (
        (vec_ref, packed),
        (qkv_ref, columns),
        (out_ref, out_matrix),
        (up_ref, up_matrix),
        (down_ref, down_matrix),
    )
    vec, qkv, out, up, down = [
        (GatherColumns if k == 1 else Gather)(w, src, dst, gather_sems.at[k], local_sems.at[k])
        for k, (src, dst) in enumerate(sources)
    ]
    queue = []

    def pump(count):
        for _ in range(min(count, len(queue))):
            queue.pop(0)()

    def run(steps):
        for step in steps:
            step()

    for unit in (qkv, vec):
        unit.own_seq()
        unit.own_chips()
    out.own_chips()
    up.own_chips()
    page[w.z] = x_ref[...]
    for unit in (qkv, vec):
        run(unit.seq_steps())
    line.take(1)
    out.own_seq()
    for unit in (qkv, vec):
        run(unit.chip_steps(0))
    for unit in (qkv, vec):
        run(unit.chip_steps(1))
    line.take(2)
    up.own_seq()
    qkv.over_cores()
    vec.over_cores()
    keeps = []

    def keep(src, dst):
        keeps.append(pltpu.make_async_copy(src, dst, local_sems.at[5 + len(keeps)]))
        keeps[-1].start()

    keep(columns, columns_out)
    groups = part // 128
    biases = [
        jnp.concatenate([group_lanes(packed, b, w.z * groups + g, n_seq) for g in range(groups)], axis=1)
        for b in range(2)
    ]
    matrix = columns[...].reshape(width, 3 * part)

    def project(s):
        piece = jnp.dot(page[s], matrix, preferred_element_type=jnp.float32)
        for t in range(3):
            third = piece[:, t * part : (t + 1) * part]
            if t != 1:
                third = third + biases[t // 2]
            held[t, s] = third.astype(jnp.bfloat16)

    project(w.z)
    project(w.far[1])
    run(out.seq_steps())
    down.own_chips()
    project(w.far[2])
    line.take(3)
    project(w.far[3])
    for t, ref in enumerate((query_out, key_out, value_out)):
        keep(held.at[t], ref)
    position = lax.broadcasted_iota(jnp.int32, (stream, 128), 0)
    lane = lax.broadcasted_iota(jnp.int32, (stream, 128), 1)
    guard = jnp.where((position >= valid_ref[0]) & (lane == 0), MASKED, 0.0).astype(jnp.bfloat16)
    value_turned[...] = held[2].reshape(stream, part).T
    one_lane = lax.broadcasted_iota(jnp.int32, (rows, 128), 1)
    ones = jnp.where(one_lane == 0, 1.0, 0.0).astype(jnp.bfloat16)
    per_block = 128 // head_dim
    scale = 1.0 / math.sqrt(head_dim)
    queue += up.seq_steps()[:1] + out.chip_steps(0) + up.seq_steps()[1:] + [down.own_seq]
    queue += out.chip_steps(1) + up.chip_steps(0) + down.seq_steps()
    counts = (2, 4, 3, 5)
    for h in range(local_heads):
        pair = slice(h // per_block * 128, h // per_block * 128 + 128)
        low = h % per_block * head_dim
        keys = jnp.concatenate([held[1, :, :, pair].reshape(stream, 128), guard], axis=1)

        def attend(c, _, keys=keys, pair=pair, low=low, h=h):
            query = held[0, c, :, pair]
            mine = (one_lane >= low) & (one_lane < low + head_dim)
            query = jnp.where(mine, query.astype(jnp.float32) * scale, 0.0).astype(jnp.bfloat16)
            query = jnp.concatenate([query, ones], axis=1)
            scores = lax.dot_general(keys, query, FLAT, preferred_element_type=jnp.float32)
            peak = jnp.max(scores, axis=0, keepdims=True)
            raised = jnp.exp(scores - peak)
            total = jnp.sum(raised, axis=0, keepdims=True)
            mixed = jnp.dot(
                value_turned[h * head_dim : (h + 1) * head_dim, :],
                raised.astype(jnp.bfloat16),
                preferred_element_type=jnp.float32,
            )
            context_turned[c, h * head_dim : (h + 1) * head_dim, :] = mixed / total
            logs[c, h : h + 1, :] = peak + jnp.log(total)
            return 0

        lax.fori_loop(0, n_seq, attend, 0)
        pump(counts[h])
    for j in range(n_seq):
        context_sent[j] = context_turned[j].T.astype(jnp.bfloat16)
    for i in range(1, n_seq):
        w.send(context_sent.at[w.zs[i]], context_held.at[w.z], context_sems.at[i], w.peer(0, i))
    context_held[w.z] = context_sent[w.z]
    keep(logs, logs_out)
    for s in range(n_seq):
        page_turned[:, s * rows : (s + 1) * rows] = page[s].T
    keep(page_turned, page_out)
    pump(len(queue))
    out.over_cores()
    keep(out_matrix, full_out)

    def line_of(row):
        return jnp.concatenate([group_lanes(packed, row, d, n_seq) for d in range(n_dp)], axis=1)

    for i in range(1, n_seq):
        w.arrived(context_held.at[w.zs[i]], context_sems.at[i])
    total = x_ref[...].astype(jnp.float32) + line_of(2)
    per_part = part // out_matrix.shape[1]
    for j in range(n_seq):
        block = out_matrix[j * per_part : (j + 1) * per_part].reshape(part, width)
        total = total + jnp.dot(context_held[j], block, preferred_element_type=jnp.float32)
        context_rows_turned[j * part : (j + 1) * part, :] = context_held[j].T
    keep(context_rows_turned, context_out)
    gain_one = line_of(3)
    rows_hidden, normed, inv = norm_forward(total, gain_one, line_of(4))
    normed_one[...] = normed
    inv_one[...] = jnp.broadcast_to(inv, inv_one.shape)
    hidden[...] = rows_hidden
    hidden_low[...] = rows_hidden.astype(jnp.bfloat16)
    hidden_turned[...] = rows_hidden.T.astype(jnp.bfloat16)
    keep(hidden_turned, hidden_out)
    run(up.chip_steps(1))
    run(down.chip_steps(0))
    up.over_cores()
    keep(up_matrix, full_up)
    run(down.chip_steps(1))
    chunk = 512
    chunks = up_matrix.shape[2] // chunk
    per_chunk = chunk // down_matrix.shape[1]

    def activate(f, _):
        at = pl.ds(pl.multiple_of(f * chunk, chunk), chunk)
        block = up_matrix[:, :, at].reshape(width, chunk)
        up_bias = jnp.concatenate(
            [packed[f * per_chunk + e, 8:9, :] for e in range(per_chunk)], axis=1
        )
        act = jnp.dot(hidden_low[...], block, preferred_element_type=jnp.float32) + up_bias
        below = 0.5 + 0.5 * lax.erf(act * math.sqrt(0.5))
        gelu = act * below
        gelu_low[:, at] = gelu.astype(jnp.bfloat16)
        gelu_turned[at, :] = gelu.T.astype(jnp.bfloat16)
        bell = jnp.exp(-0.5 * act * act) * (1.0 / math.sqrt(2.0 * math.pi))
        slopes[:, at] = (below + act * bell).astype(jnp.bfloat16)
        return 0

    lax.fori_loop(0, chunks, activate, 0)
    keep(gelu_turned, gelu_out)
    keep(slopes, slope_out)
    down.over_cores()
    keep(down_matrix, full_down)
    branch[...] = hidden[...] + line_of(5)

    def shrink(f, _):
        at = pl.ds(pl.multiple_of(f * chunk, chunk), chunk)
        block = down_matrix[pl.ds(f * per_chunk, per_chunk)].reshape(chunk, width)
        branch[...] += jnp.dot(gelu_low[:, at], block, preferred_element_type=jnp.float32)
        return 0

    lax.fori_loop(0, chunks, shrink, 0)
    gain_two = line_of(6)
    result, normed, inv = norm_forward(branch[...], gain_two, line_of(7))
    output[...] = result.astype(jnp.bfloat16)
    grad = cotangent[...].astype(jnp.float32)
    mid, grad_gain, grad_shift = norm_backward(grad, normed, inv, gain_two)
    grad_mid[...] = mid
    grad_bias = jnp.sum(mid.astype(jnp.bfloat16).astype(jnp.float32), axis=0)
    sums_out[...] = jnp.zeros_like(sums_out)
    for row, line_sum in enumerate((grad_bias, grad_gain, grad_shift)):
        sums_out[5 + row : 6 + row, :] = line_sum.reshape(1, width)
    sums_out[3:4, :] = gain_one
    for copy in keeps:
        copy.wait()
    w.drain()


def front(sizes, heads, valid, rows, cotangent, vec, w_columns, w_out, w_up, w_down):
    n_dp, n_seq = sizes
    devices = n_dp * n_seq
    count, width = rows.shape
    part = width // n_seq
    stream = count * n_seq
    wide = w_up.shape[1]
    low = jnp.bfloat16
    pieces = jax.ShapeDtypeStruct((n_seq, count, part), low)

    def full(shard):
        return jax.ShapeDtypeStruct((devices,) + shard.shape, shard.dtype)

    anywhere = pl.BlockSpec(memory_space=pl.ANY)
    local = pl.BlockSpec(memory_space=pltpu.VMEM)
    sends = 5 * sends_of_gather(n_dp, n_seq) + 5 + n_seq - 1
    return pl.pallas_call(
        lambda *refs: front_kernel(sizes, heads, *refs),
        out_shape=(
            jax.ShapeDtypeStruct((devices,) + w_columns.shape[1:], low),
            full(w_out),
            full(w_up),
            full(w_down),
            jax.ShapeDtypeStruct((width, stream), low),
            pieces,
            pieces,
            pieces,
            jax.ShapeDtypeStruct((width, count), low),
            jax.ShapeDtypeStruct((n_seq, 8, count), jnp.float32),
            jax.ShapeDtypeStruct((width, count), low),
            jax.ShapeDtypeStruct((wide, count), low),
            jax.ShapeDtypeStruct((count, wide), low),
            jax.ShapeDtypeStruct((count, width), low),
            jax.ShapeDtypeStruct((count, width), jnp.float32),
            jax.ShapeDtypeStruct((count, 128), jnp.float32),
            jax.ShapeDtypeStruct((count, width), jnp.float32),
            jax.ShapeDtypeStruct((8, width), jnp.float32),
        ),
        in_specs=[
            pl.BlockSpec(memory_space=pltpu.SMEM),
            local,
            local,
        ]
        + [anywhere] * 5,
        out_specs=[anywhere] * 13 + [local] * 5,
        scratch_shapes=[
            pltpu.VMEM((devices,) + vec.shape, jnp.float32),
            pltpu.VMEM((devices,) + w_columns.shape[1:], low),
            pltpu.VMEM((n_seq, count, width), low),
            pltpu.VMEM((3, n_seq, count, part), low),
            pltpu.VMEM((n_seq, count, part), low),
            pltpu.VMEM((n_seq, count, part), low),
            pltpu.VMEM((n_seq, part, count), jnp.float32),
            pltpu.VMEM((part, stream), low),
            pltpu.VMEM((n_seq, 8, count), jnp.float32),
            pltpu.VMEM((devices,) + w_out.shape, low),
            pltpu.VMEM((devices,) + w_up.shape, low),
            pltpu.VMEM((devices,) + w_down.shape, low),
            pltpu.VMEM((width, stream), low),
            pltpu.VMEM((width, count), low),
            pltpu.VMEM((count, width), jnp.float32),
            pltpu.VMEM((count, width), low),
            pltpu.VMEM((width, count), low),
            pltpu.VMEM((count, wide), low),
            pltpu.VMEM((wide, count), low),
            pltpu.VMEM((count, wide), low),
            pltpu.VMEM((count, width), jnp.float32),
            pltpu.SemaphoreType.DMA((sends,)),
            pltpu.SemaphoreType.DMA((5, n_dp, n_seq)),
            pltpu.SemaphoreType.DMA((n_seq,)),
            pltpu.SemaphoreType.DMA((n_seq,)),
            pltpu.SemaphoreType.DMA((20,)),
        ],
        compiler_params=pltpu.CompilerParams(
            collective_id=0, has_side_effects=True, vmem_limit_bytes=60 * 2**20
        ),
        name="front",
    )(valid, rows, cotangent, vec, w_columns, w_out, w_up, w_down)


def add_rows(into, term):
    rows = into.shape[0]
    step = min(16, rows)

    def body(r, _):
        at = pl.ds(pl.multiple_of(r * step, step), step)
        total = into[at, :].astype(jnp.float32) + term[at, :].astype(jnp.float32)
        into[at, :] = total.astype(into.dtype)
        return 0

    lax.fori_loop(0, rows // step, body, 0)


class LineSum:
    def __init__(self, wires, block, last, sems):
        self.w, self.block, self.last, self.sems = wires, block, last, sems

    def into(self, src, index, device, when):
        self.w.send(src, self.last.at[index], self.sems.at[index], device, when)

    def add(self, k, index):
        def action():
            self.w.arrived(self.last.at[index], self.sems.at[index])
            add_rows(self.block(k), self.last.at[index])

        pl.when(self.w.inner)(action)

    def offer(self, k):
        self.into(self.block(k), k - 1, (self.w.dp, self.w.right), self.w.outer)

    def relay(self, k):
        w, block = self.w, self.block(k)
        if k == 1:
            self.add(1, 4)
            self.into(block, 3, (w.dp, w.left), w.inner)
        else:
            self.add(k, k - 1)
            self.into(block, 3 if k == 2 else 4, (w.dp, w.right), w.inner)

    def finish(self, start, out):
        w = self.w
        w.arrived(self.last.at[3], self.sems.at[3])
        w.arrived(self.last.at[0], self.sems.at[0], w.inner)
        rows = out.shape[0]
        step = min(16, rows)

        def total_of(count):
            def body(r, _):
                at = pl.ds(pl.multiple_of(r * step, step), step)
                total = start(at) + self.last[3, at, :].astype(jnp.float32)
                if count == 2:
                    total = total + self.last[0, at, :].astype(jnp.float32)
                out[at, :] = total.astype(out.dtype)
                return 0

            lax.fori_loop(0, rows // step, body, 0)

        pl.when(w.inner)(lambda: total_of(2))
        pl.when(w.outer)(lambda: total_of(1))


class Scatter:
    def __init__(self, wires, kind, source, resident, bufs, sems, local, out):
        self.w, self.kind, self.source, self.resident = wires, kind, source, resident
        self.mine, self.total, self.first, self.second, self.last = bufs
        self.core_sems, self.first_sems, self.second_sems, self.last_sems = sems
        self.local, self.out = local, out
        self.n_seq = wires.sizes[1]
        self.offsets = [6, 2, 4, 0]
        self.loads = {}
        self.slots = wires.far if kind == "line" else wires.zs
        self.line = LineSum(wires, lambda k: self.total.at[0, self.slots[k]], self.last, self.last_sems)

    def order(self, step):
        return (2, 4) if step % 2 == 0 else (4, 2)

    def group(self, offset):
        return self.source.at[pl.ds(self.w.dps[offset] * self.n_seq, self.n_seq)]

    def load(self, k):
        if self.resident or k >= 4:
            return
        self.loads[k] = pltpu.make_async_copy(
            self.group(self.offsets[k]), self.mine.at[k % 2], self.local.at[k % 2]
        )
        self.loads[k].start()

    def start(self):
        for o in self.offsets:
            self.w.send(self.group(o ^ 1), self.total.at[o // 2], self.core_sems.at[o // 2], self.w.peer(1, 0))
        self.load(0)
        self.load(1)

    def over_cores(self, k):
        o = self.offsets[k]
        self.w.arrived(self.total.at[o // 2], self.core_sems.at[o // 2])
        if not self.resident:
            self.loads[k].wait()
        for i in range(self.n_seq):
            slot = self.slots[i]
            mask = self.order(i)[0]
            block = self.total.at[o // 2, slot]
            if self.resident:
                own = self.source.at[self.w.dps[o] * self.n_seq + slot]
            else:
                own = self.mine.at[k % 2, slot]
            add_rows(block, own)
            if o & mask:
                keep = (o ^ mask) // (6 ^ mask)
                self.w.send(block, self.first.at[i, keep], self.first_sems.at[i, keep], self.w.peer(mask, 0))
        self.load(k + 2)

    def over_chips(self, i):
        mask = self.order(i)[1]
        for keep in (1, 0):
            o = mask * keep
            block = self.total.at[o // 2, self.slots[i]]
            self.w.arrived(self.first.at[i, keep], self.first_sems.at[i, keep])
            add_rows(block, self.first.at[i, keep])
            if keep:
                self.w.send(block, self.second.at[i], self.second_sems.at[i], self.w.peer(mask, 0))

    def to_seq(self, i):
        block = self.total.at[0, self.slots[i]]
        self.w.arrived(self.second.at[i], self.second_sems.at[i])
        add_rows(block, self.second.at[i])
        if self.kind == "line":
            if i:
                self.line.offer(i)
                self.line.relay(i)
        elif i:
            self.w.send(block, self.last.at[i], self.last_sems.at[i], self.w.peer(0, i))

    def finish(self):
        block = self.total.at[0, self.w.z]
        if self.kind == "line":
            self.line.finish(lambda at: block[at, :].astype(jnp.float32), self.out)
            return
        self.out[self.w.z] = block[...].astype(jnp.float32)
        for i in range(1, self.n_seq):
            self.w.arrived(self.last.at[i], self.last_sems.at[i])
            self.out[self.w.zs[i]] = self.last[i].astype(jnp.float32)

    def core_steps(self):
        return [lambda k=k: self.over_cores(k) for k in range(4)]

    def chip_steps(self):
        return [lambda i=i: self.over_chips(i) for i in range(self.n_seq)]

    def seq_steps(self):
        return [lambda i=i: self.to_seq(i) for i in (3, 2, 1, 0)]


def back_kernel(sizes, heads, *refs):
    n_dp, n_seq = sizes
    (
        valid_ref,
        page_in,
        grad_context,
        grad_first,
        query_in,
        key_in,
        value_in,
        logs,
        columns_in,
        down_in,
        up_in,
        out_in,
        vec_in,
        grad_rows,
        *outs,
    ) = refs[:19]
    scratch = list(refs[19:])

    def take(count):
        got = scratch[:count]
        del scratch[:count]
        return got

    send_sems, core_sems, first_sems, second_sems, last_sems, load_sems = take(6)
    head_sems, local_sems, row_sems = take(3)
    held, masked_query, masked_grad, keys, values, key_turned = take(6)
    query_grad, key_grad, value_grad = take(3)
    project, page_turned, columns, vec = take(4)
    row_terms, row_last, own_rows, partial = take(4)
    units = [take(5 if k < 3 else 4) for k in range(5)]
    w = Wires(send_sems, sizes)
    rows, width = grad_first.shape
    part = width // n_seq
    head_dim = width // heads
    local_heads = heads // n_seq
    stream = rows * n_seq
    per_block = 128 // head_dim
    scale = 1.0 / math.sqrt(head_dim)
    loads = []
    for t, (ref, into) in enumerate(
        (
            (query_in, held.at[0]),
            (key_in, held.at[1]),
            (value_in, held.at[2]),
            (vec_in, vec),
            (page_in, page_turned),
            (columns_in, columns),
        )
    ):
        loads.append(pltpu.make_async_copy(ref, into, local_sems.at[t]))
        loads[-1].start()
    w.greet()

    def lanes_of_part(j):
        return pl.ds(pl.multiple_of(j * part, part), part)

    for i in range(1, n_seq):
        w.send(grad_context.at[:, lanes_of_part(w.zs[i])], held.at[3, w.z], head_sems.at[i], w.peer(0, i))
    own_grad = pltpu.make_async_copy(grad_context.at[:, lanes_of_part(w.z)], held.at[3, w.z], local_sems.at[6])
    own_grad.start()
    sources = (down_in, up_in, out_in, partial, vec)
    scatters = []
    for k in range(5):
        bufs = units[k] if k < 3 else [None] + units[k]
        scatters.append(
            Scatter(
                w,
                "columns" if k == 3 else "line",
                sources[k],
                k >= 3,
                bufs,
                (core_sems.at[k], first_sems.at[k], second_sems.at[k], last_sems.at[k]),
                load_sems.at[min(k, 2)],
                outs[k],
            )
        )
    down, up, out, qkv, small = scatters
    for unit in (down, up, out):
        unit.start()
    queue = []

    def pump(count):
        for _ in range(min(count, len(queue))):
            queue.pop(0)()

    for copy in loads:
        copy.wait()
    lane = lax.broadcasted_iota(jnp.int32, (stream, 128), 1)
    position = lax.broadcasted_iota(jnp.int32, (stream, 128), 0)
    guard = jnp.where((position >= valid_ref[0]) & (lane == 0), MASKED, 0.0).astype(jnp.bfloat16)

    def spread(source, h, factor):
        block = h // per_block * 128
        low = h % per_block * head_dim
        rows_of = source[:, :, block : block + 128].reshape(stream, 128).astype(jnp.float32)
        mine = (lane >= low) & (lane < low + head_dim)
        return jnp.where(mine, rows_of * factor, 0.0).astype(jnp.bfloat16).reshape(n_seq, rows, 128)

    for h in range(local_heads):
        masked_query[h] = spread(held.at[0], h, scale)
    for b in range(local_heads // per_block):
        lanes = slice(b * 128, (b + 1) * 128)
        keys[b, :, :128] = held[1, :, :, lanes].reshape(stream, 128)
        keys[b, :, 128:] = guard
        values[b] = held[2, :, :, lanes].reshape(stream, 128)
    turned = held[1].reshape(stream, part).T
    for h in range(local_heads):
        key_turned[h] = turned[h * head_dim : (h + 1) * head_dim, :]
    key_grad[...] = jnp.zeros_like(key_grad)
    value_grad[...] = jnp.zeros_like(value_grad)
    queue += down.core_steps()
    pump(4)
    own_grad.wait()
    for i in range(1, n_seq):
        w.arrived(held.at[3, w.zs[i]], head_sems.at[i])
    for h in range(local_heads):
        masked_grad[h] = spread(held.at[3], h, 1.0)
    queue += up.core_steps() + down.chip_steps() + out.core_steps() + down.seq_steps()[:2] + up.chip_steps()
    queue += down.seq_steps()[2:] + out.chip_steps() + up.seq_steps() + out.seq_steps()
    pump(4)
    ones = jnp.where(lax.broadcasted_iota(jnp.int32, (rows, 128), 1) == 0, 1.0, 0.0).astype(jnp.bfloat16)
    for c in range(n_seq):

        def head(h, _, c=c):
            block = h // per_block
            query, grad = masked_query[h, c], masked_grad[h, c]
            scores = lax.dot_general(
                keys[block], jnp.concatenate([query, ones], axis=1), FLAT, preferred_element_type=jnp.float32
            )
            probs = jnp.exp(scores - logs[c, pl.ds(h, 1), :])
            moved = lax.dot_general(values[block], grad, FLAT, preferred_element_type=jnp.float32)
            centre = jnp.sum(probs * moved, axis=0, keepdims=True)
            slope = (probs * (moved - centre)).astype(jnp.bfloat16)
            query_grad[h] = jnp.dot(key_turned[h], slope, preferred_element_type=jnp.float32) * scale
            key_grad[block] += jnp.dot(slope, query, preferred_element_type=jnp.float32)
            value_grad[block] += jnp.dot(
                probs.astype(jnp.bfloat16), grad, preferred_element_type=jnp.float32
            )
            return 0

        lax.fori_loop(0, local_heads, head, 0)
        project[c * rows : (c + 1) * rows, :part] = (
            query_grad[...].reshape(part, rows).T.astype(jnp.bfloat16)
        )
        pump(5)
    for t, total in ((1, key_grad), (2, value_grad)):
        for b in range(local_heads // per_block):
            at = t * part + b * 128
            project[:, at : at + 128] = total[b].astype(jnp.bfloat16)
    matrix = columns[...].reshape(width, 3 * part)
    row_sum = LineSum(w, lambda k: row_terms.at[k], row_last, row_sems)

    def row_term(k):
        at = pl.ds(pl.multiple_of(w.far[k] * rows, rows), rows)
        return lax.dot_general(project[at, :], matrix, FLAT, preferred_element_type=jnp.float32)

    for k in (3, 2, 1):
        row_terms[k] = row_term(k).astype(jnp.bfloat16)
        row_sum.offer(k)
    for t in range(3):
        block = jnp.dot(
            page_turned[...], project[:, t * part : (t + 1) * part], preferred_element_type=jnp.float32
        )
        partial[:, :, t * part : (t + 1) * part] = block.astype(jnp.bfloat16).reshape(n_dp * n_seq, -1, part)
    qkv.start()
    groups = part // 128
    for b, t in ((0, 0), (1, 2)):
        sums = jnp.sum(project[:, t * part : (t + 1) * part].astype(jnp.float32), axis=0, keepdims=True)
        for g in range(groups):
            for s in range(n_seq):
                vec[(w.z * groups + g) * n_seq + s, b : b + 1, :] = sums[:, g * 128 : (g + 1) * 128]
    small.start()
    row_sum.relay(3)
    row_sum.relay(2)
    own_rows[...] = row_term(0) + grad_first[...]
    queue[:0] = qkv.core_steps() + small.core_steps()
    pump(8)
    row_sum.relay(1)
    queue += qkv.chip_steps() + small.chip_steps() + qkv.seq_steps() + small.seq_steps()
    pump(len(queue))
    for unit in scatters:
        unit.finish()
    row_sum.finish(lambda at: own_rows[at, :], grad_rows)
    w.drain()


def back(sizes, heads, valid, page, grad_context, grad_first, heads_in, logs, columns, partial_sums):
    n_dp, n_seq = sizes
    devices = n_dp * n_seq
    count, width = grad_first.shape
    part = width // n_seq
    stream = count * n_seq
    head_dim = width // heads
    local_heads = heads // n_seq
    blocks = local_heads * head_dim // 128
    low = jnp.bfloat16
    shapes = [p.shape[1:] for p in partial_sums[:3]] + [columns.shape[1:], partial_sums[3].shape[1:]]
    kinds = [low] * 4 + [jnp.float32]
    results = [jax.ShapeDtypeStruct(shape, jnp.float32) for shape in shapes]
    results[3] = jax.ShapeDtypeStruct((n_seq,) + shapes[3], jnp.float32)
    anywhere = pl.BlockSpec(memory_space=pl.ANY)
    local = pl.BlockSpec(memory_space=pltpu.VMEM)
    sends = 5 * (4 + 3 * n_seq + 6) + 6 + n_seq - 1
    chips = n_dp // 2
    scratch = [
        pltpu.SemaphoreType.DMA((sends,)),
        pltpu.SemaphoreType.DMA((5, chips)),
        pltpu.SemaphoreType.DMA((5, n_seq, 2)),
        pltpu.SemaphoreType.DMA((5, n_seq)),
        pltpu.SemaphoreType.DMA((5, 5)),
        pltpu.SemaphoreType.DMA((3, 2)),
        pltpu.SemaphoreType.DMA((n_seq,)),
        pltpu.SemaphoreType.DMA((7,)),
        pltpu.SemaphoreType.DMA((5,)),
        pltpu.VMEM((4, n_seq, count, part), low),
        pltpu.VMEM((local_heads, n_seq, count, 128), low),
        pltpu.VMEM((local_heads, n_seq, count, 128), low),
        pltpu.VMEM((blocks, stream, 256), low),
        pltpu.VMEM((blocks, stream, 128), low),
        pltpu.VMEM((local_heads, head_dim, stream), low),
        pltpu.VMEM((local_heads, head_dim, count), jnp.float32),
        pltpu.VMEM((blocks, stream, 128), jnp.float32),
        pltpu.VMEM((blocks, stream, 128), jnp.float32),
        pltpu.VMEM((stream, 3 * part), low),
        pltpu.VMEM((width, stream), low),
        pltpu.VMEM(columns.shape, low),
        pltpu.VMEM(partial_sums[3].shape, jnp.float32),
        pltpu.VMEM((n_seq, count, width), low),
        pltpu.VMEM((5, count, width), low),
        pltpu.VMEM((count, width), jnp.float32),
        pltpu.VMEM(columns.shape, low),
    ]
    for k, (shape, kind) in enumerate(zip(shapes, kinds)):
        if k < 3:
            scratch.append(pltpu.VMEM((2, n_seq) + shape, kind))
        scratch += [
            pltpu.VMEM((chips, n_seq) + shape, kind),
            pltpu.VMEM((n_seq, 2) + shape, kind),
            pltpu.VMEM((n_seq,) + shape, kind),
            pltpu.VMEM((5,) + shape, kind),
        ]
    return pl.pallas_call(
        lambda *refs: back_kernel(sizes, heads, *refs),
        out_shape=[jax.ShapeDtypeStruct((count, width), low)] + results,
        in_specs=[pl.BlockSpec(memory_space=pltpu.SMEM), anywhere, anywhere, local]
        + [anywhere] * 3
        + [local]
        + [anywhere] * 5,
        out_specs=[local] * 6,
        scratch_shapes=scratch,
        compiler_params=pltpu.CompilerParams(
            collective_id=1, has_side_effects=True, vmem_limit_bytes=62 * 2**20
        ),
        name="back",
    )(valid, page, grad_context, grad_first, *heads_in, logs, columns, *partial_sums)


def spread_lanes(vectors, n_seq):
    stacked = jnp.stack(vectors).astype(jnp.float32)
    tiled = jnp.tile(stacked, (1, n_seq))
    owner = jnp.arange(tiled.shape[1], dtype=jnp.int32) // stacked.shape[1]
    return jnp.where(owner[None, :] == lax.axis_index("seq"), tiled, 0.0)


def kernel_plan(
    x_in,
    w_qkv,
    q_bias,
    v_bias,
    w_out,
    out_bias,
    ln1_gain,
    ln1_shift,
    w_up,
    up_bias,
    w_down,
    down_bias,
    ln2_gain,
    ln2_shift,
    valid,
    cotangent,
):
    sizes = (lax.axis_size("dp"), lax.axis_size("seq"))
    n_dp, groups = sizes
    rows = x_in[0]
    count, width = rows.shape
    vectors = (q_bias, v_bias, out_bias, ln1_gain, ln1_shift, down_bias, ln2_gain, ln2_shift)
    spread = spread_lanes(vectors, groups)
    vec = jnp.concatenate(
        [spread, up_bias.astype(jnp.float32)[None], jnp.zeros((7, spread.shape[1]), jnp.float32)]
    )
    third = width // groups
    w_columns = (
        w_qkv.reshape(-1, 3, groups, third).transpose(2, 0, 1, 3).reshape(groups, -1, 3 * third)
    )
    (
        columns,
        full_out,
        full_up,
        full_down,
        page_turned,
        query_heads,
        key_heads,
        value_heads,
        context_turned,
        logs,
        hidden_turned,
        gelu_turned,
        slopes,
        output,
        normed_one,
        inv_one,
        grad_mid,
        sums,
    ) = front(sizes, HEADS, valid, rows, cotangent[0], vec, w_columns, w_out, w_up, w_down)
    full_out = full_out.reshape(width, -1)
    full_up = full_up.reshape(width, -1)
    full_down = full_down.reshape(-1, width)
    grad_branch = grad_mid.astype(jnp.bfloat16)
    grad_w_down = jnp.dot(gelu_turned, grad_branch, preferred_element_type=jnp.float32)
    grad_gelu = times_back(grad_branch, full_down)
    grad_up = (grad_gelu * slopes.astype(jnp.float32)).astype(jnp.bfloat16)
    grad_w_up = jnp.dot(hidden_turned, grad_up, preferred_element_type=jnp.float32)
    grad_up_bias = jnp.sum(grad_up.astype(jnp.float32), axis=0)
    grad_hidden = times_back(grad_up, full_up) + grad_mid
    grad_first, grad_ln1_gain, grad_ln1_shift = norm_backward(
        grad_hidden, normed_one, inv_one[:, :1], sums[3]
    )
    grad_down_bias, grad_ln2_gain, grad_ln2_shift = sums[5], sums[6], sums[7]
    grad_attn = grad_first.astype(jnp.bfloat16)
    grad_w_out = jnp.dot(context_turned, grad_attn, preferred_element_type=jnp.float32)
    grad_out_bias = jnp.sum(grad_attn.astype(jnp.float32), axis=0)
    grad_context = times_back(grad_attn, full_out).astype(jnp.bfloat16)

    def packed(vector):
        return vector.reshape(n_dp, 1, -1)

    zero = jnp.zeros((width,), jnp.float32)
    sums = (zero, zero, grad_out_bias, grad_ln1_gain, grad_ln1_shift)
    sums += (grad_down_bias, grad_ln2_gain, grad_ln2_shift)
    by_group = jnp.concatenate([packed(v) for v in sums], axis=1)
    by_group = jnp.broadcast_to(by_group[:, None], (n_dp, groups) + by_group.shape[1:])
    by_device = jnp.concatenate(
        [
            by_group.reshape(n_dp * groups, 8, -1),
            grad_up_bias.reshape(n_dp * groups, 1, -1),
            jnp.zeros((n_dp * groups, 7, by_group.shape[-1]), jnp.float32),
        ],
        axis=1,
    )
    devices = n_dp * groups

    def cut(grad):
        return grad.astype(jnp.bfloat16).reshape(devices, -1, grad.shape[1])

    grad_rows, *sums = back(
        sizes,
        HEADS,
        valid,
        page_turned,
        grad_context,
        grad_first,
        (query_heads, key_heads, value_heads),
        logs,
        columns,
        (cut(grad_w_down), cut(grad_w_up), cut(grad_w_out), by_device),
    )
    vec_sums = sums[4]
    mine = lax.dynamic_slice(
        vec_sums[:8], (0, lax.axis_index("seq") * (width // devices)), (8, width // devices)
    )
    return (
        output[None],
        grad_rows[None],
        sums[3].reshape(groups, -1, 3, third).transpose(1, 2, 0, 3).reshape(-1, 3 * width),
        mine[0],
        mine[1],
        sums[2],
        mine[2],
        mine[3],
        mine[4],
        sums[1],
        vec_sums[8],
        sums[0],
        mine[5],
        mine[6],
        mine[7],
    )


def solution(mesh):
    n_dp, n_seq = mesh.shape["dp"], mesh.shape["seq"]

    def per_device(x_in, w_qkv, *rest):
        part, width = w_qkv.shape[0], x_in.shape[2]
        fits = (n_dp, n_seq) == (8, 4) and part % 32 == 0 and part * n_seq == 128 and width // n_seq % 128 == 0 and x_in.shape[0] == 1
        plan = kernel_plan if fits else general_plan
        return plan(x_in, w_qkv, *rest)

    return jax.shard_map(
        per_device,
        mesh=mesh,
        in_specs=(
            P("dp", "seq", None),
            P(("dp", "seq"), None),
            P(("dp", "seq")),
            P(("dp", "seq")),
            P(("dp", "seq"), None),
            P(("dp", "seq")),
            P(("dp", "seq")),
            P(("dp", "seq")),
            P(("dp", "seq"), None),
            P(("dp", "seq")),
            P(("dp", "seq"), None),
            P(("dp", "seq")),
            P(("dp", "seq")),
            P(("dp", "seq")),
            P("dp"),
            P("dp", "seq", None),
        ),
        out_specs=(
            P("dp", "seq", None),
            P("dp", "seq", None),
            P(("dp", "seq"), None),
            P(("dp", "seq")),
            P(("dp", "seq")),
            P(("dp", "seq"), None),
            P(("dp", "seq")),
            P(("dp", "seq")),
            P(("dp", "seq")),
            P(("dp", "seq"), None),
            P(("dp", "seq")),
            P(("dp", "seq"), None),
            P(("dp", "seq")),
            P(("dp", "seq")),
            P(("dp", "seq")),
        ),
        check_vma=False,
    )
```

```python
import math

import jax
import jax.numpy as jnp
from jax import lax
from jax.experimental import pallas as pl
from jax.experimental.pallas import tpu as pltpu
from jax.sharding import PartitionSpec as P

HEADS = 16


eps_norm = 1e-05


def outer_sum(left, right):
    return lax.dot_general(
        left, right, (((0,), (0,)), ((), ())), preferred_element_type=jnp.float32
    )


def times_back(rows, matrix):
    return lax.dot_general(
        rows, matrix, (((1,), (1,)), ((), ())), preferred_element_type=jnp.float32
    )


def gelu_exact(values):
    return jax.nn.gelu(values, approximate=False)


def norm_forward(rows, gain, shift):
    center = rows - jnp.mean(rows, axis=-1, keepdims=True)
    inv_std = lax.rsqrt(jnp.mean(center * center, axis=-1, keepdims=True) + eps_norm)
    normed = center * inv_std
    return (normed * gain + shift, normed, inv_std)


def norm_backward(grad_out, normed, inv_std, gain):
    scaled = grad_out * gain
    grad_rows = inv_std * (
        scaled
        - jnp.mean(scaled, axis=-1, keepdims=True)
        - normed * jnp.mean(scaled * normed, axis=-1, keepdims=True)
    )
    return (grad_rows, jnp.sum(grad_out * normed, axis=0), jnp.sum(grad_out, axis=0))


def to_heads(rows, groups):
    count, width = rows.shape
    return rows.reshape(count, groups, width // groups).transpose(1, 0, 2).reshape(groups, -1)


def from_heads(pieces, part_width):
    groups = pieces.shape[0]
    return (
        pieces.reshape(groups, -1, part_width).transpose(1, 0, 2).reshape(-1, groups * part_width)
    )


def general_plan(
    x_in,
    w_qkv,
    q_bias,
    v_bias,
    w_out,
    out_bias,
    ln1_gain,
    ln1_shift,
    w_up,
    up_bias,
    w_down,
    down_bias,
    ln2_gain,
    ln2_shift,
    valid,
    cotangent,
):
    shards = (
        w_qkv,
        q_bias,
        v_bias,
        w_out,
        out_bias,
        ln1_gain,
        ln1_shift,
        w_up,
        up_bias,
        w_down,
        down_bias,
        ln2_gain,
        ln2_shift,
    )
    weights = (
        lax.all_gather(shards[0], ("dp", "seq"), axis=0, tiled=True),
        lax.all_gather(shards[1], ("dp", "seq"), axis=0, tiled=True),
        lax.all_gather(shards[2], ("dp", "seq"), axis=0, tiled=True),
        lax.all_gather(shards[3], ("dp", "seq"), axis=0, tiled=True),
        lax.all_gather(shards[4], ("dp", "seq"), axis=0, tiled=True),
        lax.all_gather(shards[5], ("dp", "seq"), axis=0, tiled=True),
        lax.all_gather(shards[6], ("dp", "seq"), axis=0, tiled=True),
        lax.all_gather(shards[7], ("dp", "seq"), axis=0, tiled=True),
        lax.all_gather(shards[8], ("dp", "seq"), axis=0, tiled=True),
        lax.all_gather(shards[9], ("dp", "seq"), axis=0, tiled=True),
        lax.all_gather(shards[10], ("dp", "seq"), axis=0, tiled=True),
        lax.all_gather(shards[11], ("dp", "seq"), axis=0, tiled=True),
        lax.all_gather(shards[12], ("dp", "seq"), axis=0, tiled=True),
    )
    (
        full_qkv,
        full_qbias,
        full_vbias,
        full_out,
        full_obias,
        full_gain1,
        full_shift1,
        full_up,
        full_ubias,
        full_down,
        full_dbias,
        full_gain2,
        full_shift2,
    ) = weights
    groups = lax.axis_size("seq")
    rows = x_in[0]
    count, width = rows.shape
    head_dim = width // HEADS
    part_width = width // groups
    local_heads = HEADS // groups
    stream = count * groups
    qrows = min(512, stream)
    nblocks = stream // qrows
    scale = 1.0 / math.sqrt(head_dim)
    keep = jnp.arange(stream, dtype=jnp.int32) < valid[0]
    bias_row = jnp.concatenate([full_qbias, jnp.zeros_like(full_qbias), full_vbias]).astype(
        jnp.float32
    )
    project = (jnp.dot(rows, full_qkv, preferred_element_type=jnp.float32) + bias_row).astype(
        jnp.bfloat16
    )
    sent = (
        to_heads(project[:, :width], groups),
        to_heads(project[:, width : 2 * width], groups),
        to_heads(project[:, 2 * width :], groups),
    )
    arrived = (
        lax.all_to_all(sent[0], "seq", split_axis=0, concat_axis=0, tiled=True),
        lax.all_to_all(sent[1], "seq", split_axis=0, concat_axis=0, tiled=True),
        lax.all_to_all(sent[2], "seq", split_axis=0, concat_axis=0, tiled=True),
    )
    query_blocks = arrived[0].reshape(nblocks, qrows, local_heads, head_dim)
    key_heads = arrived[1].reshape(stream, local_heads, head_dim)
    value_heads = arrived[2].reshape(stream, local_heads, head_dim)

    def masked_scores(query):
        scores = (
            jnp.einsum("qhd,khd->hqk", query, key_heads, preferred_element_type=jnp.float32) * scale
        )
        return jnp.where(keep[None, None, :], scores, -1e30)

    def attend_forward(query):
        scores = masked_scores(query)
        peak = jnp.max(scores, axis=-1, keepdims=True)
        raised = jnp.exp(scores - peak)
        total = jnp.sum(raised, axis=-1, keepdims=True)
        probs = (raised / total).astype(jnp.bfloat16)
        context = jnp.einsum("hqk,khd->qhd", probs, value_heads, preferred_element_type=jnp.float32)
        return (context.astype(jnp.bfloat16), (peak + jnp.log(total))[..., 0])

    context, log_sums = lax.map(attend_forward, query_blocks)
    returned_ctx = lax.all_to_all(
        context.reshape(groups, -1), "seq", split_axis=0, concat_axis=0, tiled=True
    )
    context_rows = from_heads(returned_ctx, part_width)
    attn_out = jnp.dot(
        context_rows, full_out, preferred_element_type=jnp.float32
    ) + full_obias.astype(jnp.float32)
    first_rows = rows.astype(jnp.float32) + attn_out
    hidden, normed_one, inv_one = norm_forward(
        first_rows, full_gain1.astype(jnp.float32), full_shift1.astype(jnp.float32)
    )
    hidden_low = hidden.astype(jnp.bfloat16)
    up_act = jnp.dot(hidden_low, full_up, preferred_element_type=jnp.float32) + full_ubias.astype(
        jnp.float32
    )
    gelu_low = gelu_exact(up_act).astype(jnp.bfloat16)
    branch = jnp.dot(gelu_low, full_down, preferred_element_type=jnp.float32) + full_dbias.astype(
        jnp.float32
    )
    output, normed_two, inv_two = norm_forward(
        hidden + branch, full_gain2.astype(jnp.float32), full_shift2.astype(jnp.float32)
    )
    again = (
        lax.all_gather(shards[0], ("dp", "seq"), axis=0, tiled=True),
        lax.all_gather(shards[1], ("dp", "seq"), axis=0, tiled=True),
        lax.all_gather(shards[2], ("dp", "seq"), axis=0, tiled=True),
        lax.all_gather(shards[3], ("dp", "seq"), axis=0, tiled=True),
        lax.all_gather(shards[4], ("dp", "seq"), axis=0, tiled=True),
        lax.all_gather(shards[5], ("dp", "seq"), axis=0, tiled=True),
        lax.all_gather(shards[6], ("dp", "seq"), axis=0, tiled=True),
        lax.all_gather(shards[7], ("dp", "seq"), axis=0, tiled=True),
        lax.all_gather(shards[8], ("dp", "seq"), axis=0, tiled=True),
        lax.all_gather(shards[9], ("dp", "seq"), axis=0, tiled=True),
        lax.all_gather(shards[10], ("dp", "seq"), axis=0, tiled=True),
        lax.all_gather(shards[11], ("dp", "seq"), axis=0, tiled=True),
        lax.all_gather(shards[12], ("dp", "seq"), axis=0, tiled=True),
    )
    back_qkv, back_out, back_gain1, back_up, back_down, back_gain2 = (
        again[0],
        again[3],
        again[5],
        again[7],
        again[9],
        again[11],
    )
    grad_out = cotangent[0].astype(jnp.float32)
    grad_mid, grad_ln2_gain, grad_ln2_shift = norm_backward(
        grad_out, normed_two, inv_two, back_gain2.astype(jnp.float32)
    )
    grad_branch = grad_mid.astype(jnp.bfloat16)
    grad_w_down = outer_sum(gelu_low, grad_branch)
    grad_down_bias = jnp.sum(grad_branch.astype(jnp.float32), axis=0)
    grad_gelu = times_back(grad_branch, back_down)
    grad_up = jax.vjp(gelu_exact, up_act)[1](grad_gelu)[0].astype(jnp.bfloat16)
    grad_w_up = outer_sum(hidden_low, grad_up)
    grad_up_bias = jnp.sum(grad_up.astype(jnp.float32), axis=0)
    grad_hidden = times_back(grad_up, back_up) + grad_mid
    grad_first, grad_ln1_gain, grad_ln1_shift = norm_backward(
        grad_hidden, normed_one, inv_one, back_gain1.astype(jnp.float32)
    )
    grad_attn = grad_first.astype(jnp.bfloat16)
    grad_w_out = outer_sum(context_rows, grad_attn)
    grad_out_bias = jnp.sum(grad_attn.astype(jnp.float32), axis=0)
    grad_context = times_back(grad_attn, back_out).astype(jnp.bfloat16)
    grad_ctx_heads = lax.all_to_all(
        to_heads(grad_context, groups), "seq", split_axis=0, concat_axis=0, tiled=True
    )
    grad_ctx_blocks = grad_ctx_heads.reshape(nblocks, qrows, local_heads, head_dim)

    def attend_backward(carry, inputs):
        key_total, value_total = carry
        query, grad_ctx, log_rows = inputs
        scores = masked_scores(query)
        probs = jnp.exp(scores - log_rows[..., None])
        probs_low = probs.astype(jnp.bfloat16)
        d_probs = jnp.einsum(
            "qhd,khd->hqk", grad_ctx, value_heads, preferred_element_type=jnp.float32
        )
        centre = jnp.sum(probs * d_probs, axis=-1, keepdims=True)
        grad_scores = (probs * (d_probs - centre)).astype(jnp.bfloat16)
        grad_query = (
            jnp.einsum("hqk,khd->qhd", grad_scores, key_heads, preferred_element_type=jnp.float32)
            * scale
        )
        key_total = (
            key_total
            + jnp.einsum("hqk,qhd->khd", grad_scores, query, preferred_element_type=jnp.float32)
            * scale
        )
        value_total = value_total + jnp.einsum(
            "hqk,qhd->khd", probs_low, grad_ctx, preferred_element_type=jnp.float32
        )
        return ((key_total, value_total), grad_query.astype(jnp.bfloat16))

    empty = jnp.zeros((stream, local_heads, head_dim), jnp.float32)
    (key_total, value_total), grad_query = lax.scan(
        attend_backward, (empty, empty), (query_blocks, grad_ctx_blocks, log_sums)
    )
    grad_key = key_total.astype(jnp.bfloat16)
    grad_value = value_total.astype(jnp.bfloat16)
    grad_pieces = (
        lax.all_to_all(
            grad_query.reshape(groups, -1), "seq", split_axis=0, concat_axis=0, tiled=True
        ),
        lax.all_to_all(
            grad_key.reshape(groups, -1), "seq", split_axis=0, concat_axis=0, tiled=True
        ),
        lax.all_to_all(
            grad_value.reshape(groups, -1), "seq", split_axis=0, concat_axis=0, tiled=True
        ),
    )
    grad_project = jnp.concatenate(
        [
            from_heads(grad_pieces[0], part_width),
            from_heads(grad_pieces[1], part_width),
            from_heads(grad_pieces[2], part_width),
        ],
        axis=1,
    )
    grad_w_qkv = outer_sum(rows, grad_project)
    bias_sums = jnp.sum(grad_project.astype(jnp.float32), axis=0)
    grad_q_bias = bias_sums[:width]
    grad_v_bias = bias_sums[2 * width :]
    grad_rows = times_back(grad_project, back_qkv) + grad_first
    terms = (
        grad_w_qkv,
        grad_q_bias,
        grad_v_bias,
        grad_w_out,
        grad_out_bias,
        grad_ln1_gain,
        grad_ln1_shift,
        grad_w_up,
        grad_up_bias,
        grad_w_down,
        grad_down_bias,
        grad_ln2_gain,
        grad_ln2_shift,
    )
    page_sums = (
        lax.psum_scatter(
            terms[0].astype(jnp.bfloat16), "dp", scatter_dimension=0, tiled=True
        ).astype(jnp.float32),
        lax.psum_scatter(
            terms[1].astype(jnp.bfloat16), "dp", scatter_dimension=0, tiled=True
        ).astype(jnp.float32),
        lax.psum_scatter(
            terms[2].astype(jnp.bfloat16), "dp", scatter_dimension=0, tiled=True
        ).astype(jnp.float32),
        lax.psum_scatter(
            terms[3].astype(jnp.bfloat16), "dp", scatter_dimension=0, tiled=True
        ).astype(jnp.float32),
        lax.psum_scatter(
            terms[4].astype(jnp.bfloat16), "dp", scatter_dimension=0, tiled=True
        ).astype(jnp.float32),
        lax.psum_scatter(
            terms[5].astype(jnp.bfloat16), "dp", scatter_dimension=0, tiled=True
        ).astype(jnp.float32),
        lax.psum_scatter(
            terms[6].astype(jnp.bfloat16), "dp", scatter_dimension=0, tiled=True
        ).astype(jnp.float32),
        lax.psum_scatter(
            terms[7].astype(jnp.bfloat16), "dp", scatter_dimension=0, tiled=True
        ).astype(jnp.float32),
        lax.psum_scatter(
            terms[8].astype(jnp.bfloat16), "dp", scatter_dimension=0, tiled=True
        ).astype(jnp.float32),
        lax.psum_scatter(
            terms[9].astype(jnp.bfloat16), "dp", scatter_dimension=0, tiled=True
        ).astype(jnp.float32),
        lax.psum_scatter(
            terms[10].astype(jnp.bfloat16), "dp", scatter_dimension=0, tiled=True
        ).astype(jnp.float32),
        lax.psum_scatter(
            terms[11].astype(jnp.bfloat16), "dp", scatter_dimension=0, tiled=True
        ).astype(jnp.float32),
        lax.psum_scatter(
            terms[12].astype(jnp.bfloat16), "dp", scatter_dimension=0, tiled=True
        ).astype(jnp.float32),
    )
    sums = (
        lax.psum_scatter(
            page_sums[0].astype(jnp.bfloat16), "seq", scatter_dimension=0, tiled=True
        ).astype(jnp.float32),
        lax.psum_scatter(
            page_sums[1].astype(jnp.bfloat16), "seq", scatter_dimension=0, tiled=True
        ).astype(jnp.float32),
        lax.psum_scatter(
            page_sums[2].astype(jnp.bfloat16), "seq", scatter_dimension=0, tiled=True
        ).astype(jnp.float32),
        lax.psum_scatter(
            page_sums[3].astype(jnp.bfloat16), "seq", scatter_dimension=0, tiled=True
        ).astype(jnp.float32),
        lax.psum_scatter(
            page_sums[4].astype(jnp.bfloat16), "seq", scatter_dimension=0, tiled=True
        ).astype(jnp.float32),
        lax.psum_scatter(
            page_sums[5].astype(jnp.bfloat16), "seq", scatter_dimension=0, tiled=True
        ).astype(jnp.float32),
        lax.psum_scatter(
            page_sums[6].astype(jnp.bfloat16), "seq", scatter_dimension=0, tiled=True
        ).astype(jnp.float32),
        lax.psum_scatter(
            page_sums[7].astype(jnp.bfloat16), "seq", scatter_dimension=0, tiled=True
        ).astype(jnp.float32),
        lax.psum_scatter(
            page_sums[8].astype(jnp.bfloat16), "seq", scatter_dimension=0, tiled=True
        ).astype(jnp.float32),
        lax.psum_scatter(
            page_sums[9].astype(jnp.bfloat16), "seq", scatter_dimension=0, tiled=True
        ).astype(jnp.float32),
        lax.psum_scatter(
            page_sums[10].astype(jnp.bfloat16), "seq", scatter_dimension=0, tiled=True
        ).astype(jnp.float32),
        lax.psum_scatter(
            page_sums[11].astype(jnp.bfloat16), "seq", scatter_dimension=0, tiled=True
        ).astype(jnp.float32),
        lax.psum_scatter(
            page_sums[12].astype(jnp.bfloat16), "seq", scatter_dimension=0, tiled=True
        ).astype(jnp.float32),
    )
    return (
        output.astype(jnp.bfloat16)[None],
        grad_rows.astype(jnp.bfloat16)[None],
        sums[0],
        sums[1],
        sums[2],
        sums[3],
        sums[4],
        sums[5],
        sums[6],
        sums[7],
        sums[8],
        sums[9],
        sums[10],
        sums[11],
        sums[12],
    )


MESH = pl.DeviceIdType.MESH
CHUNK = 256
MASKED = -1e30
FLAT = (((1,), (1,)), ((), ()))


def flip(index, mask):
    for b in range(mask.bit_length()):
        if mask >> b & 1:
            bit = 1 << b
            index = index + bit - 2 * bit * (index // bit % 2)
    return index


def guarded(when, action):
    if when is None:
        action()
    else:
        pl.when(when)(action)


class Wires:
    def __init__(self, sems, sizes):
        self.sems, self.sizes = sems, sizes
        self.dp, self.z = lax.axis_index("dp"), lax.axis_index("seq")
        self.dps = [flip(self.dp, m) for m in range(sizes[0])]
        self.zs = [flip(self.z, m) for m in range(sizes[1])]
        last = sizes[1] - 1
        half = self.z // 2
        step = 1 - 2 * half
        depth = self.z * step + last * half
        self.inner, self.outer = depth == 1, depth == 0
        self.right = self.z + step
        self.left = self.z - step * depth
        self.far = [self.z] + [t * step + last * half for t in (1 - depth, 2, 3)]
        self.started = []

    def peer(self, offset, step):
        return (self.dps[offset], self.zs[step])

    def send(self, src, dst, recv_sem, device, when=None):
        copy = pltpu.make_async_remote_copy(
            src_ref=src,
            dst_ref=dst,
            send_sem=self.sems.at[len(self.started)],
            recv_sem=recv_sem,
            device_id=device,
            device_id_type=MESH,
        )
        guarded(when, copy.start)
        self.started.append((copy, when))
        return len(self.started) - 1

    def sent(self, index):
        copy, when = self.started[index]
        guarded(when, copy.wait_send)
        self.started[index] = None

    def arrived(self, dst, recv_sem, when=None):
        copy = pltpu.make_async_remote_copy(
            src_ref=dst,
            dst_ref=dst,
            send_sem=self.sems.at[0],
            recv_sem=recv_sem,
            device_id=self.peer(1, 0),
            device_id_type=MESH,
        )
        guarded(when, copy.wait_recv)

    def drain(self):
        for index, entry in enumerate(self.started):
            if entry is not None:
                self.sent(index)

    def greet(self):
        n_dp, n_seq = self.sizes
        barrier = pltpu.get_barrier_semaphore()
        masks = [1 << b for b in range(n_dp.bit_length() - 1)]
        partners = [self.peer(m, 0) for m in masks] + [self.peer(0, i) for i in range(1, n_seq)]
        for device in partners:
            pl.semaphore_signal(barrier, inc=1, device_id=device, device_id_type=MESH)
        pl.semaphore_wait(barrier, len(partners))


class Line:
    def __init__(self, wires, slot, recv):
        self.w, self.slot, self.recv = wires, slot, recv

    def pass_on(self, k, src, to_left):
        w = self.w
        s = w.far[k]
        dst = self.slot(s)
        if to_left:
            w.send(src, dst, self.recv.at[s], (w.dp, w.left), w.inner)
        else:
            w.send(src, dst, self.recv.at[s], (w.dp, w.right), None if k == 0 else w.inner)

    def own(self, src):
        self.pass_on(0, src, False)
        self.pass_on(0, src, True)

    def take(self, k):
        s = self.w.far[k]
        self.w.arrived(self.slot(s), self.recv.at[s])
        self.pass_on(k, self.slot(s), k > 1)


class Gather:
    def __init__(self, wires, src, full, recv, local):
        self.w, self.src, self.full, self.recv, self.local = wires, src, full, recv, local
        n_dp, self.n_seq = wires.sizes
        self.chips = [1 << b for b in range(1, n_dp.bit_length() - 1)]
        self.slots = wires.far
        self.line = Line(wires, lambda s: full.at[wires.dp * self.n_seq + s], recv.at[0])

    def at(self, offset, step):
        return self.full.at[self.w.dps[offset] * self.n_seq + self.slots[step]]

    def order(self, step):
        return self.chips if step % 2 == 0 else self.chips[::-1]

    def forward(self, src, offset, step, masks):
        for m in masks:
            sem = self.recv.at[offset ^ m, self.slots[step]]
            self.w.send(src, self.at(offset, step), sem, self.w.peer(m, 0))

    def wait(self, offset, step):
        self.w.arrived(self.at(offset, step), self.recv.at[offset, self.slots[step]])

    def mine(self):
        return self.src

    def own_chips(self):
        self.kept = pltpu.make_async_copy(self.mine(), self.at(0, 0), self.local)
        self.kept.start()
        self.forward(self.mine(), 0, 0, self.order(0) + [1])

    def own_seq(self):
        self.line.own(self.src)

    def along_seq(self, i):
        self.line.take(i)
        self.forward(self.at(0, i), 0, i, self.order(i) + [1])

    def stages(self, step):
        have, out = [0], []
        masks = self.order(step)
        for t, m in enumerate(masks):
            out.append([(o ^ m, masks[t + 1 :] + [1]) for o in have])
            have = have + [o ^ m for o in have]
        return out

    def over_chips(self, t, step):
        for offset, masks in self.stages(step)[t]:
            self.wait(offset, step)
            self.forward(self.at(offset, step), offset, step, masks)

    def over_cores(self):
        n_dp = self.w.sizes[0]
        for offset in range(1, n_dp, 2):
            for i in range(self.n_seq):
                self.wait(offset, i)
        self.kept.wait()

    def seq_steps(self):
        return [lambda i=i: self.along_seq(i) for i in range(1, self.n_seq)]

    def chip_steps(self, t):
        return [lambda i=i: self.over_chips(t, i) for i in range(self.n_seq)]


class GatherColumns(Gather):
    def __init__(self, *args):
        super().__init__(*args)
        self.slots = self.w.zs

    def mine(self):
        return self.src.at[self.w.z]

    def own_seq(self):
        for i in range(1, self.n_seq):
            sem = self.recv.at[0, self.w.z]
            self.w.send(self.src.at[self.w.zs[i]], self.at(0, 0), sem, self.w.peer(0, i))

    def along_seq(self, i):
        self.wait(0, i)
        self.forward(self.at(0, i), 0, i, self.order(i) + [1])


def sends_of_gather(n_dp, n_seq):
    return 2 + n_seq - 1 + n_seq * (n_dp - 1)


def group_lanes(packed, row, group, n_seq):
    total = packed[group * n_seq, row : row + 1, :]
    for s in range(1, n_seq):
        total = total + packed[group * n_seq + s, row : row + 1, :]
    return total


def spread_head(source, h, head_dim, factor):
    n_seq, rows, _ = source.shape
    block = h * head_dim // 128 * 128
    low = h * head_dim % 128
    lane = lax.broadcasted_iota(jnp.int32, (n_seq * rows, 128), 1)
    values = source[:, :, block : block + 128].reshape(n_seq * rows, 128).astype(jnp.float32)
    kept = jnp.where((lane >= low) & (lane < low + head_dim), values * factor, 0.0)
    return kept.astype(jnp.bfloat16).reshape(n_seq, rows, 128)


def front_kernel(
    sizes,
    heads,
    valid_ref,
    x_ref,
    cotangent,
    vec_ref,
    qkv_ref,
    out_ref,
    up_ref,
    down_ref,
    columns_out,
    full_out,
    full_up,
    full_down,
    page_out,
    query_out,
    key_out,
    value_out,
    key_turned_out,
    context_out,
    logs_out,
    hidden_out,
    gelu_out,
    slope_out,
    output,
    normed_one,
    inv_one,
    grad_mid,
    sums_out,
    packed,
    columns,
    page,
    held,
    context_sent,
    context_held,
    context_turned,
    value_turned,
    masked_query,
    keys,
    values,
    key_turned,
    logs,
    out_matrix,
    up_matrix,
    down_matrix,
    page_turned,
    context_rows_turned,
    hidden,
    hidden_low,
    hidden_turned,
    gelu_low,
    gelu_turned,
    slopes,
    branch,
    send_sems,
    gather_sems,
    page_sems,
    context_sems,
    local_sems,
):
    n_dp, n_seq = sizes
    w = Wires(send_sems, sizes)
    rows, width = x_ref.shape
    part = width // n_seq
    head_dim = width // heads
    local_heads = heads // n_seq
    stream = rows * n_seq
    w.greet()
    line = Line(w, lambda s: page.at[s], page_sems)
    line.own(x_ref)
    sources = (
        (vec_ref, packed),
        (qkv_ref, columns),
        (out_ref, out_matrix),
        (up_ref, up_matrix),
        (down_ref, down_matrix),
    )
    vec, qkv, out, up, down = [
        (GatherColumns if k == 1 else Gather)(w, src, dst, gather_sems.at[k], local_sems.at[k])
        for k, (src, dst) in enumerate(sources)
    ]
    queue = []

    def pump(count):
        for _ in range(min(count, len(queue))):
            queue.pop(0)()

    def run(steps):
        for step in steps:
            step()

    for unit in (qkv, vec):
        unit.own_seq()
        unit.own_chips()
    out.own_chips()
    up.own_chips()
    page[w.z] = x_ref[...]
    for unit in (qkv, vec):
        run(unit.seq_steps())
    line.take(1)
    out.own_seq()
    for unit in (qkv, vec):
        run(unit.chip_steps(0))
    for unit in (qkv, vec):
        run(unit.chip_steps(1))
    line.take(2)
    up.own_seq()
    qkv.over_cores()
    vec.over_cores()
    keeps = []

    def keep(src, dst):
        keeps.append(pltpu.make_async_copy(src, dst, local_sems.at[5 + len(keeps)]))
        keeps[-1].start()

    keep(columns, columns_out)
    groups = part // 128
    biases = [
        jnp.concatenate([group_lanes(packed, b, w.z * groups + g, n_seq) for g in range(groups)], axis=1)
        for b in range(2)
    ]
    matrix = columns[...].reshape(width, 3 * part)

    def project(s):
        piece = jnp.dot(page[s], matrix, preferred_element_type=jnp.float32)
        for t in range(3):
            third = piece[:, t * part : (t + 1) * part]
            if t != 1:
                third = third + biases[t // 2]
            held[t, s] = third.astype(jnp.bfloat16)

    project(w.z)
    project(w.far[1])
    run(out.seq_steps())
    down.own_chips()
    project(w.far[2])
    line.take(3)
    project(w.far[3])
    per_block = 128 // head_dim
    scale = 1.0 / math.sqrt(head_dim)
    position = lax.broadcasted_iota(jnp.int32, (stream, 128), 0)
    lane = lax.broadcasted_iota(jnp.int32, (stream, 128), 1)
    guard = jnp.where((position >= valid_ref[0]) & (lane == 0), MASKED, 0.0).astype(jnp.bfloat16)
    for h in range(local_heads):
        masked_query[h] = spread_head(held.at[0], h, head_dim, scale)
    for b in range(local_heads // per_block):
        lanes = slice(b * 128, (b + 1) * 128)
        keys[b, :, :128] = held[1, :, :, lanes].reshape(stream, 128)
        keys[b, :, 128:] = guard
        values[b] = held[2, :, :, lanes].reshape(stream, 128)
    turned = held[1].reshape(stream, part).T
    for h in range(local_heads):
        key_turned[h] = turned[h * head_dim : (h + 1) * head_dim, :]
    value_turned[...] = held[2].reshape(stream, part).T
    keep(masked_query, query_out)
    keep(keys, key_out)
    keep(values, value_out)
    keep(key_turned, key_turned_out)
    one_lane = lax.broadcasted_iota(jnp.int32, (rows, 128), 1)
    ones = jnp.where(one_lane == 0, 1.0, 0.0).astype(jnp.bfloat16)
    queue += up.seq_steps()[:1] + out.chip_steps(0) + up.seq_steps()[1:] + [down.own_seq]
    queue += out.chip_steps(1) + up.chip_steps(0) + down.seq_steps()
    counts = (2, 4, 3, 5)
    for h in range(local_heads):

        def attend(c, _, h=h):
            query = jnp.concatenate([masked_query[h, c], ones], axis=1)
            scores = lax.dot_general(
                keys[h // per_block], query, FLAT, preferred_element_type=jnp.float32
            )
            peak = jnp.max(scores, axis=0, keepdims=True)
            raised = jnp.exp(scores - peak)
            total = jnp.sum(raised, axis=0, keepdims=True)
            mixed = jnp.dot(
                value_turned[h * head_dim : (h + 1) * head_dim, :],
                raised.astype(jnp.bfloat16),
                preferred_element_type=jnp.float32,
            )
            context_turned[c, h * head_dim : (h + 1) * head_dim, :] = mixed / total
            logs[c, h : h + 1, :] = peak + jnp.log(total)
            return 0

        lax.fori_loop(0, n_seq, attend, 0)
        pump(counts[h])
    for j in range(n_seq):
        context_sent[j] = context_turned[j].T.astype(jnp.bfloat16)
    for i in range(1, n_seq):
        w.send(context_sent.at[w.zs[i]], context_held.at[w.z], context_sems.at[i], w.peer(0, i))
    context_held[w.z] = context_sent[w.z]
    keep(logs, logs_out)
    for s in range(n_seq):
        page_turned[s * width : (s + 1) * width, :] = page[s].T
    keep(page_turned, page_out)
    pump(len(queue))
    out.over_cores()
    keep(out_matrix, full_out)

    def line_of(row):
        return jnp.concatenate([group_lanes(packed, row, d, n_seq) for d in range(n_dp)], axis=1)

    for i in range(1, n_seq):
        w.arrived(context_held.at[w.zs[i]], context_sems.at[i])
    total = x_ref[...].astype(jnp.float32) + line_of(2)
    per_part = part // out_matrix.shape[1]
    for j in range(n_seq):
        block = out_matrix[j * per_part : (j + 1) * per_part].reshape(part, width)
        total = total + jnp.dot(context_held[j], block, preferred_element_type=jnp.float32)
        context_rows_turned[j * part : (j + 1) * part, :] = context_held[j].T
    keep(context_rows_turned, context_out)
    gain_one = line_of(3)
    rows_hidden, normed, inv = norm_forward(total, gain_one, line_of(4))
    normed_one[...] = normed
    inv_one[...] = jnp.broadcast_to(inv, inv_one.shape)
    hidden[...] = rows_hidden
    hidden_low[...] = rows_hidden.astype(jnp.bfloat16)
    hidden_turned[...] = rows_hidden.T.astype(jnp.bfloat16)
    keep(hidden_turned, hidden_out)
    run(up.chip_steps(1))
    run(down.chip_steps(0))
    up.over_cores()
    for b in range(up_matrix.shape[2] // width):
        keep(up_matrix.at[:, :, pl.ds(b * width, width)], full_up.at[b])
    run(down.chip_steps(1))
    chunk = 512
    chunks = up_matrix.shape[2] // chunk
    per_chunk = chunk // down_matrix.shape[1]

    def activate(f, _):
        at = pl.ds(pl.multiple_of(f * chunk, chunk), chunk)
        block = up_matrix[:, :, at].reshape(width, chunk)
        up_bias = jnp.concatenate(
            [packed[f * per_chunk + e, 8:9, :] for e in range(per_chunk)], axis=1
        )
        act = jnp.dot(hidden_low[...], block, preferred_element_type=jnp.float32) + up_bias
        below = 0.5 + 0.5 * lax.erf(act * math.sqrt(0.5))
        gelu = act * below
        gelu_low[:, at] = gelu.astype(jnp.bfloat16)
        gelu_turned[at, :] = gelu.T.astype(jnp.bfloat16)
        bell = jnp.exp(-0.5 * act * act) * (1.0 / math.sqrt(2.0 * math.pi))
        slopes[:, at] = (below + act * bell).astype(jnp.bfloat16)
        return 0

    lax.fori_loop(0, chunks, activate, 0)
    keep(gelu_turned, gelu_out)
    keep(slopes, slope_out)
    down.over_cores()
    keep(down_matrix, full_down)
    branch[...] = hidden[...] + line_of(5)

    def shrink(f, _):
        at = pl.ds(pl.multiple_of(f * chunk, chunk), chunk)
        block = down_matrix[pl.ds(f * per_chunk, per_chunk)].reshape(chunk, width)
        branch[...] += jnp.dot(gelu_low[:, at], block, preferred_element_type=jnp.float32)
        return 0

    lax.fori_loop(0, chunks, shrink, 0)
    gain_two = line_of(6)
    result, normed, inv = norm_forward(branch[...], gain_two, line_of(7))
    output[...] = result.astype(jnp.bfloat16)
    grad = cotangent[...].astype(jnp.float32)
    mid, grad_gain, grad_shift = norm_backward(grad, normed, inv, gain_two)
    grad_mid[...] = mid
    grad_bias = jnp.sum(mid.astype(jnp.bfloat16).astype(jnp.float32), axis=0)
    sums_out[...] = jnp.zeros_like(sums_out)
    for row, line_sum in enumerate((grad_bias, grad_gain, grad_shift)):
        sums_out[5 + row : 6 + row, :] = line_sum.reshape(1, width)
    sums_out[3:4, :] = gain_one
    for copy in keeps:
        copy.wait()
    w.drain()


def front(sizes, heads, valid, rows, cotangent, vec, w_columns, w_out, w_up, w_down):
    n_dp, n_seq = sizes
    devices = n_dp * n_seq
    count, width = rows.shape
    part = width // n_seq
    stream = count * n_seq
    wide = w_up.shape[1]
    low = jnp.bfloat16
    head_dim = width // heads
    local_heads = heads // n_seq
    blocks = part // 128
    attention = (
        jax.ShapeDtypeStruct((local_heads, n_seq, count, 128), low),
        jax.ShapeDtypeStruct((blocks, stream, 256), low),
        jax.ShapeDtypeStruct((blocks, stream, 128), low),
        jax.ShapeDtypeStruct((local_heads, head_dim, stream), low),
    )

    def full(shard):
        return jax.ShapeDtypeStruct((devices,) + shard.shape, shard.dtype)

    anywhere = pl.BlockSpec(memory_space=pl.ANY)
    local = pl.BlockSpec(memory_space=pltpu.VMEM)
    sends = 5 * sends_of_gather(n_dp, n_seq) + 5 + n_seq - 1
    return pl.pallas_call(
        lambda *refs: front_kernel(sizes, heads, *refs),
        out_shape=(
            jax.ShapeDtypeStruct((devices,) + w_columns.shape[1:], low),
            full(w_out),
            jax.ShapeDtypeStruct((wide // width, devices, w_up.shape[0], width), low),
            full(w_down),
            jax.ShapeDtypeStruct((n_seq * width, count), low),
        )
        + attention
        + (
            jax.ShapeDtypeStruct((width, count), low),
            jax.ShapeDtypeStruct((n_seq, 8, count), jnp.float32),
            jax.ShapeDtypeStruct((width, count), low),
            jax.ShapeDtypeStruct((wide, count), low),
            jax.ShapeDtypeStruct((count, wide), low),
            jax.ShapeDtypeStruct((count, width), low),
            jax.ShapeDtypeStruct((count, width), jnp.float32),
            jax.ShapeDtypeStruct((count, 128), jnp.float32),
            jax.ShapeDtypeStruct((count, width), jnp.float32),
            jax.ShapeDtypeStruct((8, width), jnp.float32),
        ),
        in_specs=[
            pl.BlockSpec(memory_space=pltpu.SMEM),
            local,
            local,
        ]
        + [anywhere] * 5,
        out_specs=[anywhere] * 14 + [local] * 5,
        scratch_shapes=[
            pltpu.VMEM((devices,) + vec.shape, jnp.float32),
            pltpu.VMEM((devices,) + w_columns.shape[1:], low),
            pltpu.VMEM((n_seq, count, width), low),
            pltpu.VMEM((3, n_seq, count, part), low),
            pltpu.VMEM((n_seq, count, part), low),
            pltpu.VMEM((n_seq, count, part), low),
            pltpu.VMEM((n_seq, part, count), jnp.float32),
            pltpu.VMEM((part, stream), low),
        ]
        + [pltpu.VMEM(a.shape, a.dtype) for a in attention]
        + [
            pltpu.VMEM((n_seq, 8, count), jnp.float32),
            pltpu.VMEM((devices,) + w_out.shape, low),
            pltpu.VMEM((devices,) + w_up.shape, low),
            pltpu.VMEM((devices,) + w_down.shape, low),
            pltpu.VMEM((n_seq * width, count), low),
            pltpu.VMEM((width, count), low),
            pltpu.VMEM((count, width), jnp.float32),
            pltpu.VMEM((count, width), low),
            pltpu.VMEM((width, count), low),
            pltpu.VMEM((count, wide), low),
            pltpu.VMEM((wide, count), low),
            pltpu.VMEM((count, wide), low),
            pltpu.VMEM((count, width), jnp.float32),
            pltpu.SemaphoreType.DMA((sends,)),
            pltpu.SemaphoreType.DMA((5, n_dp, n_seq)),
            pltpu.SemaphoreType.DMA((n_seq,)),
            pltpu.SemaphoreType.DMA((n_seq,)),
            pltpu.SemaphoreType.DMA((24,)),
        ],
        compiler_params=pltpu.CompilerParams(
            collective_id=0, has_side_effects=True, vmem_limit_bytes=60 * 2**20
        ),
        name="front",
    )(valid, rows, cotangent, vec, w_columns, w_out, w_up, w_down)


def add_rows(into, term):
    rows = into.shape[0]
    step = min(16, rows)

    def body(r, _):
        at = pl.ds(pl.multiple_of(r * step, step), step)
        total = into[at, :].astype(jnp.float32) + term[at, :].astype(jnp.float32)
        into[at, :] = total.astype(into.dtype)
        return 0

    lax.fori_loop(0, rows // step, body, 0)


class LineSum:
    def __init__(self, wires, block, last, sems):
        self.w, self.block, self.last, self.sems = wires, block, last, sems

    def into(self, src, index, device, when):
        self.w.send(src, self.last.at[index], self.sems.at[index], device, when)

    def add(self, k, index):
        def action():
            self.w.arrived(self.last.at[index], self.sems.at[index])
            add_rows(self.block(k), self.last.at[index])

        pl.when(self.w.inner)(action)

    def offer(self, k):
        self.into(self.block(k), k - 1, (self.w.dp, self.w.right), self.w.outer)

    def relay(self, k):
        w, block = self.w, self.block(k)
        if k == 1:
            self.add(1, 4)
            self.into(block, 3, (w.dp, w.left), w.inner)
        else:
            self.add(k, k - 1)
            self.into(block, 3 if k == 2 else 4, (w.dp, w.right), w.inner)

    def finish(self, start, out):
        w = self.w
        w.arrived(self.last.at[3], self.sems.at[3])
        w.arrived(self.last.at[0], self.sems.at[0], w.inner)
        rows = out.shape[0]
        step = min(16, rows)

        def total_of(count):
            def body(r, _):
                at = pl.ds(pl.multiple_of(r * step, step), step)
                total = start(at) + self.last[3, at, :].astype(jnp.float32)
                if count == 2:
                    total = total + self.last[0, at, :].astype(jnp.float32)
                out[at, :] = total.astype(out.dtype)
                return 0

            lax.fori_loop(0, rows // step, body, 0)

        pl.when(w.inner)(lambda: total_of(2))
        pl.when(w.outer)(lambda: total_of(1))


class Scatter:
    def __init__(self, wires, kind, make, source, stage, bufs, sems, out):
        self.w, self.kind, self.make, self.source, self.stage = wires, kind, make, source, stage
        self.total, self.first, self.second, self.last = bufs
        self.core_sems, self.first_sems, self.second_sems, self.last_sems = sems
        self.out = out
        self.n_seq = wires.sizes[1]
        self.offsets = [6, 2, 4, 0]
        self.staged = {}
        self.slots = wires.far if kind == "line" else wires.zs
        self.line = LineSum(wires, lambda k: self.total.at[0, self.slots[k]], self.last, self.last_sems)

    def order(self, step):
        return (2, 4) if step % 2 == 0 else (4, 2)

    def give(self, k):
        o = self.offsets[k]
        d = self.w.dps[o ^ 1]
        if self.stage is None:
            src = self.source.at[pl.ds(d * self.n_seq, self.n_seq)]
        else:
            depth = self.stage.shape[0]
            if k >= depth:
                self.w.sent(self.staged[k - depth])
            src = self.stage.at[k % depth]

            def fill(s, _):
                src[s] = self.make(d, s).astype(src.dtype)
                return 0

            lax.fori_loop(0, self.n_seq, fill, 0)
        sem = self.core_sems.at[o // 2]
        self.staged[k] = self.w.send(src, self.total.at[o // 2], sem, self.w.peer(1, 0))

    def give_steps(self):
        return [lambda k=k: self.give(k) for k in range(4)]

    def over_cores(self, k):
        o = self.offsets[k]
        d = self.w.dps[o]
        self.w.arrived(self.total.at[o // 2], self.core_sems.at[o // 2])

        def add(s, _):
            block = self.total.at[o // 2, s]
            block[...] = (block[...].astype(jnp.float32) + self.make(d, s)).astype(block.dtype)
            return 0

        lax.fori_loop(0, self.n_seq, add, 0)
        for i in range(self.n_seq):
            mask = self.order(i)[0]
            block = self.total.at[o // 2, self.slots[i]]
            if o & mask:
                keep = (o ^ mask) // (6 ^ mask)
                self.w.send(block, self.first.at[i, keep], self.first_sems.at[i, keep], self.w.peer(mask, 0))

    def over_chips(self, i):
        mask = self.order(i)[1]
        for keep in (1, 0):
            o = mask * keep
            block = self.total.at[o // 2, self.slots[i]]
            self.w.arrived(self.first.at[i, keep], self.first_sems.at[i, keep])
            add_rows(block, self.first.at[i, keep])
            if keep:
                self.w.send(block, self.second.at[i], self.second_sems.at[i], self.w.peer(mask, 0))

    def to_seq(self, i):
        block = self.total.at[0, self.slots[i]]
        self.w.arrived(self.second.at[i], self.second_sems.at[i])
        add_rows(block, self.second.at[i])
        if self.kind == "line":
            if i:
                self.line.offer(i)
                self.line.relay(i)
        elif i:
            self.w.send(block, self.last.at[i], self.last_sems.at[i], self.w.peer(0, i))

    def finish(self):
        block = self.total.at[0, self.w.z]
        if self.kind == "line":
            self.line.finish(lambda at: block[at, :].astype(jnp.float32), self.out)
            return
        self.out[self.w.z] = block[...].astype(jnp.float32)
        for i in range(1, self.n_seq):
            self.w.arrived(self.last.at[i], self.last_sems.at[i])
            self.out[self.w.zs[i]] = self.last[i].astype(jnp.float32)

    def core_steps(self):
        return [lambda k=k: self.over_cores(k) for k in range(4)]

    def chip_steps(self):
        return [lambda i=i: self.over_chips(i) for i in range(self.n_seq)]

    def seq_steps(self):
        return [lambda i=i: self.to_seq(i) for i in (3, 2, 1, 0)]


def back_kernel(sizes, heads, *refs):
    n_dp, n_seq = sizes
    (
        mid_in,
        normed_in,
        inv_in,
        sums_in,
        logs,
        page_in,
        query_in,
        key_in,
        value_in,
        key_turned_in,
        context_in,
        hidden_in,
        gelu_in,
        slope_in,
        columns_in,
        out_in,
        up_in,
        down_in,
        grad_rows,
        *outs,
    ) = refs[:24]
    scratch = list(refs[24:])

    def take(count):
        got = scratch[:count]
        del scratch[:count]
        return got

    send_sems, core_sems, first_sems, second_sems, last_sems, block_sems = take(6)
    head_sems, local_sems, row_sems = take(3)
    grads, masked_query, keys, values, key_turned, masked_grad = take(6)
    query_grad, key_grad, value_grad = take(3)
    project, turned, columns, vec = take(4)
    row_terms, row_last, own_rows, partial = take(4)
    hidden_turned, context_turned, slopes, normed = take(4)
    grad_low, grad_sent, out_matrix, down_blocks, up_blocks = take(5)
    down_stage, up_stage, out_stage = take(3)
    units = [take(4) for k in range(5)]
    w = Wires(send_sems, sizes)
    rows, width = normed.shape
    part = width // n_seq
    wide = slopes.shape[1]
    head_dim = width // heads
    local_heads = heads // n_seq
    stream = rows * n_seq
    per_block = 128 // head_dim
    scale = 1.0 / math.sqrt(head_dim)
    loads = {}

    def load(name, src, dst):
        loads[name] = pltpu.make_async_copy(src, dst, local_sems.at[len(loads)])
        loads[name].start()

    load("mid", mid_in, own_rows)
    load("gelu", gelu_in, turned)
    load("slope", slope_in, slopes)
    blocks = []
    for f in range(n_dp):
        sem = block_sems.at[0, f % 2]
        blocks.append(pltpu.make_async_copy(down_in.at[pl.ds(f * n_seq, n_seq)], down_blocks.at[f % 2], sem))
    shares = wide // width
    half = up_in.shape[1] // 2
    ups = []
    for e in range(2 * shares):
        src = up_in.at[e % shares, pl.ds(e // shares * half, half)]
        ups.append(pltpu.make_async_copy(src, up_blocks.at[e % 2], block_sems.at[1, e % 2]))
    for e in range(2):
        blocks[e].start()
        ups[e].start()
    load("hidden", hidden_in, hidden_turned)
    load("normed", normed_in, normed)
    load("out", out_in, out_matrix)
    load("context", context_in, context_turned)
    load("columns", columns_in, columns)
    load("query", query_in, masked_query)
    load("key", key_in, keys)
    load("value", value_in, values)
    load("turned", key_turned_in, key_turned)
    w.greet()

    def rows_from(source, first, count):
        return source[pl.ds(pl.multiple_of(first, count), count), :]

    def down_term(d, s):
        left = rows_from(turned, (d * n_seq + s) * outs[0].shape[0], outs[0].shape[0])
        return jnp.dot(left, grad_low[...], preferred_element_type=jnp.float32)

    def up_term(d, s):
        left = rows_from(hidden_turned, (d * n_seq + s) * outs[1].shape[0], outs[1].shape[0])
        return jnp.dot(left, slopes[...], preferred_element_type=jnp.float32)

    def out_term(d, s):
        left = rows_from(context_turned, (d * n_seq + s) * outs[2].shape[0], outs[2].shape[0])
        return jnp.dot(left, grad_low[...], preferred_element_type=jnp.float32)

    def held_term(source):
        return lambda d, s: source[d * n_seq + s].astype(jnp.float32)

    makes = (down_term, up_term, out_term, held_term(partial), held_term(vec))
    stages = (down_stage, up_stage, out_stage, None, None)
    scatters = []
    for k in range(5):
        scatters.append(
            Scatter(
                w,
                "columns" if k == 3 else "line",
                makes[k],
                (None, None, None, partial, vec)[k],
                stages[k],
                units[k],
                (core_sems.at[k], first_sems.at[k], second_sems.at[k], last_sems.at[k]),
                outs[k],
            )
        )
    down, up, out, qkv, small = scatters
    queue = []

    def pump(count):
        for _ in range(min(count, len(queue))):
            queue.pop(0)()

    def run(steps):
        for step in steps:
            step()

    def keep_line(row, line):
        for d in range(n_dp):
            for s in range(n_seq):
                vec[d * n_seq + s, row : row + 1, :] = line[:, d * 128 : (d + 1) * 128]

    loads["mid"].wait()
    grad_low[...] = own_rows[...].astype(jnp.bfloat16)
    loads["gelu"].wait()
    gives = down.give_steps()
    run(gives[:2])
    loads["slope"].wait()
    span = wide // n_dp
    for f in range(n_dp):
        blocks[f].wait()
        grad_gelu = lax.dot_general(
            grad_low[...], down_blocks[f % 2].reshape(span, width), FLAT, preferred_element_type=jnp.float32
        )
        if f + 2 < n_dp:
            blocks[f + 2].start()
        at = slice(f * span, (f + 1) * span)
        slopes[:, at] = (grad_gelu * slopes[:, at].astype(jnp.float32)).astype(jnp.bfloat16)
        if f == 3:
            run(gives[2:3])
        if f == 5:
            run(gives[3:])
    loads["hidden"].wait()
    gives = up.give_steps()
    run(gives[:2])
    run(down.core_steps()[:1])
    for e in range(2 * shares):
        ups[e].wait()
        columns_at = slice(e % shares * width, (e % shares + 1) * width)
        rows_at = slice(e // shares * width // 2, (e // shares + 1) * width // 2)
        own_rows[:, rows_at] += lax.dot_general(
            slopes[:, columns_at],
            up_blocks[e % 2].reshape(width // 2, width),
            FLAT,
            preferred_element_type=jnp.float32,
        )
        if e + 2 < 2 * shares:
            ups[e + 2].start()
        if e == 3:
            run(gives[2:3])
            run(down.core_steps()[1:2])
    run(gives[3:])
    run(down.core_steps()[2:])
    load("page", page_in, turned)
    vec[...] = jnp.zeros_like(vec)
    up_bias = jnp.sum(slopes[...].astype(jnp.float32), axis=0, keepdims=True)
    for d in range(n_dp * n_seq):
        vec[d, 8:9, :] = up_bias[:, d * 128 : (d + 1) * 128]
    loads["normed"].wait()
    first, grad_gain, grad_shift = norm_backward(
        own_rows[...], normed[...], inv_in[:, :1], sums_in[3:4, :]
    )
    own_rows[...] = first
    grad_low[...] = first.astype(jnp.bfloat16)
    keep_line(2, jnp.sum(grad_low[...].astype(jnp.float32), axis=0, keepdims=True))
    keep_line(3, grad_gain.reshape(1, width))
    keep_line(4, grad_shift.reshape(1, width))
    for row in (5, 6, 7):
        keep_line(row, sums_in[row : row + 1, :])
    loads["out"].wait()
    for i in (1, 2, 3, 0):
        j = w.zs[i]
        share = part // out_matrix.shape[1]
        block = out_matrix[pl.ds(j * share, share)].reshape(part, width)
        piece = lax.dot_general(grad_low[...], block, FLAT, preferred_element_type=jnp.float32)
        if i:
            grad_sent[i] = piece.astype(jnp.bfloat16)
            w.send(grad_sent.at[i], grads.at[w.z], head_sems.at[i], w.peer(0, i))
        else:
            grads[w.z] = piece.astype(jnp.bfloat16)
    loads["context"].wait()
    run(out.give_steps())
    run(up.core_steps())
    for name in ("columns", "query", "key", "value", "turned"):
        loads[name].wait()
    key_grad[...] = jnp.zeros_like(key_grad)
    value_grad[...] = jnp.zeros_like(value_grad)
    for i in range(1, n_seq):
        w.arrived(grads.at[w.zs[i]], head_sems.at[i])
    for h in range(local_heads):
        masked_grad[h] = spread_head(grads, h, head_dim, 1.0)
    queue += down.chip_steps() + out.core_steps() + down.seq_steps()[:2] + up.chip_steps()
    queue += down.seq_steps()[2:] + out.chip_steps() + up.seq_steps() + out.seq_steps()
    pump(2)
    ones = jnp.where(lax.broadcasted_iota(jnp.int32, (rows, 128), 1) == 0, 1.0, 0.0).astype(jnp.bfloat16)
    for c in range(n_seq):

        def head(h, _, c=c):
            block = h // per_block
            query, grad = masked_query[h, c], masked_grad[h, c]
            scores = lax.dot_general(
                keys[block], jnp.concatenate([query, ones], axis=1), FLAT, preferred_element_type=jnp.float32
            )
            probs = jnp.exp(scores - logs[c, pl.ds(h, 1), :])
            moved = lax.dot_general(values[block], grad, FLAT, preferred_element_type=jnp.float32)
            centre = jnp.sum(probs * moved, axis=0, keepdims=True)
            slope = (probs * (moved - centre)).astype(jnp.bfloat16)
            query_grad[h] = jnp.dot(key_turned[h], slope, preferred_element_type=jnp.float32) * scale
            key_grad[block] += jnp.dot(slope, query, preferred_element_type=jnp.float32)
            value_grad[block] += jnp.dot(
                probs.astype(jnp.bfloat16), grad, preferred_element_type=jnp.float32
            )
            return 0

        lax.fori_loop(0, local_heads, head, 0)
        project[c * rows : (c + 1) * rows, :part] = (
            query_grad[...].reshape(part, rows).T.astype(jnp.bfloat16)
        )
        pump(4)
    for t, total in ((1, key_grad), (2, value_grad)):
        for b in range(local_heads // per_block):
            at = t * part + b * 128
            project[:, at : at + 128] = total[b].astype(jnp.bfloat16)
    matrix = columns[...].reshape(width, 3 * part)
    row_sum = LineSum(w, lambda k: row_terms.at[k - 1], row_last, row_sems)

    def row_term(k):
        return lax.dot_general(
            rows_from(project, w.far[k] * rows, rows), matrix, FLAT, preferred_element_type=jnp.float32
        )

    for k in (3, 2, 1):
        row_terms[k - 1] = row_term(k).astype(jnp.bfloat16)
        row_sum.offer(k)
    loads["page"].wait()
    for t in range(3):
        at = slice(t * part, (t + 1) * part)
        block = jnp.dot(turned[:width, :], project[:rows, at], preferred_element_type=jnp.float32)
        for s in range(1, n_seq):
            block = block + jnp.dot(
                turned[s * width : (s + 1) * width, :],
                project[s * rows : (s + 1) * rows, at],
                preferred_element_type=jnp.float32,
            )
        partial[:, :, at] = block.astype(jnp.bfloat16).reshape(n_dp * n_seq, -1, part)
    run(qkv.give_steps())
    groups = part // 128
    for b, t in ((0, 0), (1, 2)):
        sums = jnp.sum(project[:, t * part : (t + 1) * part].astype(jnp.float32), axis=0, keepdims=True)
        for g in range(groups):
            for s in range(n_seq):
                vec[(w.z * groups + g) * n_seq + s, b : b + 1, :] = sums[:, g * 128 : (g + 1) * 128]
    run(small.give_steps())
    row_sum.relay(3)
    row_sum.relay(2)
    own_rows[...] += row_term(0)
    queue[:0] = qkv.core_steps() + small.core_steps()
    pump(8)
    row_sum.relay(1)
    queue += qkv.chip_steps() + small.chip_steps() + qkv.seq_steps() + small.seq_steps()
    pump(len(queue))
    for unit in scatters:
        unit.finish()
    row_sum.finish(lambda at: own_rows[at, :], grad_rows)
    w.drain()


def back(sizes, heads, saved, w_shapes):
    n_dp, n_seq = sizes
    devices = n_dp * n_seq
    mid, normed, _, _, logs, page, query, key, value, key_turned, context, hidden, gelu, slopes = saved[:14]
    columns, full_out, full_up, full_down = saved[14:]
    count, width = normed.shape
    part = width // n_seq
    stream = count * n_seq
    local_heads, head_dim, _ = key_turned.shape
    blocks = part // 128
    low = jnp.bfloat16
    shapes = [w_shapes[0], w_shapes[1], w_shapes[2], columns.shape[1:], (16, 128)]
    kinds = [low] * 4 + [jnp.float32]
    results = [jax.ShapeDtypeStruct(shape, jnp.float32) for shape in shapes]
    results[3] = jax.ShapeDtypeStruct((n_seq,) + shapes[3], jnp.float32)
    anywhere = pl.BlockSpec(memory_space=pl.ANY)
    local = pl.BlockSpec(memory_space=pltpu.VMEM)
    sends = 5 * (4 + 3 * n_seq + 6) + 6 + n_seq - 1
    chips = n_dp // 2

    def like(array):
        return pltpu.VMEM(array.shape, array.dtype)

    scratch = [
        pltpu.SemaphoreType.DMA((sends,)),
        pltpu.SemaphoreType.DMA((5, chips)),
        pltpu.SemaphoreType.DMA((5, n_seq, 2)),
        pltpu.SemaphoreType.DMA((5, n_seq)),
        pltpu.SemaphoreType.DMA((5, 5)),
        pltpu.SemaphoreType.DMA((2, 2)),
        pltpu.SemaphoreType.DMA((n_seq,)),
        pltpu.SemaphoreType.DMA((13,)),
        pltpu.SemaphoreType.DMA((5,)),
        pltpu.VMEM((n_seq, count, part), low),
        like(query),
        like(key),
        like(value),
        like(key_turned),
        like(query),
        pltpu.VMEM((local_heads, head_dim, count), jnp.float32),
        pltpu.VMEM((blocks, stream, 128), jnp.float32),
        pltpu.VMEM((blocks, stream, 128), jnp.float32),
        pltpu.VMEM((stream, 3 * part), low),
        like(gelu),
        like(columns),
        pltpu.VMEM((devices, 16, 128), jnp.float32),
        pltpu.VMEM((n_seq - 1, count, width), low),
        pltpu.VMEM((5, count, width), low),
        pltpu.VMEM((count, width), jnp.float32),
        like(columns),
        like(hidden),
        like(context),
        like(slopes),
        like(normed),
        pltpu.VMEM((count, width), low),
        pltpu.VMEM((n_seq, count, part), low),
        like(full_out),
        pltpu.VMEM((2, n_seq) + shapes[0], low),
        pltpu.VMEM((2, devices // 2) + full_up.shape[2:], low),
        pltpu.VMEM((2, n_seq) + shapes[0], low),
        pltpu.VMEM((2, n_seq) + shapes[1], low),
        pltpu.VMEM((4, n_seq) + shapes[2], low),
    ]
    for shape, kind in zip(shapes, kinds):
        scratch += [
            pltpu.VMEM((chips, n_seq) + shape, kind),
            pltpu.VMEM((n_seq, 2) + shape, kind),
            pltpu.VMEM((n_seq,) + shape, kind),
            pltpu.VMEM((5,) + shape, kind),
        ]
    return pl.pallas_call(
        lambda *refs: back_kernel(sizes, heads, *refs),
        out_shape=[jax.ShapeDtypeStruct((count, width), low)] + results,
        in_specs=[anywhere] * 2 + [local] * 3 + [anywhere] * 13,
        out_specs=[local] * 6,
        scratch_shapes=scratch,
        compiler_params=pltpu.CompilerParams(
            collective_id=1, has_side_effects=True, vmem_limit_bytes=63 * 2**20
        ),
        name="back",
    )(*saved)


def spread_lanes(vectors, n_seq):
    stacked = jnp.stack(vectors).astype(jnp.float32)
    tiled = jnp.tile(stacked, (1, n_seq))
    owner = jnp.arange(tiled.shape[1], dtype=jnp.int32) // stacked.shape[1]
    return jnp.where(owner[None, :] == lax.axis_index("seq"), tiled, 0.0)


def kernel_plan(
    x_in,
    w_qkv,
    q_bias,
    v_bias,
    w_out,
    out_bias,
    ln1_gain,
    ln1_shift,
    w_up,
    up_bias,
    w_down,
    down_bias,
    ln2_gain,
    ln2_shift,
    valid,
    cotangent,
):
    sizes = (lax.axis_size("dp"), lax.axis_size("seq"))
    n_dp, groups = sizes
    rows = x_in[0]
    count, width = rows.shape
    vectors = (q_bias, v_bias, out_bias, ln1_gain, ln1_shift, down_bias, ln2_gain, ln2_shift)
    spread = spread_lanes(vectors, groups)
    vec = jnp.concatenate(
        [spread, up_bias.astype(jnp.float32)[None], jnp.zeros((7, spread.shape[1]), jnp.float32)]
    )
    third = width // groups
    w_columns = (
        w_qkv.reshape(-1, 3, groups, third).transpose(2, 0, 1, 3).reshape(groups, -1, 3 * third)
    )
    (
        columns,
        full_out,
        full_up,
        full_down,
        page_turned,
        query,
        key,
        value,
        key_turned,
        context,
        logs,
        hidden,
        gelu,
        slopes,
        output,
        normed,
        inv,
        grad_mid,
        line_sums,
    ) = front(sizes, HEADS, valid, rows, cotangent[0], vec, w_columns, w_out, w_up, w_down)
    saved = (grad_mid, normed, inv, line_sums, logs, page_turned, query, key, value, key_turned)
    saved += (context, hidden, gelu, slopes, columns, full_out, full_up, full_down)
    devices = n_dp * groups
    grad_rows, *sums = back(sizes, HEADS, saved, (w_down.shape, w_up.shape, w_out.shape))
    vec_sums = sums[4]
    mine = lax.dynamic_slice(
        vec_sums[:8], (0, lax.axis_index("seq") * (width // devices)), (8, width // devices)
    )
    return (
        output[None],
        grad_rows[None],
        sums[3].reshape(groups, -1, 3, third).transpose(1, 2, 0, 3).reshape(-1, 3 * width),
        mine[0],
        mine[1],
        sums[2],
        mine[2],
        mine[3],
        mine[4],
        sums[1],
        vec_sums[8],
        sums[0],
        mine[5],
        mine[6],
        mine[7],
    )


def solution(mesh):
    n_dp, n_seq = mesh.shape["dp"], mesh.shape["seq"]

    def per_device(x_in, w_qkv, *rest):
        part, width = w_qkv.shape[0], x_in.shape[2]
        fits = (n_dp, n_seq) == (8, 4) and part % 32 == 0 and part * n_seq == 128 and width // n_seq % 128 == 0 and x_in.shape[0] == 1
        plan = kernel_plan if fits else general_plan
        return plan(x_in, w_qkv, *rest)

    return jax.shard_map(
        per_device,
        mesh=mesh,
        in_specs=(
            P("dp", "seq", None),
            P(("dp", "seq"), None),
            P(("dp", "seq")),
            P(("dp", "seq")),
            P(("dp", "seq"), None),
            P(("dp", "seq")),
            P(("dp", "seq")),
            P(("dp", "seq")),
            P(("dp", "seq"), None),
            P(("dp", "seq")),
            P(("dp", "seq"), None),
            P(("dp", "seq")),
            P(("dp", "seq")),
            P(("dp", "seq")),
            P("dp"),
            P("dp", "seq", None),
        ),
        out_specs=(
            P("dp", "seq", None),
            P("dp", "seq", None),
            P(("dp", "seq"), None),
            P(("dp", "seq")),
            P(("dp", "seq")),
            P(("dp", "seq"), None),
            P(("dp", "seq")),
            P(("dp", "seq")),
            P(("dp", "seq")),
            P(("dp", "seq"), None),
            P(("dp", "seq")),
            P(("dp", "seq"), None),
            P(("dp", "seq")),
            P(("dp", "seq")),
            P(("dp", "seq")),
        ),
        check_vma=False,
    )
```

```python
import math

import jax
import jax.numpy as jnp
from jax import lax
from jax.experimental import pallas as pl
from jax.experimental.pallas import tpu as pltpu
from jax.sharding import PartitionSpec as P

HEADS = 16


eps_norm = 1e-05


def outer_sum(left, right):
    return lax.dot_general(
        left, right, (((0,), (0,)), ((), ())), preferred_element_type=jnp.float32
    )


def times_back(rows, matrix):
    return lax.dot_general(
        rows, matrix, (((1,), (1,)), ((), ())), preferred_element_type=jnp.float32
    )


def gelu_exact(values):
    return jax.nn.gelu(values, approximate=False)


def norm_forward(rows, gain, shift):
    center = rows - jnp.mean(rows, axis=-1, keepdims=True)
    inv_std = lax.rsqrt(jnp.mean(center * center, axis=-1, keepdims=True) + eps_norm)
    normed = center * inv_std
    return (normed * gain + shift, normed, inv_std)


def norm_backward(grad_out, normed, inv_std, gain):
    scaled = grad_out * gain
    grad_rows = inv_std * (
        scaled
        - jnp.mean(scaled, axis=-1, keepdims=True)
        - normed * jnp.mean(scaled * normed, axis=-1, keepdims=True)
    )
    return (grad_rows, jnp.sum(grad_out * normed, axis=0), jnp.sum(grad_out, axis=0))


def to_heads(rows, groups):
    count, width = rows.shape
    return rows.reshape(count, groups, width // groups).transpose(1, 0, 2).reshape(groups, -1)


def from_heads(pieces, part_width):
    groups = pieces.shape[0]
    return (
        pieces.reshape(groups, -1, part_width).transpose(1, 0, 2).reshape(-1, groups * part_width)
    )


def general_plan(
    x_in,
    w_qkv,
    q_bias,
    v_bias,
    w_out,
    out_bias,
    ln1_gain,
    ln1_shift,
    w_up,
    up_bias,
    w_down,
    down_bias,
    ln2_gain,
    ln2_shift,
    valid,
    cotangent,
):
    shards = (
        w_qkv,
        q_bias,
        v_bias,
        w_out,
        out_bias,
        ln1_gain,
        ln1_shift,
        w_up,
        up_bias,
        w_down,
        down_bias,
        ln2_gain,
        ln2_shift,
    )
    weights = (
        lax.all_gather(shards[0], ("dp", "seq"), axis=0, tiled=True),
        lax.all_gather(shards[1], ("dp", "seq"), axis=0, tiled=True),
        lax.all_gather(shards[2], ("dp", "seq"), axis=0, tiled=True),
        lax.all_gather(shards[3], ("dp", "seq"), axis=0, tiled=True),
        lax.all_gather(shards[4], ("dp", "seq"), axis=0, tiled=True),
        lax.all_gather(shards[5], ("dp", "seq"), axis=0, tiled=True),
        lax.all_gather(shards[6], ("dp", "seq"), axis=0, tiled=True),
        lax.all_gather(shards[7], ("dp", "seq"), axis=0, tiled=True),
        lax.all_gather(shards[8], ("dp", "seq"), axis=0, tiled=True),
        lax.all_gather(shards[9], ("dp", "seq"), axis=0, tiled=True),
        lax.all_gather(shards[10], ("dp", "seq"), axis=0, tiled=True),
        lax.all_gather(shards[11], ("dp", "seq"), axis=0, tiled=True),
        lax.all_gather(shards[12], ("dp", "seq"), axis=0, tiled=True),
    )
    (
        full_qkv,
        full_qbias,
        full_vbias,
        full_out,
        full_obias,
        full_gain1,
        full_shift1,
        full_up,
        full_ubias,
        full_down,
        full_dbias,
        full_gain2,
        full_shift2,
    ) = weights
    groups = lax.axis_size("seq")
    rows = x_in[0]
    count, width = rows.shape
    head_dim = width // HEADS
    part_width = width // groups
    local_heads = HEADS // groups
    stream = count * groups
    qrows = min(512, stream)
    nblocks = stream // qrows
    scale = 1.0 / math.sqrt(head_dim)
    keep = jnp.arange(stream, dtype=jnp.int32) < valid[0]
    bias_row = jnp.concatenate([full_qbias, jnp.zeros_like(full_qbias), full_vbias]).astype(
        jnp.float32
    )
    project = (jnp.dot(rows, full_qkv, preferred_element_type=jnp.float32) + bias_row).astype(
        jnp.bfloat16
    )
    sent = (
        to_heads(project[:, :width], groups),
        to_heads(project[:, width : 2 * width], groups),
        to_heads(project[:, 2 * width :], groups),
    )
    arrived = (
        lax.all_to_all(sent[0], "seq", split_axis=0, concat_axis=0, tiled=True),
        lax.all_to_all(sent[1], "seq", split_axis=0, concat_axis=0, tiled=True),
        lax.all_to_all(sent[2], "seq", split_axis=0, concat_axis=0, tiled=True),
    )
    query_blocks = arrived[0].reshape(nblocks, qrows, local_heads, head_dim)
    key_heads = arrived[1].reshape(stream, local_heads, head_dim)
    value_heads = arrived[2].reshape(stream, local_heads, head_dim)

    def masked_scores(query):
        scores = (
            jnp.einsum("qhd,khd->hqk", query, key_heads, preferred_element_type=jnp.float32) * scale
        )
        return jnp.where(keep[None, None, :], scores, -1e30)

    def attend_forward(query):
        scores = masked_scores(query)
        peak = jnp.max(scores, axis=-1, keepdims=True)
        raised = jnp.exp(scores - peak)
        total = jnp.sum(raised, axis=-1, keepdims=True)
        probs = (raised / total).astype(jnp.bfloat16)
        context = jnp.einsum("hqk,khd->qhd", probs, value_heads, preferred_element_type=jnp.float32)
        return (context.astype(jnp.bfloat16), (peak + jnp.log(total))[..., 0])

    context, log_sums = lax.map(attend_forward, query_blocks)
    returned_ctx = lax.all_to_all(
        context.reshape(groups, -1), "seq", split_axis=0, concat_axis=0, tiled=True
    )
    context_rows = from_heads(returned_ctx, part_width)
    attn_out = jnp.dot(
        context_rows, full_out, preferred_element_type=jnp.float32
    ) + full_obias.astype(jnp.float32)
    first_rows = rows.astype(jnp.float32) + attn_out
    hidden, normed_one, inv_one = norm_forward(
        first_rows, full_gain1.astype(jnp.float32), full_shift1.astype(jnp.float32)
    )
    hidden_low = hidden.astype(jnp.bfloat16)
    up_act = jnp.dot(hidden_low, full_up, preferred_element_type=jnp.float32) + full_ubias.astype(
        jnp.float32
    )
    gelu_low = gelu_exact(up_act).astype(jnp.bfloat16)
    branch = jnp.dot(gelu_low, full_down, preferred_element_type=jnp.float32) + full_dbias.astype(
        jnp.float32
    )
    output, normed_two, inv_two = norm_forward(
        hidden + branch, full_gain2.astype(jnp.float32), full_shift2.astype(jnp.float32)
    )
    again = (
        lax.all_gather(shards[0], ("dp", "seq"), axis=0, tiled=True),
        lax.all_gather(shards[1], ("dp", "seq"), axis=0, tiled=True),
        lax.all_gather(shards[2], ("dp", "seq"), axis=0, tiled=True),
        lax.all_gather(shards[3], ("dp", "seq"), axis=0, tiled=True),
        lax.all_gather(shards[4], ("dp", "seq"), axis=0, tiled=True),
        lax.all_gather(shards[5], ("dp", "seq"), axis=0, tiled=True),
        lax.all_gather(shards[6], ("dp", "seq"), axis=0, tiled=True),
        lax.all_gather(shards[7], ("dp", "seq"), axis=0, tiled=True),
        lax.all_gather(shards[8], ("dp", "seq"), axis=0, tiled=True),
        lax.all_gather(shards[9], ("dp", "seq"), axis=0, tiled=True),
        lax.all_gather(shards[10], ("dp", "seq"), axis=0, tiled=True),
        lax.all_gather(shards[11], ("dp", "seq"), axis=0, tiled=True),
        lax.all_gather(shards[12], ("dp", "seq"), axis=0, tiled=True),
    )
    back_qkv, back_out, back_gain1, back_up, back_down, back_gain2 = (
        again[0],
        again[3],
        again[5],
        again[7],
        again[9],
        again[11],
    )
    grad_out = cotangent[0].astype(jnp.float32)
    grad_mid, grad_ln2_gain, grad_ln2_shift = norm_backward(
        grad_out, normed_two, inv_two, back_gain2.astype(jnp.float32)
    )
    grad_branch = grad_mid.astype(jnp.bfloat16)
    grad_w_down = outer_sum(gelu_low, grad_branch)
    grad_down_bias = jnp.sum(grad_branch.astype(jnp.float32), axis=0)
    grad_gelu = times_back(grad_branch, back_down)
    grad_up = jax.vjp(gelu_exact, up_act)[1](grad_gelu)[0].astype(jnp.bfloat16)
    grad_w_up = outer_sum(hidden_low, grad_up)
    grad_up_bias = jnp.sum(grad_up.astype(jnp.float32), axis=0)
    grad_hidden = times_back(grad_up, back_up) + grad_mid
    grad_first, grad_ln1_gain, grad_ln1_shift = norm_backward(
        grad_hidden, normed_one, inv_one, back_gain1.astype(jnp.float32)
    )
    grad_attn = grad_first.astype(jnp.bfloat16)
    grad_w_out = outer_sum(context_rows, grad_attn)
    grad_out_bias = jnp.sum(grad_attn.astype(jnp.float32), axis=0)
    grad_context = times_back(grad_attn, back_out).astype(jnp.bfloat16)
    grad_ctx_heads = lax.all_to_all(
        to_heads(grad_context, groups), "seq", split_axis=0, concat_axis=0, tiled=True
    )
    grad_ctx_blocks = grad_ctx_heads.reshape(nblocks, qrows, local_heads, head_dim)

    def attend_backward(carry, inputs):
        key_total, value_total = carry
        query, grad_ctx, log_rows = inputs
        scores = masked_scores(query)
        probs = jnp.exp(scores - log_rows[..., None])
        probs_low = probs.astype(jnp.bfloat16)
        d_probs = jnp.einsum(
            "qhd,khd->hqk", grad_ctx, value_heads, preferred_element_type=jnp.float32
        )
        centre = jnp.sum(probs * d_probs, axis=-1, keepdims=True)
        grad_scores = (probs * (d_probs - centre)).astype(jnp.bfloat16)
        grad_query = (
            jnp.einsum("hqk,khd->qhd", grad_scores, key_heads, preferred_element_type=jnp.float32)
            * scale
        )
        key_total = (
            key_total
            + jnp.einsum("hqk,qhd->khd", grad_scores, query, preferred_element_type=jnp.float32)
            * scale
        )
        value_total = value_total + jnp.einsum(
            "hqk,qhd->khd", probs_low, grad_ctx, preferred_element_type=jnp.float32
        )
        return ((key_total, value_total), grad_query.astype(jnp.bfloat16))

    empty = jnp.zeros((stream, local_heads, head_dim), jnp.float32)
    (key_total, value_total), grad_query = lax.scan(
        attend_backward, (empty, empty), (query_blocks, grad_ctx_blocks, log_sums)
    )
    grad_key = key_total.astype(jnp.bfloat16)
    grad_value = value_total.astype(jnp.bfloat16)
    grad_pieces = (
        lax.all_to_all(
            grad_query.reshape(groups, -1), "seq", split_axis=0, concat_axis=0, tiled=True
        ),
        lax.all_to_all(
            grad_key.reshape(groups, -1), "seq", split_axis=0, concat_axis=0, tiled=True
        ),
        lax.all_to_all(
            grad_value.reshape(groups, -1), "seq", split_axis=0, concat_axis=0, tiled=True
        ),
    )
    grad_project = jnp.concatenate(
        [
            from_heads(grad_pieces[0], part_width),
            from_heads(grad_pieces[1], part_width),
            from_heads(grad_pieces[2], part_width),
        ],
        axis=1,
    )
    grad_w_qkv = outer_sum(rows, grad_project)
    bias_sums = jnp.sum(grad_project.astype(jnp.float32), axis=0)
    grad_q_bias = bias_sums[:width]
    grad_v_bias = bias_sums[2 * width :]
    grad_rows = times_back(grad_project, back_qkv) + grad_first
    terms = (
        grad_w_qkv,
        grad_q_bias,
        grad_v_bias,
        grad_w_out,
        grad_out_bias,
        grad_ln1_gain,
        grad_ln1_shift,
        grad_w_up,
        grad_up_bias,
        grad_w_down,
        grad_down_bias,
        grad_ln2_gain,
        grad_ln2_shift,
    )
    page_sums = (
        lax.psum_scatter(
            terms[0].astype(jnp.bfloat16), "dp", scatter_dimension=0, tiled=True
        ).astype(jnp.float32),
        lax.psum_scatter(
            terms[1].astype(jnp.bfloat16), "dp", scatter_dimension=0, tiled=True
        ).astype(jnp.float32),
        lax.psum_scatter(
            terms[2].astype(jnp.bfloat16), "dp", scatter_dimension=0, tiled=True
        ).astype(jnp.float32),
        lax.psum_scatter(
            terms[3].astype(jnp.bfloat16), "dp", scatter_dimension=0, tiled=True
        ).astype(jnp.float32),
        lax.psum_scatter(
            terms[4].astype(jnp.bfloat16), "dp", scatter_dimension=0, tiled=True
        ).astype(jnp.float32),
        lax.psum_scatter(
            terms[5].astype(jnp.bfloat16), "dp", scatter_dimension=0, tiled=True
        ).astype(jnp.float32),
        lax.psum_scatter(
            terms[6].astype(jnp.bfloat16), "dp", scatter_dimension=0, tiled=True
        ).astype(jnp.float32),
        lax.psum_scatter(
            terms[7].astype(jnp.bfloat16), "dp", scatter_dimension=0, tiled=True
        ).astype(jnp.float32),
        lax.psum_scatter(
            terms[8].astype(jnp.bfloat16), "dp", scatter_dimension=0, tiled=True
        ).astype(jnp.float32),
        lax.psum_scatter(
            terms[9].astype(jnp.bfloat16), "dp", scatter_dimension=0, tiled=True
        ).astype(jnp.float32),
        lax.psum_scatter(
            terms[10].astype(jnp.bfloat16), "dp", scatter_dimension=0, tiled=True
        ).astype(jnp.float32),
        lax.psum_scatter(
            terms[11].astype(jnp.bfloat16), "dp", scatter_dimension=0, tiled=True
        ).astype(jnp.float32),
        lax.psum_scatter(
            terms[12].astype(jnp.bfloat16), "dp", scatter_dimension=0, tiled=True
        ).astype(jnp.float32),
    )
    sums = (
        lax.psum_scatter(
            page_sums[0].astype(jnp.bfloat16), "seq", scatter_dimension=0, tiled=True
        ).astype(jnp.float32),
        lax.psum_scatter(
            page_sums[1].astype(jnp.bfloat16), "seq", scatter_dimension=0, tiled=True
        ).astype(jnp.float32),
        lax.psum_scatter(
            page_sums[2].astype(jnp.bfloat16), "seq", scatter_dimension=0, tiled=True
        ).astype(jnp.float32),
        lax.psum_scatter(
            page_sums[3].astype(jnp.bfloat16), "seq", scatter_dimension=0, tiled=True
        ).astype(jnp.float32),
        lax.psum_scatter(
            page_sums[4].astype(jnp.bfloat16), "seq", scatter_dimension=0, tiled=True
        ).astype(jnp.float32),
        lax.psum_scatter(
            page_sums[5].astype(jnp.bfloat16), "seq", scatter_dimension=0, tiled=True
        ).astype(jnp.float32),
        lax.psum_scatter(
            page_sums[6].astype(jnp.bfloat16), "seq", scatter_dimension=0, tiled=True
        ).astype(jnp.float32),
        lax.psum_scatter(
            page_sums[7].astype(jnp.bfloat16), "seq", scatter_dimension=0, tiled=True
        ).astype(jnp.float32),
        lax.psum_scatter(
            page_sums[8].astype(jnp.bfloat16), "seq", scatter_dimension=0, tiled=True
        ).astype(jnp.float32),
        lax.psum_scatter(
            page_sums[9].astype(jnp.bfloat16), "seq", scatter_dimension=0, tiled=True
        ).astype(jnp.float32),
        lax.psum_scatter(
            page_sums[10].astype(jnp.bfloat16), "seq", scatter_dimension=0, tiled=True
        ).astype(jnp.float32),
        lax.psum_scatter(
            page_sums[11].astype(jnp.bfloat16), "seq", scatter_dimension=0, tiled=True
        ).astype(jnp.float32),
        lax.psum_scatter(
            page_sums[12].astype(jnp.bfloat16), "seq", scatter_dimension=0, tiled=True
        ).astype(jnp.float32),
    )
    return (
        output.astype(jnp.bfloat16)[None],
        grad_rows.astype(jnp.bfloat16)[None],
        sums[0],
        sums[1],
        sums[2],
        sums[3],
        sums[4],
        sums[5],
        sums[6],
        sums[7],
        sums[8],
        sums[9],
        sums[10],
        sums[11],
        sums[12],
    )


MESH = pl.DeviceIdType.MESH
CHUNK = 256
MASKED = -1e30
FLAT = (((1,), (1,)), ((), ()))
FRONT_ORDER = (
    "uz", "oz", "dc", "qc", "xz", "qz", "d00", "us1", "os1", "uc", "oc", "dz", "xw1", "u01", "o01", "qs1",
    "xi1", "xi2", "qs2", "q00", "qs3", "q03", "o00", "d10", "q01", "q02", "ds1", "o10", "q10", "q13", "q11",
    "o11", "us2", "q12", "us3", "xw2", "d01", "qk", "p0", "xi3", "p1", "p2", "u02", "u03", "u00", "u11",
    "xw3", "p3", "prep", "a0", "ds2", "a1", "os2", "a2", "ds3", "a3", "os3", "cs", "d11", "o02", "u12",
    "o03", "d02", "d03", "pt", "o12", "o13", "u13", "u10", "cw", "ok", "m1", "uk", "d12", "d13", "ua", "dk",
    "dm",
)

BACK_ORDER = (
    "b0", "dg0", "f0", "f1", "f2", "dg1", "h0", "dg2", "dk0", "f3", "f4", "dg3", "f5", "h1", "f6", "dk1",
    "f7", "h2", "h3", "dk3", "h4", "h5", "dk2", "h6", "h7", "ln", "gc", "ug0", "dc0", "ug1", "ug2", "dc1",
    "ug3", "og0", "dc3", "dc2", "uk0", "at", "a0", "dt1", "a1", "dt3", "a2", "dt2", "a3", "pk", "r3", "uk1",
    "dr3", "uk2", "r2", "ok0", "og1", "gw", "dr2", "og2", "uk3", "og3", "ok1", "r1", "kl", "qg", "ok3",
    "l3", "r0", "ok2", "dr1", "dt0", "vg", "uc2", "oc3", "uc3", "l2", "qk0", "oc1", "oc2", "ut3", "dF",
    "ot2", "l1", "qk2", "qk1", "qk3", "qc1", "ot3", "ut2", "qc3", "qt1", "uc1", "uc0", "ur3", "or3", "oc0",
    "qc2", "ut1", "qc0", "ur1", "or2", "ot1", "rF", "qt3", "qt2", "qr3", "qr2", "or1", "ur2", "qr1", "ut0",
    "qt0", "ot0", "qF", "uF", "oF",
)

def flip(index, mask):
    for b in range(mask.bit_length()):
        if mask >> b & 1:
            bit = 1 << b
            index = index + bit - 2 * bit * (index // bit % 2)
    return index


def guarded(when, action):
    if when is None:
        action()
    else:
        pl.when(when)(action)


class Wires:
    def __init__(self, sems, sizes):
        self.sems, self.sizes = sems, sizes
        self.dp, self.z = lax.axis_index("dp"), lax.axis_index("seq")
        self.dps = [flip(self.dp, m) for m in range(sizes[0])]
        self.zs = [flip(self.z, m) for m in range(sizes[1])]
        last = sizes[1] - 1
        half = self.z // 2
        step = 1 - 2 * half
        depth = self.z * step + last * half
        self.inner, self.outer = depth == 1, depth == 0
        self.right = self.z + step
        self.left = self.z - step * depth
        self.far = [self.z] + [t * step + last * half for t in (1 - depth, 2, 3)]
        self.started = []

    def peer(self, offset, step):
        return (self.dps[offset], self.zs[step])

    def send(self, src, dst, recv_sem, device, when=None):
        copy = pltpu.make_async_remote_copy(
            src_ref=src,
            dst_ref=dst,
            send_sem=self.sems.at[len(self.started)],
            recv_sem=recv_sem,
            device_id=device,
            device_id_type=MESH,
        )
        guarded(when, copy.start)
        self.started.append((copy, when))
        return len(self.started) - 1

    def sent(self, index):
        copy, when = self.started[index]
        guarded(when, copy.wait_send)
        self.started[index] = None

    def arrived(self, dst, recv_sem, when=None):
        copy = pltpu.make_async_remote_copy(
            src_ref=dst,
            dst_ref=dst,
            send_sem=self.sems.at[0],
            recv_sem=recv_sem,
            device_id=self.peer(1, 0),
            device_id_type=MESH,
        )
        guarded(when, copy.wait_recv)

    def drain(self):
        for index, entry in enumerate(self.started):
            if entry is not None:
                self.sent(index)

    def greet(self):
        n_dp, n_seq = self.sizes
        barrier = pltpu.get_barrier_semaphore()
        masks = [1 << b for b in range(n_dp.bit_length() - 1)]
        partners = [self.peer(m, 0) for m in masks] + [self.peer(0, i) for i in range(1, n_seq)]
        for device in partners:
            pl.semaphore_signal(barrier, inc=1, device_id=device, device_id_type=MESH)
        pl.semaphore_wait(barrier, len(partners))


class Line:
    def __init__(self, wires, slot, recv):
        self.w, self.slot, self.recv = wires, slot, recv

    def pass_on(self, k, src, to_left):
        w = self.w
        s = w.far[k]
        dst = self.slot(s)
        if to_left:
            w.send(src, dst, self.recv.at[s], (w.dp, w.left), w.inner)
        else:
            w.send(src, dst, self.recv.at[s], (w.dp, w.right), None if k == 0 else w.inner)

    def own(self, src):
        self.pass_on(0, src, False)
        self.pass_on(0, src, True)

    def take(self, k):
        s = self.w.far[k]
        self.w.arrived(self.slot(s), self.recv.at[s])
        self.pass_on(k, self.slot(s), k > 1)

    def relay(self, k):
        s = self.w.far[k]
        self.w.arrived(self.slot(s), self.recv.at[s], self.w.inner)
        self.pass_on(k, self.slot(s), k > 1)

    def end(self, k):
        s = self.w.far[k]
        self.w.arrived(self.slot(s), self.recv.at[s], self.w.outer)


class Gather:
    def __init__(self, wires, src, full, recv, local):
        self.w, self.src, self.full, self.recv, self.local = wires, src, full, recv, local
        n_dp, self.n_seq = wires.sizes
        self.chips = [1 << b for b in range(1, n_dp.bit_length() - 1)]
        self.slots = wires.far
        self.line = Line(wires, lambda s: full.at[wires.dp * self.n_seq + s], recv.at[0])

    def at(self, offset, step):
        return self.full.at[self.w.dps[offset] * self.n_seq + self.slots[step]]

    def order(self, step):
        return self.chips if step % 2 == 0 else self.chips[::-1]

    def forward(self, src, offset, step, masks):
        for m in masks:
            sem = self.recv.at[offset ^ m, self.slots[step]]
            self.w.send(src, self.at(offset, step), sem, self.w.peer(m, 0))

    def wait(self, offset, step):
        self.w.arrived(self.at(offset, step), self.recv.at[offset, self.slots[step]])

    def mine(self):
        return self.src

    def own_chips(self):
        self.kept = pltpu.make_async_copy(self.mine(), self.at(0, 0), self.local)
        self.kept.start()
        self.forward(self.mine(), 0, 0, self.order(0) + [1])

    def own_seq(self):
        self.line.own(self.src)

    def along_seq(self, i):
        self.line.take(i)
        self.forward(self.at(0, i), 0, i, self.order(i) + [1])

    def stages(self, step):
        have, out = [0], []
        masks = self.order(step)
        for t, m in enumerate(masks):
            out.append([(o ^ m, masks[t + 1 :] + [1]) for o in have])
            have = have + [o ^ m for o in have]
        return out

    def over_chips(self, t, step):
        for offset, masks in self.stages(step)[t]:
            self.wait(offset, step)
            self.forward(self.at(offset, step), offset, step, masks)

    def over_cores(self):
        n_dp = self.w.sizes[0]
        for offset in range(1, n_dp, 2):
            for i in range(self.n_seq):
                self.wait(offset, i)
        self.kept.wait()


class GatherColumns(Gather):
    def __init__(self, *args):
        super().__init__(*args)
        self.slots = self.w.zs

    def mine(self):
        return self.src.at[self.w.z]

    def own_seq(self):
        for i in range(1, self.n_seq):
            sem = self.recv.at[0, self.w.z]
            self.w.send(self.src.at[self.w.zs[i]], self.at(0, 0), sem, self.w.peer(0, i))

    def along_seq(self, i):
        self.wait(0, i)
        self.forward(self.at(0, i), 0, i, self.order(i) + [1])


def sends_of_gather(n_dp, n_seq):
    return 2 + n_seq - 1 + n_seq * (n_dp - 1)


def group_lanes(packed, row, group, n_seq):
    total = packed[group * n_seq, row : row + 1, :]
    for s in range(1, n_seq):
        total = total + packed[group * n_seq + s, row : row + 1, :]
    return total


def spread_head(source, h, head_dim, factor):
    n_seq, rows, _ = source.shape
    block = h * head_dim // 128 * 128
    low = h * head_dim % 128
    lane = lax.broadcasted_iota(jnp.int32, (n_seq * rows, 128), 1)
    values = source[:, :, block : block + 128].reshape(n_seq * rows, 128).astype(jnp.float32)
    kept = jnp.where((lane >= low) & (lane < low + head_dim), values * factor, 0.0)
    return kept.astype(jnp.bfloat16).reshape(n_seq, rows, 128)


def front_kernel(
    sizes,
    heads,
    valid_ref,
    x_ref,
    cotangent,
    vec_ref,
    qkv_ref,
    out_ref,
    up_ref,
    down_ref,
    columns_out,
    full_out,
    full_up,
    full_down,
    page_out,
    query_out,
    key_out,
    value_out,
    key_turned_out,
    context_out,
    logs_out,
    hidden_out,
    gelu_out,
    slope_out,
    output,
    normed_one,
    inv_one,
    grad_mid,
    sums_out,
    packed,
    columns,
    page,
    held,
    context_sent,
    context_held,
    context_turned,
    value_turned,
    masked_query,
    keys,
    values,
    key_turned,
    logs,
    out_matrix,
    up_matrix,
    down_matrix,
    page_turned,
    context_rows_turned,
    hidden,
    hidden_low,
    hidden_turned,
    gelu_low,
    gelu_turned,
    slopes,
    branch,
    send_sems,
    gather_sems,
    page_sems,
    context_sems,
    local_sems,
):
    n_dp, n_seq = sizes
    w = Wires(send_sems, sizes)
    rows, width = x_ref.shape
    part = width // n_seq
    head_dim = width // heads
    local_heads = heads // n_seq
    stream = rows * n_seq
    w.greet()
    line = Line(w, lambda s: page.at[s], page_sems)
    sources = (
        (vec_ref, packed),
        (qkv_ref, columns),
        (out_ref, out_matrix),
        (up_ref, up_matrix),
        (down_ref, down_matrix),
    )
    vec, qkv, out, up, down = [
        (GatherColumns if k == 1 else Gather)(w, src, dst, gather_sems.at[k], local_sems.at[k])
        for k, (src, dst) in enumerate(sources)
    ]
    def run(steps):
        for step in steps:
            step()

    keeps = []

    def keep(src, dst):
        keeps.append(pltpu.make_async_copy(src, dst, local_sems.at[5 + len(keeps)]))
        keeps[-1].start()

    per_block = 128 // head_dim
    scale = 1.0 / math.sqrt(head_dim)
    groups = part // 128
    one_lane = lax.broadcasted_iota(jnp.int32, (rows, 128), 1)
    ones = jnp.where(one_lane == 0, 1.0, 0.0).astype(jnp.bfloat16)
    chunk = 512
    chunks = up_matrix.shape[2] // chunk
    per_chunk = chunk // down_matrix.shape[1]
    per_part = part // out_matrix.shape[1]

    def line_of(row):
        return jnp.concatenate([group_lanes(packed, row, d, n_seq) for d in range(n_dp)], axis=1)

    def gathered_columns():
        qkv.over_cores()
        vec.over_cores()
        keep(columns, columns_out)

    def project(k):
        s = w.far[k]
        if k == 0:
            page[s] = x_ref[...]
        matrix = columns[...].reshape(width, 3 * part)
        piece = jnp.dot(page[s], matrix, preferred_element_type=jnp.float32)
        for t in range(3):
            third = piece[:, t * part : (t + 1) * part]
            if t != 1:
                bias = [group_lanes(packed, t // 2, w.z * groups + g, n_seq) for g in range(groups)]
                third = third + jnp.concatenate(bias, axis=1)
            held[t, s] = third.astype(jnp.bfloat16)

    def prepare():
        position = lax.broadcasted_iota(jnp.int32, (stream, 128), 0)
        lane = lax.broadcasted_iota(jnp.int32, (stream, 128), 1)
        guard = jnp.where((position >= valid_ref[0]) & (lane == 0), MASKED, 0.0).astype(jnp.bfloat16)
        for h in range(local_heads):
            masked_query[h] = spread_head(held.at[0], h, head_dim, scale)
        for b in range(local_heads // per_block):
            lanes = slice(b * 128, (b + 1) * 128)
            keys[b, :, :128] = held[1, :, :, lanes].reshape(stream, 128)
            keys[b, :, 128:] = guard
            values[b] = held[2, :, :, lanes].reshape(stream, 128)
        turned = held[1].reshape(stream, part).T
        for h in range(local_heads):
            key_turned[h] = turned[h * head_dim : (h + 1) * head_dim, :]
        value_turned[...] = held[2].reshape(stream, part).T
        keep(masked_query, query_out)
        keep(keys, key_out)
        keep(values, value_out)
        keep(key_turned, key_turned_out)

    def attention(h):
        def attend(c, _):
            query = jnp.concatenate([masked_query[h, c], ones], axis=1)
            scores = lax.dot_general(
                keys[h // per_block], query, FLAT, preferred_element_type=jnp.float32
            )
            peak = jnp.max(scores, axis=0, keepdims=True)
            raised = jnp.exp(scores - peak)
            total = jnp.sum(raised, axis=0, keepdims=True)
            mixed = jnp.dot(
                value_turned[h * head_dim : (h + 1) * head_dim, :],
                raised.astype(jnp.bfloat16),
                preferred_element_type=jnp.float32,
            )
            context_turned[c, h * head_dim : (h + 1) * head_dim, :] = mixed / total
            logs[c, h : h + 1, :] = peak + jnp.log(total)
            return 0

        lax.fori_loop(0, n_seq, attend, 0)

    def send_context():
        for i in (1, 2, 3, 0):
            context_sent[w.zs[i]] = context_turned[w.zs[i]].T.astype(jnp.bfloat16)
            if i:
                w.send(context_sent.at[w.zs[i]], context_held.at[w.z], context_sems.at[i], w.peer(0, i))
        context_held[w.z] = context_sent[w.z]
        keep(logs, logs_out)

    def turn_page():
        for s in range(n_seq):
            page_turned[s * width : (s + 1) * width, :] = page[s].T
        keep(page_turned, page_out)

    def context_arrived():
        for i in range(1, n_seq):
            w.arrived(context_held.at[w.zs[i]], context_sems.at[i])

    def gathered_out():
        out.over_cores()
        keep(out_matrix, full_out)

    def gathered_up():
        up.over_cores()
        for b in range(up_matrix.shape[2] // width):
            keep(up_matrix.at[:, :, pl.ds(b * width, width)], full_up.at[b])

    def gathered_down():
        down.over_cores()
        keep(down_matrix, full_down)

    def first_norm():
        total = x_ref[...].astype(jnp.float32) + line_of(2)
        for j in range(n_seq):
            block = out_matrix[j * per_part : (j + 1) * per_part].reshape(part, width)
            total = total + jnp.dot(context_held[j], block, preferred_element_type=jnp.float32)
            context_rows_turned[j * part : (j + 1) * part, :] = context_held[j].T
        keep(context_rows_turned, context_out)
        rows_hidden, normed, inv = norm_forward(total, line_of(3), line_of(4))
        normed_one[...] = normed
        inv_one[...] = jnp.broadcast_to(inv, inv_one.shape)
        hidden[...] = rows_hidden
        hidden_low[...] = rows_hidden.astype(jnp.bfloat16)
        hidden_turned[...] = rows_hidden.T.astype(jnp.bfloat16)
        keep(hidden_turned, hidden_out)

    def expand():
        def activate(f, _):
            at = pl.ds(pl.multiple_of(f * chunk, chunk), chunk)
            block = up_matrix[:, :, at].reshape(width, chunk)
            up_bias = jnp.concatenate(
                [packed[f * per_chunk + e, 8:9, :] for e in range(per_chunk)], axis=1
            )
            act = jnp.dot(hidden_low[...], block, preferred_element_type=jnp.float32) + up_bias
            below = 0.5 + 0.5 * lax.erf(act * math.sqrt(0.5))
            gelu = act * below
            gelu_low[:, at] = gelu.astype(jnp.bfloat16)
            gelu_turned[at, :] = gelu.T.astype(jnp.bfloat16)
            bell = jnp.exp(-0.5 * act * act) * (1.0 / math.sqrt(2.0 * math.pi))
            slopes[:, at] = (below + act * bell).astype(jnp.bfloat16)
            return 0

        lax.fori_loop(0, chunks, activate, 0)
        keep(gelu_turned, gelu_out)
        keep(slopes, slope_out)

    def shrink_all():
        branch[...] = hidden[...] + line_of(5)

        def shrink(f, _):
            at = pl.ds(pl.multiple_of(f * chunk, chunk), chunk)
            block = down_matrix[pl.ds(f * per_chunk, per_chunk)].reshape(chunk, width)
            branch[...] += jnp.dot(gelu_low[:, at], block, preferred_element_type=jnp.float32)
            return 0

        lax.fori_loop(0, chunks, shrink, 0)

    actions = {
        "xz": lambda: line.own(x_ref),
        "qk": gathered_columns,
        "ok": gathered_out,
        "uk": gathered_up,
        "dk": gathered_down,
        "prep": prepare,
        "cs": send_context,
        "cw": context_arrived,
        "pt": turn_page,
        "m1": first_norm,
        "ua": expand,
        "dm": shrink_all,
    }
    for h in range(local_heads):
        actions["a%d" % h] = lambda h=h: attention(h)
    for k in range(n_seq):
        actions["p%d" % k] = lambda k=k: project(k)
        if k:
            actions["xi%d" % k] = lambda k=k: line.relay(k)
            actions["xw%d" % k] = lambda k=k: line.end(k)
    for name, members in (("q", (qkv, vec)), ("o", (out,)), ("u", (up,)), ("d", (down,))):
        actions[name + "z"] = lambda m=members: run([unit.own_seq for unit in m])
        actions[name + "c"] = lambda m=members: run([unit.own_chips for unit in m])
        for k in range(n_seq):
            if k:
                actions["%ss%d" % (name, k)] = lambda m=members, k=k: [unit.along_seq(k) for unit in m]
            for t in range(2):
                actions["%s%d%d" % (name, t, k)] = lambda m=members, t=t, k=k: [unit.over_chips(t, k) for unit in m]
    for name in FRONT_ORDER:
        actions[name]()
    gain_one, gain_two = line_of(3), line_of(6)
    result, normed, inv = norm_forward(branch[...], gain_two, line_of(7))
    output[...] = result.astype(jnp.bfloat16)
    grad = cotangent[...].astype(jnp.float32)
    mid, grad_gain, grad_shift = norm_backward(grad, normed, inv, gain_two)
    grad_mid[...] = mid
    grad_bias = jnp.sum(mid.astype(jnp.bfloat16).astype(jnp.float32), axis=0)
    sums_out[...] = jnp.zeros_like(sums_out)
    for row, line_sum in enumerate((grad_bias, grad_gain, grad_shift)):
        sums_out[5 + row : 6 + row, :] = line_sum.reshape(1, width)
    sums_out[3:4, :] = gain_one
    for copy in keeps:
        copy.wait()
    w.drain()


def front(sizes, heads, valid, rows, cotangent, vec, w_columns, w_out, w_up, w_down):
    n_dp, n_seq = sizes
    devices = n_dp * n_seq
    count, width = rows.shape
    part = width // n_seq
    stream = count * n_seq
    wide = w_up.shape[1]
    low = jnp.bfloat16
    head_dim = width // heads
    local_heads = heads // n_seq
    blocks = part // 128
    attention = (
        jax.ShapeDtypeStruct((local_heads, n_seq, count, 128), low),
        jax.ShapeDtypeStruct((blocks, stream, 256), low),
        jax.ShapeDtypeStruct((blocks, stream, 128), low),
        jax.ShapeDtypeStruct((local_heads, head_dim, stream), low),
    )

    def full(shard):
        return jax.ShapeDtypeStruct((devices,) + shard.shape, shard.dtype)

    anywhere = pl.BlockSpec(memory_space=pl.ANY)
    local = pl.BlockSpec(memory_space=pltpu.VMEM)
    sends = 5 * sends_of_gather(n_dp, n_seq) + 5 + n_seq - 1
    return pl.pallas_call(
        lambda *refs: front_kernel(sizes, heads, *refs),
        out_shape=(
            jax.ShapeDtypeStruct((devices,) + w_columns.shape[1:], low),
            full(w_out),
            jax.ShapeDtypeStruct((wide // width, devices, w_up.shape[0], width), low),
            full(w_down),
            jax.ShapeDtypeStruct((n_seq * width, count), low),
        )
        + attention
        + (
            jax.ShapeDtypeStruct((width, count), low),
            jax.ShapeDtypeStruct((n_seq, 8, count), jnp.float32),
            jax.ShapeDtypeStruct((width, count), low),
            jax.ShapeDtypeStruct((wide, count), low),
            jax.ShapeDtypeStruct((count, wide), low),
            jax.ShapeDtypeStruct((count, width), low),
            jax.ShapeDtypeStruct((count, width), jnp.float32),
            jax.ShapeDtypeStruct((count, 128), jnp.float32),
            jax.ShapeDtypeStruct((count, width), jnp.float32),
            jax.ShapeDtypeStruct((8, width), jnp.float32),
        ),
        in_specs=[
            pl.BlockSpec(memory_space=pltpu.SMEM),
            local,
            local,
        ]
        + [anywhere] * 5,
        out_specs=[anywhere] * 14 + [local] * 5,
        scratch_shapes=[
            pltpu.VMEM((devices,) + vec.shape, jnp.float32),
            pltpu.VMEM((devices,) + w_columns.shape[1:], low),
            pltpu.VMEM((n_seq, count, width), low),
            pltpu.VMEM((3, n_seq, count, part), low),
            pltpu.VMEM((n_seq, count, part), low),
            pltpu.VMEM((n_seq, count, part), low),
            pltpu.VMEM((n_seq, part, count), jnp.float32),
            pltpu.VMEM((part, stream), low),
        ]
        + [pltpu.VMEM(a.shape, a.dtype) for a in attention]
        + [
            pltpu.VMEM((n_seq, 8, count), jnp.float32),
            pltpu.VMEM((devices,) + w_out.shape, low),
            pltpu.VMEM((devices,) + w_up.shape, low),
            pltpu.VMEM((devices,) + w_down.shape, low),
            pltpu.VMEM((n_seq * width, count), low),
            pltpu.VMEM((width, count), low),
            pltpu.VMEM((count, width), jnp.float32),
            pltpu.VMEM((count, width), low),
            pltpu.VMEM((width, count), low),
            pltpu.VMEM((count, wide), low),
            pltpu.VMEM((wide, count), low),
            pltpu.VMEM((count, wide), low),
            pltpu.VMEM((count, width), jnp.float32),
            pltpu.SemaphoreType.DMA((sends,)),
            pltpu.SemaphoreType.DMA((5, n_dp, n_seq)),
            pltpu.SemaphoreType.DMA((n_seq,)),
            pltpu.SemaphoreType.DMA((n_seq,)),
            pltpu.SemaphoreType.DMA((24,)),
        ],
        compiler_params=pltpu.CompilerParams(
            collective_id=0, has_side_effects=True, vmem_limit_bytes=60 * 2**20
        ),
        name="front",
    )(valid, rows, cotangent, vec, w_columns, w_out, w_up, w_down)


def add_rows(into, term):
    rows = into.shape[0]
    step = min(16, rows)

    def body(r, _):
        at = pl.ds(pl.multiple_of(r * step, step), step)
        total = into[at, :].astype(jnp.float32) + term[at, :].astype(jnp.float32)
        into[at, :] = total.astype(into.dtype)
        return 0

    lax.fori_loop(0, rows // step, body, 0)


class LineSum:
    def __init__(self, wires, block, last, sems):
        self.w, self.block, self.last, self.sems = wires, block, last, sems

    def into(self, src, index, device, when):
        self.w.send(src, self.last.at[index], self.sems.at[index], device, when)

    def add(self, k, index):
        def action():
            self.w.arrived(self.last.at[index], self.sems.at[index])
            add_rows(self.block(k), self.last.at[index])

        pl.when(self.w.inner)(action)

    def offer(self, k):
        self.into(self.block(k), k - 1, (self.w.dp, self.w.right), self.w.outer)

    def relay(self, k):
        w, block = self.w, self.block(k)
        if k == 1:
            self.add(1, 4)
            self.into(block, 3, (w.dp, w.left), w.inner)
        else:
            self.add(k, k - 1)
            self.into(block, 3 if k == 2 else 4, (w.dp, w.right), w.inner)

    def finish(self, start, out):
        w = self.w
        w.arrived(self.last.at[3], self.sems.at[3])
        w.arrived(self.last.at[0], self.sems.at[0], w.inner)
        rows = out.shape[0]
        step = min(16, rows)

        def total_of(count):
            def body(r, _):
                at = pl.ds(pl.multiple_of(r * step, step), step)
                total = start(at) + self.last[3, at, :].astype(jnp.float32)
                if count == 2:
                    total = total + self.last[0, at, :].astype(jnp.float32)
                out[at, :] = total.astype(out.dtype)
                return 0

            lax.fori_loop(0, rows // step, body, 0)

        pl.when(w.inner)(lambda: total_of(2))
        pl.when(w.outer)(lambda: total_of(1))


class Scatter:
    def __init__(self, wires, kind, make, source, stage, bufs, sems, out):
        self.w, self.kind, self.make, self.source, self.stage = wires, kind, make, source, stage
        self.total, self.first, self.second, self.last = bufs
        self.core_sems, self.first_sems, self.second_sems, self.last_sems = sems
        self.out = out
        self.n_seq = wires.sizes[1]
        self.offsets = [6, 2, 4, 0]
        self.staged = {}
        self.slots = wires.far if kind == "line" else wires.zs
        self.line = LineSum(wires, lambda k: self.total.at[0, self.slots[k]], self.last, self.last_sems)

    def order(self, step):
        return (2, 4) if step % 2 == 0 else (4, 2)

    def give(self, k):
        o = self.offsets[k]
        d = self.w.dps[o ^ 1]
        if self.stage is None:
            src = self.source.at[pl.ds(d * self.n_seq, self.n_seq)]
        else:
            depth = self.stage.shape[0]
            if k >= depth:
                self.w.sent(self.staged[k - depth])
            src = self.stage.at[k % depth]

            def fill(s, _):
                src[s] = self.make(d, s).astype(src.dtype)
                return 0

            lax.fori_loop(0, self.n_seq, fill, 0)
        sem = self.core_sems.at[o // 2]
        self.staged[k] = self.w.send(src, self.total.at[o // 2], sem, self.w.peer(1, 0))

    def give_steps(self):
        return [lambda k=k: self.give(k) for k in range(4)]

    def over_cores(self, k):
        o = self.offsets[k]
        d = self.w.dps[o]
        self.w.arrived(self.total.at[o // 2], self.core_sems.at[o // 2])

        def add(s, _):
            block = self.total.at[o // 2, s]
            block[...] = (block[...].astype(jnp.float32) + self.make(d, s)).astype(block.dtype)
            return 0

        lax.fori_loop(0, self.n_seq, add, 0)
        for i in range(self.n_seq):
            mask = self.order(i)[0]
            block = self.total.at[o // 2, self.slots[i]]
            if o & mask:
                keep = (o ^ mask) // (6 ^ mask)
                self.w.send(block, self.first.at[i, keep], self.first_sems.at[i, keep], self.w.peer(mask, 0))

    def over_chips(self, i):
        mask = self.order(i)[1]
        for keep in (1, 0):
            o = mask * keep
            block = self.total.at[o // 2, self.slots[i]]
            self.w.arrived(self.first.at[i, keep], self.first_sems.at[i, keep])
            add_rows(block, self.first.at[i, keep])
            if keep:
                self.w.send(block, self.second.at[i], self.second_sems.at[i], self.w.peer(mask, 0))

    def to_seq(self, i):
        block = self.total.at[0, self.slots[i]]
        self.w.arrived(self.second.at[i], self.second_sems.at[i])
        add_rows(block, self.second.at[i])
        if self.kind == "line":
            if i:
                self.line.offer(i)
        elif i:
            self.w.send(block, self.last.at[i], self.last_sems.at[i], self.w.peer(0, i))

    def relay(self, i):
        if self.kind == "line":
            self.line.relay(i)

    def finish(self):
        block = self.total.at[0, self.w.z]
        if self.kind == "line":
            self.line.finish(lambda at: block[at, :].astype(jnp.float32), self.out)
            return
        self.out[self.w.z] = block[...].astype(jnp.float32)
        for i in range(1, self.n_seq):
            self.w.arrived(self.last.at[i], self.last_sems.at[i])
            self.out[self.w.zs[i]] = self.last[i].astype(jnp.float32)


def back_kernel(sizes, heads, *refs):
    n_dp, n_seq = sizes
    (
        mid_in,
        normed_in,
        inv_in,
        sums_in,
        logs,
        page_in,
        query_in,
        key_in,
        value_in,
        key_turned_in,
        context_in,
        hidden_in,
        gelu_in,
        slope_in,
        columns_in,
        out_in,
        up_in,
        down_in,
        grad_rows,
        *outs,
    ) = refs[:24]
    scratch = list(refs[24:])

    def take(count):
        got = scratch[:count]
        del scratch[:count]
        return got

    send_sems, core_sems, first_sems, second_sems, last_sems, block_sems = take(6)
    head_sems, local_sems, row_sems = take(3)
    grads, masked_query, keys, values, key_turned, masked_grad = take(6)
    query_grad, key_grad, value_grad = take(3)
    project, turned, columns, vec = take(4)
    row_terms, row_last, own_rows, partial = take(4)
    hidden_turned, context_turned, slopes, normed = take(4)
    grad_low, grad_sent, out_matrix, down_blocks, up_blocks = take(5)
    down_stage, up_stage, out_stage = take(3)
    units = [take(4) for k in range(5)]
    w = Wires(send_sems, sizes)
    rows, width = normed.shape
    part = width // n_seq
    wide = slopes.shape[1]
    head_dim = width // heads
    local_heads = heads // n_seq
    stream = rows * n_seq
    per_block = 128 // head_dim
    scale = 1.0 / math.sqrt(head_dim)
    loads = {}

    def load(name, src, dst):
        loads[name] = pltpu.make_async_copy(src, dst, local_sems.at[len(loads)])
        loads[name].start()

    load("mid", mid_in, own_rows)
    load("gelu", gelu_in, turned)
    load("slope", slope_in, slopes)
    blocks = []
    for f in range(n_dp):
        sem = block_sems.at[0, f % 2]
        blocks.append(pltpu.make_async_copy(down_in.at[pl.ds(f * n_seq, n_seq)], down_blocks.at[f % 2], sem))
    shares = wide // width
    half = up_in.shape[1] // 2
    ups = []
    for e in range(2 * shares):
        src = up_in.at[e % shares, pl.ds(e // shares * half, half)]
        ups.append(pltpu.make_async_copy(src, up_blocks.at[e % 2], block_sems.at[1, e % 2]))
    for e in range(2):
        blocks[e].start()
        ups[e].start()
    load("hidden", hidden_in, hidden_turned)
    load("normed", normed_in, normed)
    load("out", out_in, out_matrix)
    load("context", context_in, context_turned)
    load("columns", columns_in, columns)
    load("query", query_in, masked_query)
    load("key", key_in, keys)
    load("value", value_in, values)
    load("turned", key_turned_in, key_turned)
    w.greet()

    def rows_from(source, first, count):
        return source[pl.ds(pl.multiple_of(first, count), count), :]

    def down_term(d, s):
        left = rows_from(turned, (d * n_seq + s) * outs[0].shape[0], outs[0].shape[0])
        return jnp.dot(left, grad_low[...], preferred_element_type=jnp.float32)

    def up_term(d, s):
        left = rows_from(hidden_turned, (d * n_seq + s) * outs[1].shape[0], outs[1].shape[0])
        return jnp.dot(left, slopes[...], preferred_element_type=jnp.float32)

    def out_term(d, s):
        left = rows_from(context_turned, (d * n_seq + s) * outs[2].shape[0], outs[2].shape[0])
        return jnp.dot(left, grad_low[...], preferred_element_type=jnp.float32)

    def held_term(source):
        return lambda d, s: source[d * n_seq + s].astype(jnp.float32)

    makes = (down_term, up_term, out_term, held_term(partial), held_term(vec))
    stages = (down_stage, up_stage, out_stage, None, None)
    scatters = []
    for k in range(5):
        scatters.append(
            Scatter(
                w,
                "columns" if k == 3 else "line",
                makes[k],
                (None, None, None, partial, vec)[k],
                stages[k],
                units[k],
                (core_sems.at[k], first_sems.at[k], second_sems.at[k], last_sems.at[k]),
                outs[k],
            )
        )
    down, up, out, qkv, small = scatters
    row_sum = LineSum(w, lambda k: row_terms.at[k - 1], row_last, row_sems)
    span = wide // n_dp

    def run(steps):
        for step in steps:
            step()

    ones = jnp.where(lax.broadcasted_iota(jnp.int32, (rows, 128), 1) == 0, 1.0, 0.0).astype(jnp.bfloat16)

    def keep_line(row, line):
        for d in range(n_dp):
            for s in range(n_seq):
                vec[d * n_seq + s, row : row + 1, :] = line[:, d * 128 : (d + 1) * 128]

    def begin():
        loads["mid"].wait()
        grad_low[...] = own_rows[...].astype(jnp.bfloat16)
        loads["gelu"].wait()

    def slope_of(f):
        if f == 0:
            loads["slope"].wait()
        blocks[f].wait()
        grad_gelu = lax.dot_general(
            grad_low[...], down_blocks[f % 2].reshape(span, width), FLAT, preferred_element_type=jnp.float32
        )
        if f + 2 < n_dp:
            blocks[f + 2].start()
        at = slice(f * span, (f + 1) * span)
        slopes[:, at] = (grad_gelu * slopes[:, at].astype(jnp.float32)).astype(jnp.bfloat16)
        if f == n_dp - 1:
            loads["hidden"].wait()

    def hidden_of(e):
        ups[e].wait()
        columns_at = slice(e % shares * width, (e % shares + 1) * width)
        rows_at = slice(e // shares * width // 2, (e // shares + 1) * width // 2)
        own_rows[:, rows_at] += lax.dot_general(
            slopes[:, columns_at],
            up_blocks[e % 2].reshape(width // 2, width),
            FLAT,
            preferred_element_type=jnp.float32,
        )
        if e + 2 < 2 * shares:
            ups[e + 2].start()

    def norm_back():
        load("page", page_in, turned)
        loads["normed"].wait()
        first, grad_gain, grad_shift = norm_backward(
            own_rows[...], normed[...], inv_in[:, :1], sums_in[3:4, :]
        )
        own_rows[...] = first
        grad_low[...] = first.astype(jnp.bfloat16)
        vec[...] = jnp.zeros_like(vec)
        keep_line(3, grad_gain.reshape(1, width))
        keep_line(4, grad_shift.reshape(1, width))

    def send_grads():
        loads["out"].wait()
        for i in (1, 2, 3, 0):
            j = w.zs[i]
            share = part // out_matrix.shape[1]
            block = out_matrix[pl.ds(j * share, share)].reshape(part, width)
            piece = lax.dot_general(grad_low[...], block, FLAT, preferred_element_type=jnp.float32)
            if i:
                grad_sent[i] = piece.astype(jnp.bfloat16)
                w.send(grad_sent.at[i], grads.at[w.z], head_sems.at[i], w.peer(0, i))
            else:
                grads[w.z] = piece.astype(jnp.bfloat16)
        loads["context"].wait()

    def keep_lines():
        up_bias = jnp.sum(slopes[...].astype(jnp.float32), axis=0, keepdims=True)
        for d in range(n_dp * n_seq):
            vec[d, 8:9, :] = up_bias[:, d * 128 : (d + 1) * 128]
        keep_line(2, jnp.sum(grad_low[...].astype(jnp.float32), axis=0, keepdims=True))
        for row in (5, 6, 7):
            keep_line(row, sums_in[row : row + 1, :])

    def prepare():
        for name in ("columns", "query", "key", "value", "turned"):
            loads[name].wait()
        key_grad[...] = jnp.zeros_like(key_grad)
        value_grad[...] = jnp.zeros_like(value_grad)
        for i in range(1, n_seq):
            w.arrived(grads.at[w.zs[i]], head_sems.at[i])
        for h in range(local_heads):
            masked_grad[h] = spread_head(grads, h, head_dim, 1.0)

    def attention(c):
        def head(h, _):
            block = h // per_block
            query, grad = masked_query[h, c], masked_grad[h, c]
            scores = lax.dot_general(
                keys[block], jnp.concatenate([query, ones], axis=1), FLAT, preferred_element_type=jnp.float32
            )
            probs = jnp.exp(scores - logs[c, pl.ds(h, 1), :])
            moved = lax.dot_general(values[block], grad, FLAT, preferred_element_type=jnp.float32)
            centre = jnp.sum(probs * moved, axis=0, keepdims=True)
            slope = (probs * (moved - centre)).astype(jnp.bfloat16)
            query_grad[h] = jnp.dot(key_turned[h], slope, preferred_element_type=jnp.float32) * scale
            key_grad[block] += jnp.dot(slope, query, preferred_element_type=jnp.float32)
            value_grad[block] += jnp.dot(
                probs.astype(jnp.bfloat16), grad, preferred_element_type=jnp.float32
            )
            return 0

        lax.fori_loop(0, local_heads, head, 0)
        project[c * rows : (c + 1) * rows, :part] = (
            query_grad[...].reshape(part, rows).T.astype(jnp.bfloat16)
        )

    def keep_project():
        for t, total in ((1, key_grad), (2, value_grad)):
            for b in range(local_heads // per_block):
                at = t * part + b * 128
                project[:, at : at + 128] = total[b].astype(jnp.bfloat16)

    def row_term(k):
        term = lax.dot_general(
            rows_from(project, w.far[k] * rows, rows),
            columns[...].reshape(width, 3 * part),
            FLAT,
            preferred_element_type=jnp.float32,
        )
        if k:
            row_terms[k - 1] = term.astype(jnp.bfloat16)
            row_sum.offer(k)
        else:
            own_rows[...] += term

    def weight_grad():
        loads["page"].wait()
        for t in range(3):
            at = slice(t * part, (t + 1) * part)
            block = jnp.dot(turned[:width, :], project[:rows, at], preferred_element_type=jnp.float32)
            for s in range(1, n_seq):
                block = block + jnp.dot(
                    turned[s * width : (s + 1) * width, :],
                    project[s * rows : (s + 1) * rows, at],
                    preferred_element_type=jnp.float32,
                )
            partial[:, :, at] = block.astype(jnp.bfloat16).reshape(n_dp * n_seq, -1, part)

    def give_small():
        groups = part // 128
        for b, t in ((0, 0), (1, 2)):
            sums = jnp.sum(project[:, t * part : (t + 1) * part].astype(jnp.float32), axis=0, keepdims=True)
            for g in range(groups):
                for s in range(n_seq):
                    vec[(w.z * groups + g) * n_seq + s, b : b + 1, :] = sums[:, g * 128 : (g + 1) * 128]
        run(small.give_steps())

    actions = {
        "b0": begin,
        "ln": norm_back,
        "gc": send_grads,
        "kl": keep_lines,
        "at": prepare,
        "pk": keep_project,
        "gw": weight_grad,
        "qg": lambda: run(qkv.give_steps()),
        "vg": give_small,
        "rF": lambda: row_sum.finish(lambda at: own_rows[at, :], grad_rows),
    }
    for k in range(2 * shares):
        actions["h%d" % k] = lambda k=k: hidden_of(k)
    for k in range(n_dp):
        actions["f%d" % k] = lambda k=k: slope_of(k)
    for k in range(n_seq):
        actions["a%d" % k] = lambda k=k: attention(k)
        actions["r%d" % k] = lambda k=k: row_term(k)
        if k:
            actions["l%d" % k] = lambda k=k: row_sum.relay(k)
    for name, members in (("q", (qkv, small)), ("o", (out,)), ("u", (up,)), ("d", (down,))):
        for k in range(4):
            if name != "q":
                actions["%sg%d" % (name, k)] = lambda m=members, k=k: [unit.give(k) for unit in m]
            actions["%sk%d" % (name, k)] = lambda m=members, k=k: [unit.over_cores(k) for unit in m]
            actions["%sc%d" % (name, k)] = lambda m=members, k=k: [unit.over_chips(k) for unit in m]
            actions["%st%d" % (name, k)] = lambda m=members, k=k: [unit.to_seq(k) for unit in m]
            if k:
                actions["%sr%d" % (name, k)] = lambda m=members, k=k: [unit.relay(k) for unit in m]
        actions[name + "F"] = lambda m=members: [unit.finish() for unit in m]
    for name in BACK_ORDER:
        actions[name]()
    w.drain()


def back(sizes, heads, saved, w_shapes):
    n_dp, n_seq = sizes
    devices = n_dp * n_seq
    mid, normed, _, _, logs, page, query, key, value, key_turned, context, hidden, gelu, slopes = saved[:14]
    columns, full_out, full_up, full_down = saved[14:]
    count, width = normed.shape
    part = width // n_seq
    stream = count * n_seq
    local_heads, head_dim, _ = key_turned.shape
    blocks = part // 128
    low = jnp.bfloat16
    shapes = [w_shapes[0], w_shapes[1], w_shapes[2], columns.shape[1:], (16, 128)]
    kinds = [low] * 4 + [jnp.float32]
    results = [jax.ShapeDtypeStruct(shape, jnp.float32) for shape in shapes]
    results[3] = jax.ShapeDtypeStruct((n_seq,) + shapes[3], jnp.float32)
    anywhere = pl.BlockSpec(memory_space=pl.ANY)
    local = pl.BlockSpec(memory_space=pltpu.VMEM)
    sends = 5 * (4 + 3 * n_seq + 6) + 6 + n_seq - 1
    chips = n_dp // 2

    def like(array):
        return pltpu.VMEM(array.shape, array.dtype)

    scratch = [
        pltpu.SemaphoreType.DMA((sends,)),
        pltpu.SemaphoreType.DMA((5, chips)),
        pltpu.SemaphoreType.DMA((5, n_seq, 2)),
        pltpu.SemaphoreType.DMA((5, n_seq)),
        pltpu.SemaphoreType.DMA((5, 5)),
        pltpu.SemaphoreType.DMA((2, 2)),
        pltpu.SemaphoreType.DMA((n_seq,)),
        pltpu.SemaphoreType.DMA((13,)),
        pltpu.SemaphoreType.DMA((5,)),
        pltpu.VMEM((n_seq, count, part), low),
        like(query),
        like(key),
        like(value),
        like(key_turned),
        like(query),
        pltpu.VMEM((local_heads, head_dim, count), jnp.float32),
        pltpu.VMEM((blocks, stream, 128), jnp.float32),
        pltpu.VMEM((blocks, stream, 128), jnp.float32),
        pltpu.VMEM((stream, 3 * part), low),
        like(gelu),
        like(columns),
        pltpu.VMEM((devices, 16, 128), jnp.float32),
        pltpu.VMEM((n_seq - 1, count, width), low),
        pltpu.VMEM((5, count, width), low),
        pltpu.VMEM((count, width), jnp.float32),
        like(columns),
        like(hidden),
        like(context),
        like(slopes),
        like(normed),
        pltpu.VMEM((count, width), low),
        pltpu.VMEM((n_seq, count, part), low),
        like(full_out),
        pltpu.VMEM((2, n_seq) + shapes[0], low),
        pltpu.VMEM((2, devices // 2) + full_up.shape[2:], low),
        pltpu.VMEM((2, n_seq) + shapes[0], low),
        pltpu.VMEM((2, n_seq) + shapes[1], low),
        pltpu.VMEM((4, n_seq) + shapes[2], low),
    ]
    for shape, kind in zip(shapes, kinds):
        scratch += [
            pltpu.VMEM((chips, n_seq) + shape, kind),
            pltpu.VMEM((n_seq, 2) + shape, kind),
            pltpu.VMEM((n_seq,) + shape, kind),
            pltpu.VMEM((5,) + shape, kind),
        ]
    return pl.pallas_call(
        lambda *refs: back_kernel(sizes, heads, *refs),
        out_shape=[jax.ShapeDtypeStruct((count, width), low)] + results,
        in_specs=[anywhere] * 2 + [local] * 3 + [anywhere] * 13,
        out_specs=[local] * 6,
        scratch_shapes=scratch,
        compiler_params=pltpu.CompilerParams(
            collective_id=1, has_side_effects=True, vmem_limit_bytes=63 * 2**20
        ),
        name="back",
    )(*saved)


def spread_lanes(vectors, n_seq):
    stacked = jnp.stack(vectors).astype(jnp.float32)
    tiled = jnp.tile(stacked, (1, n_seq))
    owner = jnp.arange(tiled.shape[1], dtype=jnp.int32) // stacked.shape[1]
    return jnp.where(owner[None, :] == lax.axis_index("seq"), tiled, 0.0)


def kernel_plan(
    x_in,
    w_qkv,
    q_bias,
    v_bias,
    w_out,
    out_bias,
    ln1_gain,
    ln1_shift,
    w_up,
    up_bias,
    w_down,
    down_bias,
    ln2_gain,
    ln2_shift,
    valid,
    cotangent,
):
    sizes = (lax.axis_size("dp"), lax.axis_size("seq"))
    n_dp, groups = sizes
    rows = x_in[0]
    count, width = rows.shape
    vectors = (q_bias, v_bias, out_bias, ln1_gain, ln1_shift, down_bias, ln2_gain, ln2_shift)
    spread = spread_lanes(vectors, groups)
    vec = jnp.concatenate(
        [spread, up_bias.astype(jnp.float32)[None], jnp.zeros((7, spread.shape[1]), jnp.float32)]
    )
    third = width // groups
    w_columns = (
        w_qkv.reshape(-1, 3, groups, third).transpose(2, 0, 1, 3).reshape(groups, -1, 3 * third)
    )
    (
        columns,
        full_out,
        full_up,
        full_down,
        page_turned,
        query,
        key,
        value,
        key_turned,
        context,
        logs,
        hidden,
        gelu,
        slopes,
        output,
        normed,
        inv,
        grad_mid,
        line_sums,
    ) = front(sizes, HEADS, valid, rows, cotangent[0], vec, w_columns, w_out, w_up, w_down)
    saved = (grad_mid, normed, inv, line_sums, logs, page_turned, query, key, value, key_turned)
    saved += (context, hidden, gelu, slopes, columns, full_out, full_up, full_down)
    devices = n_dp * groups
    grad_rows, *sums = back(sizes, HEADS, saved, (w_down.shape, w_up.shape, w_out.shape))
    vec_sums = sums[4]
    mine = lax.dynamic_slice(
        vec_sums[:8], (0, lax.axis_index("seq") * (width // devices)), (8, width // devices)
    )
    return (
        output[None],
        grad_rows[None],
        sums[3].reshape(groups, -1, 3, third).transpose(1, 2, 0, 3).reshape(-1, 3 * width),
        mine[0],
        mine[1],
        sums[2],
        mine[2],
        mine[3],
        mine[4],
        sums[1],
        vec_sums[8],
        sums[0],
        mine[5],
        mine[6],
        mine[7],
    )


def solution(mesh):
    n_dp, n_seq = mesh.shape["dp"], mesh.shape["seq"]

    def per_device(x_in, w_qkv, *rest):
        part, width = w_qkv.shape[0], x_in.shape[2]
        fits = (n_dp, n_seq) == (8, 4) and part % 32 == 0 and part * n_seq == 128 and width // n_seq % 128 == 0 and x_in.shape[0] == 1
        plan = kernel_plan if fits else general_plan
        return plan(x_in, w_qkv, *rest)

    return jax.shard_map(
        per_device,
        mesh=mesh,
        in_specs=(
            P("dp", "seq", None),
            P(("dp", "seq"), None),
            P(("dp", "seq")),
            P(("dp", "seq")),
            P(("dp", "seq"), None),
            P(("dp", "seq")),
            P(("dp", "seq")),
            P(("dp", "seq")),
            P(("dp", "seq"), None),
            P(("dp", "seq")),
            P(("dp", "seq"), None),
            P(("dp", "seq")),
            P(("dp", "seq")),
            P(("dp", "seq")),
            P("dp"),
            P("dp", "seq", None),
        ),
        out_specs=(
            P("dp", "seq", None),
            P("dp", "seq", None),
            P(("dp", "seq"), None),
            P(("dp", "seq")),
            P(("dp", "seq")),
            P(("dp", "seq"), None),
            P(("dp", "seq")),
            P(("dp", "seq")),
            P(("dp", "seq")),
            P(("dp", "seq"), None),
            P(("dp", "seq")),
            P(("dp", "seq"), None),
            P(("dp", "seq")),
            P(("dp", "seq")),
            P(("dp", "seq")),
        ),
        check_vma=False,
    )
```

```python
import math

import jax
import jax.numpy as jnp
from jax import lax
from jax.experimental import pallas as pl
from jax.experimental.pallas import tpu as pltpu
from jax.sharding import PartitionSpec as P

HEADS = 16


eps_norm = 1e-05


def outer_sum(left, right):
    return lax.dot_general(
        left, right, (((0,), (0,)), ((), ())), preferred_element_type=jnp.float32
    )


def times_back(rows, matrix):
    return lax.dot_general(
        rows, matrix, (((1,), (1,)), ((), ())), preferred_element_type=jnp.float32
    )


def gelu_exact(values):
    return jax.nn.gelu(values, approximate=False)


def norm_forward(rows, gain, shift):
    center = rows - jnp.mean(rows, axis=-1, keepdims=True)
    inv_std = lax.rsqrt(jnp.mean(center * center, axis=-1, keepdims=True) + eps_norm)
    normed = center * inv_std
    return (normed * gain + shift, normed, inv_std)


def norm_backward(grad_out, normed, inv_std, gain):
    scaled = grad_out * gain
    grad_rows = inv_std * (
        scaled
        - jnp.mean(scaled, axis=-1, keepdims=True)
        - normed * jnp.mean(scaled * normed, axis=-1, keepdims=True)
    )
    return (grad_rows, jnp.sum(grad_out * normed, axis=0), jnp.sum(grad_out, axis=0))


def to_heads(rows, groups):
    count, width = rows.shape
    return rows.reshape(count, groups, width // groups).transpose(1, 0, 2).reshape(groups, -1)


def from_heads(pieces, part_width):
    groups = pieces.shape[0]
    return (
        pieces.reshape(groups, -1, part_width).transpose(1, 0, 2).reshape(-1, groups * part_width)
    )


def general_plan(
    x_in,
    w_qkv,
    q_bias,
    v_bias,
    w_out,
    out_bias,
    ln1_gain,
    ln1_shift,
    w_up,
    up_bias,
    w_down,
    down_bias,
    ln2_gain,
    ln2_shift,
    valid,
    cotangent,
):
    shards = (
        w_qkv,
        q_bias,
        v_bias,
        w_out,
        out_bias,
        ln1_gain,
        ln1_shift,
        w_up,
        up_bias,
        w_down,
        down_bias,
        ln2_gain,
        ln2_shift,
    )
    weights = (
        lax.all_gather(shards[0], ("dp", "seq"), axis=0, tiled=True),
        lax.all_gather(shards[1], ("dp", "seq"), axis=0, tiled=True),
        lax.all_gather(shards[2], ("dp", "seq"), axis=0, tiled=True),
        lax.all_gather(shards[3], ("dp", "seq"), axis=0, tiled=True),
        lax.all_gather(shards[4], ("dp", "seq"), axis=0, tiled=True),
        lax.all_gather(shards[5], ("dp", "seq"), axis=0, tiled=True),
        lax.all_gather(shards[6], ("dp", "seq"), axis=0, tiled=True),
        lax.all_gather(shards[7], ("dp", "seq"), axis=0, tiled=True),
        lax.all_gather(shards[8], ("dp", "seq"), axis=0, tiled=True),
        lax.all_gather(shards[9], ("dp", "seq"), axis=0, tiled=True),
        lax.all_gather(shards[10], ("dp", "seq"), axis=0, tiled=True),
        lax.all_gather(shards[11], ("dp", "seq"), axis=0, tiled=True),
        lax.all_gather(shards[12], ("dp", "seq"), axis=0, tiled=True),
    )
    (
        full_qkv,
        full_qbias,
        full_vbias,
        full_out,
        full_obias,
        full_gain1,
        full_shift1,
        full_up,
        full_ubias,
        full_down,
        full_dbias,
        full_gain2,
        full_shift2,
    ) = weights
    groups = lax.axis_size("seq")
    rows = x_in[0]
    count, width = rows.shape
    head_dim = width // HEADS
    part_width = width // groups
    local_heads = HEADS // groups
    stream = count * groups
    qrows = min(512, stream)
    nblocks = stream // qrows
    scale = 1.0 / math.sqrt(head_dim)
    keep = jnp.arange(stream, dtype=jnp.int32) < valid[0]
    bias_row = jnp.concatenate([full_qbias, jnp.zeros_like(full_qbias), full_vbias]).astype(
        jnp.float32
    )
    project = (jnp.dot(rows, full_qkv, preferred_element_type=jnp.float32) + bias_row).astype(
        jnp.bfloat16
    )
    sent = (
        to_heads(project[:, :width], groups),
        to_heads(project[:, width : 2 * width], groups),
        to_heads(project[:, 2 * width :], groups),
    )
    arrived = (
        lax.all_to_all(sent[0], "seq", split_axis=0, concat_axis=0, tiled=True),
        lax.all_to_all(sent[1], "seq", split_axis=0, concat_axis=0, tiled=True),
        lax.all_to_all(sent[2], "seq", split_axis=0, concat_axis=0, tiled=True),
    )
    query_blocks = arrived[0].reshape(nblocks, qrows, local_heads, head_dim)
    key_heads = arrived[1].reshape(stream, local_heads, head_dim)
    value_heads = arrived[2].reshape(stream, local_heads, head_dim)

    def masked_scores(query):
        scores = (
            jnp.einsum("qhd,khd->hqk", query, key_heads, preferred_element_type=jnp.float32) * scale
        )
        return jnp.where(keep[None, None, :], scores, -1e30)

    def attend_forward(query):
        scores = masked_scores(query)
        peak = jnp.max(scores, axis=-1, keepdims=True)
        raised = jnp.exp(scores - peak)
        total = jnp.sum(raised, axis=-1, keepdims=True)
        probs = (raised / total).astype(jnp.bfloat16)
        context = jnp.einsum("hqk,khd->qhd", probs, value_heads, preferred_element_type=jnp.float32)
        return (context.astype(jnp.bfloat16), (peak + jnp.log(total))[..., 0])

    context, log_sums = lax.map(attend_forward, query_blocks)
    returned_ctx = lax.all_to_all(
        context.reshape(groups, -1), "seq", split_axis=0, concat_axis=0, tiled=True
    )
    context_rows = from_heads(returned_ctx, part_width)
    attn_out = jnp.dot(
        context_rows, full_out, preferred_element_type=jnp.float32
    ) + full_obias.astype(jnp.float32)
    first_rows = rows.astype(jnp.float32) + attn_out
    hidden, normed_one, inv_one = norm_forward(
        first_rows, full_gain1.astype(jnp.float32), full_shift1.astype(jnp.float32)
    )
    hidden_low = hidden.astype(jnp.bfloat16)
    up_act = jnp.dot(hidden_low, full_up, preferred_element_type=jnp.float32) + full_ubias.astype(
        jnp.float32
    )
    gelu_low = gelu_exact(up_act).astype(jnp.bfloat16)
    branch = jnp.dot(gelu_low, full_down, preferred_element_type=jnp.float32) + full_dbias.astype(
        jnp.float32
    )
    output, normed_two, inv_two = norm_forward(
        hidden + branch, full_gain2.astype(jnp.float32), full_shift2.astype(jnp.float32)
    )
    again = (
        lax.all_gather(shards[0], ("dp", "seq"), axis=0, tiled=True),
        lax.all_gather(shards[1], ("dp", "seq"), axis=0, tiled=True),
        lax.all_gather(shards[2], ("dp", "seq"), axis=0, tiled=True),
        lax.all_gather(shards[3], ("dp", "seq"), axis=0, tiled=True),
        lax.all_gather(shards[4], ("dp", "seq"), axis=0, tiled=True),
        lax.all_gather(shards[5], ("dp", "seq"), axis=0, tiled=True),
        lax.all_gather(shards[6], ("dp", "seq"), axis=0, tiled=True),
        lax.all_gather(shards[7], ("dp", "seq"), axis=0, tiled=True),
        lax.all_gather(shards[8], ("dp", "seq"), axis=0, tiled=True),
        lax.all_gather(shards[9], ("dp", "seq"), axis=0, tiled=True),
        lax.all_gather(shards[10], ("dp", "seq"), axis=0, tiled=True),
        lax.all_gather(shards[11], ("dp", "seq"), axis=0, tiled=True),
        lax.all_gather(shards[12], ("dp", "seq"), axis=0, tiled=True),
    )
    back_qkv, back_out, back_gain1, back_up, back_down, back_gain2 = (
        again[0],
        again[3],
        again[5],
        again[7],
        again[9],
        again[11],
    )
    grad_out = cotangent[0].astype(jnp.float32)
    grad_mid, grad_ln2_gain, grad_ln2_shift = norm_backward(
        grad_out, normed_two, inv_two, back_gain2.astype(jnp.float32)
    )
    grad_branch = grad_mid.astype(jnp.bfloat16)
    grad_w_down = outer_sum(gelu_low, grad_branch)
    grad_down_bias = jnp.sum(grad_branch.astype(jnp.float32), axis=0)
    grad_gelu = times_back(grad_branch, back_down)
    grad_up = jax.vjp(gelu_exact, up_act)[1](grad_gelu)[0].astype(jnp.bfloat16)
    grad_w_up = outer_sum(hidden_low, grad_up)
    grad_up_bias = jnp.sum(grad_up.astype(jnp.float32), axis=0)
    grad_hidden = times_back(grad_up, back_up) + grad_mid
    grad_first, grad_ln1_gain, grad_ln1_shift = norm_backward(
        grad_hidden, normed_one, inv_one, back_gain1.astype(jnp.float32)
    )
    grad_attn = grad_first.astype(jnp.bfloat16)
    grad_w_out = outer_sum(context_rows, grad_attn)
    grad_out_bias = jnp.sum(grad_attn.astype(jnp.float32), axis=0)
    grad_context = times_back(grad_attn, back_out).astype(jnp.bfloat16)
    grad_ctx_heads = lax.all_to_all(
        to_heads(grad_context, groups), "seq", split_axis=0, concat_axis=0, tiled=True
    )
    grad_ctx_blocks = grad_ctx_heads.reshape(nblocks, qrows, local_heads, head_dim)

    def attend_backward(carry, inputs):
        key_total, value_total = carry
        query, grad_ctx, log_rows = inputs
        scores = masked_scores(query)
        probs = jnp.exp(scores - log_rows[..., None])
        probs_low = probs.astype(jnp.bfloat16)
        d_probs = jnp.einsum(
            "qhd,khd->hqk", grad_ctx, value_heads, preferred_element_type=jnp.float32
        )
        centre = jnp.sum(probs * d_probs, axis=-1, keepdims=True)
        grad_scores = (probs * (d_probs - centre)).astype(jnp.bfloat16)
        grad_query = (
            jnp.einsum("hqk,khd->qhd", grad_scores, key_heads, preferred_element_type=jnp.float32)
            * scale
        )
        key_total = (
            key_total
            + jnp.einsum("hqk,qhd->khd", grad_scores, query, preferred_element_type=jnp.float32)
            * scale
        )
        value_total = value_total + jnp.einsum(
            "hqk,qhd->khd", probs_low, grad_ctx, preferred_element_type=jnp.float32
        )
        return ((key_total, value_total), grad_query.astype(jnp.bfloat16))

    empty = jnp.zeros((stream, local_heads, head_dim), jnp.float32)
    (key_total, value_total), grad_query = lax.scan(
        attend_backward, (empty, empty), (query_blocks, grad_ctx_blocks, log_sums)
    )
    grad_key = key_total.astype(jnp.bfloat16)
    grad_value = value_total.astype(jnp.bfloat16)
    grad_pieces = (
        lax.all_to_all(
            grad_query.reshape(groups, -1), "seq", split_axis=0, concat_axis=0, tiled=True
        ),
        lax.all_to_all(
            grad_key.reshape(groups, -1), "seq", split_axis=0, concat_axis=0, tiled=True
        ),
        lax.all_to_all(
            grad_value.reshape(groups, -1), "seq", split_axis=0, concat_axis=0, tiled=True
        ),
    )
    grad_project = jnp.concatenate(
        [
            from_heads(grad_pieces[0], part_width),
            from_heads(grad_pieces[1], part_width),
            from_heads(grad_pieces[2], part_width),
        ],
        axis=1,
    )
    grad_w_qkv = outer_sum(rows, grad_project)
    bias_sums = jnp.sum(grad_project.astype(jnp.float32), axis=0)
    grad_q_bias = bias_sums[:width]
    grad_v_bias = bias_sums[2 * width :]
    grad_rows = times_back(grad_project, back_qkv) + grad_first
    terms = (
        grad_w_qkv,
        grad_q_bias,
        grad_v_bias,
        grad_w_out,
        grad_out_bias,
        grad_ln1_gain,
        grad_ln1_shift,
        grad_w_up,
        grad_up_bias,
        grad_w_down,
        grad_down_bias,
        grad_ln2_gain,
        grad_ln2_shift,
    )
    page_sums = (
        lax.psum_scatter(
            terms[0].astype(jnp.bfloat16), "dp", scatter_dimension=0, tiled=True
        ).astype(jnp.float32),
        lax.psum_scatter(
            terms[1].astype(jnp.bfloat16), "dp", scatter_dimension=0, tiled=True
        ).astype(jnp.float32),
        lax.psum_scatter(
            terms[2].astype(jnp.bfloat16), "dp", scatter_dimension=0, tiled=True
        ).astype(jnp.float32),
        lax.psum_scatter(
            terms[3].astype(jnp.bfloat16), "dp", scatter_dimension=0, tiled=True
        ).astype(jnp.float32),
        lax.psum_scatter(
            terms[4].astype(jnp.bfloat16), "dp", scatter_dimension=0, tiled=True
        ).astype(jnp.float32),
        lax.psum_scatter(
            terms[5].astype(jnp.bfloat16), "dp", scatter_dimension=0, tiled=True
        ).astype(jnp.float32),
        lax.psum_scatter(
            terms[6].astype(jnp.bfloat16), "dp", scatter_dimension=0, tiled=True
        ).astype(jnp.float32),
        lax.psum_scatter(
            terms[7].astype(jnp.bfloat16), "dp", scatter_dimension=0, tiled=True
        ).astype(jnp.float32),
        lax.psum_scatter(
            terms[8].astype(jnp.bfloat16), "dp", scatter_dimension=0, tiled=True
        ).astype(jnp.float32),
        lax.psum_scatter(
            terms[9].astype(jnp.bfloat16), "dp", scatter_dimension=0, tiled=True
        ).astype(jnp.float32),
        lax.psum_scatter(
            terms[10].astype(jnp.bfloat16), "dp", scatter_dimension=0, tiled=True
        ).astype(jnp.float32),
        lax.psum_scatter(
            terms[11].astype(jnp.bfloat16), "dp", scatter_dimension=0, tiled=True
        ).astype(jnp.float32),
        lax.psum_scatter(
            terms[12].astype(jnp.bfloat16), "dp", scatter_dimension=0, tiled=True
        ).astype(jnp.float32),
    )
    sums = (
        lax.psum_scatter(
            page_sums[0].astype(jnp.bfloat16), "seq", scatter_dimension=0, tiled=True
        ).astype(jnp.float32),
        lax.psum_scatter(
            page_sums[1].astype(jnp.bfloat16), "seq", scatter_dimension=0, tiled=True
        ).astype(jnp.float32),
        lax.psum_scatter(
            page_sums[2].astype(jnp.bfloat16), "seq", scatter_dimension=0, tiled=True
        ).astype(jnp.float32),
        lax.psum_scatter(
            page_sums[3].astype(jnp.bfloat16), "seq", scatter_dimension=0, tiled=True
        ).astype(jnp.float32),
        lax.psum_scatter(
            page_sums[4].astype(jnp.bfloat16), "seq", scatter_dimension=0, tiled=True
        ).astype(jnp.float32),
        lax.psum_scatter(
            page_sums[5].astype(jnp.bfloat16), "seq", scatter_dimension=0, tiled=True
        ).astype(jnp.float32),
        lax.psum_scatter(
            page_sums[6].astype(jnp.bfloat16), "seq", scatter_dimension=0, tiled=True
        ).astype(jnp.float32),
        lax.psum_scatter(
            page_sums[7].astype(jnp.bfloat16), "seq", scatter_dimension=0, tiled=True
        ).astype(jnp.float32),
        lax.psum_scatter(
            page_sums[8].astype(jnp.bfloat16), "seq", scatter_dimension=0, tiled=True
        ).astype(jnp.float32),
        lax.psum_scatter(
            page_sums[9].astype(jnp.bfloat16), "seq", scatter_dimension=0, tiled=True
        ).astype(jnp.float32),
        lax.psum_scatter(
            page_sums[10].astype(jnp.bfloat16), "seq", scatter_dimension=0, tiled=True
        ).astype(jnp.float32),
        lax.psum_scatter(
            page_sums[11].astype(jnp.bfloat16), "seq", scatter_dimension=0, tiled=True
        ).astype(jnp.float32),
        lax.psum_scatter(
            page_sums[12].astype(jnp.bfloat16), "seq", scatter_dimension=0, tiled=True
        ).astype(jnp.float32),
    )
    return (
        output.astype(jnp.bfloat16)[None],
        grad_rows.astype(jnp.bfloat16)[None],
        sums[0],
        sums[1],
        sums[2],
        sums[3],
        sums[4],
        sums[5],
        sums[6],
        sums[7],
        sums[8],
        sums[9],
        sums[10],
        sums[11],
        sums[12],
    )


MESH = pl.DeviceIdType.MESH
CHUNK = 256
MASKED = -1e30
FLAT = (((1,), (1,)), ((), ()))


def flip(index, mask):
    for b in range(mask.bit_length()):
        if mask >> b & 1:
            bit = 1 << b
            index = index + bit - 2 * bit * (index // bit % 2)
    return index


def guarded(when, action):
    if when is None:
        action()
    else:
        pl.when(when)(action)


class Wires:
    def __init__(self, sems, sizes):
        self.sems, self.sizes = sems, sizes
        self.dp, self.z = lax.axis_index("dp"), lax.axis_index("seq")
        self.dps = [flip(self.dp, m) for m in range(sizes[0])]
        self.zs = [flip(self.z, m) for m in range(sizes[1])]
        last = sizes[1] - 1
        half = self.z // 2
        step = 1 - 2 * half
        depth = self.z * step + last * half
        self.inner, self.outer = depth == 1, depth == 0
        self.right = self.z + step
        self.left = self.z - step * depth
        self.far = [self.z] + [t * step + last * half for t in (1 - depth, 2, 3)]
        self.started = []

    def peer(self, offset, step):
        return (self.dps[offset], self.zs[step])

    def send(self, src, dst, recv_sem, device, when=None):
        copy = pltpu.make_async_remote_copy(
            src_ref=src,
            dst_ref=dst,
            send_sem=self.sems.at[len(self.started)],
            recv_sem=recv_sem,
            device_id=device,
            device_id_type=MESH,
        )
        guarded(when, copy.start)
        self.started.append((copy, when))
        return len(self.started) - 1

    def sent(self, index):
        copy, when = self.started[index]
        guarded(when, copy.wait_send)
        self.started[index] = None

    def arrived(self, dst, recv_sem, when=None):
        copy = pltpu.make_async_remote_copy(
            src_ref=dst,
            dst_ref=dst,
            send_sem=self.sems.at[0],
            recv_sem=recv_sem,
            device_id=self.peer(1, 0),
            device_id_type=MESH,
        )
        guarded(when, copy.wait_recv)

    def drain(self):
        for index, entry in enumerate(self.started):
            if entry is not None:
                self.sent(index)

    def greet(self):
        n_dp, n_seq = self.sizes
        barrier = pltpu.get_barrier_semaphore()
        masks = [1 << b for b in range(n_dp.bit_length() - 1)]
        partners = [self.peer(m, 0) for m in masks] + [self.peer(0, i) for i in range(1, n_seq)]
        for device in partners:
            pl.semaphore_signal(barrier, inc=1, device_id=device, device_id_type=MESH)
        pl.semaphore_wait(barrier, len(partners))


class Line:
    def __init__(self, wires, slot, recv):
        self.w, self.slot, self.recv = wires, slot, recv

    def pass_on(self, k, src, to_left):
        w = self.w
        s = w.far[k]
        dst = self.slot(s)
        if to_left:
            w.send(src, dst, self.recv.at[s], (w.dp, w.left), w.inner)
        else:
            w.send(src, dst, self.recv.at[s], (w.dp, w.right), None if k == 0 else w.inner)

    def own(self, src):
        self.pass_on(0, src, False)
        self.pass_on(0, src, True)

    def take(self, k):
        s = self.w.far[k]
        self.w.arrived(self.slot(s), self.recv.at[s])
        self.pass_on(k, self.slot(s), k > 1)

    def relay(self, k):
        s = self.w.far[k]
        self.w.arrived(self.slot(s), self.recv.at[s], self.w.inner)
        self.pass_on(k, self.slot(s), k > 1)

    def end(self, k):
        s = self.w.far[k]
        self.w.arrived(self.slot(s), self.recv.at[s], self.w.outer)


class Gather:
    def __init__(self, wires, src, full, recv, local):
        self.w, self.src, self.full, self.recv, self.local = wires, src, full, recv, local
        n_dp, self.n_seq = wires.sizes
        self.chips = [1 << b for b in range(1, n_dp.bit_length() - 1)]
        self.slots = wires.far
        self.line = Line(wires, lambda s: full.at[wires.dp * self.n_seq + s], recv.at[0])

    def at(self, offset, step):
        return self.full.at[self.w.dps[offset] * self.n_seq + self.slots[step]]

    def order(self, step):
        return self.chips if step % 2 == 0 else self.chips[::-1]

    def forward(self, src, offset, step, masks):
        for m in masks:
            sem = self.recv.at[offset ^ m, self.slots[step]]
            self.w.send(src, self.at(offset, step), sem, self.w.peer(m, 0))

    def wait(self, offset, step):
        self.w.arrived(self.at(offset, step), self.recv.at[offset, self.slots[step]])

    def mine(self):
        return self.src

    def own_chips(self):
        self.kept = pltpu.make_async_copy(self.mine(), self.at(0, 0), self.local)
        self.kept.start()
        self.forward(self.mine(), 0, 0, self.order(0) + [1])

    def own_seq(self):
        self.line.own(self.src)

    def along_seq(self, i):
        self.line.take(i)
        self.forward(self.at(0, i), 0, i, self.order(i) + [1])

    def stages(self, step):
        have, out = [0], []
        masks = self.order(step)
        for t, m in enumerate(masks):
            out.append([(o ^ m, masks[t + 1 :] + [1]) for o in have])
            have = have + [o ^ m for o in have]
        return out

    def over_chips(self, t, step):
        for offset, masks in self.stages(step)[t]:
            self.wait(offset, step)
            self.forward(self.at(offset, step), offset, step, masks)

    def over_cores(self):
        n_dp = self.w.sizes[0]
        for offset in range(1, n_dp, 2):
            for i in range(self.n_seq):
                self.wait(offset, i)
        self.kept.wait()


class GatherDirect(Gather):
    def __init__(self, *args):
        super().__init__(*args)
        self.slots = self.w.zs

    def part_for(self, i):
        return self.src

    def own_seq(self):
        for i in range(1, self.n_seq):
            sem = self.recv.at[0, self.w.z]
            self.w.send(self.part_for(i), self.at(0, 0), sem, self.w.peer(0, i))

    def along_seq(self, i):
        self.wait(0, i)
        self.forward(self.at(0, i), 0, i, self.order(i) + [1])


class GatherColumns(GatherDirect):
    def mine(self):
        return self.src.at[self.w.z]

    def part_for(self, i):
        return self.src.at[self.w.zs[i]]


def sends_of_gather(n_dp, n_seq):
    return 2 + n_seq - 1 + n_seq * (n_dp - 1)


def group_lanes(packed, row, group, n_seq):
    total = packed[group * n_seq, row : row + 1, :]
    for s in range(1, n_seq):
        total = total + packed[group * n_seq + s, row : row + 1, :]
    return total


def spread_head(source, h, head_dim, factor):
    n_seq, rows, _ = source.shape
    block = h * head_dim // 128 * 128
    low = h * head_dim % 128
    lane = lax.broadcasted_iota(jnp.int32, (n_seq * rows, 128), 1)
    values = source[:, :, block : block + 128].reshape(n_seq * rows, 128).astype(jnp.float32)
    kept = jnp.where((lane >= low) & (lane < low + head_dim), values * factor, 0.0)
    return kept.astype(jnp.bfloat16).reshape(n_seq, rows, 128)


def front_kernel(
    sizes,
    heads,
    valid_ref,
    x_ref,
    cotangent,
    lines_ref,
    up_line_ref,
    qkv_shard,
    out_ref,
    up_ref,
    down_ref,
    columns_out,
    full_out,
    full_up,
    full_down,
    page_out,
    query_out,
    key_out,
    value_out,
    key_turned_out,
    context_out,
    logs_out,
    hidden_out,
    gelu_out,
    slope_out,
    output,
    normed_one,
    inv_one,
    grad_mid,
    sums_out,
    vec_own,
    qkv_own,
    packed,
    columns,
    page,
    held,
    context_sent,
    context_held,
    context_turned,
    value_turned,
    masked_query,
    keys,
    values,
    key_turned,
    logs,
    out_matrix,
    up_matrix,
    down_matrix,
    page_turned,
    context_rows_turned,
    hidden,
    hidden_low,
    hidden_turned,
    gelu_low,
    gelu_turned,
    slopes,
    branch,
    send_sems,
    gather_sems,
    page_sems,
    context_sems,
    local_sems,
):
    n_dp, n_seq = sizes
    w = Wires(send_sems, sizes)
    rows, width = x_ref.shape
    part = width // n_seq
    head_dim = width // heads
    local_heads = heads // n_seq
    stream = rows * n_seq
    low_lane = lax.broadcasted_iota(jnp.int32, (8, 128), 1) // lines_ref.shape[1]
    lines = jnp.concatenate([lines_ref[...].astype(jnp.float32)] * n_seq, axis=1)
    vec_own[:8, :] = jnp.where(low_lane == w.z, lines, 0.0)
    vec_own[8:, :] = jnp.broadcast_to(up_line_ref[...].astype(jnp.float32), (8, 128))
    for t in range(3):
        for j in range(n_seq):
            at = t * width + j * part
            qkv_own[j, :, t * part : (t + 1) * part] = qkv_shard[:, at : at + part]
    w.greet()
    line = Line(w, lambda s: page.at[s], page_sems)
    sources = (
        (vec_own, packed),
        (qkv_own, columns),
        (out_ref, out_matrix),
        (up_ref, up_matrix),
        (down_ref, down_matrix),
    )
    vec, qkv, out, up, down = [
        (GatherDirect, GatherColumns, Gather, Gather, Gather)[k](w, src, dst, gather_sems.at[k], local_sems.at[k])
        for k, (src, dst) in enumerate(sources)
    ]
    def run(steps):
        for step in steps:
            step()

    keeps = []

    def keep(src, dst):
        keeps.append(pltpu.make_async_copy(src, dst, local_sems.at[5 + len(keeps)]))
        keeps[-1].start()

    per_block = 128 // head_dim
    scale = 1.0 / math.sqrt(head_dim)
    groups = part // 128
    one_lane = lax.broadcasted_iota(jnp.int32, (rows, 128), 1)
    ones = jnp.where(one_lane == 0, 1.0, 0.0).astype(jnp.bfloat16)
    chunk = 512
    chunks = up_matrix.shape[2] // chunk
    per_chunk = chunk // down_matrix.shape[1]
    per_part = part // out_matrix.shape[1]

    def line_of(row):
        return jnp.concatenate([group_lanes(packed, row, d, n_seq) for d in range(n_dp)], axis=1)

    def gathered_columns():
        qkv.over_cores()
        vec.over_cores()
        keep(columns, columns_out)

    def project(k):
        s = w.far[k]
        if k == 0:
            page[s] = x_ref[...]
        matrix = columns[...].reshape(width, 3 * part)
        piece = jnp.dot(page[s], matrix, preferred_element_type=jnp.float32)
        for t in range(3):
            third = piece[:, t * part : (t + 1) * part]
            if t != 1:
                bias = [group_lanes(packed, t // 2, w.z * groups + g, n_seq) for g in range(groups)]
                third = third + jnp.concatenate(bias, axis=1)
            held[t, s] = third.astype(jnp.bfloat16)

    def prepare():
        position = lax.broadcasted_iota(jnp.int32, (stream, 128), 0)
        lane = lax.broadcasted_iota(jnp.int32, (stream, 128), 1)
        guard = jnp.where((position >= valid_ref[0]) & (lane == 0), MASKED, 0.0).astype(jnp.bfloat16)
        for h in range(local_heads):
            masked_query[h] = spread_head(held.at[0], h, head_dim, scale)
        for b in range(local_heads // per_block):
            lanes = slice(b * 128, (b + 1) * 128)
            keys[b, :, :128] = held[1, :, :, lanes].reshape(stream, 128)
            keys[b, :, 128:] = guard
            values[b] = held[2, :, :, lanes].reshape(stream, 128)
        turned = held[1].reshape(stream, part).T
        for h in range(local_heads):
            key_turned[h] = turned[h * head_dim : (h + 1) * head_dim, :]
        value_turned[...] = held[2].reshape(stream, part).T
        keep(masked_query, query_out)
        keep(keys, key_out)
        keep(values, value_out)
        keep(key_turned, key_turned_out)

    def attention(h):
        def attend(c, _):
            query = jnp.concatenate([masked_query[h, c], ones], axis=1)
            scores = lax.dot_general(
                keys[h // per_block], query, FLAT, preferred_element_type=jnp.float32
            )
            peak = jnp.max(scores, axis=0, keepdims=True)
            raised = jnp.exp(scores - peak)
            total = jnp.sum(raised, axis=0, keepdims=True)
            mixed = jnp.dot(
                value_turned[h * head_dim : (h + 1) * head_dim, :],
                raised.astype(jnp.bfloat16),
                preferred_element_type=jnp.float32,
            )
            context_turned[c, h * head_dim : (h + 1) * head_dim, :] = mixed / total
            logs[c, h : h + 1, :] = peak + jnp.log(total)
            return 0

        lax.fori_loop(0, n_seq, attend, 0)

    def send_context():
        for i in (1, 2, 3, 0):
            context_sent[w.zs[i]] = context_turned[w.zs[i]].T.astype(jnp.bfloat16)
            if i:
                w.send(context_sent.at[w.zs[i]], context_held.at[w.z], context_sems.at[i], w.peer(0, i))
        context_held[w.z] = context_sent[w.z]
        keep(logs, logs_out)

    def turn_page():
        for s in range(n_seq):
            page_turned[s * width : (s + 1) * width, :] = page[s].T
        keep(page_turned, page_out)

    def context_arrived():
        for i in range(1, n_seq):
            w.arrived(context_held.at[w.zs[i]], context_sems.at[i])

    def gathered_out():
        out.over_cores()
        keep(out_matrix, full_out)

    def gathered_up():
        up.over_cores()
        for b in range(up_matrix.shape[2] // width):
            keep(up_matrix.at[:, :, pl.ds(b * width, width)], full_up.at[b])

    def gathered_down():
        down.over_cores()
        keep(down_matrix, full_down)

    def first_norm():
        total = x_ref[...].astype(jnp.float32) + line_of(2)
        for j in range(n_seq):
            block = out_matrix[j * per_part : (j + 1) * per_part].reshape(part, width)
            total = total + jnp.dot(context_held[j], block, preferred_element_type=jnp.float32)
            context_rows_turned[j * part : (j + 1) * part, :] = context_held[j].T
        keep(context_rows_turned, context_out)
        rows_hidden, normed, inv = norm_forward(total, line_of(3), line_of(4))
        normed_one[...] = normed
        inv_one[...] = jnp.broadcast_to(inv, inv_one.shape)
        hidden[...] = rows_hidden
        hidden_low[...] = rows_hidden.astype(jnp.bfloat16)
        hidden_turned[...] = rows_hidden.T.astype(jnp.bfloat16)
        keep(hidden_turned, hidden_out)

    def expand():
        def activate(f, _):
            at = pl.ds(pl.multiple_of(f * chunk, chunk), chunk)
            block = up_matrix[:, :, at].reshape(width, chunk)
            up_bias = jnp.concatenate(
                [packed[f * per_chunk + e, 8:9, :] for e in range(per_chunk)], axis=1
            )
            act = jnp.dot(hidden_low[...], block, preferred_element_type=jnp.float32) + up_bias
            below = 0.5 + 0.5 * lax.erf(act * math.sqrt(0.5))
            gelu = act * below
            gelu_low[:, at] = gelu.astype(jnp.bfloat16)
            gelu_turned[at, :] = gelu.T.astype(jnp.bfloat16)
            bell = jnp.exp(-0.5 * act * act) * (1.0 / math.sqrt(2.0 * math.pi))
            slopes[:, at] = (below + act * bell).astype(jnp.bfloat16)
            return 0

        lax.fori_loop(0, chunks, activate, 0)
        keep(gelu_turned, gelu_out)
        keep(slopes, slope_out)

    def shrink_all():
        branch[...] = hidden[...] + line_of(5)

        def shrink(f, _):
            at = pl.ds(pl.multiple_of(f * chunk, chunk), chunk)
            block = down_matrix[pl.ds(f * per_chunk, per_chunk)].reshape(chunk, width)
            branch[...] += jnp.dot(gelu_low[:, at], block, preferred_element_type=jnp.float32)
            return 0

        lax.fori_loop(0, chunks, shrink, 0)

    up.own_seq()
    out.own_seq()
    down.own_chips()
    qkv.own_chips()
    vec.own_chips()
    line.own(x_ref)
    qkv.own_seq()
    vec.own_seq()
    down.over_chips(0, 0)
    up.along_seq(1)
    out.along_seq(1)
    up.own_chips()
    out.own_chips()
    down.own_seq()
    line.end(1)
    up.over_chips(0, 1)
    out.over_chips(0, 1)
    qkv.along_seq(1)
    vec.along_seq(1)
    line.relay(1)
    line.relay(2)
    qkv.along_seq(2)
    vec.along_seq(2)
    qkv.over_chips(0, 0)
    vec.over_chips(0, 0)
    qkv.along_seq(3)
    vec.along_seq(3)
    qkv.over_chips(0, 3)
    vec.over_chips(0, 3)
    out.over_chips(0, 0)
    down.over_chips(1, 0)
    qkv.over_chips(0, 1)
    vec.over_chips(0, 1)
    qkv.over_chips(0, 2)
    vec.over_chips(0, 2)
    down.along_seq(1)
    out.over_chips(1, 0)
    qkv.over_chips(1, 0)
    vec.over_chips(1, 0)
    qkv.over_chips(1, 3)
    vec.over_chips(1, 3)
    qkv.over_chips(1, 1)
    vec.over_chips(1, 1)
    out.over_chips(1, 1)
    up.along_seq(2)
    qkv.over_chips(1, 2)
    vec.over_chips(1, 2)
    up.along_seq(3)
    line.end(2)
    down.over_chips(0, 1)
    gathered_columns()
    project(0)
    line.relay(3)
    project(1)
    project(2)
    up.over_chips(0, 2)
    up.over_chips(0, 3)
    up.over_chips(0, 0)
    up.over_chips(1, 1)
    line.end(3)
    project(3)
    prepare()
    attention(0)
    down.along_seq(2)
    attention(1)
    out.along_seq(2)
    attention(2)
    down.along_seq(3)
    attention(3)
    out.along_seq(3)
    send_context()
    down.over_chips(1, 1)
    out.over_chips(0, 2)
    up.over_chips(1, 2)
    out.over_chips(0, 3)
    down.over_chips(0, 2)
    down.over_chips(0, 3)
    turn_page()
    out.over_chips(1, 2)
    out.over_chips(1, 3)
    up.over_chips(1, 3)
    up.over_chips(1, 0)
    context_arrived()
    gathered_out()
    first_norm()
    gathered_up()
    down.over_chips(1, 2)
    down.over_chips(1, 3)
    expand()
    gathered_down()
    shrink_all()
    gain_one, gain_two = line_of(3), line_of(6)
    result, normed, inv = norm_forward(branch[...], gain_two, line_of(7))
    output[...] = result.astype(jnp.bfloat16)
    grad = cotangent[...].astype(jnp.float32)
    mid, grad_gain, grad_shift = norm_backward(grad, normed, inv, gain_two)
    grad_mid[...] = mid
    grad_bias = jnp.sum(mid.astype(jnp.bfloat16).astype(jnp.float32), axis=0)
    sums_out[...] = jnp.zeros_like(sums_out)
    for row, line_sum in enumerate((grad_bias, grad_gain, grad_shift)):
        sums_out[5 + row : 6 + row, :] = line_sum.reshape(1, width)
    sums_out[3:4, :] = gain_one
    for copy in keeps:
        copy.wait()
    w.drain()


def front(sizes, heads, valid, rows, cotangent, lines, up_line, w_qkv, w_out, w_up, w_down):
    n_dp, n_seq = sizes
    devices = n_dp * n_seq
    count, width = rows.shape
    part = width // n_seq
    stream = count * n_seq
    wide = w_up.shape[1]
    low = jnp.bfloat16
    head_dim = width // heads
    local_heads = heads // n_seq
    blocks = part // 128
    attention = (
        jax.ShapeDtypeStruct((local_heads, n_seq, count, 128), low),
        jax.ShapeDtypeStruct((blocks, stream, 256), low),
        jax.ShapeDtypeStruct((blocks, stream, 128), low),
        jax.ShapeDtypeStruct((local_heads, head_dim, stream), low),
    )

    def full(shard):
        return jax.ShapeDtypeStruct((devices,) + shard.shape, shard.dtype)

    anywhere = pl.BlockSpec(memory_space=pl.ANY)
    local = pl.BlockSpec(memory_space=pltpu.VMEM)
    sends = 5 * sends_of_gather(n_dp, n_seq) + 5 + n_seq - 1
    return pl.pallas_call(
        lambda *refs: front_kernel(sizes, heads, *refs),
        out_shape=(
            jax.ShapeDtypeStruct((devices, w_qkv.shape[0], 3 * part), low),
            full(w_out),
            jax.ShapeDtypeStruct((wide // width, devices, w_up.shape[0], width), low),
            full(w_down),
            jax.ShapeDtypeStruct((n_seq * width, count), low),
        )
        + attention
        + (
            jax.ShapeDtypeStruct((width, count), low),
            jax.ShapeDtypeStruct((n_seq, 8, count), jnp.float32),
            jax.ShapeDtypeStruct((width, count), low),
            jax.ShapeDtypeStruct((wide, count), low),
            jax.ShapeDtypeStruct((count, wide), low),
            jax.ShapeDtypeStruct((count, width), low),
            jax.ShapeDtypeStruct((count, width), jnp.float32),
            jax.ShapeDtypeStruct((count, 128), jnp.float32),
            jax.ShapeDtypeStruct((count, width), jnp.float32),
            jax.ShapeDtypeStruct((8, width), jnp.float32),
        ),
        in_specs=[
            pl.BlockSpec(memory_space=pltpu.SMEM),
        ]
        + [local] * 5
        + [anywhere] * 3,
        out_specs=[anywhere] * 14 + [local] * 5,
        scratch_shapes=[
            pltpu.VMEM((16, 128), jnp.float32),
            pltpu.VMEM((n_seq, w_qkv.shape[0], 3 * part), low),
            pltpu.VMEM((devices, 16, 128), jnp.float32),
            pltpu.VMEM((devices, w_qkv.shape[0], 3 * part), low),
            pltpu.VMEM((n_seq, count, width), low),
            pltpu.VMEM((3, n_seq, count, part), low),
            pltpu.VMEM((n_seq, count, part), low),
            pltpu.VMEM((n_seq, count, part), low),
            pltpu.VMEM((n_seq, part, count), jnp.float32),
            pltpu.VMEM((part, stream), low),
        ]
        + [pltpu.VMEM(a.shape, a.dtype) for a in attention]
        + [
            pltpu.VMEM((n_seq, 8, count), jnp.float32),
            pltpu.VMEM((devices,) + w_out.shape, low),
            pltpu.VMEM((devices,) + w_up.shape, low),
            pltpu.VMEM((devices,) + w_down.shape, low),
            pltpu.VMEM((n_seq * width, count), low),
            pltpu.VMEM((width, count), low),
            pltpu.VMEM((count, width), jnp.float32),
            pltpu.VMEM((count, width), low),
            pltpu.VMEM((width, count), low),
            pltpu.VMEM((count, wide), low),
            pltpu.VMEM((wide, count), low),
            pltpu.VMEM((count, wide), low),
            pltpu.VMEM((count, width), jnp.float32),
            pltpu.SemaphoreType.DMA((sends,)),
            pltpu.SemaphoreType.DMA((5, n_dp, n_seq)),
            pltpu.SemaphoreType.DMA((n_seq,)),
            pltpu.SemaphoreType.DMA((n_seq,)),
            pltpu.SemaphoreType.DMA((24,)),
        ],
        compiler_params=pltpu.CompilerParams(
            collective_id=0, has_side_effects=True, vmem_limit_bytes=60 * 2**20
        ),
        name="front",
    )(valid, rows, cotangent, lines, up_line, w_qkv, w_out, w_up, w_down)


def add_rows(into, term):
    rows = into.shape[0]
    step = min(16, rows)

    def body(r, _):
        at = pl.ds(pl.multiple_of(r * step, step), step)
        total = into[at, :].astype(jnp.float32) + term[at, :].astype(jnp.float32)
        into[at, :] = total.astype(into.dtype)
        return 0

    lax.fori_loop(0, rows // step, body, 0)


class LineSum:
    def __init__(self, wires, block, last, sems):
        self.w, self.block, self.last, self.sems = wires, block, last, sems

    def into(self, src, index, device, when):
        self.w.send(src, self.last.at[index], self.sems.at[index], device, when)

    def add(self, k, index):
        def action():
            self.w.arrived(self.last.at[index], self.sems.at[index])
            add_rows(self.block(k), self.last.at[index])

        pl.when(self.w.inner)(action)

    def offer(self, k):
        self.into(self.block(k), k - 1, (self.w.dp, self.w.right), self.w.outer)

    def relay(self, k):
        w, block = self.w, self.block(k)
        if k == 1:
            self.add(1, 4)
            self.into(block, 3, (w.dp, w.left), w.inner)
        else:
            self.add(k, k - 1)
            self.into(block, 3 if k == 2 else 4, (w.dp, w.right), w.inner)

    def finish(self, start, out):
        w = self.w
        w.arrived(self.last.at[3], self.sems.at[3])
        w.arrived(self.last.at[0], self.sems.at[0], w.inner)
        rows = out.shape[0]
        step = min(16, rows)

        def total_of(count):
            def body(r, _):
                at = pl.ds(pl.multiple_of(r * step, step), step)
                total = start(at) + self.last[3, at, :].astype(jnp.float32)
                if count == 2:
                    total = total + self.last[0, at, :].astype(jnp.float32)
                out[at, :] = total.astype(out.dtype)
                return 0

            lax.fori_loop(0, rows // step, body, 0)

        pl.when(w.inner)(lambda: total_of(2))
        pl.when(w.outer)(lambda: total_of(1))


class Scatter:
    def __init__(self, wires, kind, make, source, stage, bufs, sems, out):
        self.w, self.kind, self.make, self.source, self.stage = wires, kind, make, source, stage
        self.total, self.first, self.second, self.last = bufs
        self.core_sems, self.first_sems, self.second_sems, self.last_sems = sems
        self.out = out
        self.n_seq = wires.sizes[1]
        self.offsets = [6, 2, 4, 0]
        self.staged = {}
        self.slots = wires.far if kind == "line" else wires.zs
        self.line = LineSum(wires, lambda k: self.total.at[0, self.slots[k]], self.last, self.last_sems)

    def order(self, step):
        return (2, 4) if step % 2 == 0 else (4, 2)

    def give(self, k):
        o = self.offsets[k]
        d = self.w.dps[o ^ 1]
        if self.stage is None:
            src = self.source.at[pl.ds(d * self.n_seq, self.n_seq)]
        else:
            depth = self.stage.shape[0]
            if k >= depth:
                self.w.sent(self.staged[k - depth])
            src = self.stage.at[k % depth]

            def fill(s, _):
                src[s] = self.make(d, s).astype(src.dtype)
                return 0

            lax.fori_loop(0, self.n_seq, fill, 0)
        sem = self.core_sems.at[o // 2]
        self.staged[k] = self.w.send(src, self.total.at[o // 2], sem, self.w.peer(1, 0))

    def give_steps(self):
        return [lambda k=k: self.give(k) for k in range(4)]

    def over_cores(self, k):
        o = self.offsets[k]
        d = self.w.dps[o]
        self.w.arrived(self.total.at[o // 2], self.core_sems.at[o // 2])

        def add(s, _):
            block = self.total.at[o // 2, s]
            block[...] = (block[...].astype(jnp.float32) + self.make(d, s)).astype(block.dtype)
            return 0

        lax.fori_loop(0, self.n_seq, add, 0)
        self.hand_on(k, (3, 2))

    def spread(self, k):
        self.hand_on(k, (1, 0))

    def hand_on(self, k, steps):
        o = self.offsets[k]
        for i in steps:
            mask = self.order(i)[0]
            block = self.total.at[o // 2, self.slots[i]]
            if o & mask:
                keep = (o ^ mask) // (6 ^ mask)
                self.w.send(block, self.first.at[i, keep], self.first_sems.at[i, keep], self.w.peer(mask, 0))

    def over_chips(self, i):
        mask = self.order(i)[1]
        for keep in (1, 0):
            o = mask * keep
            block = self.total.at[o // 2, self.slots[i]]
            self.w.arrived(self.first.at[i, keep], self.first_sems.at[i, keep])
            add_rows(block, self.first.at[i, keep])
            if keep:
                self.w.send(block, self.second.at[i], self.second_sems.at[i], self.w.peer(mask, 0))

    def to_seq(self, i):
        block = self.total.at[0, self.slots[i]]
        self.w.arrived(self.second.at[i], self.second_sems.at[i])
        add_rows(block, self.second.at[i])
        if self.kind == "line":
            if i:
                self.line.offer(i)
        elif i:
            self.w.send(block, self.last.at[i], self.last_sems.at[i], self.w.peer(0, i))

    def relay(self, i):
        self.line.relay(i)

    def finish(self):
        block = self.total.at[0, self.w.z]
        if self.kind == "line":
            self.line.finish(lambda at: block[at, :].astype(jnp.float32), self.out)
            return
        for i in range(1, self.n_seq):
            self.w.arrived(self.last.at[i], self.last_sems.at[i])
        if self.kind == "direct":
            total = block[...]
            for i in range(1, self.n_seq):
                total = total + self.last[i]
            lines, up_line = self.out
            up_line[...] = total[8:9, :]
            share = lines.shape[1]
            total = total[:8, :]
            shown = total[:, :share]
            for s in range(1, self.n_seq):
                shown = jnp.where(self.w.z == s, total[:, s * share : (s + 1) * share], shown)
            lines[...] = shown
            return
        for i in range(self.n_seq):
            term = block[...] if i == 0 else self.last[i]
            part = term.shape[1] // 3
            for t in range(3):
                at = t * part * self.n_seq + self.w.zs[i] * part
                self.out[:, pl.ds(pl.multiple_of(at, part), part)] = term[
                    :, t * part : (t + 1) * part
                ].astype(jnp.float32)


def back_kernel(sizes, heads, *refs):
    n_dp, n_seq = sizes
    (
        mid_in,
        normed_in,
        inv_in,
        sums_in,
        logs,
        page_in,
        query_in,
        key_in,
        value_in,
        key_turned_in,
        context_in,
        hidden_in,
        gelu_in,
        slope_in,
        columns_in,
        out_in,
        up_in,
        down_in,
        grad_rows,
        *outs,
    ) = refs[:25]
    scratch = list(refs[25:])

    def take(count):
        got = scratch[:count]
        del scratch[:count]
        return got

    send_sems, core_sems, first_sems, second_sems, last_sems, block_sems = take(6)
    head_sems, local_sems, row_sems = take(3)
    grads, masked_query, keys, values, key_turned, masked_grad = take(6)
    query_grad, key_grad, value_grad = take(3)
    project, turned, columns, vec = take(4)
    row_terms, row_last, own_rows, partial = take(4)
    hidden_turned, context_turned, slopes, normed = take(4)
    grad_low, grad_sent, out_matrix, down_blocks, up_blocks = take(5)
    down_stage, up_stage, out_stage = take(3)
    units = [take(4) for k in range(5)]
    w = Wires(send_sems, sizes)
    rows, width = normed.shape
    part = width // n_seq
    wide = slopes.shape[1]
    head_dim = width // heads
    local_heads = heads // n_seq
    stream = rows * n_seq
    per_block = 128 // head_dim
    scale = 1.0 / math.sqrt(head_dim)
    loads = {}

    def load(name, src, dst):
        loads[name] = pltpu.make_async_copy(src, dst, local_sems.at[len(loads)])
        loads[name].start()

    load("mid", mid_in, own_rows)
    load("gelu", gelu_in, turned)
    load("slope", slope_in, slopes)
    blocks = []
    for f in range(n_dp):
        sem = block_sems.at[0, f % 2]
        blocks.append(pltpu.make_async_copy(down_in.at[pl.ds(f * n_seq, n_seq)], down_blocks.at[f % 2], sem))
    shares = wide // width
    half = up_in.shape[1] // 2
    ups = []
    for e in range(2 * shares):
        src = up_in.at[e % shares, pl.ds(e // shares * half, half)]
        ups.append(pltpu.make_async_copy(src, up_blocks.at[e % 2], block_sems.at[1, e % 2]))
    for e in range(2):
        blocks[e].start()
        ups[e].start()
    load("hidden", hidden_in, hidden_turned)
    load("normed", normed_in, normed)
    load("out", out_in, out_matrix)
    load("context", context_in, context_turned)
    load("columns", columns_in, columns)
    load("query", query_in, masked_query)
    load("key", key_in, keys)
    load("value", value_in, values)
    load("turned", key_turned_in, key_turned)
    w.greet()

    def rows_from(source, first, count):
        return source[pl.ds(pl.multiple_of(first, count), count), :]

    def down_term(d, s):
        left = rows_from(turned, (d * n_seq + s) * outs[0].shape[0], outs[0].shape[0])
        return jnp.dot(left, grad_low[...], preferred_element_type=jnp.float32)

    def up_term(d, s):
        left = rows_from(hidden_turned, (d * n_seq + s) * outs[1].shape[0], outs[1].shape[0])
        return jnp.dot(left, slopes[...], preferred_element_type=jnp.float32)

    def out_term(d, s):
        left = rows_from(context_turned, (d * n_seq + s) * outs[2].shape[0], outs[2].shape[0])
        return jnp.dot(left, grad_low[...], preferred_element_type=jnp.float32)

    def held_term(source):
        return lambda d, s: source[d * n_seq + s].astype(jnp.float32)

    makes = (down_term, up_term, out_term, held_term(partial), held_term(vec))
    stages = (down_stage, up_stage, out_stage, None, None)
    scatters = []
    for k in range(5):
        scatters.append(
            Scatter(
                w,
                ("line", "line", "line", "columns", "direct")[k],
                makes[k],
                (None, None, None, partial, vec)[k],
                stages[k],
                units[k],
                (core_sems.at[k], first_sems.at[k], second_sems.at[k], last_sems.at[k]),
                outs[k] if k < 4 else outs[4:],
            )
        )
    down, up, out, qkv, small = scatters
    row_sum = LineSum(w, lambda k: row_terms.at[k - 1], row_last, row_sems)
    span = wide // n_dp

    def run(steps):
        for step in steps:
            step()

    ones = jnp.where(lax.broadcasted_iota(jnp.int32, (rows, 128), 1) == 0, 1.0, 0.0).astype(jnp.bfloat16)

    def keep_line(row, line):
        for d in range(n_dp):
            for s in range(n_seq):
                vec[d * n_seq + s, row : row + 1, :] = line[:, d * 128 : (d + 1) * 128]

    def begin():
        loads["mid"].wait()
        grad_low[...] = own_rows[...].astype(jnp.bfloat16)
        loads["gelu"].wait()

    def slope_of(f):
        if f == 0:
            loads["slope"].wait()
        blocks[f].wait()
        grad_gelu = lax.dot_general(
            grad_low[...], down_blocks[f % 2].reshape(span, width), FLAT, preferred_element_type=jnp.float32
        )
        if f + 2 < n_dp:
            blocks[f + 2].start()
        at = slice(f * span, (f + 1) * span)
        slopes[:, at] = (grad_gelu * slopes[:, at].astype(jnp.float32)).astype(jnp.bfloat16)
        if f == n_dp - 1:
            loads["hidden"].wait()

    def hidden_of(e):
        ups[e].wait()
        columns_at = slice(e % shares * width, (e % shares + 1) * width)
        rows_at = slice(e // shares * width // 2, (e // shares + 1) * width // 2)
        own_rows[:, rows_at] += lax.dot_general(
            slopes[:, columns_at],
            up_blocks[e % 2].reshape(width // 2, width),
            FLAT,
            preferred_element_type=jnp.float32,
        )
        if e + 2 < 2 * shares:
            ups[e + 2].start()

    def norm_back():
        load("page", page_in, turned)
        loads["normed"].wait()
        first, grad_gain, grad_shift = norm_backward(
            own_rows[...], normed[...], inv_in[:, :1], sums_in[3:4, :]
        )
        own_rows[...] = first
        grad_low[...] = first.astype(jnp.bfloat16)
        vec[...] = jnp.zeros_like(vec)
        keep_line(3, grad_gain.reshape(1, width))
        keep_line(4, grad_shift.reshape(1, width))

    def send_grads():
        loads["out"].wait()
        for i in (1, 2, 3, 0):
            j = w.zs[i]
            share = part // out_matrix.shape[1]
            block = out_matrix[pl.ds(j * share, share)].reshape(part, width)
            piece = lax.dot_general(grad_low[...], block, FLAT, preferred_element_type=jnp.float32)
            if i:
                grad_sent[i] = piece.astype(jnp.bfloat16)
                w.send(grad_sent.at[i], grads.at[w.z], head_sems.at[i], w.peer(0, i))
            else:
                grads[w.z] = piece.astype(jnp.bfloat16)
        loads["context"].wait()

    def keep_lines():
        up_bias = jnp.sum(slopes[...].astype(jnp.float32), axis=0, keepdims=True)
        for d in range(n_dp * n_seq):
            vec[d, 8:9, :] = up_bias[:, d * 128 : (d + 1) * 128]
        keep_line(2, jnp.sum(grad_low[...].astype(jnp.float32), axis=0, keepdims=True))
        for row in (5, 6, 7):
            keep_line(row, sums_in[row : row + 1, :])

    def prepare():
        for name in ("columns", "query", "key", "value", "turned"):
            loads[name].wait()
        key_grad[...] = jnp.zeros_like(key_grad)
        value_grad[...] = jnp.zeros_like(value_grad)
        for i in range(1, n_seq):
            w.arrived(grads.at[w.zs[i]], head_sems.at[i])
        for h in range(local_heads):
            masked_grad[h] = spread_head(grads, h, head_dim, 1.0)

    def attention(c):
        def head(h, _):
            block = h // per_block
            query, grad = masked_query[h, c], masked_grad[h, c]
            scores = lax.dot_general(
                keys[block], jnp.concatenate([query, ones], axis=1), FLAT, preferred_element_type=jnp.float32
            )
            probs = jnp.exp(scores - logs[c, pl.ds(h, 1), :])
            moved = lax.dot_general(values[block], grad, FLAT, preferred_element_type=jnp.float32)
            centre = jnp.sum(probs * moved, axis=0, keepdims=True)
            slope = (probs * (moved - centre)).astype(jnp.bfloat16)
            query_grad[h] = jnp.dot(key_turned[h], slope, preferred_element_type=jnp.float32) * scale
            key_grad[block] += jnp.dot(slope, query, preferred_element_type=jnp.float32)
            value_grad[block] += jnp.dot(
                probs.astype(jnp.bfloat16), grad, preferred_element_type=jnp.float32
            )
            return 0

        lax.fori_loop(0, local_heads, head, 0)
        project[c * rows : (c + 1) * rows, :part] = (
            query_grad[...].reshape(part, rows).T.astype(jnp.bfloat16)
        )

    def keep_project():
        for t, total in ((1, key_grad), (2, value_grad)):
            for b in range(local_heads // per_block):
                at = t * part + b * 128
                project[:, at : at + 128] = total[b].astype(jnp.bfloat16)

    def row_term(k):
        term = lax.dot_general(
            rows_from(project, w.far[k] * rows, rows),
            columns[...].reshape(width, 3 * part),
            FLAT,
            preferred_element_type=jnp.float32,
        )
        if k:
            row_terms[k - 1] = term.astype(jnp.bfloat16)
            row_sum.offer(k)
        else:
            own_rows[...] += term

    def weight_grad():
        loads["page"].wait()
        for t in range(3):
            at = slice(t * part, (t + 1) * part)
            block = jnp.dot(turned[:width, :], project[:rows, at], preferred_element_type=jnp.float32)
            for s in range(1, n_seq):
                block = block + jnp.dot(
                    turned[s * width : (s + 1) * width, :],
                    project[s * rows : (s + 1) * rows, at],
                    preferred_element_type=jnp.float32,
                )
            partial[:, :, at] = block.astype(jnp.bfloat16).reshape(n_dp * n_seq, -1, part)

    def give_small():
        groups = part // 128
        for b, t in ((0, 0), (1, 2)):
            sums = jnp.sum(project[:, t * part : (t + 1) * part].astype(jnp.float32), axis=0, keepdims=True)
            for g in range(groups):
                for s in range(n_seq):
                    vec[(w.z * groups + g) * n_seq + s, b : b + 1, :] = sums[:, g * 128 : (g + 1) * 128]
        run(small.give_steps())

    begin()
    slope_of(0)
    slope_of(1)
    down.give(0)
    down.give(1)
    slope_of(2)
    slope_of(3)
    slope_of(4)
    hidden_of(0)
    down.give(2)
    down.over_cores(0)
    slope_of(5)
    hidden_of(1)
    slope_of(6)
    down.give(3)
    down.spread(0)
    slope_of(7)
    down.over_cores(1)
    hidden_of(2)
    hidden_of(3)
    down.over_cores(2)
    hidden_of(4)
    hidden_of(5)
    hidden_of(6)
    hidden_of(7)
    down.over_cores(3)
    norm_back()
    send_grads()
    down.spread(2)
    out.give(0)
    up.give(0)
    down.over_chips(3)
    up.give(1)
    down.over_chips(2)
    up.give(2)
    up.over_cores(0)
    up.give(3)
    down.over_chips(1)
    up.spread(0)
    down.to_seq(3)
    prepare()
    attention(0)
    attention(1)
    down.to_seq(1)
    attention(2)
    down.relay(3)
    down.to_seq(2)
    attention(3)
    down.relay(2)
    keep_project()
    row_term(3)
    up.over_cores(1)
    down.relay(1)
    up.spread(1)
    up.over_cores(2)
    out.give(1)
    up.over_cores(3)
    out.give(2)
    out.give(3)
    keep_lines()
    out.over_cores(0)
    up.over_chips(2)
    up.spread(2)
    out.over_cores(3)
    out.over_cores(1)
    up.over_chips(3)
    row_sum.relay(3)
    row_term(2)
    weight_grad()
    out.over_cores(2)
    give_small()
    down.spread(1)
    qkv.give(0)
    qkv.give(1)
    qkv.give(2)
    qkv.give(3)
    up.to_seq(3)
    out.spread(1)
    qkv.over_cores(2)
    small.over_cores(2)
    out.spread(2)
    out.over_chips(2)
    row_sum.relay(2)
    up.over_chips(1)
    up.over_chips(0)
    up.to_seq(2)
    row_term(0)
    row_term(1)
    up.relay(3)
    row_sum.relay(1)
    down.over_chips(0)
    out.to_seq(2)
    qkv.over_cores(1)
    small.over_cores(1)
    qkv.over_cores(0)
    small.over_cores(0)
    qkv.spread(1)
    small.spread(1)
    out.over_chips(3)
    qkv.spread(0)
    small.spread(0)
    out.to_seq(3)
    qkv.spread(2)
    small.spread(2)
    out.spread(0)
    up.to_seq(1)
    up.relay(2)
    qkv.over_cores(3)
    small.over_cores(3)
    up.relay(1)
    qkv.over_chips(0)
    small.over_chips(0)
    qkv.over_chips(1)
    small.over_chips(1)
    out.over_chips(0)
    out.over_chips(1)
    qkv.over_chips(2)
    small.over_chips(2)
    out.relay(3)
    qkv.to_seq(1)
    small.to_seq(1)
    qkv.over_chips(3)
    small.over_chips(3)
    up.to_seq(0)
    qkv.to_seq(0)
    small.to_seq(0)
    out.to_seq(1)
    out.relay(2)
    row_sum.finish(lambda at: own_rows[at, :], grad_rows)
    qkv.to_seq(3)
    small.to_seq(3)
    qkv.to_seq(2)
    small.to_seq(2)
    out.relay(1)
    down.to_seq(0)
    out.to_seq(0)
    down.finish()
    qkv.finish()
    small.finish()
    up.finish()
    out.finish()
    w.drain()


def back(sizes, heads, saved, w_shapes):
    n_dp, n_seq = sizes
    devices = n_dp * n_seq
    mid, normed, _, _, logs, page, query, key, value, key_turned, context, hidden, gelu, slopes = saved[:14]
    columns, full_out, full_up, full_down = saved[14:]
    count, width = normed.shape
    part = width // n_seq
    stream = count * n_seq
    local_heads, head_dim, _ = key_turned.shape
    blocks = part // 128
    low = jnp.bfloat16
    shapes = [w_shapes[0], w_shapes[1], w_shapes[2], columns.shape[1:], (16, 128)]
    kinds = [low] * 4 + [jnp.float32]
    results = [jax.ShapeDtypeStruct(shape, jnp.float32) for shape in shapes]
    results[3] = jax.ShapeDtypeStruct((shapes[3][0], n_seq * shapes[3][1]), jnp.float32)
    results[4:] = [
        jax.ShapeDtypeStruct((8, width // devices), jnp.float32),
        jax.ShapeDtypeStruct((1, 128), jnp.float32),
    ]
    anywhere = pl.BlockSpec(memory_space=pl.ANY)
    local = pl.BlockSpec(memory_space=pltpu.VMEM)
    sends = 5 * (4 + 3 * n_seq + 6) + 6 + n_seq - 1
    chips = n_dp // 2

    def like(array):
        return pltpu.VMEM(array.shape, array.dtype)

    scratch = [
        pltpu.SemaphoreType.DMA((sends,)),
        pltpu.SemaphoreType.DMA((5, chips)),
        pltpu.SemaphoreType.DMA((5, n_seq, 2)),
        pltpu.SemaphoreType.DMA((5, n_seq)),
        pltpu.SemaphoreType.DMA((5, 5)),
        pltpu.SemaphoreType.DMA((2, 2)),
        pltpu.SemaphoreType.DMA((n_seq,)),
        pltpu.SemaphoreType.DMA((13,)),
        pltpu.SemaphoreType.DMA((5,)),
        pltpu.VMEM((n_seq, count, part), low),
        like(query),
        like(key),
        like(value),
        like(key_turned),
        like(query),
        pltpu.VMEM((local_heads, head_dim, count), jnp.float32),
        pltpu.VMEM((blocks, stream, 128), jnp.float32),
        pltpu.VMEM((blocks, stream, 128), jnp.float32),
        pltpu.VMEM((stream, 3 * part), low),
        like(gelu),
        like(columns),
        pltpu.VMEM((devices, 16, 128), jnp.float32),
        pltpu.VMEM((n_seq - 1, count, width), low),
        pltpu.VMEM((5, count, width), low),
        pltpu.VMEM((count, width), jnp.float32),
        like(columns),
        like(hidden),
        like(context),
        like(slopes),
        like(normed),
        pltpu.VMEM((count, width), low),
        pltpu.VMEM((n_seq, count, part), low),
        like(full_out),
        pltpu.VMEM((2, n_seq) + shapes[0], low),
        pltpu.VMEM((2, devices // 2) + full_up.shape[2:], low),
        pltpu.VMEM((2, n_seq) + shapes[0], low),
        pltpu.VMEM((2, n_seq) + shapes[1], low),
        pltpu.VMEM((4, n_seq) + shapes[2], low),
    ]
    for shape, kind in zip(shapes, kinds):
        scratch += [
            pltpu.VMEM((chips, n_seq) + shape, kind),
            pltpu.VMEM((n_seq, 2) + shape, kind),
            pltpu.VMEM((n_seq,) + shape, kind),
            pltpu.VMEM((5,) + shape, kind),
        ]
    return pl.pallas_call(
        lambda *refs: back_kernel(sizes, heads, *refs),
        out_shape=[jax.ShapeDtypeStruct((count, width), low)] + results,
        in_specs=[anywhere] * 2 + [local] * 3 + [anywhere] * 13,
        out_specs=[local] * 7,
        scratch_shapes=scratch,
        compiler_params=pltpu.CompilerParams(
            collective_id=1, has_side_effects=True, vmem_limit_bytes=63 * 2**20
        ),
        name="back",
    )(*saved)


def kernel_plan(
    x_in,
    w_qkv,
    q_bias,
    v_bias,
    w_out,
    out_bias,
    ln1_gain,
    ln1_shift,
    w_up,
    up_bias,
    w_down,
    down_bias,
    ln2_gain,
    ln2_shift,
    valid,
    cotangent,
):
    sizes = (lax.axis_size("dp"), lax.axis_size("seq"))
    n_dp, groups = sizes
    rows = x_in[0]
    count, width = rows.shape
    vectors = (q_bias, v_bias, out_bias, ln1_gain, ln1_shift, down_bias, ln2_gain, ln2_shift)
    lines = jnp.stack(vectors)
    (
        columns,
        full_out,
        full_up,
        full_down,
        page_turned,
        query,
        key,
        value,
        key_turned,
        context,
        logs,
        hidden,
        gelu,
        slopes,
        output,
        normed,
        inv,
        grad_mid,
        line_sums,
    ) = front(sizes, HEADS, valid, rows, cotangent[0], lines, up_bias[None], w_qkv, w_out, w_up, w_down)
    saved = (grad_mid, normed, inv, line_sums, logs, page_turned, query, key, value, key_turned)
    saved += (context, hidden, gelu, slopes, columns, full_out, full_up, full_down)
    devices = n_dp * groups
    grad_rows, *sums = back(sizes, HEADS, saved, (w_down.shape, w_up.shape, w_out.shape))
    mine = sums[4]
    return (
        output[None],
        grad_rows[None],
        sums[3],
        mine[0],
        mine[1],
        sums[2],
        mine[2],
        mine[3],
        mine[4],
        sums[1],
        sums[5].reshape(-1),
        sums[0],
        mine[5],
        mine[6],
        mine[7],
    )


def solution(mesh):
    n_dp, n_seq = mesh.shape["dp"], mesh.shape["seq"]

    def per_device(x_in, w_qkv, *rest):
        part, width = w_qkv.shape[0], x_in.shape[2]
        fits = (n_dp, n_seq) == (8, 4) and part % 32 == 0 and part * n_seq == 128 and width // n_seq % 128 == 0 and x_in.shape[0] == 1
        plan = kernel_plan if fits else general_plan
        return plan(x_in, w_qkv, *rest)

    return jax.shard_map(
        per_device,
        mesh=mesh,
        in_specs=(
            P("dp", "seq", None),
            P(("dp", "seq"), None),
            P(("dp", "seq")),
            P(("dp", "seq")),
            P(("dp", "seq"), None),
            P(("dp", "seq")),
            P(("dp", "seq")),
            P(("dp", "seq")),
            P(("dp", "seq"), None),
            P(("dp", "seq")),
            P(("dp", "seq"), None),
            P(("dp", "seq")),
            P(("dp", "seq")),
            P(("dp", "seq")),
            P("dp"),
            P("dp", "seq", None),
        ),
        out_specs=(
            P("dp", "seq", None),
            P("dp", "seq", None),
            P(("dp", "seq"), None),
            P(("dp", "seq")),
            P(("dp", "seq")),
            P(("dp", "seq"), None),
            P(("dp", "seq")),
            P(("dp", "seq")),
            P(("dp", "seq")),
            P(("dp", "seq"), None),
            P(("dp", "seq")),
            P(("dp", "seq"), None),
            P(("dp", "seq")),
            P(("dp", "seq")),
            P(("dp", "seq")),
        ),
        check_vma=False,
    )
```

```python
import math

import jax
import jax.numpy as jnp
from jax import lax
from jax.experimental import pallas as pl
from jax.experimental.pallas import tpu as pltpu
from jax.sharding import PartitionSpec as P

HEADS = 16


eps_norm = 1e-05


def outer_sum(left, right):
    return lax.dot_general(
        left, right, (((0,), (0,)), ((), ())), preferred_element_type=jnp.float32
    )


def times_back(rows, matrix):
    return lax.dot_general(
        rows, matrix, (((1,), (1,)), ((), ())), preferred_element_type=jnp.float32
    )


def gelu_exact(values):
    return jax.nn.gelu(values, approximate=False)


def norm_forward(rows, gain, shift):
    center = rows - jnp.mean(rows, axis=-1, keepdims=True)
    inv_std = lax.rsqrt(jnp.mean(center * center, axis=-1, keepdims=True) + eps_norm)
    normed = center * inv_std
    return (normed * gain + shift, normed, inv_std)


def norm_backward(grad_out, normed, inv_std, gain):
    scaled = grad_out * gain
    grad_rows = inv_std * (
        scaled
        - jnp.mean(scaled, axis=-1, keepdims=True)
        - normed * jnp.mean(scaled * normed, axis=-1, keepdims=True)
    )
    return (grad_rows, jnp.sum(grad_out * normed, axis=0), jnp.sum(grad_out, axis=0))


def to_heads(rows, groups):
    count, width = rows.shape
    return rows.reshape(count, groups, width // groups).transpose(1, 0, 2).reshape(groups, -1)


def from_heads(pieces, part_width):
    groups = pieces.shape[0]
    return (
        pieces.reshape(groups, -1, part_width).transpose(1, 0, 2).reshape(-1, groups * part_width)
    )


def general_plan(
    x_in,
    w_qkv,
    q_bias,
    v_bias,
    w_out,
    out_bias,
    ln1_gain,
    ln1_shift,
    w_up,
    up_bias,
    w_down,
    down_bias,
    ln2_gain,
    ln2_shift,
    valid,
    cotangent,
):
    shards = (
        w_qkv,
        q_bias,
        v_bias,
        w_out,
        out_bias,
        ln1_gain,
        ln1_shift,
        w_up,
        up_bias,
        w_down,
        down_bias,
        ln2_gain,
        ln2_shift,
    )
    weights = (
        lax.all_gather(shards[0], ("dp", "seq"), axis=0, tiled=True),
        lax.all_gather(shards[1], ("dp", "seq"), axis=0, tiled=True),
        lax.all_gather(shards[2], ("dp", "seq"), axis=0, tiled=True),
        lax.all_gather(shards[3], ("dp", "seq"), axis=0, tiled=True),
        lax.all_gather(shards[4], ("dp", "seq"), axis=0, tiled=True),
        lax.all_gather(shards[5], ("dp", "seq"), axis=0, tiled=True),
        lax.all_gather(shards[6], ("dp", "seq"), axis=0, tiled=True),
        lax.all_gather(shards[7], ("dp", "seq"), axis=0, tiled=True),
        lax.all_gather(shards[8], ("dp", "seq"), axis=0, tiled=True),
        lax.all_gather(shards[9], ("dp", "seq"), axis=0, tiled=True),
        lax.all_gather(shards[10], ("dp", "seq"), axis=0, tiled=True),
        lax.all_gather(shards[11], ("dp", "seq"), axis=0, tiled=True),
        lax.all_gather(shards[12], ("dp", "seq"), axis=0, tiled=True),
    )
    (
        full_qkv,
        full_qbias,
        full_vbias,
        full_out,
        full_obias,
        full_gain1,
        full_shift1,
        full_up,
        full_ubias,
        full_down,
        full_dbias,
        full_gain2,
        full_shift2,
    ) = weights
    groups = lax.axis_size("seq")
    rows = x_in[0]
    count, width = rows.shape
    head_dim = width // HEADS
    part_width = width // groups
    local_heads = HEADS // groups
    stream = count * groups
    qrows = min(512, stream)
    nblocks = stream // qrows
    scale = 1.0 / math.sqrt(head_dim)
    keep = jnp.arange(stream, dtype=jnp.int32) < valid[0]
    bias_row = jnp.concatenate([full_qbias, jnp.zeros_like(full_qbias), full_vbias]).astype(
        jnp.float32
    )
    project = (jnp.dot(rows, full_qkv, preferred_element_type=jnp.float32) + bias_row).astype(
        jnp.bfloat16
    )
    sent = (
        to_heads(project[:, :width], groups),
        to_heads(project[:, width : 2 * width], groups),
        to_heads(project[:, 2 * width :], groups),
    )
    arrived = (
        lax.all_to_all(sent[0], "seq", split_axis=0, concat_axis=0, tiled=True),
        lax.all_to_all(sent[1], "seq", split_axis=0, concat_axis=0, tiled=True),
        lax.all_to_all(sent[2], "seq", split_axis=0, concat_axis=0, tiled=True),
    )
    query_blocks = arrived[0].reshape(nblocks, qrows, local_heads, head_dim)
    key_heads = arrived[1].reshape(stream, local_heads, head_dim)
    value_heads = arrived[2].reshape(stream, local_heads, head_dim)

    def masked_scores(query):
        scores = (
            jnp.einsum("qhd,khd->hqk", query, key_heads, preferred_element_type=jnp.float32) * scale
        )
        return jnp.where(keep[None, None, :], scores, -1e30)

    def attend_forward(query):
        scores = masked_scores(query)
        peak = jnp.max(scores, axis=-1, keepdims=True)
        raised = jnp.exp(scores - peak)
        total = jnp.sum(raised, axis=-1, keepdims=True)
        probs = (raised / total).astype(jnp.bfloat16)
        context = jnp.einsum("hqk,khd->qhd", probs, value_heads, preferred_element_type=jnp.float32)
        return (context.astype(jnp.bfloat16), (peak + jnp.log(total))[..., 0])

    context, log_sums = lax.map(attend_forward, query_blocks)
    returned_ctx = lax.all_to_all(
        context.reshape(groups, -1), "seq", split_axis=0, concat_axis=0, tiled=True
    )
    context_rows = from_heads(returned_ctx, part_width)
    attn_out = jnp.dot(
        context_rows, full_out, preferred_element_type=jnp.float32
    ) + full_obias.astype(jnp.float32)
    first_rows = rows.astype(jnp.float32) + attn_out
    hidden, normed_one, inv_one = norm_forward(
        first_rows, full_gain1.astype(jnp.float32), full_shift1.astype(jnp.float32)
    )
    hidden_low = hidden.astype(jnp.bfloat16)
    up_act = jnp.dot(hidden_low, full_up, preferred_element_type=jnp.float32) + full_ubias.astype(
        jnp.float32
    )
    gelu_low = gelu_exact(up_act).astype(jnp.bfloat16)
    branch = jnp.dot(gelu_low, full_down, preferred_element_type=jnp.float32) + full_dbias.astype(
        jnp.float32
    )
    output, normed_two, inv_two = norm_forward(
        hidden + branch, full_gain2.astype(jnp.float32), full_shift2.astype(jnp.float32)
    )
    again = (
        lax.all_gather(shards[0], ("dp", "seq"), axis=0, tiled=True),
        lax.all_gather(shards[1], ("dp", "seq"), axis=0, tiled=True),
        lax.all_gather(shards[2], ("dp", "seq"), axis=0, tiled=True),
        lax.all_gather(shards[3], ("dp", "seq"), axis=0, tiled=True),
        lax.all_gather(shards[4], ("dp", "seq"), axis=0, tiled=True),
        lax.all_gather(shards[5], ("dp", "seq"), axis=0, tiled=True),
        lax.all_gather(shards[6], ("dp", "seq"), axis=0, tiled=True),
        lax.all_gather(shards[7], ("dp", "seq"), axis=0, tiled=True),
        lax.all_gather(shards[8], ("dp", "seq"), axis=0, tiled=True),
        lax.all_gather(shards[9], ("dp", "seq"), axis=0, tiled=True),
        lax.all_gather(shards[10], ("dp", "seq"), axis=0, tiled=True),
        lax.all_gather(shards[11], ("dp", "seq"), axis=0, tiled=True),
        lax.all_gather(shards[12], ("dp", "seq"), axis=0, tiled=True),
    )
    back_qkv, back_out, back_gain1, back_up, back_down, back_gain2 = (
        again[0],
        again[3],
        again[5],
        again[7],
        again[9],
        again[11],
    )
    grad_out = cotangent[0].astype(jnp.float32)
    grad_mid, grad_ln2_gain, grad_ln2_shift = norm_backward(
        grad_out, normed_two, inv_two, back_gain2.astype(jnp.float32)
    )
    grad_branch = grad_mid.astype(jnp.bfloat16)
    grad_w_down = outer_sum(gelu_low, grad_branch)
    grad_down_bias = jnp.sum(grad_branch.astype(jnp.float32), axis=0)
    grad_gelu = times_back(grad_branch, back_down)
    grad_up = jax.vjp(gelu_exact, up_act)[1](grad_gelu)[0].astype(jnp.bfloat16)
    grad_w_up = outer_sum(hidden_low, grad_up)
    grad_up_bias = jnp.sum(grad_up.astype(jnp.float32), axis=0)
    grad_hidden = times_back(grad_up, back_up) + grad_mid
    grad_first, grad_ln1_gain, grad_ln1_shift = norm_backward(
        grad_hidden, normed_one, inv_one, back_gain1.astype(jnp.float32)
    )
    grad_attn = grad_first.astype(jnp.bfloat16)
    grad_w_out = outer_sum(context_rows, grad_attn)
    grad_out_bias = jnp.sum(grad_attn.astype(jnp.float32), axis=0)
    grad_context = times_back(grad_attn, back_out).astype(jnp.bfloat16)
    grad_ctx_heads = lax.all_to_all(
        to_heads(grad_context, groups), "seq", split_axis=0, concat_axis=0, tiled=True
    )
    grad_ctx_blocks = grad_ctx_heads.reshape(nblocks, qrows, local_heads, head_dim)

    def attend_backward(carry, inputs):
        key_total, value_total = carry
        query, grad_ctx, log_rows = inputs
        scores = masked_scores(query)
        probs = jnp.exp(scores - log_rows[..., None])
        probs_low = probs.astype(jnp.bfloat16)
        d_probs = jnp.einsum(
            "qhd,khd->hqk", grad_ctx, value_heads, preferred_element_type=jnp.float32
        )
        centre = jnp.sum(probs * d_probs, axis=-1, keepdims=True)
        grad_scores = (probs * (d_probs - centre)).astype(jnp.bfloat16)
        grad_query = (
            jnp.einsum("hqk,khd->qhd", grad_scores, key_heads, preferred_element_type=jnp.float32)
            * scale
        )
        key_total = (
            key_total
            + jnp.einsum("hqk,qhd->khd", grad_scores, query, preferred_element_type=jnp.float32)
            * scale
        )
        value_total = value_total + jnp.einsum(
            "hqk,qhd->khd", probs_low, grad_ctx, preferred_element_type=jnp.float32
        )
        return ((key_total, value_total), grad_query.astype(jnp.bfloat16))

    empty = jnp.zeros((stream, local_heads, head_dim), jnp.float32)
    (key_total, value_total), grad_query = lax.scan(
        attend_backward, (empty, empty), (query_blocks, grad_ctx_blocks, log_sums)
    )
    grad_key = key_total.astype(jnp.bfloat16)
    grad_value = value_total.astype(jnp.bfloat16)
    grad_pieces = (
        lax.all_to_all(
            grad_query.reshape(groups, -1), "seq", split_axis=0, concat_axis=0, tiled=True
        ),
        lax.all_to_all(
            grad_key.reshape(groups, -1), "seq", split_axis=0, concat_axis=0, tiled=True
        ),
        lax.all_to_all(
            grad_value.reshape(groups, -1), "seq", split_axis=0, concat_axis=0, tiled=True
        ),
    )
    grad_project = jnp.concatenate(
        [
            from_heads(grad_pieces[0], part_width),
            from_heads(grad_pieces[1], part_width),
            from_heads(grad_pieces[2], part_width),
        ],
        axis=1,
    )
    grad_w_qkv = outer_sum(rows, grad_project)
    bias_sums = jnp.sum(grad_project.astype(jnp.float32), axis=0)
    grad_q_bias = bias_sums[:width]
    grad_v_bias = bias_sums[2 * width :]
    grad_rows = times_back(grad_project, back_qkv) + grad_first
    terms = (
        grad_w_qkv,
        grad_q_bias,
        grad_v_bias,
        grad_w_out,
        grad_out_bias,
        grad_ln1_gain,
        grad_ln1_shift,
        grad_w_up,
        grad_up_bias,
        grad_w_down,
        grad_down_bias,
        grad_ln2_gain,
        grad_ln2_shift,
    )
    page_sums = (
        lax.psum_scatter(
            terms[0].astype(jnp.bfloat16), "dp", scatter_dimension=0, tiled=True
        ).astype(jnp.float32),
        lax.psum_scatter(
            terms[1].astype(jnp.bfloat16), "dp", scatter_dimension=0, tiled=True
        ).astype(jnp.float32),
        lax.psum_scatter(
            terms[2].astype(jnp.bfloat16), "dp", scatter_dimension=0, tiled=True
        ).astype(jnp.float32),
        lax.psum_scatter(
            terms[3].astype(jnp.bfloat16), "dp", scatter_dimension=0, tiled=True
        ).astype(jnp.float32),
        lax.psum_scatter(
            terms[4].astype(jnp.bfloat16), "dp", scatter_dimension=0, tiled=True
        ).astype(jnp.float32),
        lax.psum_scatter(
            terms[5].astype(jnp.bfloat16), "dp", scatter_dimension=0, tiled=True
        ).astype(jnp.float32),
        lax.psum_scatter(
            terms[6].astype(jnp.bfloat16), "dp", scatter_dimension=0, tiled=True
        ).astype(jnp.float32),
        lax.psum_scatter(
            terms[7].astype(jnp.bfloat16), "dp", scatter_dimension=0, tiled=True
        ).astype(jnp.float32),
        lax.psum_scatter(
            terms[8].astype(jnp.bfloat16), "dp", scatter_dimension=0, tiled=True
        ).astype(jnp.float32),
        lax.psum_scatter(
            terms[9].astype(jnp.bfloat16), "dp", scatter_dimension=0, tiled=True
        ).astype(jnp.float32),
        lax.psum_scatter(
            terms[10].astype(jnp.bfloat16), "dp", scatter_dimension=0, tiled=True
        ).astype(jnp.float32),
        lax.psum_scatter(
            terms[11].astype(jnp.bfloat16), "dp", scatter_dimension=0, tiled=True
        ).astype(jnp.float32),
        lax.psum_scatter(
            terms[12].astype(jnp.bfloat16), "dp", scatter_dimension=0, tiled=True
        ).astype(jnp.float32),
    )
    sums = (
        lax.psum_scatter(
            page_sums[0].astype(jnp.bfloat16), "seq", scatter_dimension=0, tiled=True
        ).astype(jnp.float32),
        lax.psum_scatter(
            page_sums[1].astype(jnp.bfloat16), "seq", scatter_dimension=0, tiled=True
        ).astype(jnp.float32),
        lax.psum_scatter(
            page_sums[2].astype(jnp.bfloat16), "seq", scatter_dimension=0, tiled=True
        ).astype(jnp.float32),
        lax.psum_scatter(
            page_sums[3].astype(jnp.bfloat16), "seq", scatter_dimension=0, tiled=True
        ).astype(jnp.float32),
        lax.psum_scatter(
            page_sums[4].astype(jnp.bfloat16), "seq", scatter_dimension=0, tiled=True
        ).astype(jnp.float32),
        lax.psum_scatter(
            page_sums[5].astype(jnp.bfloat16), "seq", scatter_dimension=0, tiled=True
        ).astype(jnp.float32),
        lax.psum_scatter(
            page_sums[6].astype(jnp.bfloat16), "seq", scatter_dimension=0, tiled=True
        ).astype(jnp.float32),
        lax.psum_scatter(
            page_sums[7].astype(jnp.bfloat16), "seq", scatter_dimension=0, tiled=True
        ).astype(jnp.float32),
        lax.psum_scatter(
            page_sums[8].astype(jnp.bfloat16), "seq", scatter_dimension=0, tiled=True
        ).astype(jnp.float32),
        lax.psum_scatter(
            page_sums[9].astype(jnp.bfloat16), "seq", scatter_dimension=0, tiled=True
        ).astype(jnp.float32),
        lax.psum_scatter(
            page_sums[10].astype(jnp.bfloat16), "seq", scatter_dimension=0, tiled=True
        ).astype(jnp.float32),
        lax.psum_scatter(
            page_sums[11].astype(jnp.bfloat16), "seq", scatter_dimension=0, tiled=True
        ).astype(jnp.float32),
        lax.psum_scatter(
            page_sums[12].astype(jnp.bfloat16), "seq", scatter_dimension=0, tiled=True
        ).astype(jnp.float32),
    )
    return (
        output.astype(jnp.bfloat16)[None],
        grad_rows.astype(jnp.bfloat16)[None],
        sums[0],
        sums[1],
        sums[2],
        sums[3],
        sums[4],
        sums[5],
        sums[6],
        sums[7],
        sums[8],
        sums[9],
        sums[10],
        sums[11],
        sums[12],
    )


MESH = pl.DeviceIdType.MESH
CHUNK = 256
MASKED = -1e30
FLAT = (((1,), (1,)), ((), ()))


def flip(index, mask):
    for b in range(mask.bit_length()):
        if mask >> b & 1:
            bit = 1 << b
            index = index + bit - 2 * bit * (index // bit % 2)
    return index


def guarded(when, action):
    if when is None:
        action()
    else:
        pl.when(when)(action)


class Wires:
    def __init__(self, sems, sizes):
        self.sems, self.sizes = sems, sizes
        self.dp, self.z = lax.axis_index("dp"), lax.axis_index("seq")
        self.dps = [flip(self.dp, m) for m in range(sizes[0])]
        self.zs = [flip(self.z, m) for m in range(sizes[1])]
        last = sizes[1] - 1
        half = self.z // 2
        step = 1 - 2 * half
        depth = self.z * step + last * half
        self.inner, self.outer = depth == 1, depth == 0
        self.right = self.z + step
        self.left = self.z - step * depth
        self.far = [self.z] + [t * step + last * half for t in (1 - depth, 2, 3)]
        self.started = []

    def peer(self, offset, step):
        return (self.dps[offset], self.zs[step])

    def send(self, src, dst, recv_sem, device, when=None):
        copy = pltpu.make_async_remote_copy(
            src_ref=src,
            dst_ref=dst,
            send_sem=self.sems.at[len(self.started)],
            recv_sem=recv_sem,
            device_id=device,
            device_id_type=MESH,
        )
        guarded(when, copy.start)
        self.started.append((copy, when))
        return len(self.started) - 1

    def sent(self, index):
        copy, when = self.started[index]
        guarded(when, copy.wait_send)
        self.started[index] = None

    def arrived(self, dst, recv_sem, when=None):
        copy = pltpu.make_async_remote_copy(
            src_ref=dst,
            dst_ref=dst,
            send_sem=self.sems.at[0],
            recv_sem=recv_sem,
            device_id=self.peer(1, 0),
            device_id_type=MESH,
        )
        guarded(when, copy.wait_recv)

    def drain(self):
        for index, entry in enumerate(self.started):
            if entry is not None:
                self.sent(index)

    def greet(self):
        n_dp, n_seq = self.sizes
        barrier = pltpu.get_barrier_semaphore()
        masks = [1 << b for b in range(n_dp.bit_length() - 1)]
        partners = [self.peer(m, 0) for m in masks] + [self.peer(0, i) for i in range(1, n_seq)]
        for device in partners:
            pl.semaphore_signal(barrier, inc=1, device_id=device, device_id_type=MESH)
        pl.semaphore_wait(barrier, len(partners))


class Line:
    def __init__(self, wires, slot, recv):
        self.w, self.slot, self.recv = wires, slot, recv

    def pass_on(self, k, src, to_left):
        w = self.w
        s = w.far[k]
        dst = self.slot(s)
        if to_left:
            w.send(src, dst, self.recv.at[s], (w.dp, w.left), w.inner)
        else:
            w.send(src, dst, self.recv.at[s], (w.dp, w.right), None if k == 0 else w.inner)

    def own(self, src):
        self.pass_on(0, src, False)
        self.pass_on(0, src, True)

    def take(self, k):
        s = self.w.far[k]
        self.w.arrived(self.slot(s), self.recv.at[s])
        self.pass_on(k, self.slot(s), k > 1)

    def relay(self, k):
        s = self.w.far[k]
        self.w.arrived(self.slot(s), self.recv.at[s], self.w.inner)
        self.pass_on(k, self.slot(s), k > 1)

    def end(self, k):
        s = self.w.far[k]
        self.w.arrived(self.slot(s), self.recv.at[s], self.w.outer)


class Gather:
    def __init__(self, wires, src, full, recv, local):
        self.w, self.src, self.full, self.recv, self.local = wires, src, full, recv, local
        n_dp, self.n_seq = wires.sizes
        self.chips = [1 << b for b in range(1, n_dp.bit_length() - 1)]
        self.slots = wires.far
        self.line = Line(wires, lambda s: full.at[wires.dp * self.n_seq + s], recv.at[0])

    def at(self, offset, step):
        return self.full.at[self.w.dps[offset] * self.n_seq + self.slots[step]]

    def order(self, step):
        return self.chips if step % 2 == 0 else self.chips[::-1]

    def forward(self, src, offset, step, masks):
        for m in masks:
            sem = self.recv.at[offset ^ m, self.slots[step]]
            self.w.send(src, self.at(offset, step), sem, self.w.peer(m, 0))

    def wait(self, offset, step):
        self.w.arrived(self.at(offset, step), self.recv.at[offset, self.slots[step]])

    def mine(self):
        return self.src

    def own_chips(self):
        self.kept = pltpu.make_async_copy(self.mine(), self.at(0, 0), self.local)
        self.kept.start()
        self.forward(self.mine(), 0, 0, self.order(0) + [1])

    def own_seq(self):
        self.line.own(self.src)

    def along_seq(self, i):
        self.line.take(i)
        self.forward(self.at(0, i), 0, i, self.order(i) + [1])

    def stages(self, step):
        have, out = [0], []
        masks = self.order(step)
        for t, m in enumerate(masks):
            out.append([(o ^ m, masks[t + 1 :] + [1]) for o in have])
            have = have + [o ^ m for o in have]
        return out

    def over_chips(self, t, step):
        for offset, masks in self.stages(step)[t]:
            self.wait(offset, step)
            self.forward(self.at(offset, step), offset, step, masks)

    def over_cores(self, stored=None):
        n_dp = self.w.sizes[0]
        for offset in list(range(0, n_dp, 2)) + list(range(1, n_dp, 2)):
            if offset % 2:
                for i in range(self.n_seq):
                    self.wait(offset, i)
            elif offset == 0:
                self.kept.wait()
            if stored is not None:
                stored(self.w.dps[offset] * self.n_seq)


class GatherDirect(Gather):
    def __init__(self, *args):
        super().__init__(*args)
        self.slots = self.w.zs

    def part_for(self, i):
        return self.src

    def own_seq(self):
        for i in range(1, self.n_seq):
            sem = self.recv.at[0, self.w.z]
            self.w.send(self.part_for(i), self.at(0, 0), sem, self.w.peer(0, i))

    def along_seq(self, i):
        self.wait(0, i)
        self.forward(self.at(0, i), 0, i, self.order(i) + [1])


class GatherColumns(GatherDirect):
    def mine(self):
        return self.src.at[self.w.z]

    def part_for(self, i):
        return self.src.at[self.w.zs[i]]


def sends_of_gather(n_dp, n_seq):
    return 2 + n_seq - 1 + n_seq * (n_dp - 1)


def group_lanes(packed, row, group, n_seq):
    total = packed[group * n_seq, row : row + 1, :]
    for s in range(1, n_seq):
        total = total + packed[group * n_seq + s, row : row + 1, :]
    return total


def spread_head(source, h, head_dim, factor):
    n_seq, rows, _ = source.shape
    block = h * head_dim // 128 * 128
    low = h * head_dim % 128
    lane = lax.broadcasted_iota(jnp.int32, (n_seq * rows, 128), 1)
    values = source[:, :, block : block + 128].reshape(n_seq * rows, 128).astype(jnp.float32)
    kept = jnp.where((lane >= low) & (lane < low + head_dim), values * factor, 0.0)
    return kept.astype(jnp.bfloat16).reshape(n_seq, rows, 128)


def front_kernel(
    sizes,
    heads,
    valid_ref,
    x_ref,
    cotangent,
    lines_ref,
    up_line_ref,
    qkv_shard,
    out_ref,
    up_ref,
    down_ref,
    columns_out,
    full_out,
    full_up,
    full_down,
    page_out,
    query_out,
    key_out,
    value_out,
    key_turned_out,
    context_out,
    logs_out,
    own_context_out,
    hidden_out,
    gelu_out,
    slope_out,
    output,
    normed_one,
    inv_one,
    grad_mid,
    sums_out,
    vec_own,
    qkv_own,
    packed,
    columns,
    page,
    held,
    context_sent,
    context_held,
    context_turned,
    value_turned,
    masked_query,
    keys,
    values,
    key_turned,
    logs,
    log_columns,
    normed_rows,
    inv_rows,
    out_matrix,
    up_matrix,
    down_matrix,
    page_turned,
    context_rows_turned,
    hidden,
    hidden_low,
    hidden_turned,
    gelu_low,
    gelu_turned,
    slopes,
    branch,
    send_sems,
    gather_sems,
    page_sems,
    context_sems,
    local_sems,
):
    n_dp, n_seq = sizes
    w = Wires(send_sems, sizes)
    rows, width = x_ref.shape
    part = width // n_seq
    head_dim = width // heads
    local_heads = heads // n_seq
    stream = rows * n_seq
    low_lane = lax.broadcasted_iota(jnp.int32, (8, 128), 1) // lines_ref.shape[1]
    lines = jnp.concatenate([lines_ref[...].astype(jnp.float32)] * n_seq, axis=1)
    vec_own[:8, :] = jnp.where(low_lane == w.z, lines, 0.0)
    vec_own[8:, :] = jnp.broadcast_to(up_line_ref[...].astype(jnp.float32), (8, 128))
    for t in range(3):
        for j in range(n_seq):
            at = t * width + j * part
            qkv_own[j, :, t * part : (t + 1) * part] = qkv_shard[:, at : at + part]
    w.greet()
    line = Line(w, lambda s: page.at[s], page_sems)
    sources = (
        (vec_own, packed),
        (qkv_own, columns),
        (out_ref, out_matrix),
        (up_ref, up_matrix),
        (down_ref, down_matrix),
    )
    vec, qkv, out, up, down = [
        (GatherDirect, GatherColumns, Gather, Gather, Gather)[k](w, src, dst, gather_sems.at[k], local_sems.at[k])
        for k, (src, dst) in enumerate(sources)
    ]
    def run(steps):
        for step in steps:
            step()

    keeps = []

    def keep(src, dst):
        keeps.append(pltpu.make_async_copy(src, dst, local_sems.at[5 + len(keeps)]))
        keeps[-1].start()

    per_block = 128 // head_dim
    scale = 1.0 / math.sqrt(head_dim)
    groups = part // 128
    one_lane = lax.broadcasted_iota(jnp.int32, (rows, 128), 1)
    ones = jnp.where(one_lane == 0, 1.0, 0.0).astype(jnp.bfloat16)
    chunk = 512
    chunks = up_matrix.shape[2] // chunk
    per_chunk = chunk // down_matrix.shape[1]
    per_part = part // out_matrix.shape[1]

    def line_of(row):
        return jnp.concatenate([group_lanes(packed, row, d, n_seq) for d in range(n_dp)], axis=1)

    def gathered_columns():
        qkv.over_cores()
        vec.over_cores()
        keep(columns, columns_out)

    def project(k):
        s = w.far[k]
        if k == 0:
            page[s] = x_ref[...]
        matrix = columns[...].reshape(width, 3 * part)
        piece = jnp.dot(page[s], matrix, preferred_element_type=jnp.float32)
        for t in range(3):
            third = piece[:, t * part : (t + 1) * part]
            if t != 1:
                bias = [group_lanes(packed, t // 2, w.z * groups + g, n_seq) for g in range(groups)]
                third = third + jnp.concatenate(bias, axis=1)
            held[t, s] = third.astype(jnp.bfloat16)

    def prepare():
        position = lax.broadcasted_iota(jnp.int32, (stream, 128), 0)
        lane = lax.broadcasted_iota(jnp.int32, (stream, 128), 1)
        guard = jnp.where(position >= valid_ref[0], MASKED, 0.0)
        guard = jnp.where(lane == 0, guard, jnp.where(lane < 4, 1.0, 0.0)).astype(jnp.bfloat16)
        for h in range(local_heads):
            masked_query[h] = spread_head(held.at[0], h, head_dim, scale)
        for b in range(local_heads // per_block):
            lanes = slice(b * 128, (b + 1) * 128)
            keys[b, :, :128] = held[1, :, :, lanes].reshape(stream, 128)
            keys[b, :, 128:] = guard
            values[b, :, :128] = held[2, :, :, lanes].reshape(stream, 128)
            values[b, :, 128:] = jnp.where(lane < 3, 1.0, 0.0).astype(jnp.bfloat16)
        turned = held[1].reshape(stream, part).T
        for h in range(local_heads):
            key_turned[h] = turned[h * head_dim : (h + 1) * head_dim, :]
        value_turned[...] = held[2].reshape(stream, part).T
        keep(masked_query, query_out)
        keep(keys, key_out)
        keep(values, value_out)
        keep(key_turned, key_turned_out)

    def attention(i):
        c = w.zs[i]

        def attend(h, _):
            at = pl.ds(pl.multiple_of(h * head_dim, head_dim), head_dim)
            query = jnp.concatenate([masked_query[h, c], ones], axis=1)
            scores = lax.dot_general(
                keys[h // per_block], query, FLAT, preferred_element_type=jnp.float32
            )
            peak = jnp.max(scores, axis=0, keepdims=True)
            raised = jnp.exp(scores - peak)
            total = jnp.sum(raised, axis=0, keepdims=True)
            mixed = jnp.dot(
                value_turned[at, :], raised.astype(jnp.bfloat16), preferred_element_type=jnp.float32
            )
            context_turned[c, at, :] = mixed / total
            logs[pl.ds(h, 1), :] = peak + jnp.log(total)
            return 0

        lax.fori_loop(0, local_heads, attend, 0)
        log_columns[c, :, :8] = logs[...].T
        piece = context_turned[c].T.astype(jnp.bfloat16)
        context_sent[i] = piece
        if i:
            w.send(context_sent.at[i], context_held.at[w.z], context_sems.at[i], w.peer(0, i))
        else:
            context_held[w.z] = piece

    def keep_logs():
        keep(log_columns, logs_out)
        keep(context_sent, own_context_out)

    def turn_page():
        for s in range(n_seq):
            page_turned[s * width : (s + 1) * width, :] = page[s].T
        keep(page_turned, page_out)

    def context_arrived():
        for i in range(1, n_seq):
            w.arrived(context_held.at[w.zs[i]], context_sems.at[i])

    def gathered_out():
        out.over_cores()
        keep(out_matrix, full_out)

    def keep_groups(unit, src, dst):
        def store(first):
            group = pl.ds(first, n_seq)
            keep(src.at[group], dst.at[group])

        unit.over_cores(store)

    def gathered_up():
        keep_groups(up, up_matrix, full_up)

    def gathered_down():
        keep_groups(down, down_matrix, full_down)

    def first_norm():
        total = x_ref[...].astype(jnp.float32) + line_of(2)
        for j in range(n_seq):
            block = out_matrix[j * per_part : (j + 1) * per_part].reshape(part, width)
            total = total + jnp.dot(context_held[j], block, preferred_element_type=jnp.float32)
            context_rows_turned[j * part : (j + 1) * part, :] = context_held[j].T
        keep(context_rows_turned, context_out)
        rows_hidden, normed, inv = norm_forward(total, line_of(3), line_of(4))
        normed_rows[...] = normed
        inv_rows[...] = jnp.broadcast_to(inv, inv_rows.shape)
        keep(normed_rows, normed_one)
        keep(inv_rows, inv_one)
        hidden[...] = rows_hidden
        hidden_low[...] = rows_hidden.astype(jnp.bfloat16)
        hidden_turned[...] = rows_hidden.T.astype(jnp.bfloat16)
        keep(hidden_turned, hidden_out)

    def expand():
        def activate(f, _):
            at = pl.ds(pl.multiple_of(f * chunk, chunk), chunk)
            block = up_matrix[:, :, at].reshape(width, chunk)
            up_bias = jnp.concatenate(
                [packed[f * per_chunk + e, 8:9, :] for e in range(per_chunk)], axis=1
            )
            act = jnp.dot(hidden_low[...], block, preferred_element_type=jnp.float32) + up_bias
            below = 0.5 + 0.5 * lax.erf(act * math.sqrt(0.5))
            gelu = act * below
            gelu_low[:, at] = gelu.astype(jnp.bfloat16)
            gelu_turned[at, :] = gelu.T.astype(jnp.bfloat16)
            bell = jnp.exp(-0.5 * act * act) * (1.0 / math.sqrt(2.0 * math.pi))
            slopes[:, at] = (below + act * bell).astype(jnp.bfloat16)
            return 0

        lax.fori_loop(0, chunks, activate, 0)
        keep(gelu_turned, gelu_out)
        keep(slopes, slope_out)

    def shrink_all():
        branch[...] = hidden[...] + line_of(5)

        def shrink(f, _):
            at = pl.ds(pl.multiple_of(f * chunk, chunk), chunk)
            block = down_matrix[pl.ds(f * per_chunk, per_chunk)].reshape(chunk, width)
            branch[...] += jnp.dot(gelu_low[:, at], block, preferred_element_type=jnp.float32)
            return 0

        lax.fori_loop(0, chunks, shrink, 0)

    out.own_seq()
    qkv.own_seq()
    vec.own_seq()
    down.own_chips()
    up.own_seq()
    qkv.own_chips()
    vec.own_chips()
    qkv.along_seq(1)
    vec.along_seq(1)
    qkv.along_seq(2)
    vec.along_seq(2)
    line.own(x_ref)
    qkv.along_seq(3)
    vec.along_seq(3)
    qkv.over_chips(0, 0)
    vec.over_chips(0, 0)
    out.own_chips()
    up.along_seq(1)
    out.along_seq(1)
    out.over_chips(0, 0)
    qkv.over_chips(0, 3)
    vec.over_chips(0, 3)
    qkv.over_chips(1, 0)
    vec.over_chips(1, 0)
    out.along_seq(2)
    out.over_chips(1, 0)
    down.own_seq()
    out.over_chips(0, 1)
    qkv.over_chips(1, 3)
    vec.over_chips(1, 3)
    line.relay(1)
    qkv.over_chips(0, 1)
    vec.over_chips(0, 1)
    qkv.over_chips(0, 2)
    vec.over_chips(0, 2)
    up.own_chips()
    up.over_chips(0, 1)
    qkv.over_chips(1, 2)
    vec.over_chips(1, 2)
    qkv.over_chips(1, 1)
    vec.over_chips(1, 1)
    out.over_chips(1, 1)
    line.end(1)
    up.along_seq(2)
    line.relay(2)
    up.over_chips(0, 0)
    out.over_chips(0, 2)
    gathered_columns()
    down.along_seq(1)
    up.along_seq(3)
    line.end(2)
    down.over_chips(0, 0)
    project(2)
    up.over_chips(1, 1)
    out.over_chips(1, 2)
    up.over_chips(0, 2)
    project(1)
    line.relay(3)
    down.over_chips(0, 1)
    line.end(3)
    project(0)
    project(3)
    up.over_chips(0, 3)
    prepare()
    up.over_chips(1, 0)
    down.over_chips(1, 1)
    down.over_chips(1, 0)
    down.along_seq(2)
    attention(0)
    down.along_seq(3)
    attention(2)
    attention(1)
    out.along_seq(3)
    attention(3)
    out.over_chips(0, 3)
    keep_logs()
    down.over_chips(0, 2)
    down.over_chips(0, 3)
    turn_page()
    out.over_chips(1, 3)
    up.over_chips(1, 2)
    up.over_chips(1, 3)
    gathered_out()
    context_arrived()
    first_norm()
    down.over_chips(1, 2)
    down.over_chips(1, 3)
    gathered_up()
    expand()
    gathered_down()
    shrink_all()
    gain_one, gain_two = line_of(3), line_of(6)
    result, normed, inv = norm_forward(branch[...], gain_two, line_of(7))
    output[...] = result.astype(jnp.bfloat16)
    grad = cotangent[...].astype(jnp.float32)
    mid, grad_gain, grad_shift = norm_backward(grad, normed, inv, gain_two)
    grad_mid[...] = mid
    grad_bias = jnp.sum(mid.astype(jnp.bfloat16).astype(jnp.float32), axis=0)
    sums_out[...] = jnp.zeros_like(sums_out)
    for row, line_sum in enumerate((grad_bias, grad_gain, grad_shift)):
        sums_out[5 + row : 6 + row, :] = line_sum.reshape(1, width)
    sums_out[3:4, :] = gain_one
    for copy in keeps:
        copy.wait()
    w.drain()


def front(sizes, heads, valid, rows, cotangent, lines, up_line, w_qkv, w_out, w_up, w_down):
    n_dp, n_seq = sizes
    devices = n_dp * n_seq
    count, width = rows.shape
    part = width // n_seq
    stream = count * n_seq
    wide = w_up.shape[1]
    low = jnp.bfloat16
    head_dim = width // heads
    local_heads = heads // n_seq
    blocks = part // 128
    attention = (
        jax.ShapeDtypeStruct((local_heads, n_seq, count, 128), low),
        jax.ShapeDtypeStruct((blocks, stream, 256), low),
        jax.ShapeDtypeStruct((blocks, stream, 256), low),
        jax.ShapeDtypeStruct((local_heads, head_dim, stream), low),
    )

    def full(shard):
        return jax.ShapeDtypeStruct((devices,) + shard.shape, shard.dtype)

    anywhere = pl.BlockSpec(memory_space=pl.ANY)
    local = pl.BlockSpec(memory_space=pltpu.VMEM)
    sends = 5 * sends_of_gather(n_dp, n_seq) + 5 + n_seq - 1
    return pl.pallas_call(
        lambda *refs: front_kernel(sizes, heads, *refs),
        out_shape=(
            jax.ShapeDtypeStruct((devices, w_qkv.shape[0], 3 * part), low),
            full(w_out),
            full(w_up),
            full(w_down),
            jax.ShapeDtypeStruct((n_seq * width, count), low),
        )
        + attention
        + (
            jax.ShapeDtypeStruct((width, count), low),
            jax.ShapeDtypeStruct((n_seq, count, 128), jnp.float32),
            jax.ShapeDtypeStruct((n_seq, count, part), low),
            jax.ShapeDtypeStruct((width, count), low),
            jax.ShapeDtypeStruct((wide, count), low),
            jax.ShapeDtypeStruct((count, wide), low),
            jax.ShapeDtypeStruct((count, width), low),
            jax.ShapeDtypeStruct((count, width), jnp.float32),
            jax.ShapeDtypeStruct((count, 128), jnp.float32),
            jax.ShapeDtypeStruct((count, width), jnp.float32),
            jax.ShapeDtypeStruct((8, width), jnp.float32),
        ),
        in_specs=[
            pl.BlockSpec(memory_space=pltpu.SMEM),
        ]
        + [local] * 5
        + [anywhere] * 3,
        out_specs=[anywhere] * 15 + [local] + [anywhere] * 2 + [local] * 2,
        scratch_shapes=[
            pltpu.VMEM((16, 128), jnp.float32),
            pltpu.VMEM((n_seq, w_qkv.shape[0], 3 * part), low),
            pltpu.VMEM((devices, 16, 128), jnp.float32),
            pltpu.VMEM((devices, w_qkv.shape[0], 3 * part), low),
            pltpu.VMEM((n_seq, count, width), low),
            pltpu.VMEM((3, n_seq, count, part), low),
            pltpu.VMEM((n_seq, count, part), low),
            pltpu.VMEM((n_seq, count, part), low),
            pltpu.VMEM((n_seq, part, count), jnp.float32),
            pltpu.VMEM((part, stream), low),
        ]
        + [pltpu.VMEM(a.shape, a.dtype) for a in attention]
        + [
            pltpu.VMEM((8, count), jnp.float32),
            pltpu.VMEM((n_seq, count, 128), jnp.float32),
            pltpu.VMEM((count, width), jnp.float32),
            pltpu.VMEM((count, 128), jnp.float32),
            pltpu.VMEM((devices,) + w_out.shape, low),
            pltpu.VMEM((devices,) + w_up.shape, low),
            pltpu.VMEM((devices,) + w_down.shape, low),
            pltpu.VMEM((n_seq * width, count), low),
            pltpu.VMEM((width, count), low),
            pltpu.VMEM((count, width), jnp.float32),
            pltpu.VMEM((count, width), low),
            pltpu.VMEM((width, count), low),
            pltpu.VMEM((count, wide), low),
            pltpu.VMEM((wide, count), low),
            pltpu.VMEM((count, wide), low),
            pltpu.VMEM((count, width), jnp.float32),
            pltpu.SemaphoreType.DMA((sends,)),
            pltpu.SemaphoreType.DMA((5, n_dp, n_seq)),
            pltpu.SemaphoreType.DMA((n_seq,)),
            pltpu.SemaphoreType.DMA((n_seq,)),
            pltpu.SemaphoreType.DMA((40,)),
        ],
        compiler_params=pltpu.CompilerParams(
            collective_id=0, has_side_effects=True, vmem_limit_bytes=60 * 2**20
        ),
        name="front",
    )(valid, rows, cotangent, lines, up_line, w_qkv, w_out, w_up, w_down)


def add_rows(into, term):
    rows = into.shape[0]
    step = min(16, rows)

    def body(r, _):
        at = pl.ds(pl.multiple_of(r * step, step), step)
        total = into[at, :].astype(jnp.float32) + term[at, :].astype(jnp.float32)
        into[at, :] = total.astype(into.dtype)
        return 0

    lax.fori_loop(0, rows // step, body, 0)


class LineSum:
    def __init__(self, wires, block, last, sems):
        self.w, self.block, self.last, self.sems = wires, block, last, sems

    def into(self, src, index, device, when):
        self.w.send(src, self.last.at[index], self.sems.at[index], device, when)

    def add(self, k, index):
        def action():
            self.w.arrived(self.last.at[index], self.sems.at[index])
            add_rows(self.block(k), self.last.at[index])

        pl.when(self.w.inner)(action)

    def offer(self, k):
        self.into(self.block(k), k - 1, (self.w.dp, self.w.right), self.w.outer)

    def relay(self, k):
        w, block = self.w, self.block(k)
        if k == 1:
            self.add(1, 4)
            self.into(block, 3, (w.dp, w.left), w.inner)
        else:
            self.add(k, k - 1)
            self.into(block, 3 if k == 2 else 4, (w.dp, w.right), w.inner)

    def finish(self, start, out):
        w = self.w
        w.arrived(self.last.at[3], self.sems.at[3])
        w.arrived(self.last.at[0], self.sems.at[0], w.inner)
        rows = out.shape[0]
        step = min(16, rows)

        def total_of(count):
            def body(r, _):
                at = pl.ds(pl.multiple_of(r * step, step), step)
                total = start(at) + self.last[3, at, :].astype(jnp.float32)
                if count == 2:
                    total = total + self.last[0, at, :].astype(jnp.float32)
                out[at, :] = total.astype(out.dtype)
                return 0

            lax.fori_loop(0, rows // step, body, 0)

        pl.when(w.inner)(lambda: total_of(2))
        pl.when(w.outer)(lambda: total_of(1))


class Scatter:
    def __init__(self, wires, kind, make, source, stage, bufs, sems, out):
        self.w, self.kind, self.make, self.source, self.stage = wires, kind, make, source, stage
        self.total, self.first, self.second, self.last = bufs
        self.core_sems, self.first_sems, self.second_sems, self.last_sems = sems
        self.out = out
        self.n_seq = wires.sizes[1]
        self.offsets = [6, 2, 4, 0]
        self.staged = {}
        self.slots = wires.far if kind == "line" else wires.zs
        self.line = LineSum(wires, lambda k: self.total.at[0, self.slots[k]], self.last, self.last_sems)

    def order(self, step):
        return (2, 4) if step % 2 == 0 else (4, 2)

    def give(self, k):
        o = self.offsets[k]
        d = self.w.dps[o ^ 1]
        if self.stage is None:
            src = self.source.at[pl.ds(d * self.n_seq, self.n_seq)]
        else:
            depth = self.stage.shape[0]
            if k >= depth:
                self.w.sent(self.staged[k - depth])
            src = self.stage.at[k % depth]

            def fill(s, _):
                src[s] = self.make(d, s).astype(src.dtype)
                return 0

            lax.fori_loop(0, self.n_seq, fill, 0)
        sem = self.core_sems.at[o // 2]
        self.staged[k] = self.w.send(src, self.total.at[o // 2], sem, self.w.peer(1, 0))

    def give_steps(self):
        return [lambda k=k: self.give(k) for k in range(4)]

    def over_cores(self, k):
        o = self.offsets[k]
        d = self.w.dps[o]
        self.w.arrived(self.total.at[o // 2], self.core_sems.at[o // 2])

        def add(s, _):
            block = self.total.at[o // 2, s]
            block[...] = (block[...].astype(jnp.float32) + self.make(d, s)).astype(block.dtype)
            return 0

        lax.fori_loop(0, self.n_seq, add, 0)
        self.hand_on(k, (3, 2))

    def spread(self, k):
        self.hand_on(k, (1, 0))

    def hand_on(self, k, steps):
        o = self.offsets[k]
        for i in steps:
            mask = self.order(i)[0]
            block = self.total.at[o // 2, self.slots[i]]
            if o & mask:
                keep = (o ^ mask) // (6 ^ mask)
                self.w.send(block, self.first.at[i, keep], self.first_sems.at[i, keep], self.w.peer(mask, 0))

    def over_chips(self, i):
        mask = self.order(i)[1]
        for keep in (1, 0):
            o = mask * keep
            block = self.total.at[o // 2, self.slots[i]]
            self.w.arrived(self.first.at[i, keep], self.first_sems.at[i, keep])
            add_rows(block, self.first.at[i, keep])
            if keep:
                self.w.send(block, self.second.at[i], self.second_sems.at[i], self.w.peer(mask, 0))

    def to_seq(self, i):
        block = self.total.at[0, self.slots[i]]
        self.w.arrived(self.second.at[i], self.second_sems.at[i])
        add_rows(block, self.second.at[i])
        if self.kind == "line":
            if i:
                self.line.offer(i)
        elif i:
            self.w.send(block, self.last.at[i], self.last_sems.at[i], self.w.peer(0, i))

    def relay(self, i):
        self.line.relay(i)

    def finish(self):
        block = self.total.at[0, self.w.z]
        if self.kind == "line":
            self.line.finish(lambda at: block[at, :].astype(jnp.float32), self.out)
            return
        for i in range(1, self.n_seq):
            self.w.arrived(self.last.at[i], self.last_sems.at[i])
        if self.kind == "direct":
            total = block[...]
            for i in range(1, self.n_seq):
                total = total + self.last[i]
            lines, up_line = self.out
            up_line[...] = total[8:9, :]
            share = lines.shape[1]
            total = total[:8, :]
            shown = total[:, :share]
            for s in range(1, self.n_seq):
                shown = jnp.where(self.w.z == s, total[:, s * share : (s + 1) * share], shown)
            lines[...] = shown
            return
        for i in range(self.n_seq):
            term = block[...] if i == 0 else self.last[i]
            part = term.shape[1] // 3
            for t in range(3):
                at = t * part * self.n_seq + self.w.zs[i] * part
                self.out[:, pl.ds(pl.multiple_of(at, part), part)] = term[
                    :, t * part : (t + 1) * part
                ].astype(jnp.float32)


def back_kernel(sizes, heads, *refs):
    n_dp, n_seq = sizes
    (
        mid_in,
        normed_in,
        inv_in,
        sums_in,
        logs_in,
        page_in,
        query_in,
        key_in,
        value_in,
        key_turned_in,
        context_in,
        hidden_in,
        gelu_in,
        slope_in,
        own_context_in,
        columns_in,
        out_in,
        up_in,
        down_in,
        grad_rows,
        *outs,
    ) = refs[:26]
    scratch = list(refs[26:])

    def take(count):
        got = scratch[:count]
        del scratch[:count]
        return got

    send_sems, core_sems, first_sems, second_sems, last_sems, block_sems = take(6)
    head_sems, local_sems, row_sems = take(3)
    logs, own_context, grads, masked_query, keys, values, key_turned, masked_grad = take(8)
    query_lanes, query_grad, key_grad, value_grad = take(4)
    project, turned, columns, vec = take(4)
    row_terms, row_last, own_rows, partial = take(4)
    hidden_turned, context_turned, slopes, normed = take(4)
    grad_low, grad_sent, out_matrix, down_blocks, up_blocks = take(5)
    down_stage, up_stage, out_stage = take(3)
    units = [take(4) for k in range(5)]
    w = Wires(send_sems, sizes)
    rows, width = normed.shape
    part = width // n_seq
    wide = slopes.shape[1]
    head_dim = width // heads
    local_heads = heads // n_seq
    stream = rows * n_seq
    per_block = 128 // head_dim
    scale = 1.0 / math.sqrt(head_dim)
    loads = {}

    def load(name, src, dst):
        loads[name] = pltpu.make_async_copy(src, dst, local_sems.at[len(loads)])
        loads[name].start()

    load("mid", mid_in, own_rows)
    load("gelu", gelu_in, turned)
    load("slope", slope_in, slopes)
    blocks = []
    for f in range(n_dp):
        sem = block_sems.at[0, f % 2]
        blocks.append(pltpu.make_async_copy(down_in.at[pl.ds(f * n_seq, n_seq)], down_blocks.at[f % 2], sem))
    shares = wide // width
    half = up_in.shape[0] // 2
    ups = []
    for e in range(2 * shares):
        src = up_in.at[pl.ds(e // shares * half, half), :, pl.ds(e % shares * width, width)]
        ups.append(pltpu.make_async_copy(src, up_blocks.at[e % 2], block_sems.at[1, e % 2]))
    for e in range(2):
        blocks[e].start()
        ups[e].start()
    load("hidden", hidden_in, hidden_turned)
    load("normed", normed_in, normed)
    load("out", out_in, out_matrix)
    load("context", context_in, context_turned)
    load("logs", logs_in, logs)
    load("own", own_context_in, own_context)
    load("columns", columns_in, columns)
    load("query", query_in, masked_query)
    load("key", key_in, keys)
    load("value", value_in, values)
    load("turned", key_turned_in, key_turned)
    w.greet()

    def rows_from(source, first, count):
        return source[pl.ds(pl.multiple_of(first, count), count), :]

    def down_term(d, s):
        left = rows_from(turned, (d * n_seq + s) * outs[0].shape[0], outs[0].shape[0])
        return jnp.dot(left, grad_low[...], preferred_element_type=jnp.float32)

    def up_term(d, s):
        left = rows_from(hidden_turned, (d * n_seq + s) * outs[1].shape[0], outs[1].shape[0])
        return jnp.dot(left, slopes[...], preferred_element_type=jnp.float32)

    def out_term(d, s):
        left = rows_from(context_turned, (d * n_seq + s) * outs[2].shape[0], outs[2].shape[0])
        return jnp.dot(left, grad_low[...], preferred_element_type=jnp.float32)

    def held_term(source):
        return lambda d, s: source[d * n_seq + s].astype(jnp.float32)

    makes = (down_term, up_term, out_term, held_term(partial), held_term(vec))
    stages = (down_stage, up_stage, out_stage, None, None)
    scatters = []
    for k in range(5):
        scatters.append(
            Scatter(
                w,
                ("line", "line", "line", "columns", "direct")[k],
                makes[k],
                (None, None, None, partial, vec)[k],
                stages[k],
                units[k],
                (core_sems.at[k], first_sems.at[k], second_sems.at[k], last_sems.at[k]),
                outs[k] if k < 4 else outs[4:],
            )
        )
    down, up, out, qkv, small = scatters
    row_sum = LineSum(w, lambda k: row_terms.at[k - 1], row_last, row_sems)
    span = wide // n_dp

    def run(steps):
        for step in steps:
            step()

    low_lane = lax.broadcasted_iota(jnp.int32, (rows, 128), 1)

    def in_lanes(column, first, base):
        rest = -column
        for n in range(3):
            piece = rest.astype(jnp.bfloat16).astype(jnp.float32)
            base = jnp.where(low_lane == first + n, piece, base)
            rest = rest - piece
        return base.astype(jnp.bfloat16)

    def keep_line(row, line):
        for d in range(n_dp):
            for s in range(n_seq):
                vec[d * n_seq + s, row : row + 1, :] = line[:, d * 128 : (d + 1) * 128]

    def begin():
        loads["mid"].wait()
        grad_low[...] = own_rows[...].astype(jnp.bfloat16)
        loads["gelu"].wait()

    def slope_of(f):
        if f == 0:
            loads["slope"].wait()
        blocks[f].wait()
        grad_gelu = lax.dot_general(
            grad_low[...], down_blocks[f % 2].reshape(span, width), FLAT, preferred_element_type=jnp.float32
        )
        if f + 2 < n_dp:
            blocks[f + 2].start()
        at = slice(f * span, (f + 1) * span)
        slopes[:, at] = (grad_gelu * slopes[:, at].astype(jnp.float32)).astype(jnp.bfloat16)
        if f == n_dp - 1:
            loads["hidden"].wait()

    def hidden_of(e):
        ups[e].wait()
        columns_at = slice(e % shares * width, (e % shares + 1) * width)
        rows_at = slice(e // shares * width // 2, (e // shares + 1) * width // 2)
        own_rows[:, rows_at] += lax.dot_general(
            slopes[:, columns_at],
            up_blocks[e % 2].reshape(width // 2, width),
            FLAT,
            preferred_element_type=jnp.float32,
        )
        if e + 2 < 2 * shares:
            ups[e + 2].start()

    def norm_back():
        load("page", page_in, turned)
        loads["normed"].wait()
        first, grad_gain, grad_shift = norm_backward(
            own_rows[...], normed[...], inv_in[:, :1], sums_in[3:4, :]
        )
        own_rows[...] = first
        grad_low[...] = first.astype(jnp.bfloat16)
        vec[...] = jnp.zeros_like(vec)
        keep_line(3, grad_gain.reshape(1, width))
        keep_line(4, grad_shift.reshape(1, width))

    def send_grads():
        loads["out"].wait()
        for i in (1, 2, 3, 0):
            j = w.zs[i]
            share = part // out_matrix.shape[1]
            block = out_matrix[pl.ds(j * share, share)].reshape(part, width)
            piece = lax.dot_general(grad_low[...], block, FLAT, preferred_element_type=jnp.float32)
            if i:
                grad_sent[i] = piece.astype(jnp.bfloat16)
                w.send(grad_sent.at[i], grads.at[w.z], head_sems.at[i], w.peer(0, i))
            else:
                grads[w.z] = piece.astype(jnp.bfloat16)
        loads["context"].wait()

    def keep_lines():
        up_bias = jnp.sum(slopes[...].astype(jnp.float32), axis=0, keepdims=True)
        for d in range(n_dp * n_seq):
            vec[d, 8:9, :] = up_bias[:, d * 128 : (d + 1) * 128]
        keep_line(2, jnp.sum(grad_low[...].astype(jnp.float32), axis=0, keepdims=True))
        for row in (5, 6, 7):
            keep_line(row, sums_in[row : row + 1, :])

    def prepare():
        for name in ("columns", "logs", "own", "query", "key", "value", "turned"):
            loads[name].wait()
        key_grad[...] = jnp.zeros_like(key_grad)
        value_grad[...] = jnp.zeros_like(value_grad)

    def attention(i):
        c = w.zs[i]
        if i:
            w.arrived(grads.at[c], head_sems.at[i])
        one = jnp.where(low_lane == 0, 1.0, 0.0)
        for h in range(local_heads):
            block = h // per_block * 128
            grad = spread_head(grads.at[pl.ds(c, 1)], h, head_dim, 1.0)[0]
            centre = jnp.sum(
                grad.astype(jnp.float32) * own_context[i, :, block : block + 128].astype(jnp.float32),
                axis=1,
                keepdims=True,
            )
            masked_grad[h, :, :128] = grad
            masked_grad[h, :, 128:] = in_lanes(centre, 0, jnp.zeros_like(one))
            query_lanes[h] = in_lanes(logs[c, :, h : h + 1], 1, one)

        def head(h, _):
            block = h // per_block
            query, grad = masked_query[h, c], masked_grad[h, :, :128]
            scores = lax.dot_general(
                keys[block],
                jnp.concatenate([query, query_lanes[h]], axis=1),
                FLAT,
                preferred_element_type=jnp.float32,
            )
            probs = jnp.exp(scores)
            moved = lax.dot_general(values[block], masked_grad[h], FLAT, preferred_element_type=jnp.float32)
            slope = (probs * moved).astype(jnp.bfloat16)
            query_grad[h] = jnp.dot(key_turned[h], slope, preferred_element_type=jnp.float32) * scale
            key_grad[block] += jnp.dot(slope, query, preferred_element_type=jnp.float32)
            value_grad[block] += jnp.dot(
                probs.astype(jnp.bfloat16), grad, preferred_element_type=jnp.float32
            )
            return 0

        lax.fori_loop(0, local_heads, head, 0)
        project[pl.ds(pl.multiple_of(c * rows, rows), rows), :part] = (
            query_grad[...].reshape(part, rows).T.astype(jnp.bfloat16)
        )

    def keep_project():
        for t, total in ((1, key_grad), (2, value_grad)):
            for b in range(local_heads // per_block):
                at = t * part + b * 128
                project[:, at : at + 128] = total[b].astype(jnp.bfloat16)

    def row_term(k):
        term = lax.dot_general(
            rows_from(project, w.far[k] * rows, rows),
            columns[...].reshape(width, 3 * part),
            FLAT,
            preferred_element_type=jnp.float32,
        )
        if k:
            row_terms[k - 1] = term.astype(jnp.bfloat16)
            row_sum.offer(k)
        else:
            own_rows[...] += term

    def weight_grad():
        loads["page"].wait()
        for t in range(3):
            at = slice(t * part, (t + 1) * part)
            block = jnp.dot(turned[:width, :], project[:rows, at], preferred_element_type=jnp.float32)
            for s in range(1, n_seq):
                block = block + jnp.dot(
                    turned[s * width : (s + 1) * width, :],
                    project[s * rows : (s + 1) * rows, at],
                    preferred_element_type=jnp.float32,
                )
            partial[:, :, at] = block.astype(jnp.bfloat16).reshape(n_dp * n_seq, -1, part)

    def give_small():
        groups = part // 128
        for b, t in ((0, 0), (1, 2)):
            sums = jnp.sum(project[:, t * part : (t + 1) * part].astype(jnp.float32), axis=0, keepdims=True)
            for g in range(groups):
                for s in range(n_seq):
                    vec[(w.z * groups + g) * n_seq + s, b : b + 1, :] = sums[:, g * 128 : (g + 1) * 128]
        run(small.give_steps())

    begin()
    down.give(0)
    down.give(1)
    slope_of(0)
    slope_of(1)
    down.give(2)
    down.give(3)
    down.over_cores(0)
    slope_of(2)
    slope_of(3)
    hidden_of(0)
    hidden_of(1)
    down.over_cores(1)
    slope_of(4)
    down.over_cores(2)
    down.spread(0)
    slope_of(5)
    slope_of(6)
    slope_of(7)
    hidden_of(2)
    down.spread(2)
    hidden_of(3)
    hidden_of(4)
    hidden_of(5)
    down.over_cores(3)
    up.give(0)
    hidden_of(6)
    hidden_of(7)
    down.over_chips(3)
    norm_back()
    send_grads()
    down.over_chips(2)
    prepare()
    attention(0)
    down.over_chips(1)
    down.to_seq(3)
    attention(2)
    down.to_seq(2)
    attention(3)
    down.to_seq(1)
    attention(1)
    keep_project()
    row_term(3)
    down.spread(1)
    up.over_cores(0)
    up.spread(0)
    up.give(1)
    out.give(0)
    out.give(1)
    down.relay(2)
    out.give(2)
    up.give(2)
    up.give(3)
    down.relay(3)
    row_term(2)
    out.give(3)
    weight_grad()
    keep_lines()
    up.over_cores(2)
    up.over_cores(1)
    qkv.give(0)
    qkv.give(1)
    qkv.give(2)
    qkv.give(3)
    row_sum.relay(3)
    out.over_cores(0)
    up.over_cores(3)
    give_small()
    qkv.over_cores(2)
    small.over_cores(2)
    down.relay(1)
    qkv.over_cores(0)
    small.over_cores(0)
    qkv.spread(2)
    small.spread(2)
    qkv.spread(0)
    small.spread(0)
    row_term(1)
    qkv.over_cores(3)
    small.over_cores(3)
    up.over_chips(3)
    row_sum.relay(2)
    out.over_cores(2)
    qkv.over_cores(1)
    small.over_cores(1)
    up.over_chips(2)
    row_term(0)
    out.over_cores(3)
    row_sum.relay(1)
    qkv.spread(1)
    small.spread(1)
    qkv.over_chips(1)
    small.over_chips(1)
    up.spread(2)
    out.spread(0)
    up.to_seq(3)
    out.over_cores(1)
    out.spread(2)
    up.to_seq(2)
    out.over_chips(3)
    qkv.over_chips(2)
    small.over_chips(2)
    qkv.to_seq(1)
    small.to_seq(1)
    up.over_chips(1)
    up.relay(3)
    qkv.over_chips(0)
    small.over_chips(0)
    out.over_chips(2)
    up.spread(1)
    down.over_chips(0)
    out.to_seq(3)
    out.to_seq(2)
    up.relay(2)
    out.over_chips(1)
    qkv.to_seq(0)
    small.to_seq(0)
    row_sum.finish(lambda at: own_rows[at, :], grad_rows)
    qkv.to_seq(2)
    small.to_seq(2)
    out.spread(1)
    up.to_seq(1)
    up.relay(1)
    qkv.over_chips(3)
    small.over_chips(3)
    up.over_chips(0)
    out.relay(3)
    out.over_chips(0)
    out.to_seq(1)
    out.relay(1)
    down.to_seq(0)
    down.finish()
    out.relay(2)
    qkv.to_seq(3)
    small.to_seq(3)
    up.to_seq(0)
    up.finish()
    qkv.finish()
    small.finish()
    out.to_seq(0)
    out.finish()
    w.drain()


def back(sizes, heads, saved, w_shapes):
    n_dp, n_seq = sizes
    devices = n_dp * n_seq
    mid, normed, _, _, logs, page, query, key, value, key_turned, context, hidden, gelu, slopes, own_context = saved[:15]
    columns, full_out, full_up, full_down = saved[15:]
    count, width = normed.shape
    part = width // n_seq
    stream = count * n_seq
    local_heads, head_dim, _ = key_turned.shape
    blocks = part // 128
    low = jnp.bfloat16
    shapes = [w_shapes[0], w_shapes[1], w_shapes[2], columns.shape[1:], (16, 128)]
    kinds = [low] * 4 + [jnp.float32]
    results = [jax.ShapeDtypeStruct(shape, jnp.float32) for shape in shapes]
    results[3] = jax.ShapeDtypeStruct((shapes[3][0], n_seq * shapes[3][1]), jnp.float32)
    results[4:] = [
        jax.ShapeDtypeStruct((8, width // devices), jnp.float32),
        jax.ShapeDtypeStruct((1, 128), jnp.float32),
    ]
    anywhere = pl.BlockSpec(memory_space=pl.ANY)
    local = pl.BlockSpec(memory_space=pltpu.VMEM)
    sends = 5 * (4 + 3 * n_seq + 6) + 6 + n_seq - 1
    chips = n_dp // 2

    def like(array):
        return pltpu.VMEM(array.shape, array.dtype)

    scratch = [
        pltpu.SemaphoreType.DMA((sends,)),
        pltpu.SemaphoreType.DMA((5, chips)),
        pltpu.SemaphoreType.DMA((5, n_seq, 2)),
        pltpu.SemaphoreType.DMA((5, n_seq)),
        pltpu.SemaphoreType.DMA((5, 5)),
        pltpu.SemaphoreType.DMA((2, 2)),
        pltpu.SemaphoreType.DMA((n_seq,)),
        pltpu.SemaphoreType.DMA((15,)),
        pltpu.SemaphoreType.DMA((5,)),
        like(logs),
        like(own_context),
        pltpu.VMEM((n_seq, count, part), low),
        like(query),
        like(key),
        like(value),
        like(key_turned),
        pltpu.VMEM((local_heads, count, 256), low),
        pltpu.VMEM((local_heads, count, 128), low),
        pltpu.VMEM((local_heads, head_dim, count), jnp.float32),
        pltpu.VMEM((blocks, stream, 128), jnp.float32),
        pltpu.VMEM((blocks, stream, 128), jnp.float32),
        pltpu.VMEM((stream, 3 * part), low),
        like(gelu),
        like(columns),
        pltpu.VMEM((devices, 16, 128), jnp.float32),
        pltpu.VMEM((n_seq - 1, count, width), low),
        pltpu.VMEM((5, count, width), low),
        pltpu.VMEM((count, width), jnp.float32),
        like(columns),
        like(hidden),
        like(context),
        like(slopes),
        like(normed),
        pltpu.VMEM((count, width), low),
        pltpu.VMEM((n_seq, count, part), low),
        like(full_out),
        pltpu.VMEM((2, n_seq) + shapes[0], low),
        pltpu.VMEM((2, devices // 2, full_up.shape[1], width), low),
        pltpu.VMEM((2, n_seq) + shapes[0], low),
        pltpu.VMEM((2, n_seq) + shapes[1], low),
        pltpu.VMEM((2, n_seq) + shapes[2], low),
    ]
    for shape, kind in zip(shapes, kinds):
        scratch += [
            pltpu.VMEM((chips, n_seq) + shape, kind),
            pltpu.VMEM((n_seq, 2) + shape, kind),
            pltpu.VMEM((n_seq,) + shape, kind),
            pltpu.VMEM((5,) + shape, kind),
        ]
    return pl.pallas_call(
        lambda *refs: back_kernel(sizes, heads, *refs),
        out_shape=[jax.ShapeDtypeStruct((count, width), low)] + results,
        in_specs=[anywhere] * 2 + [local] * 2 + [anywhere] * 15,
        out_specs=[local] * 7,
        scratch_shapes=scratch,
        compiler_params=pltpu.CompilerParams(
            collective_id=1, has_side_effects=True, vmem_limit_bytes=63 * 2**20
        ),
        name="back",
    )(*saved)


def kernel_plan(
    x_in,
    w_qkv,
    q_bias,
    v_bias,
    w_out,
    out_bias,
    ln1_gain,
    ln1_shift,
    w_up,
    up_bias,
    w_down,
    down_bias,
    ln2_gain,
    ln2_shift,
    valid,
    cotangent,
):
    sizes = (lax.axis_size("dp"), lax.axis_size("seq"))
    n_dp, groups = sizes
    rows = x_in[0]
    count, width = rows.shape
    vectors = (q_bias, v_bias, out_bias, ln1_gain, ln1_shift, down_bias, ln2_gain, ln2_shift)
    lines = jnp.stack(vectors)
    (
        columns,
        full_out,
        full_up,
        full_down,
        page_turned,
        query,
        key,
        value,
        key_turned,
        context,
        logs,
        own_context,
        hidden,
        gelu,
        slopes,
        output,
        normed,
        inv,
        grad_mid,
        line_sums,
    ) = front(sizes, HEADS, valid, rows, cotangent[0], lines, up_bias[None], w_qkv, w_out, w_up, w_down)
    saved = (grad_mid, normed, inv, line_sums, logs, page_turned, query, key, value, key_turned)
    saved += (context, hidden, gelu, slopes, own_context, columns, full_out, full_up, full_down)
    devices = n_dp * groups
    grad_rows, *sums = back(sizes, HEADS, saved, (w_down.shape, w_up.shape, w_out.shape))
    mine = sums[4]
    return (
        output[None],
        grad_rows[None],
        sums[3],
        mine[0],
        mine[1],
        sums[2],
        mine[2],
        mine[3],
        mine[4],
        sums[1],
        sums[5].reshape(-1),
        sums[0],
        mine[5],
        mine[6],
        mine[7],
    )


def solution(mesh):
    n_dp, n_seq = mesh.shape["dp"], mesh.shape["seq"]

    def per_device(x_in, w_qkv, *rest):
        part, width = w_qkv.shape[0], x_in.shape[2]
        fits = (n_dp, n_seq) == (8, 4) and part % 32 == 0 and part * n_seq == 128 and width // n_seq % 128 == 0 and x_in.shape[0] == 1
        plan = kernel_plan if fits else general_plan
        return plan(x_in, w_qkv, *rest)

    return jax.shard_map(
        per_device,
        mesh=mesh,
        in_specs=(
            P("dp", "seq", None),
            P(("dp", "seq"), None),
            P(("dp", "seq")),
            P(("dp", "seq")),
            P(("dp", "seq"), None),
            P(("dp", "seq")),
            P(("dp", "seq")),
            P(("dp", "seq")),
            P(("dp", "seq"), None),
            P(("dp", "seq")),
            P(("dp", "seq"), None),
            P(("dp", "seq")),
            P(("dp", "seq")),
            P(("dp", "seq")),
            P("dp"),
            P("dp", "seq", None),
        ),
        out_specs=(
            P("dp", "seq", None),
            P("dp", "seq", None),
            P(("dp", "seq"), None),
            P(("dp", "seq")),
            P(("dp", "seq")),
            P(("dp", "seq"), None),
            P(("dp", "seq")),
            P(("dp", "seq")),
            P(("dp", "seq")),
            P(("dp", "seq"), None),
            P(("dp", "seq")),
            P(("dp", "seq"), None),
            P(("dp", "seq")),
            P(("dp", "seq")),
            P(("dp", "seq")),
        ),
        check_vma=False,
    )
```

```python
import math

import jax
import jax.numpy as jnp
from jax import lax
from jax.experimental import pallas as pl
from jax.experimental.pallas import tpu as pltpu
from jax.sharding import PartitionSpec as P

HEADS = 16


eps_norm = 1e-05


def outer_sum(left, right):
    return lax.dot_general(
        left, right, (((0,), (0,)), ((), ())), preferred_element_type=jnp.float32
    )


def times_back(rows, matrix):
    return lax.dot_general(
        rows, matrix, (((1,), (1,)), ((), ())), preferred_element_type=jnp.float32
    )


def gelu_exact(values):
    return jax.nn.gelu(values, approximate=False)


def norm_forward(rows, gain, shift):
    center = rows - jnp.mean(rows, axis=-1, keepdims=True)
    inv_std = lax.rsqrt(jnp.mean(center * center, axis=-1, keepdims=True) + eps_norm)
    normed = center * inv_std
    return (normed * gain + shift, normed, inv_std)


def norm_backward(grad_out, normed, inv_std, gain):
    scaled = grad_out * gain
    grad_rows = inv_std * (
        scaled
        - jnp.mean(scaled, axis=-1, keepdims=True)
        - normed * jnp.mean(scaled * normed, axis=-1, keepdims=True)
    )
    return (grad_rows, jnp.sum(grad_out * normed, axis=0), jnp.sum(grad_out, axis=0))


def to_heads(rows, groups):
    count, width = rows.shape
    return rows.reshape(count, groups, width // groups).transpose(1, 0, 2).reshape(groups, -1)


def from_heads(pieces, part_width):
    groups = pieces.shape[0]
    return (
        pieces.reshape(groups, -1, part_width).transpose(1, 0, 2).reshape(-1, groups * part_width)
    )


def general_plan(
    x_in,
    w_qkv,
    q_bias,
    v_bias,
    w_out,
    out_bias,
    ln1_gain,
    ln1_shift,
    w_up,
    up_bias,
    w_down,
    down_bias,
    ln2_gain,
    ln2_shift,
    valid,
    cotangent,
):
    shards = (
        w_qkv,
        q_bias,
        v_bias,
        w_out,
        out_bias,
        ln1_gain,
        ln1_shift,
        w_up,
        up_bias,
        w_down,
        down_bias,
        ln2_gain,
        ln2_shift,
    )
    weights = (
        lax.all_gather(shards[0], ("dp", "seq"), axis=0, tiled=True),
        lax.all_gather(shards[1], ("dp", "seq"), axis=0, tiled=True),
        lax.all_gather(shards[2], ("dp", "seq"), axis=0, tiled=True),
        lax.all_gather(shards[3], ("dp", "seq"), axis=0, tiled=True),
        lax.all_gather(shards[4], ("dp", "seq"), axis=0, tiled=True),
        lax.all_gather(shards[5], ("dp", "seq"), axis=0, tiled=True),
        lax.all_gather(shards[6], ("dp", "seq"), axis=0, tiled=True),
        lax.all_gather(shards[7], ("dp", "seq"), axis=0, tiled=True),
        lax.all_gather(shards[8], ("dp", "seq"), axis=0, tiled=True),
        lax.all_gather(shards[9], ("dp", "seq"), axis=0, tiled=True),
        lax.all_gather(shards[10], ("dp", "seq"), axis=0, tiled=True),
        lax.all_gather(shards[11], ("dp", "seq"), axis=0, tiled=True),
        lax.all_gather(shards[12], ("dp", "seq"), axis=0, tiled=True),
    )
    (
        full_qkv,
        full_qbias,
        full_vbias,
        full_out,
        full_obias,
        full_gain1,
        full_shift1,
        full_up,
        full_ubias,
        full_down,
        full_dbias,
        full_gain2,
        full_shift2,
    ) = weights
    groups = lax.axis_size("seq")
    rows = x_in[0]
    count, width = rows.shape
    head_dim = width // HEADS
    part_width = width // groups
    local_heads = HEADS // groups
    stream = count * groups
    qrows = min(512, stream)
    nblocks = stream // qrows
    scale = 1.0 / math.sqrt(head_dim)
    keep = jnp.arange(stream, dtype=jnp.int32) < valid[0]
    bias_row = jnp.concatenate([full_qbias, jnp.zeros_like(full_qbias), full_vbias]).astype(
        jnp.float32
    )
    project = (jnp.dot(rows, full_qkv, preferred_element_type=jnp.float32) + bias_row).astype(
        jnp.bfloat16
    )
    sent = (
        to_heads(project[:, :width], groups),
        to_heads(project[:, width : 2 * width], groups),
        to_heads(project[:, 2 * width :], groups),
    )
    arrived = (
        lax.all_to_all(sent[0], "seq", split_axis=0, concat_axis=0, tiled=True),
        lax.all_to_all(sent[1], "seq", split_axis=0, concat_axis=0, tiled=True),
        lax.all_to_all(sent[2], "seq", split_axis=0, concat_axis=0, tiled=True),
    )
    query_blocks = arrived[0].reshape(nblocks, qrows, local_heads, head_dim)
    key_heads = arrived[1].reshape(stream, local_heads, head_dim)
    value_heads = arrived[2].reshape(stream, local_heads, head_dim)

    def masked_scores(query):
        scores = (
            jnp.einsum("qhd,khd->hqk", query, key_heads, preferred_element_type=jnp.float32) * scale
        )
        return jnp.where(keep[None, None, :], scores, -1e30)

    def attend_forward(query):
        scores = masked_scores(query)
        peak = jnp.max(scores, axis=-1, keepdims=True)
        raised = jnp.exp(scores - peak)
        total = jnp.sum(raised, axis=-1, keepdims=True)
        probs = (raised / total).astype(jnp.bfloat16)
        context = jnp.einsum("hqk,khd->qhd", probs, value_heads, preferred_element_type=jnp.float32)
        return (context.astype(jnp.bfloat16), (peak + jnp.log(total))[..., 0])

    context, log_sums = lax.map(attend_forward, query_blocks)
    returned_ctx = lax.all_to_all(
        context.reshape(groups, -1), "seq", split_axis=0, concat_axis=0, tiled=True
    )
    context_rows = from_heads(returned_ctx, part_width)
    attn_out = jnp.dot(
        context_rows, full_out, preferred_element_type=jnp.float32
    ) + full_obias.astype(jnp.float32)
    first_rows = rows.astype(jnp.float32) + attn_out
    hidden, normed_one, inv_one = norm_forward(
        first_rows, full_gain1.astype(jnp.float32), full_shift1.astype(jnp.float32)
    )
    hidden_low = hidden.astype(jnp.bfloat16)
    up_act = jnp.dot(hidden_low, full_up, preferred_element_type=jnp.float32) + full_ubias.astype(
        jnp.float32
    )
    gelu_low = gelu_exact(up_act).astype(jnp.bfloat16)
    branch = jnp.dot(gelu_low, full_down, preferred_element_type=jnp.float32) + full_dbias.astype(
        jnp.float32
    )
    output, normed_two, inv_two = norm_forward(
        hidden + branch, full_gain2.astype(jnp.float32), full_shift2.astype(jnp.float32)
    )
    again = (
        lax.all_gather(shards[0], ("dp", "seq"), axis=0, tiled=True),
        lax.all_gather(shards[1], ("dp", "seq"), axis=0, tiled=True),
        lax.all_gather(shards[2], ("dp", "seq"), axis=0, tiled=True),
        lax.all_gather(shards[3], ("dp", "seq"), axis=0, tiled=True),
        lax.all_gather(shards[4], ("dp", "seq"), axis=0, tiled=True),
        lax.all_gather(shards[5], ("dp", "seq"), axis=0, tiled=True),
        lax.all_gather(shards[6], ("dp", "seq"), axis=0, tiled=True),
        lax.all_gather(shards[7], ("dp", "seq"), axis=0, tiled=True),
        lax.all_gather(shards[8], ("dp", "seq"), axis=0, tiled=True),
        lax.all_gather(shards[9], ("dp", "seq"), axis=0, tiled=True),
        lax.all_gather(shards[10], ("dp", "seq"), axis=0, tiled=True),
        lax.all_gather(shards[11], ("dp", "seq"), axis=0, tiled=True),
        lax.all_gather(shards[12], ("dp", "seq"), axis=0, tiled=True),
    )
    back_qkv, back_out, back_gain1, back_up, back_down, back_gain2 = (
        again[0],
        again[3],
        again[5],
        again[7],
        again[9],
        again[11],
    )
    grad_out = cotangent[0].astype(jnp.float32)
    grad_mid, grad_ln2_gain, grad_ln2_shift = norm_backward(
        grad_out, normed_two, inv_two, back_gain2.astype(jnp.float32)
    )
    grad_branch = grad_mid.astype(jnp.bfloat16)
    grad_w_down = outer_sum(gelu_low, grad_branch)
    grad_down_bias = jnp.sum(grad_branch.astype(jnp.float32), axis=0)
    grad_gelu = times_back(grad_branch, back_down)
    grad_up = jax.vjp(gelu_exact, up_act)[1](grad_gelu)[0].astype(jnp.bfloat16)
    grad_w_up = outer_sum(hidden_low, grad_up)
    grad_up_bias = jnp.sum(grad_up.astype(jnp.float32), axis=0)
    grad_hidden = times_back(grad_up, back_up) + grad_mid
    grad_first, grad_ln1_gain, grad_ln1_shift = norm_backward(
        grad_hidden, normed_one, inv_one, back_gain1.astype(jnp.float32)
    )
    grad_attn = grad_first.astype(jnp.bfloat16)
    grad_w_out = outer_sum(context_rows, grad_attn)
    grad_out_bias = jnp.sum(grad_attn.astype(jnp.float32), axis=0)
    grad_context = times_back(grad_attn, back_out).astype(jnp.bfloat16)
    grad_ctx_heads = lax.all_to_all(
        to_heads(grad_context, groups), "seq", split_axis=0, concat_axis=0, tiled=True
    )
    grad_ctx_blocks = grad_ctx_heads.reshape(nblocks, qrows, local_heads, head_dim)

    def attend_backward(carry, inputs):
        key_total, value_total = carry
        query, grad_ctx, log_rows = inputs
        scores = masked_scores(query)
        probs = jnp.exp(scores - log_rows[..., None])
        probs_low = probs.astype(jnp.bfloat16)
        d_probs = jnp.einsum(
            "qhd,khd->hqk", grad_ctx, value_heads, preferred_element_type=jnp.float32
        )
        centre = jnp.sum(probs * d_probs, axis=-1, keepdims=True)
        grad_scores = (probs * (d_probs - centre)).astype(jnp.bfloat16)
        grad_query = (
            jnp.einsum("hqk,khd->qhd", grad_scores, key_heads, preferred_element_type=jnp.float32)
            * scale
        )
        key_total = (
            key_total
            + jnp.einsum("hqk,qhd->khd", grad_scores, query, preferred_element_type=jnp.float32)
            * scale
        )
        value_total = value_total + jnp.einsum(
            "hqk,qhd->khd", probs_low, grad_ctx, preferred_element_type=jnp.float32
        )
        return ((key_total, value_total), grad_query.astype(jnp.bfloat16))

    empty = jnp.zeros((stream, local_heads, head_dim), jnp.float32)
    (key_total, value_total), grad_query = lax.scan(
        attend_backward, (empty, empty), (query_blocks, grad_ctx_blocks, log_sums)
    )
    grad_key = key_total.astype(jnp.bfloat16)
    grad_value = value_total.astype(jnp.bfloat16)
    grad_pieces = (
        lax.all_to_all(
            grad_query.reshape(groups, -1), "seq", split_axis=0, concat_axis=0, tiled=True
        ),
        lax.all_to_all(
            grad_key.reshape(groups, -1), "seq", split_axis=0, concat_axis=0, tiled=True
        ),
        lax.all_to_all(
            grad_value.reshape(groups, -1), "seq", split_axis=0, concat_axis=0, tiled=True
        ),
    )
    grad_project = jnp.concatenate(
        [
            from_heads(grad_pieces[0], part_width),
            from_heads(grad_pieces[1], part_width),
            from_heads(grad_pieces[2], part_width),
        ],
        axis=1,
    )
    grad_w_qkv = outer_sum(rows, grad_project)
    bias_sums = jnp.sum(grad_project.astype(jnp.float32), axis=0)
    grad_q_bias = bias_sums[:width]
    grad_v_bias = bias_sums[2 * width :]
    grad_rows = times_back(grad_project, back_qkv) + grad_first
    terms = (
        grad_w_qkv,
        grad_q_bias,
        grad_v_bias,
        grad_w_out,
        grad_out_bias,
        grad_ln1_gain,
        grad_ln1_shift,
        grad_w_up,
        grad_up_bias,
        grad_w_down,
        grad_down_bias,
        grad_ln2_gain,
        grad_ln2_shift,
    )
    page_sums = (
        lax.psum_scatter(
            terms[0].astype(jnp.bfloat16), "dp", scatter_dimension=0, tiled=True
        ).astype(jnp.float32),
        lax.psum_scatter(
            terms[1].astype(jnp.bfloat16), "dp", scatter_dimension=0, tiled=True
        ).astype(jnp.float32),
        lax.psum_scatter(
            terms[2].astype(jnp.bfloat16), "dp", scatter_dimension=0, tiled=True
        ).astype(jnp.float32),
        lax.psum_scatter(
            terms[3].astype(jnp.bfloat16), "dp", scatter_dimension=0, tiled=True
        ).astype(jnp.float32),
        lax.psum_scatter(
            terms[4].astype(jnp.bfloat16), "dp", scatter_dimension=0, tiled=True
        ).astype(jnp.float32),
        lax.psum_scatter(
            terms[5].astype(jnp.bfloat16), "dp", scatter_dimension=0, tiled=True
        ).astype(jnp.float32),
        lax.psum_scatter(
            terms[6].astype(jnp.bfloat16), "dp", scatter_dimension=0, tiled=True
        ).astype(jnp.float32),
        lax.psum_scatter(
            terms[7].astype(jnp.bfloat16), "dp", scatter_dimension=0, tiled=True
        ).astype(jnp.float32),
        lax.psum_scatter(
            terms[8].astype(jnp.bfloat16), "dp", scatter_dimension=0, tiled=True
        ).astype(jnp.float32),
        lax.psum_scatter(
            terms[9].astype(jnp.bfloat16), "dp", scatter_dimension=0, tiled=True
        ).astype(jnp.float32),
        lax.psum_scatter(
            terms[10].astype(jnp.bfloat16), "dp", scatter_dimension=0, tiled=True
        ).astype(jnp.float32),
        lax.psum_scatter(
            terms[11].astype(jnp.bfloat16), "dp", scatter_dimension=0, tiled=True
        ).astype(jnp.float32),
        lax.psum_scatter(
            terms[12].astype(jnp.bfloat16), "dp", scatter_dimension=0, tiled=True
        ).astype(jnp.float32),
    )
    sums = (
        lax.psum_scatter(
            page_sums[0].astype(jnp.bfloat16), "seq", scatter_dimension=0, tiled=True
        ).astype(jnp.float32),
        lax.psum_scatter(
            page_sums[1].astype(jnp.bfloat16), "seq", scatter_dimension=0, tiled=True
        ).astype(jnp.float32),
        lax.psum_scatter(
            page_sums[2].astype(jnp.bfloat16), "seq", scatter_dimension=0, tiled=True
        ).astype(jnp.float32),
        lax.psum_scatter(
            page_sums[3].astype(jnp.bfloat16), "seq", scatter_dimension=0, tiled=True
        ).astype(jnp.float32),
        lax.psum_scatter(
            page_sums[4].astype(jnp.bfloat16), "seq", scatter_dimension=0, tiled=True
        ).astype(jnp.float32),
        lax.psum_scatter(
            page_sums[5].astype(jnp.bfloat16), "seq", scatter_dimension=0, tiled=True
        ).astype(jnp.float32),
        lax.psum_scatter(
            page_sums[6].astype(jnp.bfloat16), "seq", scatter_dimension=0, tiled=True
        ).astype(jnp.float32),
        lax.psum_scatter(
            page_sums[7].astype(jnp.bfloat16), "seq", scatter_dimension=0, tiled=True
        ).astype(jnp.float32),
        lax.psum_scatter(
            page_sums[8].astype(jnp.bfloat16), "seq", scatter_dimension=0, tiled=True
        ).astype(jnp.float32),
        lax.psum_scatter(
            page_sums[9].astype(jnp.bfloat16), "seq", scatter_dimension=0, tiled=True
        ).astype(jnp.float32),
        lax.psum_scatter(
            page_sums[10].astype(jnp.bfloat16), "seq", scatter_dimension=0, tiled=True
        ).astype(jnp.float32),
        lax.psum_scatter(
            page_sums[11].astype(jnp.bfloat16), "seq", scatter_dimension=0, tiled=True
        ).astype(jnp.float32),
        lax.psum_scatter(
            page_sums[12].astype(jnp.bfloat16), "seq", scatter_dimension=0, tiled=True
        ).astype(jnp.float32),
    )
    return (
        output.astype(jnp.bfloat16)[None],
        grad_rows.astype(jnp.bfloat16)[None],
        sums[0],
        sums[1],
        sums[2],
        sums[3],
        sums[4],
        sums[5],
        sums[6],
        sums[7],
        sums[8],
        sums[9],
        sums[10],
        sums[11],
        sums[12],
    )


MESH = pl.DeviceIdType.MESH
CHUNK = 256
MASKED = -1e30
FLAT = (((1,), (1,)), ((), ()))


def flip(index, mask):
    for b in range(mask.bit_length()):
        if mask >> b & 1:
            bit = 1 << b
            index = index + bit - 2 * bit * (index // bit % 2)
    return index


def guarded(when, action):
    if when is None:
        action()
    else:
        pl.when(when)(action)


class Wires:
    def __init__(self, sems, sizes):
        self.sems, self.sizes = sems, sizes
        self.dp, self.z = lax.axis_index("dp"), lax.axis_index("seq")
        self.dps = [flip(self.dp, m) for m in range(sizes[0])]
        self.zs = [flip(self.z, m) for m in range(sizes[1])]
        last = sizes[1] - 1
        half = self.z // 2
        step = 1 - 2 * half
        depth = self.z * step + last * half
        self.inner, self.outer = depth == 1, depth == 0
        self.right = self.z + step
        self.left = self.z - step * depth
        self.far = [self.z] + [t * step + last * half for t in (1 - depth, 2, 3)]
        self.started = []

    def peer(self, offset, step):
        return (self.dps[offset], self.zs[step])

    def send(self, src, dst, recv_sem, device, when=None):
        copy = pltpu.make_async_remote_copy(
            src_ref=src,
            dst_ref=dst,
            send_sem=self.sems.at[len(self.started)],
            recv_sem=recv_sem,
            device_id=device,
            device_id_type=MESH,
        )
        guarded(when, copy.start)
        self.started.append((copy, when))
        return len(self.started) - 1

    def sent(self, index):
        copy, when = self.started[index]
        guarded(when, copy.wait_send)
        self.started[index] = None

    def arrived(self, dst, recv_sem, when=None):
        copy = pltpu.make_async_remote_copy(
            src_ref=dst,
            dst_ref=dst,
            send_sem=self.sems.at[0],
            recv_sem=recv_sem,
            device_id=self.peer(1, 0),
            device_id_type=MESH,
        )
        guarded(when, copy.wait_recv)

    def drain(self):
        for index, entry in enumerate(self.started):
            if entry is not None:
                self.sent(index)

    def greet(self):
        n_dp, n_seq = self.sizes
        barrier = pltpu.get_barrier_semaphore()
        masks = [1 << b for b in range(n_dp.bit_length() - 1)]
        partners = [self.peer(m, 0) for m in masks] + [self.peer(0, i) for i in range(1, n_seq)]
        for device in partners:
            pl.semaphore_signal(barrier, inc=1, device_id=device, device_id_type=MESH)
        pl.semaphore_wait(barrier, len(partners))


class Line:
    def __init__(self, wires, slot, recv):
        self.w, self.slot, self.recv = wires, slot, recv

    def pass_on(self, k, src, to_left):
        w = self.w
        s = w.far[k]
        dst = self.slot(s)
        if to_left:
            w.send(src, dst, self.recv.at[s], (w.dp, w.left), w.inner)
        else:
            w.send(src, dst, self.recv.at[s], (w.dp, w.right), None if k == 0 else w.inner)

    def own(self, src):
        self.pass_on(0, src, False)
        self.pass_on(0, src, True)

    def take(self, k):
        s = self.w.far[k]
        self.w.arrived(self.slot(s), self.recv.at[s])
        self.pass_on(k, self.slot(s), k > 1)

    def relay(self, k):
        s = self.w.far[k]
        self.w.arrived(self.slot(s), self.recv.at[s], self.w.inner)
        self.pass_on(k, self.slot(s), k > 1)

    def end(self, k):
        s = self.w.far[k]
        self.w.arrived(self.slot(s), self.recv.at[s], self.w.outer)


class Gather:
    def __init__(self, wires, src, full, recv, local):
        self.w, self.src, self.full, self.recv, self.local = wires, src, full, recv, local
        n_dp, self.n_seq = wires.sizes
        self.chips = [1 << b for b in range(1, n_dp.bit_length() - 1)]
        self.slots = wires.far
        self.line = Line(wires, lambda s: full.at[wires.dp * self.n_seq + s], recv.at[0])

    def at(self, offset, step):
        return self.full.at[self.w.dps[offset] * self.n_seq + self.slots[step]]

    def order(self, step):
        return self.chips if step % 2 == 0 else self.chips[::-1]

    def forward(self, src, offset, step, masks):
        for m in masks:
            sem = self.recv.at[offset ^ m, self.slots[step]]
            self.w.send(src, self.at(offset, step), sem, self.w.peer(m, 0))

    def wait(self, offset, step):
        self.w.arrived(self.at(offset, step), self.recv.at[offset, self.slots[step]])

    def mine(self):
        return self.src

    def own_chips(self):
        self.kept = pltpu.make_async_copy(self.mine(), self.at(0, 0), self.local)
        self.kept.start()
        self.forward(self.mine(), 0, 0, self.order(0) + [1])

    def own_seq(self):
        self.line.own(self.src)

    def along_seq(self, i):
        self.line.take(i)
        self.forward(self.at(0, i), 0, i, self.order(i) + [1])

    def stages(self, step):
        have, out = [0], []
        masks = self.order(step)
        for t, m in enumerate(masks):
            out.append([(o ^ m, masks[t + 1 :] + [1]) for o in have])
            have = have + [o ^ m for o in have]
        return out

    def over_chips(self, t, step):
        for offset, masks in self.stages(step)[t]:
            self.wait(offset, step)
            self.forward(self.at(offset, step), offset, step, masks)

    def over_cores(self, stored=None):
        n_dp = self.w.sizes[0]
        for offset in list(range(0, n_dp, 2)) + list(range(1, n_dp, 2)):
            if offset % 2:
                for i in range(self.n_seq):
                    self.wait(offset, i)
            elif offset == 0:
                self.kept.wait()
            if stored is not None:
                stored(self.w.dps[offset] * self.n_seq)


class GatherDirect(Gather):
    def __init__(self, *args):
        super().__init__(*args)
        self.slots = self.w.zs

    def part_for(self, i):
        return self.src

    def own_seq(self):
        for i in range(1, self.n_seq):
            sem = self.recv.at[0, self.w.z]
            self.w.send(self.part_for(i), self.at(0, 0), sem, self.w.peer(0, i))

    def along_seq(self, i):
        self.wait(0, i)
        self.forward(self.at(0, i), 0, i, self.order(i) + [1])


class GatherColumns(GatherDirect):
    def mine(self):
        return self.src.at[self.w.z]

    def part_for(self, i):
        return self.src.at[self.w.zs[i]]


def sends_of_gather(n_dp, n_seq):
    return 2 + n_seq - 1 + n_seq * (n_dp - 1)


def group_lanes(packed, row, group, n_seq):
    total = packed[group * n_seq, row : row + 1, :]
    for s in range(1, n_seq):
        total = total + packed[group * n_seq + s, row : row + 1, :]
    return total


def spread_head(source, h, head_dim, factor):
    n_seq, rows, _ = source.shape
    block = h * head_dim // 128 * 128
    low = h * head_dim % 128
    lane = lax.broadcasted_iota(jnp.int32, (n_seq * rows, 128), 1)
    values = source[:, :, block : block + 128].reshape(n_seq * rows, 128).astype(jnp.float32)
    kept = jnp.where((lane >= low) & (lane < low + head_dim), values * factor, 0.0)
    return kept.astype(jnp.bfloat16).reshape(n_seq, rows, 128)


def front_kernel(
    sizes,
    heads,
    valid_ref,
    x_ref,
    cotangent,
    lines_ref,
    up_line_ref,
    qkv_shard,
    out_ref,
    up_ref,
    down_ref,
    columns_out,
    full_out,
    full_up,
    full_down,
    page_out,
    query_out,
    key_out,
    value_out,
    key_turned_out,
    context_out,
    logs_out,
    own_context_out,
    hidden_out,
    gelu_out,
    slope_out,
    output,
    normed_one,
    inv_one,
    grad_mid,
    sums_out,
    vec_own,
    qkv_own,
    packed,
    columns,
    page,
    held,
    context_sent,
    context_held,
    context_turned,
    value_turned,
    masked_query,
    keys,
    values,
    key_turned,
    logs,
    log_columns,
    normed_rows,
    inv_rows,
    out_matrix,
    up_matrix,
    down_matrix,
    page_turned,
    context_rows_turned,
    hidden,
    hidden_low,
    hidden_turned,
    gelu_low,
    gelu_turned,
    slopes,
    branch,
    send_sems,
    gather_sems,
    page_sems,
    context_sems,
    local_sems,
):
    n_dp, n_seq = sizes
    w = Wires(send_sems, sizes)
    rows, width = x_ref.shape
    part = width // n_seq
    head_dim = width // heads
    local_heads = heads // n_seq
    stream = rows * n_seq
    low_lane = lax.broadcasted_iota(jnp.int32, (8, 128), 1) // lines_ref.shape[1]
    lines = jnp.concatenate([lines_ref[...].astype(jnp.float32)] * n_seq, axis=1)
    vec_own[:8, :] = jnp.where(low_lane == w.z, lines, 0.0)
    vec_own[8:, :] = jnp.broadcast_to(up_line_ref[...].astype(jnp.float32), (8, 128))
    for t in range(3):
        for j in range(n_seq):
            at = t * width + j * part
            qkv_own[j, :, t * part : (t + 1) * part] = qkv_shard[:, at : at + part]
    w.greet()
    line = Line(w, lambda s: page.at[s], page_sems)
    sources = (
        (vec_own, packed),
        (qkv_own, columns),
        (out_ref, out_matrix),
        (up_ref, up_matrix),
        (down_ref, down_matrix),
    )
    vec, qkv, out, up, down = [
        (GatherDirect, GatherColumns, Gather, Gather, Gather)[k](w, src, dst, gather_sems.at[k], local_sems.at[k])
        for k, (src, dst) in enumerate(sources)
    ]
    def run(steps):
        for step in steps:
            step()

    keeps = []

    def keep(src, dst):
        keeps.append(pltpu.make_async_copy(src, dst, local_sems.at[5 + len(keeps)]))
        keeps[-1].start()

    per_block = 128 // head_dim
    scale = 1.0 / math.sqrt(head_dim)
    groups = part // 128
    one_lane = lax.broadcasted_iota(jnp.int32, (rows, 128), 1)
    ones = jnp.where(one_lane == 0, 1.0, 0.0).astype(jnp.bfloat16)
    chunk = 512
    chunks = up_matrix.shape[2] // chunk
    per_chunk = chunk // down_matrix.shape[1]
    per_part = part // out_matrix.shape[1]

    def line_of(row):
        return jnp.concatenate([group_lanes(packed, row, d, n_seq) for d in range(n_dp)], axis=1)

    def gathered_columns():
        qkv.over_cores()
        vec.over_cores()
        keep(columns, columns_out)

    def project(k):
        s = w.far[k]
        if k == 0:
            page[s] = x_ref[...]
        matrix = columns[...].reshape(width, 3 * part)
        piece = jnp.dot(page[s], matrix, preferred_element_type=jnp.float32)
        for t in range(3):
            third = piece[:, t * part : (t + 1) * part]
            if t != 1:
                bias = [group_lanes(packed, t // 2, w.z * groups + g, n_seq) for g in range(groups)]
                third = third + jnp.concatenate(bias, axis=1)
            held[t, s] = third.astype(jnp.bfloat16)

    def prepare():
        position = lax.broadcasted_iota(jnp.int32, (stream, 128), 0)
        lane = lax.broadcasted_iota(jnp.int32, (stream, 128), 1)
        guard = jnp.where(position >= valid_ref[0], MASKED, 0.0)
        guard = jnp.where(lane == 0, guard, jnp.where(lane < 4, 1.0, 0.0)).astype(jnp.bfloat16)
        for h in range(local_heads):
            masked_query[h] = spread_head(held.at[0], h, head_dim, scale)
        for b in range(local_heads // per_block):
            lanes = slice(b * 128, (b + 1) * 128)
            keys[b, :, :128] = held[1, :, :, lanes].reshape(stream, 128)
            keys[b, :, 128:] = guard
            values[b, :, :128] = held[2, :, :, lanes].reshape(stream, 128)
            values[b, :, 128:] = jnp.where(lane < 3, 1.0, 0.0).astype(jnp.bfloat16)
        turned = held[1].reshape(stream, part).T
        for h in range(local_heads):
            key_turned[h] = turned[h * head_dim : (h + 1) * head_dim, :]
        value_turned[...] = held[2].reshape(stream, part).T
        keep(masked_query, query_out)
        keep(keys, key_out)
        keep(values, value_out)
        keep(key_turned, key_turned_out)

    def attention(i):
        c = w.zs[i]

        def attend(h, _):
            at = pl.ds(pl.multiple_of(h * head_dim, head_dim), head_dim)
            query = jnp.concatenate([masked_query[h, c], ones], axis=1)
            scores = lax.dot_general(
                keys[h // per_block], query, FLAT, preferred_element_type=jnp.float32
            )
            peak = jnp.max(scores, axis=0, keepdims=True)
            raised = jnp.exp(scores - peak)
            total = jnp.sum(raised, axis=0, keepdims=True)
            mixed = jnp.dot(
                value_turned[at, :], raised.astype(jnp.bfloat16), preferred_element_type=jnp.float32
            )
            context_turned[c, at, :] = mixed / total
            logs[pl.ds(h, 1), :] = peak + jnp.log(total)
            return 0

        lax.fori_loop(0, local_heads, attend, 0)
        log_columns[c, :, :8] = logs[...].T
        piece = context_turned[c].T.astype(jnp.bfloat16)
        context_sent[i] = piece
        if i:
            w.send(context_sent.at[i], context_held.at[w.z], context_sems.at[i], w.peer(0, i))
        else:
            context_held[w.z] = piece

    def keep_logs():
        keep(log_columns, logs_out)
        keep(context_sent, own_context_out)

    def turn_page():
        for s in range(n_seq):
            page_turned[s * width : (s + 1) * width, :] = page[s].T
        keep(page_turned, page_out)

    def context_arrived():
        for i in range(1, n_seq):
            w.arrived(context_held.at[w.zs[i]], context_sems.at[i])

    def gathered_out():
        out.over_cores()
        keep(out_matrix, full_out)

    def keep_groups(unit, src, dst):
        def store(first):
            group = pl.ds(first, n_seq)
            keep(src.at[group], dst.at[group])

        unit.over_cores(store)

    def gathered_up():
        keep_groups(up, up_matrix, full_up)

    def gathered_down():
        keep_groups(down, down_matrix, full_down)

    def first_norm():
        total = x_ref[...].astype(jnp.float32) + line_of(2)
        for j in range(n_seq):
            block = out_matrix[j * per_part : (j + 1) * per_part].reshape(part, width)
            total = total + jnp.dot(context_held[j], block, preferred_element_type=jnp.float32)
            context_rows_turned[j * part : (j + 1) * part, :] = context_held[j].T
        keep(context_rows_turned, context_out)
        rows_hidden, normed, inv = norm_forward(total, line_of(3), line_of(4))
        normed_rows[...] = normed
        inv_rows[...] = jnp.broadcast_to(inv, inv_rows.shape)
        keep(normed_rows, normed_one)
        keep(inv_rows, inv_one)
        hidden[...] = rows_hidden
        hidden_low[...] = rows_hidden.astype(jnp.bfloat16)
        hidden_turned[...] = hidden_low[...].T
        keep(hidden_turned, hidden_out)

    def expand():
        def activate(f, _):
            at = pl.ds(pl.multiple_of(f * chunk, chunk), chunk)
            block = up_matrix[:, :, at].reshape(width, chunk)
            up_bias = jnp.concatenate(
                [packed[f * per_chunk + e, 8:9, :] for e in range(per_chunk)], axis=1
            )
            act = jnp.dot(hidden_low[...], block, preferred_element_type=jnp.float32) + up_bias
            below = 0.5 + 0.5 * lax.erf(act * math.sqrt(0.5))
            gelu = act * below
            gelu = gelu.astype(jnp.bfloat16)
            gelu_low[:, at] = gelu
            gelu_turned[at, :] = gelu.T
            bell = jnp.exp(-0.5 * act * act) * (1.0 / math.sqrt(2.0 * math.pi))
            slopes[:, at] = (below + act * bell).astype(jnp.bfloat16)
            return 0

        half = chunks // 2
        for part_of in range(2):
            lax.fori_loop(part_of * half, (part_of + 1) * half, activate, 0)
            at = pl.ds(part_of * half * chunk, half * chunk)
            keep(gelu_turned.at[at], gelu_out.at[at])
            keep(slopes.at[:, at], slope_out.at[:, at])

    def shrink_all():
        branch[...] = hidden[...] + line_of(5)

        wider = 2 * chunk

        def shrink(f, _):
            at = pl.ds(pl.multiple_of(f * wider, wider), wider)
            block = down_matrix[pl.ds(f * 2 * per_chunk, 2 * per_chunk)].reshape(wider, width)
            branch[...] += jnp.dot(gelu_low[:, at], block, preferred_element_type=jnp.float32)
            return 0

        lax.fori_loop(0, chunks // 2, shrink, 0)

    out.own_seq()
    down.own_chips()
    qkv.own_seq()
    vec.own_seq()
    up.own_chips()
    up.own_seq()
    out.along_seq(1)
    qkv.own_chips()
    vec.own_chips()
    qkv.along_seq(1)
    vec.along_seq(1)
    down.own_seq()
    up.along_seq(1)
    qkv.along_seq(2)
    vec.along_seq(2)
    up.along_seq(2)
    out.along_seq(2)
    line.own(x_ref)
    qkv.over_chips(0, 0)
    vec.over_chips(0, 0)
    out.over_chips(0, 1)
    up.over_chips(0, 0)
    qkv.over_chips(0, 2)
    vec.over_chips(0, 2)
    qkv.along_seq(3)
    vec.along_seq(3)
    up.over_chips(0, 1)
    up.along_seq(3)
    qkv.over_chips(0, 1)
    vec.over_chips(0, 1)
    qkv.over_chips(1, 0)
    vec.over_chips(1, 0)
    line.relay(1)
    line.relay(2)
    qkv.over_chips(0, 3)
    vec.over_chips(0, 3)
    up.over_chips(1, 1)
    line.end(1)
    down.along_seq(1)
    up.over_chips(0, 3)
    qkv.over_chips(1, 3)
    vec.over_chips(1, 3)
    qkv.over_chips(1, 2)
    vec.over_chips(1, 2)
    up.over_chips(0, 2)
    down.over_chips(0, 0)
    out.own_chips()
    qkv.over_chips(1, 1)
    vec.over_chips(1, 1)
    gathered_columns()
    up.over_chips(1, 0)
    line.relay(3)
    out.over_chips(0, 2)
    project(0)
    line.end(2)
    project(2)
    out.over_chips(0, 0)
    down.over_chips(0, 1)
    up.over_chips(1, 3)
    project(1)
    up.over_chips(1, 2)
    line.end(3)
    out.over_chips(1, 1)
    down.along_seq(2)
    project(3)
    prepare()
    attention(0)
    down.along_seq(3)
    attention(1)
    out.along_seq(3)
    attention(3)
    gathered_up()
    down.over_chips(0, 2)
    down.over_chips(1, 0)
    out.over_chips(0, 3)
    down.over_chips(0, 3)
    attention(2)
    out.over_chips(1, 0)
    out.over_chips(1, 3)
    turn_page()
    out.over_chips(1, 2)
    down.over_chips(1, 1)
    keep_logs()
    gathered_out()
    down.over_chips(1, 2)
    down.over_chips(1, 3)
    context_arrived()
    first_norm()
    expand()
    gathered_down()
    shrink_all()
    gain_one, gain_two = line_of(3), line_of(6)
    result, normed, inv = norm_forward(branch[...], gain_two, line_of(7))
    output[...] = result.astype(jnp.bfloat16)
    grad = cotangent[...].astype(jnp.float32)
    mid, grad_gain, grad_shift = norm_backward(grad, normed, inv, gain_two)
    grad_mid[...] = mid
    grad_bias = jnp.sum(mid.astype(jnp.bfloat16).astype(jnp.float32), axis=0)
    sums_out[...] = jnp.zeros_like(sums_out)
    for row, line_sum in enumerate((grad_bias, grad_gain, grad_shift)):
        sums_out[5 + row : 6 + row, :] = line_sum.reshape(1, width)
    sums_out[3:4, :] = gain_one
    for copy in keeps:
        copy.wait()
    w.drain()


def front(sizes, heads, valid, rows, cotangent, lines, up_line, w_qkv, w_out, w_up, w_down):
    n_dp, n_seq = sizes
    devices = n_dp * n_seq
    count, width = rows.shape
    part = width // n_seq
    stream = count * n_seq
    wide = w_up.shape[1]
    low = jnp.bfloat16
    head_dim = width // heads
    local_heads = heads // n_seq
    blocks = part // 128
    attention = (
        jax.ShapeDtypeStruct((local_heads, n_seq, count, 128), low),
        jax.ShapeDtypeStruct((blocks, stream, 256), low),
        jax.ShapeDtypeStruct((blocks, stream, 256), low),
        jax.ShapeDtypeStruct((local_heads, head_dim, stream), low),
    )

    def full(shard):
        return jax.ShapeDtypeStruct((devices,) + shard.shape, shard.dtype)

    anywhere = pl.BlockSpec(memory_space=pl.ANY)
    local = pl.BlockSpec(memory_space=pltpu.VMEM)
    sends = 5 * sends_of_gather(n_dp, n_seq) + 5 + n_seq - 1
    return pl.pallas_call(
        lambda *refs: front_kernel(sizes, heads, *refs),
        out_shape=(
            jax.ShapeDtypeStruct((devices, w_qkv.shape[0], 3 * part), low),
            full(w_out),
            full(w_up),
            full(w_down),
            jax.ShapeDtypeStruct((n_seq * width, count), low),
        )
        + attention
        + (
            jax.ShapeDtypeStruct((width, count), low),
            jax.ShapeDtypeStruct((n_seq, count, 128), jnp.float32),
            jax.ShapeDtypeStruct((n_seq, count, part), low),
            jax.ShapeDtypeStruct((width, count), low),
            jax.ShapeDtypeStruct((wide, count), low),
            jax.ShapeDtypeStruct((count, wide), low),
            jax.ShapeDtypeStruct((count, width), low),
            jax.ShapeDtypeStruct((count, width), jnp.float32),
            jax.ShapeDtypeStruct((count, 128), jnp.float32),
            jax.ShapeDtypeStruct((count, width), jnp.float32),
            jax.ShapeDtypeStruct((8, width), jnp.float32),
        ),
        in_specs=[
            pl.BlockSpec(memory_space=pltpu.SMEM),
        ]
        + [local] * 5
        + [anywhere] * 3,
        out_specs=[anywhere] * 15 + [local] + [anywhere] * 2 + [local] * 2,
        scratch_shapes=[
            pltpu.VMEM((16, 128), jnp.float32),
            pltpu.VMEM((n_seq, w_qkv.shape[0], 3 * part), low),
            pltpu.VMEM((devices, 16, 128), jnp.float32),
            pltpu.VMEM((devices, w_qkv.shape[0], 3 * part), low),
            pltpu.VMEM((n_seq, count, width), low),
            pltpu.VMEM((3, n_seq, count, part), low),
            pltpu.VMEM((n_seq, count, part), low),
            pltpu.VMEM((n_seq, count, part), low),
            pltpu.VMEM((n_seq, part, count), jnp.float32),
            pltpu.VMEM((part, stream), low),
        ]
        + [pltpu.VMEM(a.shape, a.dtype) for a in attention]
        + [
            pltpu.VMEM((8, count), jnp.float32),
            pltpu.VMEM((n_seq, count, 128), jnp.float32),
            pltpu.VMEM((count, width), jnp.float32),
            pltpu.VMEM((count, 128), jnp.float32),
            pltpu.VMEM((devices,) + w_out.shape, low),
            pltpu.VMEM((devices,) + w_up.shape, low),
            pltpu.VMEM((devices,) + w_down.shape, low),
            pltpu.VMEM((n_seq * width, count), low),
            pltpu.VMEM((width, count), low),
            pltpu.VMEM((count, width), jnp.float32),
            pltpu.VMEM((count, width), low),
            pltpu.VMEM((width, count), low),
            pltpu.VMEM((count, wide), low),
            pltpu.VMEM((wide, count), low),
            pltpu.VMEM((count, wide), low),
            pltpu.VMEM((count, width), jnp.float32),
            pltpu.SemaphoreType.DMA((sends,)),
            pltpu.SemaphoreType.DMA((5, n_dp, n_seq)),
            pltpu.SemaphoreType.DMA((n_seq,)),
            pltpu.SemaphoreType.DMA((n_seq,)),
            pltpu.SemaphoreType.DMA((40,)),
        ],
        compiler_params=pltpu.CompilerParams(
            collective_id=0, has_side_effects=True, vmem_limit_bytes=60 * 2**20
        ),
        name="front",
    )(valid, rows, cotangent, lines, up_line, w_qkv, w_out, w_up, w_down)


def add_rows(into, term):
    rows = into.shape[0]
    step = min(16, rows)

    def body(r, _):
        at = pl.ds(pl.multiple_of(r * step, step), step)
        total = into[at, :].astype(jnp.float32) + term[at, :].astype(jnp.float32)
        into[at, :] = total.astype(into.dtype)
        return 0

    lax.fori_loop(0, rows // step, body, 0)


class LineSum:
    def __init__(self, wires, block, last, sems):
        self.w, self.block, self.last, self.sems = wires, block, last, sems

    def into(self, src, index, device, when):
        self.w.send(src, self.last.at[index], self.sems.at[index], device, when)

    def add(self, k, index):
        def action():
            self.w.arrived(self.last.at[index], self.sems.at[index])
            add_rows(self.block(k), self.last.at[index])

        pl.when(self.w.inner)(action)

    def offer(self, k):
        self.into(self.block(k), k - 1, (self.w.dp, self.w.right), self.w.outer)

    def relay(self, k):
        w, block = self.w, self.block(k)
        if k == 1:
            self.add(1, 4)
            self.into(block, 3, (w.dp, w.left), w.inner)
        else:
            self.add(k, k - 1)
            self.into(block, 3 if k == 2 else 4, (w.dp, w.right), w.inner)

    def finish(self, start, out):
        w = self.w
        w.arrived(self.last.at[3], self.sems.at[3])
        w.arrived(self.last.at[0], self.sems.at[0], w.inner)
        rows = out.shape[0]
        step = min(16, rows)

        def total_of(count):
            def body(r, _):
                at = pl.ds(pl.multiple_of(r * step, step), step)
                total = start(at) + self.last[3, at, :].astype(jnp.float32)
                if count == 2:
                    total = total + self.last[0, at, :].astype(jnp.float32)
                out[at, :] = total.astype(out.dtype)
                return 0

            lax.fori_loop(0, rows // step, body, 0)

        pl.when(w.inner)(lambda: total_of(2))
        pl.when(w.outer)(lambda: total_of(1))


class Scatter:
    def __init__(self, wires, kind, make, source, stage, bufs, sems, out):
        self.w, self.kind, self.make, self.source, self.stage = wires, kind, make, source, stage
        self.total, self.first, self.second, self.last = bufs
        self.core_sems, self.first_sems, self.second_sems, self.last_sems = sems
        self.out = out
        self.n_seq = wires.sizes[1]
        self.offsets = [6, 2, 4, 0]
        self.staged = {}
        self.slots = wires.far if kind == "line" else wires.zs
        self.line = LineSum(wires, lambda k: self.total.at[0, self.slots[k]], self.last, self.last_sems)

    def order(self, step):
        return (2, 4) if step % 2 == 0 else (4, 2)

    def give(self, k):
        o = self.offsets[k]
        d = self.w.dps[o ^ 1]
        if self.stage is None:
            src = self.source.at[pl.ds(d * self.n_seq, self.n_seq)]
        else:
            depth = self.stage.shape[0]
            if k >= depth:
                self.w.sent(self.staged[k - depth])
            src = self.stage.at[k % depth]

            def fill(s, _):
                src[s] = self.make(d, s).astype(src.dtype)
                return 0

            lax.fori_loop(0, self.n_seq, fill, 0)
        sem = self.core_sems.at[o // 2]
        self.staged[k] = self.w.send(src, self.total.at[o // 2], sem, self.w.peer(1, 0))

    def give_steps(self):
        return [lambda k=k: self.give(k) for k in range(4)]

    def over_cores(self, k):
        o = self.offsets[k]
        d = self.w.dps[o]
        self.w.arrived(self.total.at[o // 2], self.core_sems.at[o // 2])

        def add(s, _):
            block = self.total.at[o // 2, s]
            block[...] = (block[...].astype(jnp.float32) + self.make(d, s)).astype(block.dtype)
            return 0

        lax.fori_loop(0, self.n_seq, add, 0)
        self.hand_on(k, (3, 2))

    def spread(self, k):
        self.hand_on(k, (1, 0))

    def hand_on(self, k, steps):
        o = self.offsets[k]
        for i in steps:
            mask = self.order(i)[0]
            block = self.total.at[o // 2, self.slots[i]]
            if o & mask:
                keep = (o ^ mask) // (6 ^ mask)
                self.w.send(block, self.first.at[i, keep], self.first_sems.at[i, keep], self.w.peer(mask, 0))

    def over_chips(self, i):
        mask = self.order(i)[1]
        for keep in (1, 0):
            o = mask * keep
            block = self.total.at[o // 2, self.slots[i]]
            self.w.arrived(self.first.at[i, keep], self.first_sems.at[i, keep])
            add_rows(block, self.first.at[i, keep])
            if keep:
                self.w.send(block, self.second.at[i], self.second_sems.at[i], self.w.peer(mask, 0))

    def to_seq(self, i):
        block = self.total.at[0, self.slots[i]]
        self.w.arrived(self.second.at[i], self.second_sems.at[i])
        add_rows(block, self.second.at[i])
        if self.kind == "line":
            if i:
                self.line.offer(i)
        elif i:
            self.w.send(block, self.last.at[i], self.last_sems.at[i], self.w.peer(0, i))

    def relay(self, i):
        self.line.relay(i)

    def finish(self):
        block = self.total.at[0, self.w.z]
        if self.kind == "line":
            self.line.finish(lambda at: block[at, :].astype(jnp.float32), self.out)
            return
        for i in range(1, self.n_seq):
            self.w.arrived(self.last.at[i], self.last_sems.at[i])
        if self.kind == "direct":
            total = block[...]
            for i in range(1, self.n_seq):
                total = total + self.last[i]
            lines, up_line = self.out
            up_line[...] = total[8:9, :]
            share = lines.shape[1]
            total = total[:8, :]
            shown = total[:, :share]
            for s in range(1, self.n_seq):
                shown = jnp.where(self.w.z == s, total[:, s * share : (s + 1) * share], shown)
            lines[...] = shown
            return
        for i in range(self.n_seq):
            term = block[...] if i == 0 else self.last[i]
            part = term.shape[1] // 3
            for t in range(3):
                at = t * part * self.n_seq + self.w.zs[i] * part
                self.out[:, pl.ds(pl.multiple_of(at, part), part)] = term[
                    :, t * part : (t + 1) * part
                ].astype(jnp.float32)


def back_kernel(sizes, heads, *refs):
    n_dp, n_seq = sizes
    (
        mid_in,
        normed_in,
        inv_in,
        sums_in,
        logs_in,
        page_in,
        query_in,
        key_in,
        value_in,
        key_turned_in,
        context_in,
        hidden_in,
        gelu_in,
        slope_in,
        own_context_in,
        columns_in,
        out_in,
        up_in,
        down_in,
        grad_rows,
        *outs,
    ) = refs[:26]
    scratch = list(refs[26:])

    def take(count):
        got = scratch[:count]
        del scratch[:count]
        return got

    send_sems, core_sems, first_sems, second_sems, last_sems, block_sems = take(6)
    head_sems, local_sems, row_sems = take(3)
    logs, own_context, grads, masked_query, keys, values, key_turned, masked_grad = take(8)
    query_lanes, query_grad, key_grad, value_grad = take(4)
    project, turned, columns, vec = take(4)
    row_terms, row_last, own_rows, partial = take(4)
    hidden_turned, context_turned, slopes, normed = take(4)
    grad_low, grad_sent, out_matrix, down_blocks, up_blocks = take(5)
    down_stage, up_stage, out_stage = take(3)
    units = [take(4) for k in range(5)]
    w = Wires(send_sems, sizes)
    rows, width = normed.shape
    part = width // n_seq
    wide = slopes.shape[1]
    head_dim = width // heads
    local_heads = heads // n_seq
    stream = rows * n_seq
    per_block = 128 // head_dim
    scale = 1.0 / math.sqrt(head_dim)
    loads = {}

    def load(name, src, dst):
        loads[name] = pltpu.make_async_copy(src, dst, local_sems.at[len(loads)])
        loads[name].start()

    load("mid", mid_in, own_rows)
    load("gelu", gelu_in, turned)
    load("slope", slope_in, slopes)
    blocks = []
    for f in range(n_dp):
        sem = block_sems.at[0, f % 2]
        blocks.append(pltpu.make_async_copy(down_in.at[pl.ds(f * n_seq, n_seq)], down_blocks.at[f % 2], sem))
    shares = wide // width
    half = up_in.shape[0] // 2
    ups = []
    for e in range(2 * shares):
        src = up_in.at[pl.ds(e // shares * half, half), :, pl.ds(e % shares * width, width)]
        ups.append(pltpu.make_async_copy(src, up_blocks.at[e % 2], block_sems.at[1, e % 2]))
    for e in range(2):
        blocks[e].start()
        ups[e].start()
    load("hidden", hidden_in, hidden_turned)
    load("normed", normed_in, normed)
    load("out", out_in, out_matrix)
    load("context", context_in, context_turned)
    load("logs", logs_in, logs)
    load("own", own_context_in, own_context)
    load("columns", columns_in, columns)
    load("query", query_in, masked_query)
    load("key", key_in, keys)
    load("value", value_in, values)
    load("turned", key_turned_in, key_turned)
    w.greet()

    def rows_from(source, first, count):
        return source[pl.ds(pl.multiple_of(first, count), count), :]

    def down_term(d, s):
        left = rows_from(turned, (d * n_seq + s) * outs[0].shape[0], outs[0].shape[0])
        return jnp.dot(left, grad_low[...], preferred_element_type=jnp.float32)

    def up_term(d, s):
        left = rows_from(hidden_turned, (d * n_seq + s) * outs[1].shape[0], outs[1].shape[0])
        return jnp.dot(left, slopes[...], preferred_element_type=jnp.float32)

    def out_term(d, s):
        left = rows_from(context_turned, (d * n_seq + s) * outs[2].shape[0], outs[2].shape[0])
        return jnp.dot(left, grad_low[...], preferred_element_type=jnp.float32)

    def held_term(source):
        return lambda d, s: source[d * n_seq + s].astype(jnp.float32)

    makes = (down_term, up_term, out_term, held_term(partial), held_term(vec))
    stages = (down_stage, up_stage, out_stage, None, None)
    scatters = []
    for k in range(5):
        scatters.append(
            Scatter(
                w,
                ("line", "line", "line", "columns", "direct")[k],
                makes[k],
                (None, None, None, partial, vec)[k],
                stages[k],
                units[k],
                (core_sems.at[k], first_sems.at[k], second_sems.at[k], last_sems.at[k]),
                outs[k] if k < 4 else outs[4:],
            )
        )
    down, up, out, qkv, small = scatters
    row_sum = LineSum(w, lambda k: row_terms.at[k - 1], row_last, row_sems)
    span = wide // n_dp

    def run(steps):
        for step in steps:
            step()

    low_lane = lax.broadcasted_iota(jnp.int32, (rows, 128), 1)

    def in_lanes(column, first, base):
        rest = -column
        for n in range(3):
            piece = rest.astype(jnp.bfloat16).astype(jnp.float32)
            base = jnp.where(low_lane == first + n, piece, base)
            rest = rest - piece
        return base.astype(jnp.bfloat16)

    def keep_line(row, line):
        for d in range(n_dp):
            for s in range(n_seq):
                vec[d * n_seq + s, row : row + 1, :] = line[:, d * 128 : (d + 1) * 128]

    def begin():
        loads["mid"].wait()
        grad_low[...] = own_rows[...].astype(jnp.bfloat16)
        loads["gelu"].wait()

    def slope_of(f):
        if f == 0:
            loads["slope"].wait()
        blocks[f].wait()
        grad_gelu = lax.dot_general(
            grad_low[...], down_blocks[f % 2].reshape(span, width), FLAT, preferred_element_type=jnp.float32
        )
        if f + 2 < n_dp:
            blocks[f + 2].start()
        at = slice(f * span, (f + 1) * span)
        slopes[:, at] = (grad_gelu * slopes[:, at].astype(jnp.float32)).astype(jnp.bfloat16)
        if f == n_dp - 1:
            loads["hidden"].wait()

    def hidden_of(e):
        ups[e].wait()
        columns_at = slice(e % shares * width, (e % shares + 1) * width)
        rows_at = slice(e // shares * width // 2, (e // shares + 1) * width // 2)
        own_rows[:, rows_at] += lax.dot_general(
            slopes[:, columns_at],
            up_blocks[e % 2].reshape(width // 2, width),
            FLAT,
            preferred_element_type=jnp.float32,
        )
        if e + 2 < 2 * shares:
            ups[e + 2].start()

    def norm_back():
        load("page", page_in, turned)
        loads["normed"].wait()
        first, grad_gain, grad_shift = norm_backward(
            own_rows[...], normed[...], inv_in[:, :1], sums_in[3:4, :]
        )
        own_rows[...] = first
        grad_low[...] = first.astype(jnp.bfloat16)
        vec[...] = jnp.zeros_like(vec)
        keep_line(3, grad_gain.reshape(1, width))
        keep_line(4, grad_shift.reshape(1, width))

    def send_grads():
        loads["out"].wait()
        for i in (1, 2, 3, 0):
            j = w.zs[i]
            share = part // out_matrix.shape[1]
            block = out_matrix[pl.ds(j * share, share)].reshape(part, width)
            piece = lax.dot_general(grad_low[...], block, FLAT, preferred_element_type=jnp.float32)
            if i:
                grad_sent[i] = piece.astype(jnp.bfloat16)
                w.send(grad_sent.at[i], grads.at[w.z], head_sems.at[i], w.peer(0, i))
            else:
                grads[w.z] = piece.astype(jnp.bfloat16)
        loads["context"].wait()

    def keep_lines():
        up_bias = jnp.sum(slopes[...].astype(jnp.float32), axis=0, keepdims=True)
        for d in range(n_dp * n_seq):
            vec[d, 8:9, :] = up_bias[:, d * 128 : (d + 1) * 128]
        keep_line(2, jnp.sum(grad_low[...].astype(jnp.float32), axis=0, keepdims=True))
        for row in (5, 6, 7):
            keep_line(row, sums_in[row : row + 1, :])

    def prepare():
        for name in ("columns", "logs", "own", "query", "key", "value", "turned"):
            loads[name].wait()
        key_grad[...] = jnp.zeros_like(key_grad)
        value_grad[...] = jnp.zeros_like(value_grad)

    def attention(i):
        c = w.zs[i]
        if i:
            w.arrived(grads.at[c], head_sems.at[i])
        one = jnp.where(low_lane == 0, 1.0, 0.0)
        for h in range(local_heads):
            block = h // per_block * 128
            grad = spread_head(grads.at[pl.ds(c, 1)], h, head_dim, 1.0)[0]
            centre = jnp.sum(
                grad.astype(jnp.float32) * own_context[i, :, block : block + 128].astype(jnp.float32),
                axis=1,
                keepdims=True,
            )
            masked_grad[h, :, :128] = grad
            masked_grad[h, :, 128:] = in_lanes(centre, 0, jnp.zeros_like(one))
            query_lanes[h] = in_lanes(logs[c, :, h : h + 1], 1, one)

        def head(h, _):
            block = h // per_block
            query, grad = masked_query[h, c], masked_grad[h, :, :128]
            scores = lax.dot_general(
                keys[block],
                jnp.concatenate([query, query_lanes[h]], axis=1),
                FLAT,
                preferred_element_type=jnp.float32,
            )
            probs = jnp.exp(scores)
            moved = lax.dot_general(values[block], masked_grad[h], FLAT, preferred_element_type=jnp.float32)
            slope = (probs * moved).astype(jnp.bfloat16)
            query_grad[h] = jnp.dot(key_turned[h], slope, preferred_element_type=jnp.float32) * scale
            key_grad[block] += jnp.dot(slope, query, preferred_element_type=jnp.float32)
            value_grad[block] += jnp.dot(
                probs.astype(jnp.bfloat16), grad, preferred_element_type=jnp.float32
            )
            return 0

        lax.fori_loop(0, local_heads, head, 0)
        project[pl.ds(pl.multiple_of(c * rows, rows), rows), :part] = (
            query_grad[...].reshape(part, rows).T.astype(jnp.bfloat16)
        )

    def keep_project():
        for t, total in ((1, key_grad), (2, value_grad)):
            for b in range(local_heads // per_block):
                at = t * part + b * 128
                project[:, at : at + 128] = total[b].astype(jnp.bfloat16)

    def row_term(k):
        term = lax.dot_general(
            rows_from(project, w.far[k] * rows, rows),
            columns[...].reshape(width, 3 * part),
            FLAT,
            preferred_element_type=jnp.float32,
        )
        if k:
            row_terms[k - 1] = term.astype(jnp.bfloat16)
            row_sum.offer(k)
        else:
            own_rows[...] += term

    def weight_grad():
        loads["page"].wait()
        for t in range(3):
            at = slice(t * part, (t + 1) * part)
            block = jnp.dot(turned[:width, :], project[:rows, at], preferred_element_type=jnp.float32)
            for s in range(1, n_seq):
                block = block + jnp.dot(
                    turned[s * width : (s + 1) * width, :],
                    project[s * rows : (s + 1) * rows, at],
                    preferred_element_type=jnp.float32,
                )
            partial[:, :, at] = block.astype(jnp.bfloat16).reshape(n_dp * n_seq, -1, part)

    def give_small():
        groups = part // 128
        for b, t in ((0, 0), (1, 2)):
            sums = jnp.sum(project[:, t * part : (t + 1) * part].astype(jnp.float32), axis=0, keepdims=True)
            for g in range(groups):
                for s in range(n_seq):
                    vec[(w.z * groups + g) * n_seq + s, b : b + 1, :] = sums[:, g * 128 : (g + 1) * 128]
        run(small.give_steps())

    begin()
    down.give(0)
    down.give(1)
    slope_of(0)
    slope_of(1)
    down.give(2)
    down.give(3)
    down.over_cores(0)
    slope_of(2)
    slope_of(3)
    hidden_of(0)
    hidden_of(1)
    down.over_cores(1)
    slope_of(4)
    down.over_cores(2)
    down.spread(0)
    slope_of(5)
    slope_of(6)
    slope_of(7)
    hidden_of(2)
    down.spread(2)
    hidden_of(3)
    hidden_of(4)
    hidden_of(5)
    down.over_cores(3)
    up.give(0)
    hidden_of(6)
    hidden_of(7)
    down.over_chips(3)
    norm_back()
    send_grads()
    down.over_chips(2)
    prepare()
    attention(0)
    down.over_chips(1)
    down.to_seq(3)
    attention(2)
    down.to_seq(2)
    attention(3)
    down.to_seq(1)
    attention(1)
    keep_project()
    row_term(3)
    down.spread(1)
    up.over_cores(0)
    up.spread(0)
    up.give(1)
    out.give(0)
    out.give(1)
    down.relay(2)
    out.give(2)
    up.give(2)
    up.give(3)
    down.relay(3)
    row_term(2)
    out.give(3)
    weight_grad()
    keep_lines()
    up.over_cores(2)
    up.over_cores(1)
    qkv.give(0)
    qkv.give(1)
    qkv.give(2)
    qkv.give(3)
    row_sum.relay(3)
    out.over_cores(0)
    up.over_cores(3)
    give_small()
    qkv.over_cores(2)
    small.over_cores(2)
    down.relay(1)
    qkv.over_cores(0)
    small.over_cores(0)
    qkv.spread(2)
    small.spread(2)
    qkv.spread(0)
    small.spread(0)
    row_term(1)
    qkv.over_cores(3)
    small.over_cores(3)
    up.over_chips(3)
    row_sum.relay(2)
    out.over_cores(2)
    qkv.over_cores(1)
    small.over_cores(1)
    up.over_chips(2)
    row_term(0)
    out.over_cores(3)
    row_sum.relay(1)
    qkv.spread(1)
    small.spread(1)
    qkv.over_chips(1)
    small.over_chips(1)
    up.spread(2)
    out.spread(0)
    up.to_seq(3)
    out.over_cores(1)
    out.spread(2)
    up.to_seq(2)
    out.over_chips(3)
    qkv.over_chips(2)
    small.over_chips(2)
    qkv.to_seq(1)
    small.to_seq(1)
    up.over_chips(1)
    up.relay(3)
    qkv.over_chips(0)
    small.over_chips(0)
    out.over_chips(2)
    up.spread(1)
    down.over_chips(0)
    out.to_seq(3)
    out.to_seq(2)
    up.relay(2)
    out.over_chips(1)
    qkv.to_seq(0)
    small.to_seq(0)
    row_sum.finish(lambda at: own_rows[at, :], grad_rows)
    qkv.to_seq(2)
    small.to_seq(2)
    out.spread(1)
    up.to_seq(1)
    up.relay(1)
    qkv.over_chips(3)
    small.over_chips(3)
    up.over_chips(0)
    out.relay(3)
    out.over_chips(0)
    out.to_seq(1)
    out.relay(1)
    down.to_seq(0)
    down.finish()
    out.relay(2)
    qkv.to_seq(3)
    small.to_seq(3)
    up.to_seq(0)
    up.finish()
    qkv.finish()
    small.finish()
    out.to_seq(0)
    out.finish()
    w.drain()


def back(sizes, heads, saved, w_shapes):
    n_dp, n_seq = sizes
    devices = n_dp * n_seq
    mid, normed, _, _, logs, page, query, key, value, key_turned, context, hidden, gelu, slopes, own_context = saved[:15]
    columns, full_out, full_up, full_down = saved[15:]
    count, width = normed.shape
    part = width // n_seq
    stream = count * n_seq
    local_heads, head_dim, _ = key_turned.shape
    blocks = part // 128
    low = jnp.bfloat16
    shapes = [w_shapes[0], w_shapes[1], w_shapes[2], columns.shape[1:], (16, 128)]
    kinds = [low] * 4 + [jnp.float32]
    results = [jax.ShapeDtypeStruct(shape, jnp.float32) for shape in shapes]
    results[3] = jax.ShapeDtypeStruct((shapes[3][0], n_seq * shapes[3][1]), jnp.float32)
    results[4:] = [
        jax.ShapeDtypeStruct((8, width // devices), jnp.float32),
        jax.ShapeDtypeStruct((1, 128), jnp.float32),
    ]
    anywhere = pl.BlockSpec(memory_space=pl.ANY)
    local = pl.BlockSpec(memory_space=pltpu.VMEM)
    sends = 5 * (4 + 3 * n_seq + 6) + 6 + n_seq - 1
    chips = n_dp // 2

    def like(array):
        return pltpu.VMEM(array.shape, array.dtype)

    scratch = [
        pltpu.SemaphoreType.DMA((sends,)),
        pltpu.SemaphoreType.DMA((5, chips)),
        pltpu.SemaphoreType.DMA((5, n_seq, 2)),
        pltpu.SemaphoreType.DMA((5, n_seq)),
        pltpu.SemaphoreType.DMA((5, 5)),
        pltpu.SemaphoreType.DMA((2, 2)),
        pltpu.SemaphoreType.DMA((n_seq,)),
        pltpu.SemaphoreType.DMA((15,)),
        pltpu.SemaphoreType.DMA((5,)),
        like(logs),
        like(own_context),
        pltpu.VMEM((n_seq, count, part), low),
        like(query),
        like(key),
        like(value),
        like(key_turned),
        pltpu.VMEM((local_heads, count, 256), low),
        pltpu.VMEM((local_heads, count, 128), low),
        pltpu.VMEM((local_heads, head_dim, count), jnp.float32),
        pltpu.VMEM((blocks, stream, 128), jnp.float32),
        pltpu.VMEM((blocks, stream, 128), jnp.float32),
        pltpu.VMEM((stream, 3 * part), low),
        like(gelu),
        like(columns),
        pltpu.VMEM((devices, 16, 128), jnp.float32),
        pltpu.VMEM((n_seq - 1, count, width), low),
        pltpu.VMEM((5, count, width), low),
        pltpu.VMEM((count, width), jnp.float32),
        like(columns),
        like(hidden),
        like(context),
        like(slopes),
        like(normed),
        pltpu.VMEM((count, width), low),
        pltpu.VMEM((n_seq, count, part), low),
        like(full_out),
        pltpu.VMEM((2, n_seq) + shapes[0], low),
        pltpu.VMEM((2, devices // 2, full_up.shape[1], width), low),
        pltpu.VMEM((2, n_seq) + shapes[0], low),
        pltpu.VMEM((2, n_seq) + shapes[1], low),
        pltpu.VMEM((2, n_seq) + shapes[2], low),
    ]
    for shape, kind in zip(shapes, kinds):
        scratch += [
            pltpu.VMEM((chips, n_seq) + shape, kind),
            pltpu.VMEM((n_seq, 2) + shape, kind),
            pltpu.VMEM((n_seq,) + shape, kind),
            pltpu.VMEM((5,) + shape, kind),
        ]
    return pl.pallas_call(
        lambda *refs: back_kernel(sizes, heads, *refs),
        out_shape=[jax.ShapeDtypeStruct((count, width), low)] + results,
        in_specs=[anywhere] * 2 + [local] * 2 + [anywhere] * 15,
        out_specs=[local] * 7,
        scratch_shapes=scratch,
        compiler_params=pltpu.CompilerParams(
            collective_id=1, has_side_effects=True, vmem_limit_bytes=63 * 2**20
        ),
        name="back",
    )(*saved)


def kernel_plan(
    x_in,
    w_qkv,
    q_bias,
    v_bias,
    w_out,
    out_bias,
    ln1_gain,
    ln1_shift,
    w_up,
    up_bias,
    w_down,
    down_bias,
    ln2_gain,
    ln2_shift,
    valid,
    cotangent,
):
    sizes = (lax.axis_size("dp"), lax.axis_size("seq"))
    n_dp, groups = sizes
    rows = x_in[0]
    count, width = rows.shape
    vectors = (q_bias, v_bias, out_bias, ln1_gain, ln1_shift, down_bias, ln2_gain, ln2_shift)
    lines = jnp.stack(vectors)
    (
        columns,
        full_out,
        full_up,
        full_down,
        page_turned,
        query,
        key,
        value,
        key_turned,
        context,
        logs,
        own_context,
        hidden,
        gelu,
        slopes,
        output,
        normed,
        inv,
        grad_mid,
        line_sums,
    ) = front(sizes, HEADS, valid, rows, cotangent[0], lines, up_bias[None], w_qkv, w_out, w_up, w_down)
    saved = (grad_mid, normed, inv, line_sums, logs, page_turned, query, key, value, key_turned)
    saved += (context, hidden, gelu, slopes, own_context, columns, full_out, full_up, full_down)
    devices = n_dp * groups
    grad_rows, *sums = back(sizes, HEADS, saved, (w_down.shape, w_up.shape, w_out.shape))
    mine = sums[4]
    return (
        output[None],
        grad_rows[None],
        sums[3],
        mine[0],
        mine[1],
        sums[2],
        mine[2],
        mine[3],
        mine[4],
        sums[1],
        sums[5].reshape(-1),
        sums[0],
        mine[5],
        mine[6],
        mine[7],
    )


def solution(mesh):
    n_dp, n_seq = mesh.shape["dp"], mesh.shape["seq"]

    def per_device(x_in, w_qkv, *rest):
        part, width = w_qkv.shape[0], x_in.shape[2]
        fits = (n_dp, n_seq) == (8, 4) and part % 32 == 0 and part * n_seq == 128 and width // n_seq % 128 == 0 and x_in.shape[0] == 1
        plan = kernel_plan if fits else general_plan
        return plan(x_in, w_qkv, *rest)

    return jax.shard_map(
        per_device,
        mesh=mesh,
        in_specs=(
            P("dp", "seq", None),
            P(("dp", "seq"), None),
            P(("dp", "seq")),
            P(("dp", "seq")),
            P(("dp", "seq"), None),
            P(("dp", "seq")),
            P(("dp", "seq")),
            P(("dp", "seq")),
            P(("dp", "seq"), None),
            P(("dp", "seq")),
            P(("dp", "seq"), None),
            P(("dp", "seq")),
            P(("dp", "seq")),
            P(("dp", "seq")),
            P("dp"),
            P("dp", "seq", None),
        ),
        out_specs=(
            P("dp", "seq", None),
            P("dp", "seq", None),
            P(("dp", "seq"), None),
            P(("dp", "seq")),
            P(("dp", "seq")),
            P(("dp", "seq"), None),
            P(("dp", "seq")),
            P(("dp", "seq")),
            P(("dp", "seq")),
            P(("dp", "seq"), None),
            P(("dp", "seq")),
            P(("dp", "seq"), None),
            P(("dp", "seq")),
            P(("dp", "seq")),
            P(("dp", "seq")),
        ),
        check_vma=False,
    )
```

```python
import math

import jax
import jax.numpy as jnp
from jax import lax
from jax.experimental import pallas as pl
from jax.experimental.pallas import tpu as pltpu
from jax.sharding import PartitionSpec as P

HEADS = 16


eps_norm = 1e-05


def outer_sum(left, right):
    return lax.dot_general(
        left, right, (((0,), (0,)), ((), ())), preferred_element_type=jnp.float32
    )


def times_back(rows, matrix):
    return lax.dot_general(
        rows, matrix, (((1,), (1,)), ((), ())), preferred_element_type=jnp.float32
    )


def gelu_exact(values):
    return jax.nn.gelu(values, approximate=False)


def norm_forward(rows, gain, shift):
    center = rows - jnp.mean(rows, axis=-1, keepdims=True)
    inv_std = lax.rsqrt(jnp.mean(center * center, axis=-1, keepdims=True) + eps_norm)
    normed = center * inv_std
    return (normed * gain + shift, normed, inv_std)


def norm_backward(grad_out, normed, inv_std, gain):
    scaled = grad_out * gain
    grad_rows = inv_std * (
        scaled
        - jnp.mean(scaled, axis=-1, keepdims=True)
        - normed * jnp.mean(scaled * normed, axis=-1, keepdims=True)
    )
    return (grad_rows, jnp.sum(grad_out * normed, axis=0), jnp.sum(grad_out, axis=0))


def to_heads(rows, groups):
    count, width = rows.shape
    return rows.reshape(count, groups, width // groups).transpose(1, 0, 2).reshape(groups, -1)


def from_heads(pieces, part_width):
    groups = pieces.shape[0]
    return (
        pieces.reshape(groups, -1, part_width).transpose(1, 0, 2).reshape(-1, groups * part_width)
    )


def general_plan(
    x_in,
    w_qkv,
    q_bias,
    v_bias,
    w_out,
    out_bias,
    ln1_gain,
    ln1_shift,
    w_up,
    up_bias,
    w_down,
    down_bias,
    ln2_gain,
    ln2_shift,
    valid,
    cotangent,
):
    shards = (
        w_qkv,
        q_bias,
        v_bias,
        w_out,
        out_bias,
        ln1_gain,
        ln1_shift,
        w_up,
        up_bias,
        w_down,
        down_bias,
        ln2_gain,
        ln2_shift,
    )
    weights = (
        lax.all_gather(shards[0], ("dp", "seq"), axis=0, tiled=True),
        lax.all_gather(shards[1], ("dp", "seq"), axis=0, tiled=True),
        lax.all_gather(shards[2], ("dp", "seq"), axis=0, tiled=True),
        lax.all_gather(shards[3], ("dp", "seq"), axis=0, tiled=True),
        lax.all_gather(shards[4], ("dp", "seq"), axis=0, tiled=True),
        lax.all_gather(shards[5], ("dp", "seq"), axis=0, tiled=True),
        lax.all_gather(shards[6], ("dp", "seq"), axis=0, tiled=True),
        lax.all_gather(shards[7], ("dp", "seq"), axis=0, tiled=True),
        lax.all_gather(shards[8], ("dp", "seq"), axis=0, tiled=True),
        lax.all_gather(shards[9], ("dp", "seq"), axis=0, tiled=True),
        lax.all_gather(shards[10], ("dp", "seq"), axis=0, tiled=True),
        lax.all_gather(shards[11], ("dp", "seq"), axis=0, tiled=True),
        lax.all_gather(shards[12], ("dp", "seq"), axis=0, tiled=True),
    )
    (
        full_qkv,
        full_qbias,
        full_vbias,
        full_out,
        full_obias,
        full_gain1,
        full_shift1,
        full_up,
        full_ubias,
        full_down,
        full_dbias,
        full_gain2,
        full_shift2,
    ) = weights
    groups = lax.axis_size("seq")
    rows = x_in[0]
    count, width = rows.shape
    head_dim = width // HEADS
    part_width = width // groups
    local_heads = HEADS // groups
    stream = count * groups
    qrows = min(512, stream)
    nblocks = stream // qrows
    scale = 1.0 / math.sqrt(head_dim)
    keep = jnp.arange(stream, dtype=jnp.int32) < valid[0]
    bias_row = jnp.concatenate([full_qbias, jnp.zeros_like(full_qbias), full_vbias]).astype(
        jnp.float32
    )
    project = (jnp.dot(rows, full_qkv, preferred_element_type=jnp.float32) + bias_row).astype(
        jnp.bfloat16
    )
    sent = (
        to_heads(project[:, :width], groups),
        to_heads(project[:, width : 2 * width], groups),
        to_heads(project[:, 2 * width :], groups),
    )
    arrived = (
        lax.all_to_all(sent[0], "seq", split_axis=0, concat_axis=0, tiled=True),
        lax.all_to_all(sent[1], "seq", split_axis=0, concat_axis=0, tiled=True),
        lax.all_to_all(sent[2], "seq", split_axis=0, concat_axis=0, tiled=True),
    )
    query_blocks = arrived[0].reshape(nblocks, qrows, local_heads, head_dim)
    key_heads = arrived[1].reshape(stream, local_heads, head_dim)
    value_heads = arrived[2].reshape(stream, local_heads, head_dim)

    def masked_scores(query):
        scores = (
            jnp.einsum("qhd,khd->hqk", query, key_heads, preferred_element_type=jnp.float32) * scale
        )
        return jnp.where(keep[None, None, :], scores, -1e30)

    def attend_forward(query):
        scores = masked_scores(query)
        peak = jnp.max(scores, axis=-1, keepdims=True)
        raised = jnp.exp(scores - peak)
        total = jnp.sum(raised, axis=-1, keepdims=True)
        probs = (raised / total).astype(jnp.bfloat16)
        context = jnp.einsum("hqk,khd->qhd", probs, value_heads, preferred_element_type=jnp.float32)
        return (context.astype(jnp.bfloat16), (peak + jnp.log(total))[..., 0])

    context, log_sums = lax.map(attend_forward, query_blocks)
    returned_ctx = lax.all_to_all(
        context.reshape(groups, -1), "seq", split_axis=0, concat_axis=0, tiled=True
    )
    context_rows = from_heads(returned_ctx, part_width)
    attn_out = jnp.dot(
        context_rows, full_out, preferred_element_type=jnp.float32
    ) + full_obias.astype(jnp.float32)
    first_rows = rows.astype(jnp.float32) + attn_out
    hidden, normed_one, inv_one = norm_forward(
        first_rows, full_gain1.astype(jnp.float32), full_shift1.astype(jnp.float32)
    )
    hidden_low = hidden.astype(jnp.bfloat16)
    up_act = jnp.dot(hidden_low, full_up, preferred_element_type=jnp.float32) + full_ubias.astype(
        jnp.float32
    )
    gelu_low = gelu_exact(up_act).astype(jnp.bfloat16)
    branch = jnp.dot(gelu_low, full_down, preferred_element_type=jnp.float32) + full_dbias.astype(
        jnp.float32
    )
    output, normed_two, inv_two = norm_forward(
        hidden + branch, full_gain2.astype(jnp.float32), full_shift2.astype(jnp.float32)
    )
    again = (
        lax.all_gather(shards[0], ("dp", "seq"), axis=0, tiled=True),
        lax.all_gather(shards[1], ("dp", "seq"), axis=0, tiled=True),
        lax.all_gather(shards[2], ("dp", "seq"), axis=0, tiled=True),
        lax.all_gather(shards[3], ("dp", "seq"), axis=0, tiled=True),
        lax.all_gather(shards[4], ("dp", "seq"), axis=0, tiled=True),
        lax.all_gather(shards[5], ("dp", "seq"), axis=0, tiled=True),
        lax.all_gather(shards[6], ("dp", "seq"), axis=0, tiled=True),
        lax.all_gather(shards[7], ("dp", "seq"), axis=0, tiled=True),
        lax.all_gather(shards[8], ("dp", "seq"), axis=0, tiled=True),
        lax.all_gather(shards[9], ("dp", "seq"), axis=0, tiled=True),
        lax.all_gather(shards[10], ("dp", "seq"), axis=0, tiled=True),
        lax.all_gather(shards[11], ("dp", "seq"), axis=0, tiled=True),
        lax.all_gather(shards[12], ("dp", "seq"), axis=0, tiled=True),
    )
    back_qkv, back_out, back_gain1, back_up, back_down, back_gain2 = (
        again[0],
        again[3],
        again[5],
        again[7],
        again[9],
        again[11],
    )
    grad_out = cotangent[0].astype(jnp.float32)
    grad_mid, grad_ln2_gain, grad_ln2_shift = norm_backward(
        grad_out, normed_two, inv_two, back_gain2.astype(jnp.float32)
    )
    grad_branch = grad_mid.astype(jnp.bfloat16)
    grad_w_down = outer_sum(gelu_low, grad_branch)
    grad_down_bias = jnp.sum(grad_branch.astype(jnp.float32), axis=0)
    grad_gelu = times_back(grad_branch, back_down)
    grad_up = jax.vjp(gelu_exact, up_act)[1](grad_gelu)[0].astype(jnp.bfloat16)
    grad_w_up = outer_sum(hidden_low, grad_up)
    grad_up_bias = jnp.sum(grad_up.astype(jnp.float32), axis=0)
    grad_hidden = times_back(grad_up, back_up) + grad_mid
    grad_first, grad_ln1_gain, grad_ln1_shift = norm_backward(
        grad_hidden, normed_one, inv_one, back_gain1.astype(jnp.float32)
    )
    grad_attn = grad_first.astype(jnp.bfloat16)
    grad_w_out = outer_sum(context_rows, grad_attn)
    grad_out_bias = jnp.sum(grad_attn.astype(jnp.float32), axis=0)
    grad_context = times_back(grad_attn, back_out).astype(jnp.bfloat16)
    grad_ctx_heads = lax.all_to_all(
        to_heads(grad_context, groups), "seq", split_axis=0, concat_axis=0, tiled=True
    )
    grad_ctx_blocks = grad_ctx_heads.reshape(nblocks, qrows, local_heads, head_dim)

    def attend_backward(carry, inputs):
        key_total, value_total = carry
        query, grad_ctx, log_rows = inputs
        scores = masked_scores(query)
        probs = jnp.exp(scores - log_rows[..., None])
        probs_low = probs.astype(jnp.bfloat16)
        d_probs = jnp.einsum(
            "qhd,khd->hqk", grad_ctx, value_heads, preferred_element_type=jnp.float32
        )
        centre = jnp.sum(probs * d_probs, axis=-1, keepdims=True)
        grad_scores = (probs * (d_probs - centre)).astype(jnp.bfloat16)
        grad_query = (
            jnp.einsum("hqk,khd->qhd", grad_scores, key_heads, preferred_element_type=jnp.float32)
            * scale
        )
        key_total = (
            key_total
            + jnp.einsum("hqk,qhd->khd", grad_scores, query, preferred_element_type=jnp.float32)
            * scale
        )
        value_total = value_total + jnp.einsum(
            "hqk,qhd->khd", probs_low, grad_ctx, preferred_element_type=jnp.float32
        )
        return ((key_total, value_total), grad_query.astype(jnp.bfloat16))

    empty = jnp.zeros((stream, local_heads, head_dim), jnp.float32)
    (key_total, value_total), grad_query = lax.scan(
        attend_backward, (empty, empty), (query_blocks, grad_ctx_blocks, log_sums)
    )
    grad_key = key_total.astype(jnp.bfloat16)
    grad_value = value_total.astype(jnp.bfloat16)
    grad_pieces = (
        lax.all_to_all(
            grad_query.reshape(groups, -1), "seq", split_axis=0, concat_axis=0, tiled=True
        ),
        lax.all_to_all(
            grad_key.reshape(groups, -1), "seq", split_axis=0, concat_axis=0, tiled=True
        ),
        lax.all_to_all(
            grad_value.reshape(groups, -1), "seq", split_axis=0, concat_axis=0, tiled=True
        ),
    )
    grad_project = jnp.concatenate(
        [
            from_heads(grad_pieces[0], part_width),
            from_heads(grad_pieces[1], part_width),
            from_heads(grad_pieces[2], part_width),
        ],
        axis=1,
    )
    grad_w_qkv = outer_sum(rows, grad_project)
    bias_sums = jnp.sum(grad_project.astype(jnp.float32), axis=0)
    grad_q_bias = bias_sums[:width]
    grad_v_bias = bias_sums[2 * width :]
    grad_rows = times_back(grad_project, back_qkv) + grad_first
    terms = (
        grad_w_qkv,
        grad_q_bias,
        grad_v_bias,
        grad_w_out,
        grad_out_bias,
        grad_ln1_gain,
        grad_ln1_shift,
        grad_w_up,
        grad_up_bias,
        grad_w_down,
        grad_down_bias,
        grad_ln2_gain,
        grad_ln2_shift,
    )
    page_sums = (
        lax.psum_scatter(
            terms[0].astype(jnp.bfloat16), "dp", scatter_dimension=0, tiled=True
        ).astype(jnp.float32),
        lax.psum_scatter(
            terms[1].astype(jnp.bfloat16), "dp", scatter_dimension=0, tiled=True
        ).astype(jnp.float32),
        lax.psum_scatter(
            terms[2].astype(jnp.bfloat16), "dp", scatter_dimension=0, tiled=True
        ).astype(jnp.float32),
        lax.psum_scatter(
            terms[3].astype(jnp.bfloat16), "dp", scatter_dimension=0, tiled=True
        ).astype(jnp.float32),
        lax.psum_scatter(
            terms[4].astype(jnp.bfloat16), "dp", scatter_dimension=0, tiled=True
        ).astype(jnp.float32),
        lax.psum_scatter(
            terms[5].astype(jnp.bfloat16), "dp", scatter_dimension=0, tiled=True
        ).astype(jnp.float32),
        lax.psum_scatter(
            terms[6].astype(jnp.bfloat16), "dp", scatter_dimension=0, tiled=True
        ).astype(jnp.float32),
        lax.psum_scatter(
            terms[7].astype(jnp.bfloat16), "dp", scatter_dimension=0, tiled=True
        ).astype(jnp.float32),
        lax.psum_scatter(
            terms[8].astype(jnp.bfloat16), "dp", scatter_dimension=0, tiled=True
        ).astype(jnp.float32),
        lax.psum_scatter(
            terms[9].astype(jnp.bfloat16), "dp", scatter_dimension=0, tiled=True
        ).astype(jnp.float32),
        lax.psum_scatter(
            terms[10].astype(jnp.bfloat16), "dp", scatter_dimension=0, tiled=True
        ).astype(jnp.float32),
        lax.psum_scatter(
            terms[11].astype(jnp.bfloat16), "dp", scatter_dimension=0, tiled=True
        ).astype(jnp.float32),
        lax.psum_scatter(
            terms[12].astype(jnp.bfloat16), "dp", scatter_dimension=0, tiled=True
        ).astype(jnp.float32),
    )
    sums = (
        lax.psum_scatter(
            page_sums[0].astype(jnp.bfloat16), "seq", scatter_dimension=0, tiled=True
        ).astype(jnp.float32),
        lax.psum_scatter(
            page_sums[1].astype(jnp.bfloat16), "seq", scatter_dimension=0, tiled=True
        ).astype(jnp.float32),
        lax.psum_scatter(
            page_sums[2].astype(jnp.bfloat16), "seq", scatter_dimension=0, tiled=True
        ).astype(jnp.float32),
        lax.psum_scatter(
            page_sums[3].astype(jnp.bfloat16), "seq", scatter_dimension=0, tiled=True
        ).astype(jnp.float32),
        lax.psum_scatter(
            page_sums[4].astype(jnp.bfloat16), "seq", scatter_dimension=0, tiled=True
        ).astype(jnp.float32),
        lax.psum_scatter(
            page_sums[5].astype(jnp.bfloat16), "seq", scatter_dimension=0, tiled=True
        ).astype(jnp.float32),
        lax.psum_scatter(
            page_sums[6].astype(jnp.bfloat16), "seq", scatter_dimension=0, tiled=True
        ).astype(jnp.float32),
        lax.psum_scatter(
            page_sums[7].astype(jnp.bfloat16), "seq", scatter_dimension=0, tiled=True
        ).astype(jnp.float32),
        lax.psum_scatter(
            page_sums[8].astype(jnp.bfloat16), "seq", scatter_dimension=0, tiled=True
        ).astype(jnp.float32),
        lax.psum_scatter(
            page_sums[9].astype(jnp.bfloat16), "seq", scatter_dimension=0, tiled=True
        ).astype(jnp.float32),
        lax.psum_scatter(
            page_sums[10].astype(jnp.bfloat16), "seq", scatter_dimension=0, tiled=True
        ).astype(jnp.float32),
        lax.psum_scatter(
            page_sums[11].astype(jnp.bfloat16), "seq", scatter_dimension=0, tiled=True
        ).astype(jnp.float32),
        lax.psum_scatter(
            page_sums[12].astype(jnp.bfloat16), "seq", scatter_dimension=0, tiled=True
        ).astype(jnp.float32),
    )
    return (
        output.astype(jnp.bfloat16)[None],
        grad_rows.astype(jnp.bfloat16)[None],
        sums[0],
        sums[1],
        sums[2],
        sums[3],
        sums[4],
        sums[5],
        sums[6],
        sums[7],
        sums[8],
        sums[9],
        sums[10],
        sums[11],
        sums[12],
    )


MESH = pl.DeviceIdType.MESH
CHUNK = 256
MASKED = -1e30
FLAT = (((1,), (1,)), ((), ()))


def flip(index, mask):
    for b in range(mask.bit_length()):
        if mask >> b & 1:
            bit = 1 << b
            index = index + bit - 2 * bit * (index // bit % 2)
    return index


def guarded(when, action):
    if when is None:
        action()
    else:
        pl.when(when)(action)


class Wires:
    def __init__(self, sems, sizes):
        self.sems, self.sizes = sems, sizes
        self.dp, self.z = lax.axis_index("dp"), lax.axis_index("seq")
        self.dps = [flip(self.dp, m) for m in range(sizes[0])]
        self.zs = [flip(self.z, m) for m in range(sizes[1])]
        last = sizes[1] - 1
        half = self.z // 2
        step = 1 - 2 * half
        depth = self.z * step + last * half
        self.inner, self.outer = depth == 1, depth == 0
        self.right = self.z + step
        self.left = self.z - step * depth
        self.far = [self.z] + [t * step + last * half for t in (1 - depth, 2, 3)]
        self.started = []

    def peer(self, offset, step):
        return (self.dps[offset], self.zs[step])

    def send(self, src, dst, recv_sem, device, when=None):
        copy = pltpu.make_async_remote_copy(
            src_ref=src,
            dst_ref=dst,
            send_sem=self.sems.at[len(self.started)],
            recv_sem=recv_sem,
            device_id=device,
            device_id_type=MESH,
        )
        guarded(when, copy.start)
        self.started.append((copy, when))
        return len(self.started) - 1

    def sent(self, index):
        copy, when = self.started[index]
        guarded(when, copy.wait_send)
        self.started[index] = None

    def arrived(self, dst, recv_sem, when=None):
        copy = pltpu.make_async_remote_copy(
            src_ref=dst,
            dst_ref=dst,
            send_sem=self.sems.at[0],
            recv_sem=recv_sem,
            device_id=self.peer(1, 0),
            device_id_type=MESH,
        )
        guarded(when, copy.wait_recv)

    def drain(self):
        for index, entry in enumerate(self.started):
            if entry is not None:
                self.sent(index)

    def greet(self):
        n_dp, n_seq = self.sizes
        barrier = pltpu.get_barrier_semaphore()
        masks = [1 << b for b in range(n_dp.bit_length() - 1)]
        partners = [self.peer(m, 0) for m in masks] + [self.peer(0, i) for i in range(1, n_seq)]
        for device in partners:
            pl.semaphore_signal(barrier, inc=1, device_id=device, device_id_type=MESH)
        pl.semaphore_wait(barrier, len(partners))


class Line:
    def __init__(self, wires, slot, recv):
        self.w, self.slot, self.recv = wires, slot, recv

    def pass_on(self, k, src, to_left):
        w = self.w
        s = w.far[k]
        dst = self.slot(s)
        if to_left:
            w.send(src, dst, self.recv.at[s], (w.dp, w.left), w.inner)
        else:
            w.send(src, dst, self.recv.at[s], (w.dp, w.right), None if k == 0 else w.inner)

    def own(self, src):
        self.pass_on(0, src, False)
        self.pass_on(0, src, True)

    def take(self, k):
        s = self.w.far[k]
        self.w.arrived(self.slot(s), self.recv.at[s])
        self.pass_on(k, self.slot(s), k > 1)

    def relay(self, k):
        s = self.w.far[k]
        self.w.arrived(self.slot(s), self.recv.at[s], self.w.inner)
        self.pass_on(k, self.slot(s), k > 1)

    def end(self, k):
        s = self.w.far[k]
        self.w.arrived(self.slot(s), self.recv.at[s], self.w.outer)


class Gather:
    def __init__(self, wires, src, full, recv, local):
        self.w, self.src, self.full, self.recv, self.local = wires, src, full, recv, local
        n_dp, self.n_seq = wires.sizes
        self.chips = [1 << b for b in range(1, n_dp.bit_length() - 1)]
        self.slots = wires.far
        self.line = Line(wires, lambda s: full.at[wires.dp * self.n_seq + s], recv.at[0])

    def at(self, offset, step):
        return self.full.at[self.w.dps[offset] * self.n_seq + self.slots[step]]

    def order(self, step):
        return self.chips if step % 2 == 0 else self.chips[::-1]

    def forward(self, src, offset, step, masks):
        for m in masks:
            sem = self.recv.at[offset ^ m, self.slots[step]]
            self.w.send(src, self.at(offset, step), sem, self.w.peer(m, 0))

    def wait(self, offset, step):
        self.w.arrived(self.at(offset, step), self.recv.at[offset, self.slots[step]])

    def mine(self):
        return self.src

    def own_chips(self):
        self.kept = pltpu.make_async_copy(self.mine(), self.at(0, 0), self.local)
        self.kept.start()
        self.forward(self.mine(), 0, 0, self.order(0) + [1])

    def own_seq(self):
        self.line.own(self.src)

    def along_seq(self, i):
        self.line.take(i)
        self.forward(self.at(0, i), 0, i, self.order(i) + [1])

    def stages(self, step):
        have, out = [0], []
        masks = self.order(step)
        for t, m in enumerate(masks):
            out.append([(o ^ m, masks[t + 1 :] + [1]) for o in have])
            have = have + [o ^ m for o in have]
        return out

    def over_chips(self, t, step):
        for offset, masks in self.stages(step)[t]:
            self.wait(offset, step)
            self.forward(self.at(offset, step), offset, step, masks)

    def over_cores(self, stored=None):
        n_dp = self.w.sizes[0]
        for offset in list(range(0, n_dp, 2)) + list(range(1, n_dp, 2)):
            if offset % 2:
                for i in range(self.n_seq):
                    self.wait(offset, i)
            elif offset == 0:
                self.kept.wait()
            if stored is not None:
                stored(self.w.dps[offset] * self.n_seq)


class GatherDirect(Gather):
    def __init__(self, *args):
        super().__init__(*args)
        self.slots = self.w.zs

    def part_for(self, i):
        return self.src

    def own_seq(self):
        for i in range(1, self.n_seq):
            sem = self.recv.at[0, self.w.z]
            self.w.send(self.part_for(i), self.at(0, 0), sem, self.w.peer(0, i))

    def along_seq(self, i):
        self.wait(0, i)
        self.forward(self.at(0, i), 0, i, self.order(i) + [1])


class GatherColumns(GatherDirect):
    def mine(self):
        return self.src.at[self.w.z]

    def part_for(self, i):
        return self.src.at[self.w.zs[i]]


def sends_of_gather(n_dp, n_seq):
    return 2 + n_seq - 1 + n_seq * (n_dp - 1)


def group_lanes(packed, row, group, n_seq):
    total = packed[group * n_seq, row : row + 1, :]
    for s in range(1, n_seq):
        total = total + packed[group * n_seq + s, row : row + 1, :]
    return total


def spread_head(source, h, head_dim, factor):
    n_seq, rows, _ = source.shape
    block = h * head_dim // 128 * 128
    low = h * head_dim % 128
    lane = lax.broadcasted_iota(jnp.int32, (n_seq * rows, 128), 1)
    values = source[:, :, block : block + 128].reshape(n_seq * rows, 128).astype(jnp.float32)
    kept = jnp.where((lane >= low) & (lane < low + head_dim), values * factor, 0.0)
    return kept.astype(jnp.bfloat16).reshape(n_seq, rows, 128)


def front_kernel(
    sizes,
    heads,
    valid_ref,
    x_ref,
    cotangent,
    lines_ref,
    up_line_ref,
    qkv_shard,
    out_ref,
    up_ref,
    down_ref,
    columns_out,
    full_out,
    full_up,
    full_down,
    page_out,
    query_out,
    key_out,
    value_out,
    key_turned_out,
    context_out,
    logs_out,
    own_context_out,
    hidden_out,
    gelu_out,
    slope_out,
    output,
    normed_one,
    inv_one,
    grad_mid,
    sums_out,
    vec_own,
    qkv_own,
    packed,
    columns,
    page,
    held,
    context_sent,
    context_held,
    context_turned,
    value_turned,
    masked_query,
    keys,
    values,
    key_turned,
    logs,
    log_columns,
    normed_rows,
    inv_rows,
    out_matrix,
    up_matrix,
    down_matrix,
    page_turned,
    context_rows_turned,
    hidden,
    hidden_low,
    hidden_turned,
    gelu_low,
    gelu_turned,
    slopes,
    branch,
    send_sems,
    gather_sems,
    page_sems,
    context_sems,
    local_sems,
):
    n_dp, n_seq = sizes
    w = Wires(send_sems, sizes)
    rows, width = x_ref.shape
    part = width // n_seq
    head_dim = width // heads
    local_heads = heads // n_seq
    stream = rows * n_seq
    low_lane = lax.broadcasted_iota(jnp.int32, (8, 128), 1) // lines_ref.shape[1]
    lines = jnp.concatenate([lines_ref[...].astype(jnp.float32)] * n_seq, axis=1)
    vec_own[:8, :] = jnp.where(low_lane == w.z, lines, 0.0)
    vec_own[8:, :] = jnp.broadcast_to(up_line_ref[...].astype(jnp.float32), (8, 128))
    for t in range(3):
        for j in range(n_seq):
            at = t * width + j * part
            qkv_own[j, :, t * part : (t + 1) * part] = qkv_shard[:, at : at + part]
    w.greet()
    line = Line(w, lambda s: page.at[s], page_sems)
    sources = (
        (vec_own, packed),
        (qkv_own, columns),
        (out_ref, out_matrix),
        (up_ref, up_matrix),
        (down_ref, down_matrix),
    )
    vec, qkv, out, up, down = [
        (GatherDirect, GatherColumns, Gather, Gather, Gather)[k](w, src, dst, gather_sems.at[k], local_sems.at[k])
        for k, (src, dst) in enumerate(sources)
    ]
    def run(steps):
        for step in steps:
            step()

    keeps = []

    def keep(src, dst):
        keeps.append(pltpu.make_async_copy(src, dst, local_sems.at[5 + len(keeps)]))
        keeps[-1].start()

    per_block = 128 // head_dim
    scale = 1.0 / math.sqrt(head_dim)
    groups = part // 128
    one_lane = lax.broadcasted_iota(jnp.int32, (rows, 128), 1)
    ones = jnp.where(one_lane == 0, 1.0, 0.0).astype(jnp.bfloat16)
    chunk = 512
    chunks = up_matrix.shape[2] // chunk
    per_chunk = chunk // down_matrix.shape[1]
    per_part = part // out_matrix.shape[1]

    def line_of(row):
        return jnp.concatenate([group_lanes(packed, row, d, n_seq) for d in range(n_dp)], axis=1)

    def gathered_columns():
        qkv.over_cores()
        vec.over_cores()
        keep(columns, columns_out)

    def project(k):
        s = w.far[k]
        if k == 0:
            page[s] = x_ref[...]
        matrix = columns[...].reshape(width, 3 * part)
        piece = jnp.dot(page[s], matrix, preferred_element_type=jnp.float32)
        for t in range(3):
            third = piece[:, t * part : (t + 1) * part]
            if t != 1:
                bias = [group_lanes(packed, t // 2, w.z * groups + g, n_seq) for g in range(groups)]
                third = third + jnp.concatenate(bias, axis=1)
            held[t, s] = third.astype(jnp.bfloat16)

    def prepare():
        position = lax.broadcasted_iota(jnp.int32, (stream, 128), 0)
        lane = lax.broadcasted_iota(jnp.int32, (stream, 128), 1)
        guard = jnp.where(position >= valid_ref[0], MASKED, 0.0)
        guard = jnp.where(lane == 0, guard, jnp.where(lane < 4, 1.0, 0.0)).astype(jnp.bfloat16)
        for h in range(local_heads):
            masked_query[h] = spread_head(held.at[0], h, head_dim, scale)
        for b in range(local_heads // per_block):
            lanes = slice(b * 128, (b + 1) * 128)
            keys[b, :, :128] = held[1, :, :, lanes].reshape(stream, 128)
            keys[b, :, 128:] = guard
            values[b, :, :128] = held[2, :, :, lanes].reshape(stream, 128)
            values[b, :, 128:] = jnp.where(lane < 3, 1.0, 0.0).astype(jnp.bfloat16)
        turned = held[1].reshape(stream, part).T
        for h in range(local_heads):
            key_turned[h] = turned[h * head_dim : (h + 1) * head_dim, :]
        value_turned[...] = held[2].reshape(stream, part).T
        keep(masked_query, query_out)
        keep(keys, key_out)
        keep(values, value_out)
        keep(key_turned, key_turned_out)

    def attention(i):
        c = w.zs[i]

        def attend(h, _):
            at = pl.ds(pl.multiple_of(h * head_dim, head_dim), head_dim)
            query = jnp.concatenate([masked_query[h, c], ones], axis=1)
            scores = lax.dot_general(
                keys[h // per_block], query, FLAT, preferred_element_type=jnp.float32
            )
            peak = jnp.max(scores, axis=0, keepdims=True)
            raised = jnp.exp(scores - peak)
            total = jnp.sum(raised, axis=0, keepdims=True)
            mixed = jnp.dot(
                value_turned[at, :], raised.astype(jnp.bfloat16), preferred_element_type=jnp.float32
            )
            context_turned[c, at, :] = mixed / total
            logs[pl.ds(h, 1), :] = peak + jnp.log(total)
            return 0

        lax.fori_loop(0, local_heads, attend, 0)
        log_columns[c, :, :8] = logs[...].T
        piece = context_turned[c].T.astype(jnp.bfloat16)
        context_sent[i] = piece
        if i:
            w.send(context_sent.at[i], context_held.at[w.z], context_sems.at[i], w.peer(0, i))
        else:
            context_held[w.z] = piece

    def keep_logs():
        keep(log_columns, logs_out)
        keep(context_sent, own_context_out)

    def turn_page():
        for s in range(n_seq):
            page_turned[s * width : (s + 1) * width, :] = page[s].T
        keep(page_turned, page_out)

    def context_arrived():
        for i in range(1, n_seq):
            w.arrived(context_held.at[w.zs[i]], context_sems.at[i])

    def gathered_out():
        out.over_cores()
        keep(out_matrix, full_out)

    def keep_groups(unit, src, dst):
        def store(first):
            group = pl.ds(first, n_seq)
            keep(src.at[group], dst.at[group])

        unit.over_cores(store)

    def gathered_up():
        keep_groups(up, up_matrix, full_up)

    def gathered_down():
        keep_groups(down, down_matrix, full_down)

    def first_norm():
        total = x_ref[...].astype(jnp.float32) + line_of(2)
        for j in range(n_seq):
            block = out_matrix[j * per_part : (j + 1) * per_part].reshape(part, width)
            total = total + jnp.dot(context_held[j], block, preferred_element_type=jnp.float32)
            context_rows_turned[j * part : (j + 1) * part, :] = context_held[j].T
        keep(context_rows_turned, context_out)
        rows_hidden, normed, inv = norm_forward(total, line_of(3), line_of(4))
        normed_rows[...] = normed
        inv_rows[...] = jnp.broadcast_to(inv, inv_rows.shape)
        keep(normed_rows, normed_one)
        keep(inv_rows, inv_one)
        hidden[...] = rows_hidden
        hidden_low[...] = rows_hidden.astype(jnp.bfloat16)
        hidden_turned[...] = hidden_low[...].T
        keep(hidden_turned, hidden_out)

    def expand():
        def activate(f, _):
            at = pl.ds(pl.multiple_of(f * chunk, chunk), chunk)
            block = up_matrix[:, :, at].reshape(width, chunk)
            up_bias = jnp.concatenate(
                [packed[f * per_chunk + e, 8:9, :] for e in range(per_chunk)], axis=1
            )
            act = jnp.dot(hidden_low[...], block, preferred_element_type=jnp.float32) + up_bias
            below = 0.5 + 0.5 * lax.erf(act * math.sqrt(0.5))
            gelu = act * below
            gelu = gelu.astype(jnp.bfloat16)
            gelu_low[:, at] = gelu
            gelu_turned[at, :] = gelu.T
            bell = jnp.exp(-0.5 * act * act) * (1.0 / math.sqrt(2.0 * math.pi))
            slopes[:, at] = (below + act * bell).astype(jnp.bfloat16)
            return 0

        half = chunks // 2
        for part_of in range(2):
            lax.fori_loop(part_of * half, (part_of + 1) * half, activate, 0)
            at = pl.ds(part_of * half * chunk, half * chunk)
            keep(gelu_turned.at[at], gelu_out.at[at])
            keep(slopes.at[:, at], slope_out.at[:, at])

    def shrink_all():
        branch[...] = hidden[...] + line_of(5)

        wider = 2 * chunk

        def shrink(f, _):
            at = pl.ds(pl.multiple_of(f * wider, wider), wider)
            block = down_matrix[pl.ds(f * 2 * per_chunk, 2 * per_chunk)].reshape(wider, width)
            branch[...] += jnp.dot(gelu_low[:, at], block, preferred_element_type=jnp.float32)
            return 0

        lax.fori_loop(0, chunks // 2, shrink, 0)

    out.own_seq()
    down.own_chips()
    qkv.own_seq()
    vec.own_seq()
    up.own_chips()
    up.own_seq()
    out.along_seq(1)
    qkv.own_chips()
    vec.own_chips()
    qkv.along_seq(1)
    vec.along_seq(1)
    down.own_seq()
    up.along_seq(1)
    qkv.along_seq(2)
    vec.along_seq(2)
    up.along_seq(2)
    out.along_seq(2)
    line.own(x_ref)
    qkv.over_chips(0, 0)
    vec.over_chips(0, 0)
    out.over_chips(0, 1)
    up.over_chips(0, 0)
    qkv.over_chips(0, 2)
    vec.over_chips(0, 2)
    qkv.along_seq(3)
    vec.along_seq(3)
    up.over_chips(0, 1)
    up.along_seq(3)
    qkv.over_chips(0, 1)
    vec.over_chips(0, 1)
    qkv.over_chips(1, 0)
    vec.over_chips(1, 0)
    line.relay(1)
    line.relay(2)
    qkv.over_chips(0, 3)
    vec.over_chips(0, 3)
    up.over_chips(1, 1)
    line.end(1)
    down.along_seq(1)
    up.over_chips(0, 3)
    qkv.over_chips(1, 3)
    vec.over_chips(1, 3)
    qkv.over_chips(1, 2)
    vec.over_chips(1, 2)
    up.over_chips(0, 2)
    down.over_chips(0, 0)
    out.own_chips()
    qkv.over_chips(1, 1)
    vec.over_chips(1, 1)
    gathered_columns()
    up.over_chips(1, 0)
    line.relay(3)
    out.over_chips(0, 2)
    project(0)
    line.end(2)
    project(2)
    out.over_chips(0, 0)
    down.over_chips(0, 1)
    up.over_chips(1, 3)
    project(1)
    up.over_chips(1, 2)
    line.end(3)
    out.over_chips(1, 1)
    down.along_seq(2)
    project(3)
    prepare()
    attention(0)
    down.along_seq(3)
    attention(1)
    out.along_seq(3)
    attention(3)
    gathered_up()
    down.over_chips(0, 2)
    down.over_chips(1, 0)
    out.over_chips(0, 3)
    down.over_chips(0, 3)
    attention(2)
    out.over_chips(1, 0)
    out.over_chips(1, 3)
    turn_page()
    out.over_chips(1, 2)
    down.over_chips(1, 1)
    keep_logs()
    gathered_out()
    down.over_chips(1, 2)
    down.over_chips(1, 3)
    context_arrived()
    first_norm()
    expand()
    gathered_down()
    shrink_all()
    gain_one, gain_two = line_of(3), line_of(6)
    result, normed, inv = norm_forward(branch[...], gain_two, line_of(7))
    output[...] = result.astype(jnp.bfloat16)
    grad = cotangent[...].astype(jnp.float32)
    mid, grad_gain, grad_shift = norm_backward(grad, normed, inv, gain_two)
    grad_mid[...] = mid
    grad_bias = jnp.sum(mid.astype(jnp.bfloat16).astype(jnp.float32), axis=0)
    sums_out[...] = jnp.zeros_like(sums_out)
    for row, line_sum in enumerate((grad_bias, grad_gain, grad_shift)):
        sums_out[5 + row : 6 + row, :] = line_sum.reshape(1, width)
    sums_out[3:4, :] = gain_one
    for copy in keeps:
        copy.wait()
    w.drain()


def front(sizes, heads, valid, rows, cotangent, lines, up_line, w_qkv, w_out, w_up, w_down):
    n_dp, n_seq = sizes
    devices = n_dp * n_seq
    count, width = rows.shape
    part = width // n_seq
    stream = count * n_seq
    wide = w_up.shape[1]
    low = jnp.bfloat16
    head_dim = width // heads
    local_heads = heads // n_seq
    blocks = part // 128
    attention = (
        jax.ShapeDtypeStruct((local_heads, n_seq, count, 128), low),
        jax.ShapeDtypeStruct((blocks, stream, 256), low),
        jax.ShapeDtypeStruct((blocks, stream, 256), low),
        jax.ShapeDtypeStruct((local_heads, head_dim, stream), low),
    )

    def full(shard):
        return jax.ShapeDtypeStruct((devices,) + shard.shape, shard.dtype)

    anywhere = pl.BlockSpec(memory_space=pl.ANY)
    local = pl.BlockSpec(memory_space=pltpu.VMEM)
    sends = 5 * sends_of_gather(n_dp, n_seq) + 5 + n_seq - 1
    return pl.pallas_call(
        lambda *refs: front_kernel(sizes, heads, *refs),
        out_shape=(
            jax.ShapeDtypeStruct((devices, w_qkv.shape[0], 3 * part), low),
            full(w_out),
            full(w_up),
            full(w_down),
            jax.ShapeDtypeStruct((n_seq * width, count), low),
        )
        + attention
        + (
            jax.ShapeDtypeStruct((width, count), low),
            jax.ShapeDtypeStruct((n_seq, count, 128), jnp.float32),
            jax.ShapeDtypeStruct((n_seq, count, part), low),
            jax.ShapeDtypeStruct((width, count), low),
            jax.ShapeDtypeStruct((wide, count), low),
            jax.ShapeDtypeStruct((count, wide), low),
            jax.ShapeDtypeStruct((count, width), low),
            jax.ShapeDtypeStruct((count, width), jnp.float32),
            jax.ShapeDtypeStruct((count, 128), jnp.float32),
            jax.ShapeDtypeStruct((count, width), jnp.float32),
            jax.ShapeDtypeStruct((8, width), jnp.float32),
        ),
        in_specs=[
            pl.BlockSpec(memory_space=pltpu.SMEM),
        ]
        + [local] * 5
        + [anywhere] * 3,
        out_specs=[anywhere] * 15 + [local] + [anywhere] * 2 + [local] * 2,
        scratch_shapes=[
            pltpu.VMEM((16, 128), jnp.float32),
            pltpu.VMEM((n_seq, w_qkv.shape[0], 3 * part), low),
            pltpu.VMEM((devices, 16, 128), jnp.float32),
            pltpu.VMEM((devices, w_qkv.shape[0], 3 * part), low),
            pltpu.VMEM((n_seq, count, width), low),
            pltpu.VMEM((3, n_seq, count, part), low),
            pltpu.VMEM((n_seq, count, part), low),
            pltpu.VMEM((n_seq, count, part), low),
            pltpu.VMEM((n_seq, part, count), jnp.float32),
            pltpu.VMEM((part, stream), low),
        ]
        + [pltpu.VMEM(a.shape, a.dtype) for a in attention]
        + [
            pltpu.VMEM((8, count), jnp.float32),
            pltpu.VMEM((n_seq, count, 128), jnp.float32),
            pltpu.VMEM((count, width), jnp.float32),
            pltpu.VMEM((count, 128), jnp.float32),
            pltpu.VMEM((devices,) + w_out.shape, low),
            pltpu.VMEM((devices,) + w_up.shape, low),
            pltpu.VMEM((devices,) + w_down.shape, low),
            pltpu.VMEM((n_seq * width, count), low),
            pltpu.VMEM((width, count), low),
            pltpu.VMEM((count, width), jnp.float32),
            pltpu.VMEM((count, width), low),
            pltpu.VMEM((width, count), low),
            pltpu.VMEM((count, wide), low),
            pltpu.VMEM((wide, count), low),
            pltpu.VMEM((count, wide), low),
            pltpu.VMEM((count, width), jnp.float32),
            pltpu.SemaphoreType.DMA((sends,)),
            pltpu.SemaphoreType.DMA((5, n_dp, n_seq)),
            pltpu.SemaphoreType.DMA((n_seq,)),
            pltpu.SemaphoreType.DMA((n_seq,)),
            pltpu.SemaphoreType.DMA((40,)),
        ],
        compiler_params=pltpu.CompilerParams(
            collective_id=0, has_side_effects=True, vmem_limit_bytes=60 * 2**20
        ),
        name="front",
    )(valid, rows, cotangent, lines, up_line, w_qkv, w_out, w_up, w_down)


def add_rows(into, term):
    rows = into.shape[0]
    step = min(16, rows)

    def body(r, _):
        at = pl.ds(pl.multiple_of(r * step, step), step)
        total = into[at, :].astype(jnp.float32) + term[at, :].astype(jnp.float32)
        into[at, :] = total.astype(into.dtype)
        return 0

    lax.fori_loop(0, rows // step, body, 0)


class LineSum:
    def __init__(self, wires, block, last, sems):
        self.w, self.block, self.last, self.sems = wires, block, last, sems

    def into(self, src, index, device, when):
        self.w.send(src, self.last.at[index], self.sems.at[index], device, when)

    def add(self, k, index):
        def action():
            self.w.arrived(self.last.at[index], self.sems.at[index])
            add_rows(self.block(k), self.last.at[index])

        pl.when(self.w.inner)(action)

    def offer(self, k):
        self.into(self.block(k), k - 1, (self.w.dp, self.w.right), self.w.outer)

    def relay(self, k):
        w, block = self.w, self.block(k)
        if k == 1:
            self.add(1, 4)
            self.into(block, 3, (w.dp, w.left), w.inner)
        else:
            self.add(k, k - 1)
            self.into(block, 3 if k == 2 else 4, (w.dp, w.right), w.inner)

    def finish(self, start, out):
        w = self.w
        w.arrived(self.last.at[3], self.sems.at[3])
        w.arrived(self.last.at[0], self.sems.at[0], w.inner)
        rows = out.shape[0]
        step = min(16, rows)

        def total_of(count):
            def body(r, _):
                at = pl.ds(pl.multiple_of(r * step, step), step)
                total = start(at) + self.last[3, at, :].astype(jnp.float32)
                if count == 2:
                    total = total + self.last[0, at, :].astype(jnp.float32)
                out[at, :] = total.astype(out.dtype)
                return 0

            lax.fori_loop(0, rows // step, body, 0)

        pl.when(w.inner)(lambda: total_of(2))
        pl.when(w.outer)(lambda: total_of(1))


class Scatter:
    def __init__(self, wires, kind, make, source, stage, bufs, sems, out):
        self.w, self.kind, self.make, self.source, self.stage = wires, kind, make, source, stage
        self.total, self.first, self.second, self.last = bufs
        self.core_sems, self.first_sems, self.second_sems, self.last_sems = sems
        self.out = out
        self.n_seq = wires.sizes[1]
        self.offsets = [6, 2, 4, 0]
        self.lanes = self.total.shape[3] // 4
        self.staged = {}
        self.slots = wires.far if kind == "line" else wires.zs
        self.line = LineSum(wires, lambda k: self.total.at[0, self.slots[k]], self.last, self.last_sems)

    def block_lanes(self, q):
        return pl.ds(pl.multiple_of(q * self.lanes, self.lanes), self.lanes)

    def order(self, step):
        return (2, 4) if step % 2 == 0 else (4, 2)

    def give(self, k):
        o = self.offsets[k]
        d = self.w.dps[o ^ 1]
        if self.stage is None:
            src = self.source.at[pl.ds(d * self.n_seq, self.n_seq)]
        else:
            depth = self.stage.shape[0]
            if k >= depth:
                self.w.sent(self.staged[k - depth])
            src = self.stage.at[k % depth]

            def fill(q, _):
                at = self.block_lanes(q)
                src[:, :, at] = self.make(d, at).reshape(self.n_seq, -1, self.lanes).astype(src.dtype)
                return 0

            lax.fori_loop(0, 4, fill, 0)
        sem = self.core_sems.at[o // 2]
        self.staged[k] = self.w.send(src, self.total.at[o // 2], sem, self.w.peer(1, 0))

    def give_steps(self):
        return [lambda k=k: self.give(k) for k in range(4)]

    def over_cores(self, k):
        o = self.offsets[k]
        d = self.w.dps[o]
        self.w.arrived(self.total.at[o // 2], self.core_sems.at[o // 2])

        group = self.total.at[o // 2]

        def add(q, _):
            at = self.block_lanes(q)
            term = self.make(d, at).reshape(self.n_seq, -1, self.lanes)
            group[:, :, at] = (group[:, :, at].astype(jnp.float32) + term).astype(group.dtype)
            return 0

        if self.stage is None:
            for s in range(self.n_seq):
                add_rows(group.at[s], self.source.at[d * self.n_seq + s])
        else:
            lax.fori_loop(0, 4, add, 0)
        self.hand_on(k, (3, 2))

    def spread(self, k):
        self.hand_on(k, (1, 0))

    def hand_on(self, k, steps):
        o = self.offsets[k]
        for i in steps:
            mask = self.order(i)[0]
            block = self.total.at[o // 2, self.slots[i]]
            if o & mask:
                keep = (o ^ mask) // (6 ^ mask)
                self.w.send(block, self.first.at[i, keep], self.first_sems.at[i, keep], self.w.peer(mask, 0))

    def over_chips(self, i):
        mask = self.order(i)[1]
        for keep in (1, 0):
            o = mask * keep
            block = self.total.at[o // 2, self.slots[i]]
            self.w.arrived(self.first.at[i, keep], self.first_sems.at[i, keep])
            add_rows(block, self.first.at[i, keep])
            if keep:
                self.w.send(block, self.second.at[i], self.second_sems.at[i], self.w.peer(mask, 0))

    def to_seq(self, i):
        block = self.total.at[0, self.slots[i]]
        self.w.arrived(self.second.at[i], self.second_sems.at[i])
        add_rows(block, self.second.at[i])
        if self.kind == "line":
            if i:
                self.line.offer(i)
        elif i:
            self.w.send(block, self.last.at[i], self.last_sems.at[i], self.w.peer(0, i))

    def relay(self, i):
        self.line.relay(i)

    def finish(self):
        block = self.total.at[0, self.w.z]
        if self.kind == "line":
            self.line.finish(lambda at: block[at, :].astype(jnp.float32), self.out)
            return
        for i in range(1, self.n_seq):
            self.w.arrived(self.last.at[i], self.last_sems.at[i])
        if self.kind == "direct":
            total = block[...]
            for i in range(1, self.n_seq):
                total = total + self.last[i]
            lines, up_line = self.out
            up_line[...] = total[8:9, :]
            share = lines.shape[1]
            total = total[:8, :]
            shown = total[:, :share]
            for s in range(1, self.n_seq):
                shown = jnp.where(self.w.z == s, total[:, s * share : (s + 1) * share], shown)
            lines[...] = shown
            return
        for i in range(self.n_seq):
            term = block[...] if i == 0 else self.last[i]
            part = term.shape[1] // 3
            for t in range(3):
                at = t * part * self.n_seq + self.w.zs[i] * part
                self.out[:, pl.ds(pl.multiple_of(at, part), part)] = term[
                    :, t * part : (t + 1) * part
                ].astype(jnp.float32)


def back_kernel(sizes, heads, *refs):
    n_dp, n_seq = sizes
    (
        mid_in,
        normed_in,
        inv_in,
        sums_in,
        logs_in,
        page_in,
        query_in,
        key_in,
        value_in,
        key_turned_in,
        context_in,
        hidden_in,
        gelu_in,
        slope_in,
        own_context_in,
        columns_in,
        out_in,
        up_in,
        down_in,
        grad_rows,
        *outs,
    ) = refs[:26]
    scratch = list(refs[26:])

    def take(count):
        got = scratch[:count]
        del scratch[:count]
        return got

    send_sems, core_sems, first_sems, second_sems, last_sems, block_sems = take(6)
    head_sems, local_sems, row_sems = take(3)
    logs, own_context, grads, masked_query, keys, values, key_turned, masked_grad = take(8)
    query_lanes, query_grad, key_grad, value_grad = take(4)
    project, turned, columns, vec = take(4)
    row_terms, row_last, own_rows, partial = take(4)
    hidden_turned, context_turned, slopes, normed = take(4)
    grad_low, grad_sent, out_matrix, down_blocks, up_blocks = take(5)
    down_stage, up_stage, out_stage = take(3)
    units = [take(4) for k in range(5)]
    w = Wires(send_sems, sizes)
    rows, width = normed.shape
    part = width // n_seq
    wide = slopes.shape[1]
    head_dim = width // heads
    local_heads = heads // n_seq
    stream = rows * n_seq
    per_block = 128 // head_dim
    scale = 1.0 / math.sqrt(head_dim)
    loads = {}

    def load(name, src, dst):
        loads[name] = pltpu.make_async_copy(src, dst, local_sems.at[len(loads)])
        loads[name].start()

    load("mid", mid_in, own_rows)
    load("gelu", gelu_in, turned)
    load("slope", slope_in, slopes)
    blocks = []
    for f in range(n_dp):
        sem = block_sems.at[0, f % 2]
        blocks.append(pltpu.make_async_copy(down_in.at[pl.ds(f * n_seq, n_seq)], down_blocks.at[f % 2], sem))
    shares = wide // width
    half = up_in.shape[0] // 2
    ups = []
    for e in range(2 * shares):
        src = up_in.at[pl.ds(e // shares * half, half), :, pl.ds(e % shares * width, width)]
        ups.append(pltpu.make_async_copy(src, up_blocks.at[e % 2], block_sems.at[1, e % 2]))
    for e in range(2):
        blocks[e].start()
        ups[e].start()
    load("hidden", hidden_in, hidden_turned)
    load("normed", normed_in, normed)
    load("out", out_in, out_matrix)
    load("context", context_in, context_turned)
    load("logs", logs_in, logs)
    load("own", own_context_in, own_context)
    load("columns", columns_in, columns)
    load("query", query_in, masked_query)
    load("key", key_in, keys)
    load("value", value_in, values)
    load("turned", key_turned_in, key_turned)
    w.greet()

    def rows_from(source, first, count):
        return source[pl.ds(pl.multiple_of(first, count), count), :]

    def down_term(d, at):
        count = n_seq * outs[0].shape[0]
        return jnp.dot(
            rows_from(turned, d * count, count), grad_low[:, at], preferred_element_type=jnp.float32
        )

    def up_term(d, at):
        count = n_seq * outs[1].shape[0]
        return jnp.dot(
            rows_from(hidden_turned, d * count, count), slopes[:, at], preferred_element_type=jnp.float32
        )

    def out_term(d, at):
        count = n_seq * outs[2].shape[0]
        return jnp.dot(
            rows_from(context_turned, d * count, count), grad_low[:, at], preferred_element_type=jnp.float32
        )

    makes = (down_term, up_term, out_term, None, None)
    stages = (down_stage, up_stage, out_stage, None, None)
    scatters = []
    for k in range(5):
        scatters.append(
            Scatter(
                w,
                ("line", "line", "line", "columns", "direct")[k],
                makes[k],
                (None, None, None, partial, vec)[k],
                stages[k],
                units[k],
                (core_sems.at[k], first_sems.at[k], second_sems.at[k], last_sems.at[k]),
                outs[k] if k < 4 else outs[4:],
            )
        )
    down, up, out, qkv, small = scatters
    row_sum = LineSum(w, lambda k: row_terms.at[k - 1], row_last, row_sems)
    span = wide // n_dp

    def run(steps):
        for step in steps:
            step()

    low_lane = lax.broadcasted_iota(jnp.int32, (rows, 128), 1)

    def in_lanes(column, first, base):
        rest = -column
        for n in range(3):
            piece = rest.astype(jnp.bfloat16).astype(jnp.float32)
            base = jnp.where(low_lane == first + n, piece, base)
            rest = rest - piece
        return base.astype(jnp.bfloat16)

    def keep_line(row, line):
        for d in range(n_dp):
            for s in range(n_seq):
                vec[d * n_seq + s, row : row + 1, :] = line[:, d * 128 : (d + 1) * 128]

    def begin():
        loads["mid"].wait()
        grad_low[...] = own_rows[...].astype(jnp.bfloat16)
        loads["gelu"].wait()

    def slope_of(f):
        if f == 0:
            loads["slope"].wait()
        blocks[f].wait()
        grad_gelu = lax.dot_general(
            grad_low[...], down_blocks[f % 2].reshape(span, width), FLAT, preferred_element_type=jnp.float32
        )
        if f + 2 < n_dp:
            blocks[f + 2].start()
        at = slice(f * span, (f + 1) * span)
        slopes[:, at] = (grad_gelu * slopes[:, at].astype(jnp.float32)).astype(jnp.bfloat16)
        if f == n_dp - 1:
            loads["hidden"].wait()

    def hidden_of(e):
        ups[e].wait()
        columns_at = slice(e % shares * width, (e % shares + 1) * width)
        rows_at = slice(e // shares * width // 2, (e // shares + 1) * width // 2)
        own_rows[:, rows_at] += lax.dot_general(
            slopes[:, columns_at],
            up_blocks[e % 2].reshape(width // 2, width),
            FLAT,
            preferred_element_type=jnp.float32,
        )
        if e + 2 < 2 * shares:
            ups[e + 2].start()

    def norm_back():
        load("page", page_in, turned)
        loads["normed"].wait()
        first, grad_gain, grad_shift = norm_backward(
            own_rows[...], normed[...], inv_in[:, :1], sums_in[3:4, :]
        )
        own_rows[...] = first
        grad_low[...] = first.astype(jnp.bfloat16)
        vec[...] = jnp.zeros_like(vec)
        keep_line(3, grad_gain.reshape(1, width))
        keep_line(4, grad_shift.reshape(1, width))

    def send_grads():
        loads["out"].wait()
        for i in (1, 2, 3, 0):
            j = w.zs[i]
            share = part // out_matrix.shape[1]
            block = out_matrix[pl.ds(j * share, share)].reshape(part, width)
            piece = lax.dot_general(grad_low[...], block, FLAT, preferred_element_type=jnp.float32)
            if i:
                grad_sent[i] = piece.astype(jnp.bfloat16)
                w.send(grad_sent.at[i], grads.at[w.z], head_sems.at[i], w.peer(0, i))
            else:
                grads[w.z] = piece.astype(jnp.bfloat16)
        loads["context"].wait()

    def keep_lines():
        up_bias = jnp.sum(slopes[...].astype(jnp.float32), axis=0, keepdims=True)
        for d in range(n_dp * n_seq):
            vec[d, 8:9, :] = up_bias[:, d * 128 : (d + 1) * 128]
        keep_line(2, jnp.sum(grad_low[...].astype(jnp.float32), axis=0, keepdims=True))
        for row in (5, 6, 7):
            keep_line(row, sums_in[row : row + 1, :])

    def prepare():
        for name in ("columns", "logs", "own", "query", "key", "value", "turned"):
            loads[name].wait()
        key_grad[...] = jnp.zeros_like(key_grad)
        value_grad[...] = jnp.zeros_like(value_grad)

    def attention(i):
        c = w.zs[i]
        if i:
            w.arrived(grads.at[c], head_sems.at[i])
        one = jnp.where(low_lane == 0, 1.0, 0.0)
        for h in range(local_heads):
            block = h // per_block * 128
            grad = spread_head(grads.at[pl.ds(c, 1)], h, head_dim, 1.0)[0]
            centre = jnp.sum(
                grad.astype(jnp.float32) * own_context[i, :, block : block + 128].astype(jnp.float32),
                axis=1,
                keepdims=True,
            )
            masked_grad[h, :, :128] = grad
            masked_grad[h, :, 128:] = in_lanes(centre, 0, jnp.zeros_like(one))
            query_lanes[h] = in_lanes(logs[c, :, h : h + 1], 1, one)

        def head(h, _):
            block = h // per_block
            query, grad = masked_query[h, c], masked_grad[h, :, :128]
            scores = lax.dot_general(
                keys[block],
                jnp.concatenate([query, query_lanes[h]], axis=1),
                FLAT,
                preferred_element_type=jnp.float32,
            )
            probs = jnp.exp(scores)
            moved = lax.dot_general(values[block], masked_grad[h], FLAT, preferred_element_type=jnp.float32)
            slope = (probs * moved).astype(jnp.bfloat16)
            query_grad[h] = jnp.dot(key_turned[h], slope, preferred_element_type=jnp.float32) * scale
            key_grad[block] += jnp.dot(slope, query, preferred_element_type=jnp.float32)
            value_grad[block] += jnp.dot(
                probs.astype(jnp.bfloat16), grad, preferred_element_type=jnp.float32
            )
            return 0

        lax.fori_loop(0, local_heads, head, 0)
        project[pl.ds(pl.multiple_of(c * rows, rows), rows), :part] = (
            query_grad[...].reshape(part, rows).T.astype(jnp.bfloat16)
        )

    def keep_project():
        for t, total in ((1, key_grad), (2, value_grad)):
            for b in range(local_heads // per_block):
                at = t * part + b * 128
                project[:, at : at + 128] = total[b].astype(jnp.bfloat16)

    def row_term(k):
        term = lax.dot_general(
            rows_from(project, w.far[k] * rows, rows),
            columns[...].reshape(width, 3 * part),
            FLAT,
            preferred_element_type=jnp.float32,
        )
        if k:
            row_terms[k - 1] = term.astype(jnp.bfloat16)
            row_sum.offer(k)
        else:
            own_rows[...] += term

    def weight_grad():
        loads["page"].wait()
        for t in range(3):
            at = slice(t * part, (t + 1) * part)
            block = jnp.dot(turned[:width, :], project[:rows, at], preferred_element_type=jnp.float32)
            for s in range(1, n_seq):
                block = block + jnp.dot(
                    turned[s * width : (s + 1) * width, :],
                    project[s * rows : (s + 1) * rows, at],
                    preferred_element_type=jnp.float32,
                )
            partial[:, :, at] = block.astype(jnp.bfloat16).reshape(n_dp * n_seq, -1, part)

    def give_small():
        groups = part // 128
        for b, t in ((0, 0), (1, 2)):
            sums = jnp.sum(project[:, t * part : (t + 1) * part].astype(jnp.float32), axis=0, keepdims=True)
            for g in range(groups):
                for s in range(n_seq):
                    vec[(w.z * groups + g) * n_seq + s, b : b + 1, :] = sums[:, g * 128 : (g + 1) * 128]
        run(small.give_steps())

    begin()
    down.give(0)
    down.give(1)
    slope_of(0)
    slope_of(1)
    down.give(2)
    down.give(3)
    down.over_cores(0)
    slope_of(2)
    slope_of(3)
    hidden_of(0)
    hidden_of(1)
    down.over_cores(1)
    slope_of(4)
    down.over_cores(2)
    down.spread(0)
    slope_of(5)
    slope_of(6)
    slope_of(7)
    hidden_of(2)
    down.spread(2)
    hidden_of(3)
    hidden_of(4)
    hidden_of(5)
    down.over_cores(3)
    up.give(0)
    hidden_of(6)
    hidden_of(7)
    down.over_chips(3)
    norm_back()
    send_grads()
    down.over_chips(2)
    prepare()
    attention(0)
    down.over_chips(1)
    down.to_seq(3)
    attention(2)
    down.to_seq(2)
    attention(3)
    down.to_seq(1)
    attention(1)
    keep_project()
    row_term(3)
    down.spread(1)
    up.over_cores(0)
    up.spread(0)
    up.give(1)
    out.give(0)
    out.give(1)
    down.relay(2)
    out.give(2)
    up.give(2)
    up.give(3)
    down.relay(3)
    row_term(2)
    out.give(3)
    weight_grad()
    keep_lines()
    up.over_cores(2)
    up.over_cores(1)
    qkv.give(0)
    qkv.give(1)
    qkv.give(2)
    qkv.give(3)
    row_sum.relay(3)
    out.over_cores(0)
    up.over_cores(3)
    give_small()
    qkv.over_cores(2)
    small.over_cores(2)
    down.relay(1)
    qkv.over_cores(0)
    small.over_cores(0)
    qkv.spread(2)
    small.spread(2)
    qkv.spread(0)
    small.spread(0)
    row_term(1)
    qkv.over_cores(3)
    small.over_cores(3)
    up.over_chips(3)
    row_sum.relay(2)
    out.over_cores(2)
    qkv.over_cores(1)
    small.over_cores(1)
    up.over_chips(2)
    row_term(0)
    out.over_cores(3)
    row_sum.relay(1)
    qkv.spread(1)
    small.spread(1)
    qkv.over_chips(1)
    small.over_chips(1)
    up.spread(2)
    out.spread(0)
    up.to_seq(3)
    out.over_cores(1)
    out.spread(2)
    up.to_seq(2)
    out.over_chips(3)
    qkv.over_chips(2)
    small.over_chips(2)
    qkv.to_seq(1)
    small.to_seq(1)
    up.over_chips(1)
    up.relay(3)
    qkv.over_chips(0)
    small.over_chips(0)
    out.over_chips(2)
    up.spread(1)
    down.over_chips(0)
    out.to_seq(3)
    out.to_seq(2)
    up.relay(2)
    out.over_chips(1)
    qkv.to_seq(0)
    small.to_seq(0)
    row_sum.finish(lambda at: own_rows[at, :], grad_rows)
    qkv.to_seq(2)
    small.to_seq(2)
    out.spread(1)
    up.to_seq(1)
    up.relay(1)
    qkv.over_chips(3)
    small.over_chips(3)
    up.over_chips(0)
    out.relay(3)
    out.over_chips(0)
    out.to_seq(1)
    out.relay(1)
    down.to_seq(0)
    down.finish()
    out.relay(2)
    qkv.to_seq(3)
    small.to_seq(3)
    up.to_seq(0)
    up.finish()
    qkv.finish()
    small.finish()
    out.to_seq(0)
    out.finish()
    w.drain()


def back(sizes, heads, saved, w_shapes):
    n_dp, n_seq = sizes
    devices = n_dp * n_seq
    mid, normed, _, _, logs, page, query, key, value, key_turned, context, hidden, gelu, slopes, own_context = saved[:15]
    columns, full_out, full_up, full_down = saved[15:]
    count, width = normed.shape
    part = width // n_seq
    stream = count * n_seq
    local_heads, head_dim, _ = key_turned.shape
    blocks = part // 128
    low = jnp.bfloat16
    shapes = [w_shapes[0], w_shapes[1], w_shapes[2], columns.shape[1:], (16, 128)]
    kinds = [low] * 4 + [jnp.float32]
    results = [jax.ShapeDtypeStruct(shape, jnp.float32) for shape in shapes]
    results[3] = jax.ShapeDtypeStruct((shapes[3][0], n_seq * shapes[3][1]), jnp.float32)
    results[4:] = [
        jax.ShapeDtypeStruct((8, width // devices), jnp.float32),
        jax.ShapeDtypeStruct((1, 128), jnp.float32),
    ]
    anywhere = pl.BlockSpec(memory_space=pl.ANY)
    local = pl.BlockSpec(memory_space=pltpu.VMEM)
    sends = 5 * (4 + 3 * n_seq + 6) + 6 + n_seq - 1
    chips = n_dp // 2

    def like(array):
        return pltpu.VMEM(array.shape, array.dtype)

    scratch = [
        pltpu.SemaphoreType.DMA((sends,)),
        pltpu.SemaphoreType.DMA((5, chips)),
        pltpu.SemaphoreType.DMA((5, n_seq, 2)),
        pltpu.SemaphoreType.DMA((5, n_seq)),
        pltpu.SemaphoreType.DMA((5, 5)),
        pltpu.SemaphoreType.DMA((2, 2)),
        pltpu.SemaphoreType.DMA((n_seq,)),
        pltpu.SemaphoreType.DMA((15,)),
        pltpu.SemaphoreType.DMA((5,)),
        like(logs),
        like(own_context),
        pltpu.VMEM((n_seq, count, part), low),
        like(query),
        like(key),
        like(value),
        like(key_turned),
        pltpu.VMEM((local_heads, count, 256), low),
        pltpu.VMEM((local_heads, count, 128), low),
        pltpu.VMEM((local_heads, head_dim, count), jnp.float32),
        pltpu.VMEM((blocks, stream, 128), jnp.float32),
        pltpu.VMEM((blocks, stream, 128), jnp.float32),
        pltpu.VMEM((stream, 3 * part), low),
        like(gelu),
        like(columns),
        pltpu.VMEM((devices, 16, 128), jnp.float32),
        pltpu.VMEM((n_seq - 1, count, width), low),
        pltpu.VMEM((5, count, width), low),
        pltpu.VMEM((count, width), jnp.float32),
        like(columns),
        like(hidden),
        like(context),
        like(slopes),
        like(normed),
        pltpu.VMEM((count, width), low),
        pltpu.VMEM((n_seq, count, part), low),
        like(full_out),
        pltpu.VMEM((2, n_seq) + shapes[0], low),
        pltpu.VMEM((2, devices // 2, full_up.shape[1], width), low),
        pltpu.VMEM((2, n_seq) + shapes[0], low),
        pltpu.VMEM((2, n_seq) + shapes[1], low),
        pltpu.VMEM((2, n_seq) + shapes[2], low),
    ]
    for shape, kind in zip(shapes, kinds):
        scratch += [
            pltpu.VMEM((chips, n_seq) + shape, kind),
            pltpu.VMEM((n_seq, 2) + shape, kind),
            pltpu.VMEM((n_seq,) + shape, kind),
            pltpu.VMEM((5,) + shape, kind),
        ]
    return pl.pallas_call(
        lambda *refs: back_kernel(sizes, heads, *refs),
        out_shape=[jax.ShapeDtypeStruct((count, width), low)] + results,
        in_specs=[anywhere] * 2 + [local] * 2 + [anywhere] * 15,
        out_specs=[local] * 7,
        scratch_shapes=scratch,
        compiler_params=pltpu.CompilerParams(
            collective_id=1, has_side_effects=True, vmem_limit_bytes=63 * 2**20
        ),
        name="back",
    )(*saved)


def kernel_plan(
    x_in,
    w_qkv,
    q_bias,
    v_bias,
    w_out,
    out_bias,
    ln1_gain,
    ln1_shift,
    w_up,
    up_bias,
    w_down,
    down_bias,
    ln2_gain,
    ln2_shift,
    valid,
    cotangent,
):
    sizes = (lax.axis_size("dp"), lax.axis_size("seq"))
    n_dp, groups = sizes
    rows = x_in[0]
    count, width = rows.shape
    vectors = (q_bias, v_bias, out_bias, ln1_gain, ln1_shift, down_bias, ln2_gain, ln2_shift)
    lines = jnp.stack(vectors)
    (
        columns,
        full_out,
        full_up,
        full_down,
        page_turned,
        query,
        key,
        value,
        key_turned,
        context,
        logs,
        own_context,
        hidden,
        gelu,
        slopes,
        output,
        normed,
        inv,
        grad_mid,
        line_sums,
    ) = front(sizes, HEADS, valid, rows, cotangent[0], lines, up_bias[None], w_qkv, w_out, w_up, w_down)
    saved = (grad_mid, normed, inv, line_sums, logs, page_turned, query, key, value, key_turned)
    saved += (context, hidden, gelu, slopes, own_context, columns, full_out, full_up, full_down)
    devices = n_dp * groups
    grad_rows, *sums = back(sizes, HEADS, saved, (w_down.shape, w_up.shape, w_out.shape))
    mine = sums[4]
    return (
        output[None],
        grad_rows[None],
        sums[3],
        mine[0],
        mine[1],
        sums[2],
        mine[2],
        mine[3],
        mine[4],
        sums[1],
        sums[5].reshape(-1),
        sums[0],
        mine[5],
        mine[6],
        mine[7],
    )


def solution(mesh):
    n_dp, n_seq = mesh.shape["dp"], mesh.shape["seq"]

    def per_device(x_in, w_qkv, *rest):
        part, width = w_qkv.shape[0], x_in.shape[2]
        fits = (n_dp, n_seq) == (8, 4) and part % 32 == 0 and part * n_seq == 128 and width // n_seq % 128 == 0 and x_in.shape[0] == 1
        plan = kernel_plan if fits else general_plan
        return plan(x_in, w_qkv, *rest)

    return jax.shard_map(
        per_device,
        mesh=mesh,
        in_specs=(
            P("dp", "seq", None),
            P(("dp", "seq"), None),
            P(("dp", "seq")),
            P(("dp", "seq")),
            P(("dp", "seq"), None),
            P(("dp", "seq")),
            P(("dp", "seq")),
            P(("dp", "seq")),
            P(("dp", "seq"), None),
            P(("dp", "seq")),
            P(("dp", "seq"), None),
            P(("dp", "seq")),
            P(("dp", "seq")),
            P(("dp", "seq")),
            P("dp"),
            P("dp", "seq", None),
        ),
        out_specs=(
            P("dp", "seq", None),
            P("dp", "seq", None),
            P(("dp", "seq"), None),
            P(("dp", "seq")),
            P(("dp", "seq")),
            P(("dp", "seq"), None),
            P(("dp", "seq")),
            P(("dp", "seq")),
            P(("dp", "seq")),
            P(("dp", "seq"), None),
            P(("dp", "seq")),
            P(("dp", "seq"), None),
            P(("dp", "seq")),
            P(("dp", "seq")),
            P(("dp", "seq")),
        ),
        check_vma=False,
    )
```
